32 devices in a mesh: dp: 2 (over x), row: 4 (over z), col: 4 (over y, core).
Axes of the slice: x: 2, y: 2, z: 4, core: 2. Of those that a mesh axis runs over, the one named last changes fastest.
Arguments:
- hidden_in: bfloat16 [8192, 1024], P(('dp', 'col'), 'row'), may hold values from -6 to 6
- out_grad: bfloat16 [8192, 1024], P(('dp', 'col'), 'row'), may hold values from -6 to 6
- first_norm_gain: bfloat16 [1024], P('row'), may hold values from 0.099609375 to 1.8984375
- first_norm_bias: bfloat16 [1024], P('row'), may hold values from -1.5 to 1.5
- qkv_weight: bfloat16 [1024, 3072], P('row', 'col'), may hold values from -0.1875 to 0.1875
- qkv_bias: bfloat16 [3072], replicated, may hold values from -1.5 to 1.5
- proj_weight: bfloat16 [1024, 1024], P('col', 'row'), may hold values from -0.375 to 0.375
- proj_bias: bfloat16 [1024], P('row'), may hold values from -1.5 to 1.5
- second_norm_gain: bfloat16 [1024], P('row'), may hold values from 0.099609375 to 1.8984375
- second_norm_bias: bfloat16 [1024], P('row'), may hold values from -1.5 to 1.5
- fc1_weight: bfloat16 [1024, 4096], P('row', 'col'), may hold values from -0.1875 to 0.1875
- fc1_bias: bfloat16 [4096], replicated, may hold values from -1.5 to 1.5
- fc2_weight: bfloat16 [4096, 1024], P('col', 'row'), may hold values from -0.09375 to 0.09375
- second_feed_bias: bfloat16 [1024], P('row'), may hold values from -1.5 to 1.5
- qkv_reduce: bfloat16 [8, 1024, 16], P(None, 'row'), may hold values from -0.1875 to 0.1875
- qkv_expand: bfloat16 [8, 16, 3072], replicated, may hold values from -0.5 to 0.5
- proj_reduce: bfloat16 [8, 1024, 16], P(None, 'col'), may hold values from -0.1875 to 0.1875
- proj_expand: bfloat16 [8, 16, 1024], P(None, None, 'row'), may hold values from -0.5 to 0.5
- fc1_reduce: bfloat16 [8, 1024, 16], P(None, 'row'), may hold values from -0.1875 to 0.1875
- fc1_expand: bfloat16 [8, 16, 4096], replicated, may hold values from -0.5 to 0.5
- fc2_reduce: bfloat16 [8, 4096, 16], P(None, 'col'), may hold values from -0.09375 to 0.09375
- fc2_expand: bfloat16 [8, 16, 1024], P(None, None, 'row'), may hold values from -0.5 to 0.5
- adapter_choice: int32 [4], P('dp'), may hold values from 0 to 7
- cont_prompt: int32 [32], P('dp'), may hold values from 0 to 3, as said below
Outputs:
- hidden_out: bfloat16 [8192, 1024], P(('dp', 'col'), 'row')
- input_gradient: float32 [8192, 1024], P(('dp', 'col'), 'row')
- qkv_reduce_grad: float32 [8, 1024, 16], replicated
- qkv_expand_grad: float32 [8, 16, 3072], replicated
- proj_reduce_grad: float32 [8, 1024, 16], replicated
- proj_expand_grad: float32 [8, 16, 1024], replicated
- fc1_reduce_grad: float32 [8, 1024, 16], replicated
- fc1_expand_grad: float32 [8, 16, 4096], replicated
- fc2_reduce_grad: float32 [8, 4096, 16], replicated
- fc2_expand_grad: float32 [8, 16, 1024], replicated
The draws below stay inside these ranges and needn't reach their ends.
Inputs may be any that keep to these rules, and one draw needn't show every extreme that they name: Continuation j belongs to one of the 2 groups whose rows lie in the same run as its own rows: cont_prompt[j] // 2 == j // 16. Every group has exactly 8 continuations. The last continuation of each run belongs to the first group of that run.
All inputs are finite; a program needn't handle non-finite values.
Results may differ from the reference program's by a relative error of at most 0.02.
Values may be sent and summed in bfloat16 or wider, within the bound.
No kernel may reach another device: no remote copies, remote signals or barrier semaphores. Data moves between devices by JAX's collectives and lax.ppermute only.
A program may use at most 128 MiB of HBM per device.

```python
import jax
import jax.numpy as jnp
from jax import lax

D = 1024
HEADS = 16
HEAD = 64
FF = 4096
ADAPTER_RANK = 16
ADAPTER_COUNT = 8
PROMPT = 1024
CONT = 128
NCONT = 8
GROUPS_DEV = 2
GROUP_TOK = 2048
GROUPS = 4
TOKENS = 8192


def block_owners(single):
    count = GROUPS_DEV * NCONT
    owners = jax.random.permutation(single, count).astype(jnp.int32) // NCONT
    first_zero = jnp.argmax(owners == 0).astype(jnp.int32)
    last_value = owners[count - 1]
    owners = owners.at[first_zero].set(last_value)
    owners = owners.at[count - 1].set(0)
    return owners.astype(jnp.int32)


def draw_cont_prompt(key, part):
    blocks = GROUPS // GROUPS_DEV
    keys = jax.random.split(jax.random.fold_in(key, 7), blocks)
    owners = jax.vmap(block_owners)(keys) + (jnp.arange(blocks, dtype=jnp.int32) * GROUPS_DEV)[:, None]
    return owners.reshape(GROUPS * NCONT).astype(jnp.int32)


def touch_ends(result, key, smallest, largest):
    longest = result.shape.index(max(result.shape))
    spots = []
    for shift in (0, 1):
        where = [jax.random.randint(jax.random.fold_in(key, axis), (), 0, length) for axis, length in enumerate(result.shape)]
        where[longest] = (where[longest] + shift) % result.shape[longest]
        spots.append(tuple(where))
    return result.at[spots[0]].set(smallest).at[spots[1]].set(largest)


def shard_levels(own_key, shape, cuts, least, largest):
    level, own = 1.0, jax.random.fold_in(own_key, 6)
    for axis_at, blocks in cuts:
        steps = jnp.exp(jax.random.uniform(jax.random.fold_in(own, axis_at), (blocks,), jnp.float32, least / len(cuts), largest / len(cuts)))
        level = level * jnp.repeat(steps, shape[axis_at] // blocks).reshape([-1 if axis == axis_at else 1 for axis in range(len(shape))])
    return level


def scatter_about(own_key, dims, scale, limit, cuts=(), kind=jnp.bfloat16):
    array = jax.random.normal(own_key, dims, jnp.float32) * scale
    if len(cuts) > 0:
        array = shard_levels(own_key, dims, cuts, -0.22, 0.18) * array
    return jnp.clip(array, min=-limit, max=limit).astype(kind)


def setup_inputs(seed: int = 0) -> dict:
    arg_keys = jax.random.split(jax.random.key(seed), 25)
    hidden_in = scatter_about(arg_keys[0], (TOKENS, D), 1.0, 6.0, ((0, 8), (1, 4)))
    out_grad = scatter_about(arg_keys[1], (TOKENS, D), 1.0, 6.0, ((0, 8), (1, 4)))
    first_norm_gain = jnp.clip(1.0 + 0.18 * jax.random.normal(arg_keys[2], (D,), jnp.float32), 0.099609375, 1.8984375).astype(jnp.bfloat16)
    first_norm_bias = scatter_about(arg_keys[3], (D,), 0.3, 1.5, ((0, 4),))
    qkv_weight = scatter_about(arg_keys[4], (D, 3 * D), D ** -0.5, 0.1875, ((0, 4), (1, 4)))
    qkv_bias = scatter_about(arg_keys[5], (3 * D,), 0.3, 1.5)
    proj_weight = scatter_about(arg_keys[6], (D, D), (D // 4) ** -0.5, 0.375, ((0, 4), (1, 4)))
    proj_bias = scatter_about(arg_keys[7], (D,), 0.3, 1.5, ((0, 4),))
    second_norm_gain = jnp.clip(1.0 + 0.18 * jax.random.normal(arg_keys[8], (D,), jnp.float32), 0.099609375, 1.8984375).astype(jnp.bfloat16)
    second_norm_bias = scatter_about(arg_keys[9], (D,), 0.3, 1.5, ((0, 4),))
    fc1_weight = scatter_about(arg_keys[10], (D, FF), D ** -0.5, 0.1875, ((0, 4), (1, 4)))
    fc1_bias = scatter_about(arg_keys[11], (FF,), 0.3, 1.5)
    fc2_weight = scatter_about(arg_keys[12], (FF, D), FF ** -0.5, 0.09375, ((0, 4), (1, 4)))
    second_feed_bias = scatter_about(arg_keys[13], (D,), 0.3, 1.5, ((0, 4),))
    qkv_reduce = scatter_about(arg_keys[14], (ADAPTER_COUNT, D, ADAPTER_RANK), D ** -0.5, 0.1875, ((1, 4),))
    qkv_expand = scatter_about(arg_keys[15], (ADAPTER_COUNT, ADAPTER_RANK, 3 * D), (ADAPTER_RANK * 8) ** -0.5, 0.5)
    proj_reduce = scatter_about(arg_keys[16], (ADAPTER_COUNT, D, ADAPTER_RANK), D ** -0.5, 0.1875, ((1, 4),))
    proj_expand = scatter_about(arg_keys[17], (ADAPTER_COUNT, ADAPTER_RANK, D), (ADAPTER_RANK * 8) ** -0.5, 0.5, ((2, 4),))
    fc1_reduce = scatter_about(arg_keys[18], (ADAPTER_COUNT, D, ADAPTER_RANK), D ** -0.5, 0.1875, ((1, 4),))
    fc1_expand = scatter_about(arg_keys[19], (ADAPTER_COUNT, ADAPTER_RANK, FF), (ADAPTER_RANK * 8) ** -0.5, 0.5)
    fc2_reduce = scatter_about(arg_keys[20], (ADAPTER_COUNT, FF, ADAPTER_RANK), FF ** -0.5, 0.09375, ((1, 4),))
    fc2_expand = scatter_about(arg_keys[21], (ADAPTER_COUNT, ADAPTER_RANK, D), (ADAPTER_RANK * 8) ** -0.5, 0.5, ((2, 4),))
    adapter_choice = touch_ends(jax.random.randint(arg_keys[22], (GROUPS,), 0, ADAPTER_COUNT), jax.random.fold_in(arg_keys[22], 1), 0, ADAPTER_COUNT - 1).astype(jnp.int32)
    cont_prompt = draw_cont_prompt(jax.random.fold_in(arg_keys[24], 71), 0)
    return dict(hidden_in=hidden_in, out_grad=out_grad, first_norm_gain=first_norm_gain, first_norm_bias=first_norm_bias, qkv_weight=qkv_weight, qkv_bias=qkv_bias, proj_weight=proj_weight, proj_bias=proj_bias, second_norm_gain=second_norm_gain, second_norm_bias=second_norm_bias, fc1_weight=fc1_weight, fc1_bias=fc1_bias, fc2_weight=fc2_weight, second_feed_bias=second_feed_bias, qkv_reduce=qkv_reduce, qkv_expand=qkv_expand, proj_reduce=proj_reduce, proj_expand=proj_expand, fc1_reduce=fc1_reduce, fc1_expand=fc1_expand, fc2_reduce=fc2_reduce, fc2_expand=fc2_expand, adapter_choice=adapter_choice, cont_prompt=cont_prompt)


@jax.custom_vjp
def low(v):
    return lax.optimization_barrier(v.astype(jnp.bfloat16)).astype(jnp.float32)

@jax.custom_vjp
def low_back(v):
    return v

def low_keep(v):
    return (low(v), None)

def low_pass(kept, grad):
    return (grad,)

def back_keep(v):
    return (v, None)

def back_low(kept, grad):
    return (low(grad),)
low.defvjp(low_keep, low_pass)
low_back.defvjp(back_keep, back_low)
EPSILON = 1e-05
ADAPTER_SCALE = 2.0
MASKED = -1000000000.0

def matrix_multiply(left, right):
    return jnp.dot(left, right, precision=lax.Precision.HIGHEST, preferred_element_type=jnp.float32)

def layer_norm(values, gain, shift):
    mean = lax.optimization_barrier(jnp.mean(values, axis=-1, keepdims=True))
    var = lax.optimization_barrier(jnp.mean((values - mean) ** 2, axis=-1, keepdims=True))
    return (values - mean) * lax.rsqrt(var + EPSILON) * gain + shift

def adapted(values, reduce_mat, expand_matrix, one_hot_choice):
    count = values.shape[0]
    wide = jnp.transpose(reduce_mat, (1, 0, 2)).reshape(reduce_mat.shape[1], ADAPTER_COUNT * ADAPTER_RANK)
    chosen = lax.optimization_barrier(jnp.sum(matrix_multiply(values, wide).reshape(count, ADAPTER_COUNT, ADAPTER_RANK) * one_hot_choice[:, :, None], axis=1))
    chosen = low(low_back(chosen))
    spread_out = (one_hot_choice[:, :, None] * chosen[:, None, :]).reshape(count, ADAPTER_COUNT * ADAPTER_RANK)
    return ADAPTER_SCALE * matrix_multiply(spread_out, expand_matrix.reshape(ADAPTER_COUNT * ADAPTER_RANK, expand_matrix.shape[2]))

def token_rows(cont_prompt):
    order = jnp.argsort(cont_prompt, stable=True).astype(jnp.int32)
    per_block = GROUPS_DEV * NCONT
    block_of = order // per_block
    local = order % per_block
    starts = block_of * (GROUPS_DEV * GROUP_TOK) + GROUPS_DEV * PROMPT + local * CONT
    cont_rows = (starts[:, None] + jnp.arange(CONT, dtype=jnp.int32)[None, :]).reshape(GROUPS, NCONT * CONT)
    groups = jnp.arange(GROUPS, dtype=jnp.int32)
    prompt_starts = groups // GROUPS_DEV * (GROUPS_DEV * GROUP_TOK) + groups % GROUPS_DEV * PROMPT
    prompt_rows = prompt_starts[:, None] + jnp.arange(PROMPT, dtype=jnp.int32)[None, :]
    return jnp.concatenate([prompt_rows, cont_rows], axis=1).astype(jnp.int32)

def group_layout():
    index = jnp.arange(GROUP_TOK, dtype=jnp.int32)
    later = index - PROMPT
    is_prompt = index < PROMPT
    segment = jnp.where(is_prompt, -1, later // CONT)
    place = jnp.where(is_prompt, index, PROMPT + later % CONT)
    after = place[None, :] <= place[:, None]
    from_prompt = (segment[None, :] < 0) & ((segment[:, None] >= 0) | after)
    same = (segment[None, :] >= 0) & (segment[None, :] == segment[:, None]) & after
    distance = (place[:, None] - place[None, :]).astype(jnp.float32)
    return (from_prompt | same, distance)

def group_attention(block, allowed, distance, slopes):
    parts = block.reshape(GROUP_TOK, HEADS, 3, HEAD)
    query = jnp.transpose(parts[:, :, 0], (1, 0, 2))
    keys = jnp.transpose(parts[:, :, 1], (1, 0, 2))
    vals = jnp.transpose(parts[:, :, 2], (1, 0, 2))
    scores = jnp.einsum('hqd,hkd->hqk', query, keys, precision=lax.Precision.HIGHEST) * HEAD ** (-0.5)
    scores = scores - slopes[:, None, None] * distance[None, :, :]
    scores = low_back(scores)
    scores = jnp.where(allowed[None, :, :], scores, MASKED)
    top = lax.optimization_barrier(jnp.max(scores, axis=-1, keepdims=True))
    weights = jnp.exp(scores - top)
    probs = low(weights / lax.optimization_barrier(jnp.sum(weights, axis=-1, keepdims=True)))
    out = jnp.einsum('hqk,hkd->hqd', probs, vals, precision=lax.Precision.HIGHEST)
    return jnp.transpose(out, (1, 0, 2)).reshape(GROUP_TOK, HEADS * HEAD)

def widen_out(values):
    return values.astype(jnp.float32)

def reference(hidden_in, out_grad, first_norm_gain, first_norm_bias, qkv_weight, qkv_bias, proj_weight, proj_bias, second_norm_gain, second_norm_bias, fc1_weight, fc1_bias, fc2_weight, second_feed_bias, qkv_reduce, qkv_expand, proj_reduce, proj_expand, fc1_reduce, fc1_expand, fc2_reduce, fc2_expand, adapter_choice, cont_prompt):
    rows = token_rows(cont_prompt)
    flat_rows = rows.reshape(GROUPS * GROUP_TOK)
    owner = jnp.zeros((TOKENS,), jnp.int32).at[flat_rows].set(jnp.repeat(jnp.arange(GROUPS, dtype=jnp.int32), GROUP_TOK))
    token_adapter = adapter_choice[owner]
    one_hot_choice = (token_adapter[:, None] == jnp.arange(ADAPTER_COUNT, dtype=jnp.int32)[None, :]).astype(jnp.float32)
    allowed, distance = group_layout()
    slopes = jnp.exp2(-8.0 * jnp.arange(1, HEADS + 1).astype(jnp.float32) / HEADS)
    g1, c1, g2, c2 = (widen_out(first_norm_gain), widen_out(first_norm_bias), widen_out(second_norm_gain), widen_out(second_norm_bias))
    w_qkv, b_qkv, w_proj, b_proj = (widen_out(qkv_weight), widen_out(qkv_bias), widen_out(proj_weight), widen_out(proj_bias))
    w_one, b_one, w_two, b_two = (widen_out(fc1_weight), widen_out(fc1_bias), widen_out(fc2_weight), widen_out(second_feed_bias))

    def attend(block):
        return group_attention(block, allowed, distance, slopes)

    def forward(input_rows, q_red, q_exp, p_red, p_exp, one_red, one_exp, two_red, two_exp):
        xn1 = low(layer_norm(input_rows, g1, c1))
        qkv = matrix_multiply(xn1, w_qkv) + b_qkv + adapted(xn1, q_red, q_exp, one_hot_choice)
        qkv = low(low_back(qkv))
        grouped = qkv[flat_rows].reshape(GROUPS, GROUP_TOK, 3 * D)
        mapped = lax.map(jax.checkpoint(attend), grouped)
        heads = jnp.zeros((TOKENS, D), jnp.float32).at[flat_rows].set(mapped.reshape(GROUPS * GROUP_TOK, D))
        heads = low(low_back(heads))
        attn_branch = low_back(matrix_multiply(heads, w_proj) + b_proj + adapted(heads, p_red, p_exp, one_hot_choice))
        middle_values = input_rows + attn_branch
        xn2 = low(layer_norm(middle_values, g2, c2))
        preactivation = low_back(matrix_multiply(xn2, w_one) + b_one + adapted(xn2, one_red, one_exp, one_hot_choice))
        act = low(jax.nn.gelu(preactivation, approximate=True))
        mlp_branch = low_back(matrix_multiply(act, w_two) + b_two + adapted(act, two_red, two_exp, one_hot_choice))
        return middle_values + mlp_branch
    out, pull = jax.vjp(forward, widen_out(hidden_in), widen_out(qkv_reduce), widen_out(qkv_expand), widen_out(proj_reduce), widen_out(proj_expand), widen_out(fc1_reduce), widen_out(fc1_expand), widen_out(fc2_reduce), widen_out(fc2_expand))
    grads = pull(widen_out(out_grad))
    return (out.astype(jnp.bfloat16), grads[0], grads[1], grads[2], grads[3], grads[4], grads[5], grads[6], grads[7], grads[8])
```

```python
import jax
import jax.numpy as jnp
from jax import lax
from jax.experimental import pallas as pl
from jax.experimental.pallas import tpu as pltpu
from jax.sharding import PartitionSpec as P

D = 1024
HEADS = 16
HEAD = 64
FF = 4096
RANK = 16
COUNT = 8
PROMPT = 1024
CONT = 128
NCONT = 8
GROUPS_DEV = 2

EPSILON = 1e-05
SCALE = 2.0
GELU_A = 0.7978845608028654
GELU_B = 0.044715
ROWS = 4
COLS = 4
TOK = 256
BLOCK = 128
LOW = -1e30

BF = jnp.bfloat16
F32 = jnp.float32

VM = pl.BlockSpec(memory_space=pltpu.VMEM)
SM = pl.BlockSpec(memory_space=pltpu.SMEM)

CORE_SWAP = [(0, 1), (1, 0), (2, 3), (3, 2)]
Y_SWAP = [(0, 2), (2, 0), (1, 3), (3, 1)]
Z_SWAP = [(0, 1), (1, 0), (2, 3), (3, 2)]


def nn(a, b):
    return lax.dot_general(a, b, (((1,), (0,)), ((), ())), preferred_element_type=F32)


def nt(a, b):
    return lax.dot_general(a, b, (((1,), (1,)), ((), ())), preferred_element_type=F32)


def tn(a, b):
    return lax.dot_general(a, b, (((0,), (0,)), ((), ())), preferred_element_type=F32)


def f32(v):
    return v.astype(F32)


def bf(v):
    return v.astype(BF)


def call(body, outs, ins, scratch=(), smem=1, limit=48, flops=0, name=None):
    nbytes = sum(v.size * v.dtype.itemsize for v in ins)
    nbytes += sum(o.size * o.dtype.itemsize for o in outs)
    return pl.pallas_call(
        body,
        out_shape=tuple(outs),
        in_specs=[SM] * smem + [VM] * (len(ins) - smem),
        out_specs=tuple([VM] * len(outs)),
        scratch_shapes=list(scratch),
        compiler_params=pltpu.CompilerParams(vmem_limit_bytes=limit << 20),
        cost_estimate=pl.CostEstimate(flops=flops, bytes_accessed=nbytes, transcendentals=0),
        name=name,
    )(*ins)


def out(shape, dtype):
    return jax.ShapeDtypeStruct(shape, dtype)


def block_at(zl, c, j):
    return c * 4 + zl + j * (3 - 2 * zl)


def fill_order(cont, base, order):
    first = jnp.int32(0)
    second = jnp.int32(NCONT)
    for j in range(GROUPS_DEV * NCONT):
        own = cont[j] == base
        slot = jnp.where(own, first, second)
        order[slot] = jnp.int32(j)
        first = first + jnp.where(own, 1, 0)
        second = second + jnp.where(own, 0, 1)


def place_of(info, order, z, core, j):
    prompt = (z // 2) * 8 + block_at(lax.rem(z, 2), core, j)
    cont = order[4 * z + 2 * core + j]
    return jnp.where(info[1] == 0, prompt, cont)


def route_body(info, cont, own, oth, o0, o1, o2, o3, order):
    fill_order(cont, info[3], order)
    c = info[2]
    for s, dst in enumerate((o0, o1, o2, o3)):
        z = lax.rem(info[0] + s, ROWS)
        for j in range(2):
            src = place_of(info, order, z, c, j)
            at = pl.ds(pl.multiple_of(lax.rem(src, 8) * BLOCK, BLOCK), BLOCK)
            mine = src // 8 == c

            @pl.when(mine)
            def _():
                dst[pl.ds(j * BLOCK, BLOCK), :] = own[at, :]

            @pl.when(jnp.logical_not(mine))
            def _():
                dst[pl.ds(j * BLOCK, BLOCK), :] = oth[at, :]


def unroute_body(info, cont, a0, a1, a2, a3, b0, b1, b2, b3, dst, order):
    fill_order(cont, info[3], order)
    c = info[2]
    for s in range(ROWS):
        z = lax.rem(info[0] + s, ROWS)
        for other, src in ((0, (a0, a1, a2, a3)[s]), (1, (b0, b1, b2, b3)[s])):
            core = c if other == 0 else 1 - c
            for j in range(2):
                at = place_of(info, order, z, core, j)

                @pl.when(at // 8 == c)
                def _():
                    rows = pl.ds(pl.multiple_of(lax.rem(at, 8) * BLOCK, BLOCK), BLOCK)
                    dst[rows, :] = src[pl.ds(j * BLOCK, BLOCK), :].astype(dst.dtype)


def cols(k, width=TOK):
    return pl.ds(k * width, width)


def row_stats(parts):
    total = sum(jnp.sum(v, axis=1, keepdims=True) for v in parts)
    mean = total * (1.0 / D)
    dev = [v - mean for v in parts]
    var = sum(jnp.sum(v * v, axis=1, keepdims=True) for v in dev) * (1.0 / D)
    rstd = lax.rsqrt(var + EPSILON)
    return [v * rstd for v in dev], rstd


def norm1_body(x0, x1, x2, x3, p0, p1, p2, p3, xn):
    for t in range(2):
        rows = pl.ds(t * 128, 128)
        parts = [f32(v[rows, :]) for v in (x0, x1, x2, x3)]
        hat, _ = row_stats(parts)
        for k, pack in enumerate((p0, p1, p2, p3)):
            xn[rows, cols(k)] = bf(hat[k] * f32(pack[0:1, :]) + f32(pack[1:2, :]))


def norm2_body(k0, rc, ry, x0, x1, x2, x3, p0, p1, p2, p3, mid, xn):
    for t in range(2):
        rows = pl.ds(t * 128, 128)
        parts = []
        for k, (x, pack) in enumerate(zip((x0, x1, x2, x3), (p0, p1, p2, p3))):
            branch = f32(k0[rows, cols(k)]) + f32(rc[rows, cols(k)]) + f32(ry[rows, cols(k)])
            v = f32(x[rows, :]) + branch + f32(pack[2:3, :])
            mid[rows, cols(k)] = v
            parts.append(v)
        hat, _ = row_stats(parts)
        for k, pack in enumerate((p0, p1, p2, p3)):
            xn[rows, cols(k)] = bf(hat[k] * f32(pack[3:4, :]) + f32(pack[4:5, :]))


def norm_back(hat, rstd, grads):
    total = sum(jnp.sum(g, axis=1, keepdims=True) for g in grads) * (1.0 / D)
    along = sum(jnp.sum(g * h, axis=1, keepdims=True) for g, h in zip(grads, hat)) * (1.0 / D)
    return [rstd * (g - total - h * along) for g, h in zip(grads, hat)]


def norm2_back_body(k0, rc, ry, mid, g0, g1, g2, g3, p0, p1, p2, p3, d_mid, g_attn):
    for t in range(2):
        rows = pl.ds(t * 128, 128)
        hat, rstd = row_stats([mid[rows, cols(k)] for k in range(4)])
        grads = []
        for k, pack in enumerate((p0, p1, p2, p3)):
            d = f32(k0[rows, cols(k)]) + f32(rc[rows, cols(k)]) + f32(ry[rows, cols(k)])
            grads.append(d * f32(pack[3:4, :]))
        back = norm_back(hat, rstd, grads)
        for k, g in enumerate((g0, g1, g2, g3)):
            v = f32(g[rows, :]) + back[k]
            d_mid[rows, cols(k)] = v
            g_attn[rows, cols(k)] = bf(v)


def norm1_back_body(
    k0, rc, ry, d_mid, x0, x1, x2, x3, p0, p1, p2, p3, i0, i1, i2, i3
):
    for t in range(2):
        rows = pl.ds(t * 128, 128)
        hat, rstd = row_stats([f32(v[rows, :]) for v in (x0, x1, x2, x3)])
        grads = []
        for k, pack in enumerate((p0, p1, p2, p3)):
            d = f32(k0[rows, cols(k)]) + f32(rc[rows, cols(k)]) + f32(ry[rows, cols(k)])
            grads.append(d * f32(pack[0:1, :]))
        back = norm_back(hat, rstd, grads)
        for k, dst in enumerate((i0, i1, i2, i3)):
            dst[rows, :] = bf(d_mid[rows, cols(k)] + back[k])


def hidden_body(k0, rc, ry, mid, p0, p1, p2, p3, h0, h1, h2, h3):
    for t in range(2):
        rows = pl.ds(t * 128, 128)
        for k, (pack, dst) in enumerate(zip((p0, p1, p2, p3), (h0, h1, h2, h3))):
            v = f32(k0[rows, cols(k)]) + f32(rc[rows, cols(k)]) + f32(ry[rows, cols(k)])
            dst[rows, :] = bf(mid[rows, cols(k)] + v + f32(pack[5:6, :]))


def slab_rows(info, b):
    y = jnp.bitwise_xor(info[1], b // 2)
    c = jnp.bitwise_xor(info[2], b % 2)
    return y, c


def low_lanes(rows):
    return lax.broadcasted_iota(jnp.int32, (rows, 128), 1) < HEAD


def qkv_body(
    info, x0, x1, x2, x3, w0, w1, w2, w3, p0, p1, p2, p3, bias, expand, q, kvp, kvc
):
    ws = (w0, w1, w2, w3)
    ps = (p0, p1, p2, p3)
    low = low_lanes(TOK)
    for b, x in enumerate((x0, x1, x2, x3)):
        y, c = slab_rows(info, b)
        acc = sum(nn(x[:, cols(k)], ws[k][...]) for k in range(4))
        u = bf(sum(nt(x[:, cols(k)], ps[k][16:32, :]) for k in range(4)))
        acc = acc + f32(bias[...]) + SCALE * nn(u, expand[...])
        kv = []
        for pair in range(2):
            g0, g1, g2 = (acc[:, 384 * pair + 128 * i : 384 * pair + 128 * i + 128] for i in range(3))
            rows = pl.ds(pl.multiple_of((y * 2 + c) * TOK, TOK), TOK)
            q[rows, cols(pair, 128)] = bf(bf(jnp.where(low, g0, g1)) * BF(0.125))
            kv.append((bf(pltpu.roll(jnp.where(low, g2, g0), 64, 1)), bf(jnp.where(low, g1, g2))))
        rows = pl.ds(pl.multiple_of(c * TOK, TOK), TOK)

        @pl.when(y == 0)
        def _():
            for pair in range(2):
                kvp[rows, cols(pair, 128)] = kv[pair][0]
                kvp[rows, cols(2 + pair, 128)] = kv[pair][1]

        @pl.when(y == 1)
        def _():
            for pair in range(2):
                kvc[rows, cols(pair, 128)] = kv[pair][0]
                kvc[rows, cols(2 + pair, 128)] = kv[pair][1]


def prompt_keys(info, own, oth, full):
    for i in range(4):
        for zl, src in ((info[4], own), (1 - info[4], oth)):
            at = block_at(zl, i // 2, i % 2)
            full[pl.ds(pl.multiple_of(at * BLOCK, BLOCK), BLOCK), :] = src[pl.ds(i * BLOCK, BLOCK), :]


def stacked(v, low):
    zero = jnp.zeros_like(v)
    return jnp.concatenate([jnp.where(low, v, zero), jnp.where(low, zero, v)], axis=0)


def attend_body(info, slopes, q, kvp, kvo, kvc, heads, lse, full):
    prompt_keys(info, kvp, kvo, full)
    zl = info[4]
    low = low_lanes(BLOCK)
    wide = 256
    row_id = lax.broadcasted_iota(jnp.int32, (2 * BLOCK, 1), 0)
    key_id = lax.broadcasted_iota(jnp.int32, (1, wide), 1)
    spot = jnp.where(row_id < BLOCK, row_id, row_id - BLOCK)
    for pair in range(2):
        slope = jnp.where(row_id < BLOCK, slopes[2 * pair], slopes[2 * pair + 1])
        lane = cols(pair, 128)
        vlane = cols(2 + pair, 128)

        def finish(state, at, idx):
            top, total, acc = state
            res = acc / total
            heads[at, lane] = bf(jnp.where(low, res[:BLOCK], res[BLOCK:]))
            kept = jnp.transpose(jnp.broadcast_to(top + jnp.log(total), (2 * BLOCK, 128)))
            lse[pl.ds(pair * 8 + idx, 1), :] = kept[0:1, :]

        def update(state, s, v):
            top, total, acc = state
            new = jnp.maximum(top, jnp.max(s, axis=1, keepdims=True))
            p = jnp.exp(s - new)
            shrink = jnp.exp(top - new)
            total = total * shrink + jnp.sum(p, axis=1, keepdims=True)
            acc = acc * shrink + nn(bf(p), v)
            return new, total, acc

        def start():
            return (
                jnp.full((2 * BLOCK, 1), LOW, F32),
                jnp.zeros((2 * BLOCK, 1), F32),
                jnp.zeros((2 * BLOCK, 128), F32),
            )

        def prompt_block(i, _):
            at = block_at(zl, i // 2, lax.rem(i, 2))
            base = at * BLOCK
            rows = pl.ds(pl.multiple_of(i * BLOCK, BLOCK), BLOCK)
            q2 = stacked(q[rows, lane], low)

            def chunk(n, state):
                keys = pl.ds(pl.multiple_of(n * wide, wide), wide)
                s = nt(q2, full[keys, lane])
                s = s + slope * (key_id + (n * wide - base)).astype(F32)
                return update(state, s, full[keys, vlane])

            state = lax.fori_loop(0, at // 2, chunk, start())
            n = at // 2
            keys = pl.ds(pl.multiple_of(n * wide, wide), wide)
            away = key_id + (n * wide - base)
            s = nt(q2, full[keys, lane]) + slope * away.astype(F32)
            s = jnp.where(away <= spot, s, LOW)
            finish(update(state, s, full[keys, vlane]), rows, i)
            return 0

        lax.fori_loop(0, 4, prompt_block, 0)

        def cont_block(i, _):
            rows = pl.ds(pl.multiple_of((i + 4) * BLOCK, BLOCK), BLOCK)
            mine = pl.ds(pl.multiple_of(i * BLOCK, BLOCK), BLOCK)
            q2 = stacked(q[rows, lane], low)
            own_id = key_id[:, :BLOCK]
            s = nt(q2, kvc[mine, lane]) + slope * own_id.astype(F32)
            s = jnp.where(own_id <= spot, s, LOW)
            state = update(start(), s, kvc[mine, vlane])
            for n in range(PROMPT // wide):
                s = nt(q2, full[n * wide : (n + 1) * wide, lane])
                s = s + slope * (key_id + (n * wide - PROMPT)).astype(F32)
                state = update(state, s, full[n * wide : (n + 1) * wide, vlane])
            finish(state, rows, i + 4)
            return 0

        lax.fori_loop(0, 4, cont_block, 0)


def attend_back_body(
    info, slopes, q, kvp, kvo, kvc, heads, d_heads, lse, dq, dkp, dko, dkc, full, d_full
):
    prompt_keys(info, kvp, kvo, full)
    d_full[...] = jnp.zeros_like(d_full)
    zl = info[4]
    low = low_lanes(BLOCK)
    wide = 256
    col_id = lax.broadcasted_iota(jnp.int32, (1, 2 * BLOCK), 1)
    key_id = lax.broadcasted_iota(jnp.int32, (wide, 1), 0)
    spot = jnp.where(col_id < BLOCK, col_id, col_id - BLOCK)
    for pair in range(2):
        slope = jnp.where(col_id < BLOCK, slopes[2 * pair], slopes[2 * pair + 1])
        lane = cols(pair, 128)
        vlane = cols(2 + pair, 128)

        def load(rows, idx):
            q2 = stacked(q[rows, lane], low)
            do = d_heads[rows, lane]
            do2 = stacked(do, low)
            both = jnp.transpose(f32(do) * f32(heads[rows, lane]))
            delta = jnp.concatenate(
                [
                    jnp.sum(both[:HEAD], axis=0, keepdims=True),
                    jnp.sum(both[HEAD:], axis=0, keepdims=True),
                ],
                axis=1,
            )
            kept = lse[pl.ds(pair * 8 + idx, 1), :]
            return q2, do2, delta, kept

        def pieces(k, v, away, masked, q2, do2, delta, kept):
            s = nt(k, q2) + (away.astype(F32) * slope - kept)
            p = jnp.exp(s)
            if masked:
                p = jnp.where(away <= spot, p, 0.0)
            dp = nt(v, do2)
            ds = bf(p * (dp - delta))
            return nn(ds, q2), nn(bf(p), do2), tn(ds, k)

        def prompt_chunk(n, base, masked, args):
            keys = pl.ds(pl.multiple_of(n * wide, wide), wide)
            away = key_id + (n * wide - base)
            dk, dv, d_q = pieces(full[keys, lane], full[keys, vlane], away, masked, *args)
            d_full[keys, lane] += dk
            d_full[keys, vlane] += dv
            return d_q

        def finish(rows, d_q):
            dq[rows, lane] = bf(jnp.where(low, d_q[:BLOCK], d_q[BLOCK:]) * 0.125)

        def prompt_block(i, _):
            at = block_at(zl, i // 2, lax.rem(i, 2))
            base = at * BLOCK
            rows = pl.ds(pl.multiple_of(i * BLOCK, BLOCK), BLOCK)
            args = load(rows, i)

            def chunk(n, d_q):
                return d_q + prompt_chunk(n, base, False, args)

            d_q = lax.fori_loop(0, at // 2, chunk, jnp.zeros((2 * BLOCK, 128), F32))
            finish(rows, d_q + prompt_chunk(at // 2, base, True, args))
            return 0

        lax.fori_loop(0, 4, prompt_block, 0)

        def cont_block(i, _):
            rows = pl.ds(pl.multiple_of((i + 4) * BLOCK, BLOCK), BLOCK)
            mine = pl.ds(pl.multiple_of(i * BLOCK, BLOCK), BLOCK)
            args = load(rows, i + 4)
            dk, dv, d_q = pieces(kvc[mine, lane], kvc[mine, vlane], key_id[:BLOCK], True, *args)
            dkc[mine, lane] = bf(dk)
            dkc[mine, vlane] = bf(dv)

            def chunk(n, d_q):
                return d_q + prompt_chunk(n, PROMPT, False, args)

            finish(rows, lax.fori_loop(0, PROMPT // wide, chunk, d_q))
            return 0

        lax.fori_loop(0, 4, cont_block, 0)
    for i in range(4):
        for side, dst in ((zl, dkp), (1 - zl, dko)):
            at = block_at(side, i // 2, i % 2)
            rows = pl.ds(pl.multiple_of(at * BLOCK, BLOCK), BLOCK)
            dst[pl.ds(i * BLOCK, BLOCK), :] = d_full[rows, :].astype(dst.dtype)


def proj_body(info, heads, w0, w1, w2, w3, reduce, p0, p1, p2, p3, o0, o1, o2, o3):
    for b, dst in enumerate((o0, o1, o2, o3)):
        y, c = slab_rows(info, b)
        h = heads[pl.ds(pl.multiple_of((y * 2 + c) * TOK, TOK), TOK), :]
        u = bf(nt(h, reduce[...]))
        for k, (w, pack) in enumerate(zip((w0, w1, w2, w3), (p0, p1, p2, p3))):
            dst[:, cols(k)] = bf(nn(h, w[...]) + SCALE * nn(u, pack[48:64, :]))


def rel_cols(info, k):
    at = lax.rem(info[0] - k + ROWS, ROWS) * TOK
    return pl.ds(pl.multiple_of(at, TOK), TOK)


def mlp_body(
    info, x0, x1, x2, x3, g0, g1, g2, g3, a0, a1, a2, a3, b0, b1, b2, b3, p0, p1, p2, p3,
    bias, expand1, reduce2,
    d0, d1, d2, d3, m0, m1, m2, m3, r1, e1, r2, e2,
    sr1, se2,
):
    ws1 = (a0, a1, a2, a3)
    ws2 = (b0, b1, b2, b3)
    ps = (p0, p1, p2, p3)
    for b, (x, g, dx, m) in enumerate(
        zip((x0, x1, x2, x3), (g0, g1, g2, g3), (d0, d1, d2, d3), (m0, m1, m2, m3))
    ):
        u1 = bf(sum(nt(x[:, cols(k)], ps[k][32:48, :]) for k in range(4)))
        pre = sum(nn(x[:, cols(k)], ws1[k][...]) for k in range(4))
        pre = pre + f32(bias[...]) + SCALE * nn(u1, expand1[...])
        t = jnp.tanh(GELU_A * (pre + GELU_B * (pre * pre * pre)))
        act = bf(0.5 * pre * (1.0 + t))
        slope = 0.5 * (1.0 + t) + 0.5 * pre * (1.0 - t * t) * (
            GELU_A * (1.0 + 3.0 * GELU_B * (pre * pre))
        )
        du2 = bf(SCALE * sum(nt(g[:, cols(k)], ps[k][64:80, :]) for k in range(4)))
        d_act = sum(nt(g[:, cols(k)], ws2[k][...]) for k in range(4)) + nn(du2, reduce2[...])
        d_pre = bf(d_act * slope)
        du1 = bf(SCALE * nt(d_pre, expand1[...]))
        u2 = bf(nt(act, reduce2[...]))
        for k in range(4):
            dx[:, cols(k)] = bf(nt(d_pre, ws1[k][...]) + nn(du1, ps[k][32:48, :]))
            m[:, cols(k)] = bf(nn(act, ws2[k][...]) + SCALE * nn(u2, ps[k][64:80, :]))
        vals = (tn(du1, x[...]), SCALE * tn(u1, d_pre), tn(du2, act), SCALE * tn(u2, g[...]))
        for dst, v in zip((sr1, e1, r2, se2), vals):
            dst[...] = v if b == 0 else dst[...] + v
    for k in range(4):
        r1[:, rel_cols(info, k)] = sr1[:, cols(k)]
        e2[:, rel_cols(info, k)] = se2[:, cols(k)]


def d_heads_body(
    info, g0, g1, g2, g3, w0, w1, w2, w3, p0, p1, p2, p3, reduce, heads,
    dh, r, e, se,
):
    ws = (w0, w1, w2, w3)
    ps = (p0, p1, p2, p3)
    for b, g in enumerate((g0, g1, g2, g3)):
        y, c = slab_rows(info, b)
        rows = pl.ds(pl.multiple_of((y * 2 + c) * TOK, TOK), TOK)
        h = heads[rows, :]
        u = bf(nt(h, reduce[...]))
        du = bf(SCALE * sum(nt(g[:, cols(k)], ps[k][48:64, :]) for k in range(4)))
        dh[rows, :] = bf(sum(nt(g[:, cols(k)], ws[k][...]) for k in range(4)) + nn(du, reduce[...]))
        rv = tn(du, h)
        ev = SCALE * tn(u, g[...])
        r[...] = rv if b == 0 else r[...] + rv
        se[...] = ev if b == 0 else se[...] + ev
    for k in range(4):
        e[:, rel_cols(info, k)] = se[:, cols(k)]


def qkv_back_body(
    info, dq, dkp, dkr, dkc, x0, x1, x2, x3, w0, w1, w2, w3, p0, p1, p2, p3, expand,
    o0, o1, o2, o3, r, e, sr,
):
    ws = (w0, w1, w2, w3)
    ps = (p0, p1, p2, p3)
    low = low_lanes(TOK)
    for b, (x, dst) in enumerate(zip((x0, x1, x2, x3), (o0, o1, o2, o3))):
        y, c = slab_rows(info, b)
        rows = pl.ds(pl.multiple_of((y * 2 + c) * TOK, TOK), TOK)
        half = pl.ds(pl.multiple_of(c * TOK, TOK), TOK)
        groups = []
        for pair in range(2):
            vq = f32(dq[rows, cols(pair, 128)])
            got = []
            for lane in (cols(pair, 128), cols(2 + pair, 128)):
                prompt = dkp[half, lane] + f32(dkr[half, lane])
                got.append(jnp.where(y == 0, prompt, f32(dkc[half, lane])))
            vk = pltpu.roll(got[0], 64, 1)
            vv = got[1]
            groups += [jnp.where(low, vq, vk), jnp.where(low, vv, vq), jnp.where(low, vk, vv)]
        d = bf(jnp.concatenate(groups, axis=1))
        u = bf(sum(nt(x[:, cols(k)], ps[k][16:32, :]) for k in range(4)))
        du = bf(SCALE * nt(d, expand[...]))
        for k in range(4):
            dst[:, cols(k)] = bf(nt(d, ws[k][...]) + nn(du, ps[k][16:32, :]))
        rv = tn(du, x[...])
        ev = SCALE * tn(u, d)
        sr[...] = rv if b == 0 else sr[...] + rv
        e[...] = ev if b == 0 else e[...] + ev
    for k in range(4):
        r[:, rel_cols(info, k)] = sr[:, cols(k)]


def shift(v, k, axis="row"):
    size = lax.axis_size(axis)
    return lax.ppermute(v, axis, [(s, (s + k) % size) for s in range(size)])


def gather_row(v):
    return [v] + [shift(v, k) for k in range(1, ROWS)]


def gather_col(v):
    core = lax.ppermute(v, "col", CORE_SWAP)
    side = lax.ppermute(v, "col", Y_SWAP)
    return [v, core, side, lax.ppermute(side, "col", CORE_SWAP)]


def reduce_col(parts):
    far = lax.ppermute(parts[3], "col", CORE_SWAP)
    side = bf(f32(parts[2]) + f32(far))
    side = lax.ppermute(side, "col", Y_SWAP)
    core = lax.ppermute(parts[1], "col", CORE_SWAP)
    return [parts[0], core, side]


def to_cols(pieces):
    return [pieces[0]] + [shift(pieces[k], ROWS - k) for k in range(1, ROWS)]


def pick(index, options):
    res = options[0]
    for k in range(1, len(options)):
        res = jnp.where(index == k, options[k], res)
    return res


def spread_grads(shared, own, col, group, choices):
    widths = [v.shape[1] for v in shared] + [v.shape[1] for v in own]
    pack = bf(jnp.concatenate(list(shared) + list(own), axis=1))
    pack = bf(f32(pack) + f32(lax.ppermute(pack, "row", Z_SWAP)))
    four = gather_col(pack)
    n_shared = sum(widths[: len(shared)])
    summed = sum(f32(v[:, :n_shared]) for v in four)
    res = [bf(summed)]
    at = n_shared
    for w in widths[len(shared) :]:
        blocks = [v[:, at : at + w] for v in four]
        res.append(
            jnp.concatenate([pick(jnp.bitwise_xor(j, col), blocks) for j in range(COLS)], axis=1)
        )
        at += w
    mine = jnp.concatenate(res, axis=1)
    other = shift(mine, 2)
    first = jnp.where(group == 0, mine, other)
    second = jnp.where(group == 0, other, mine)
    both = jnp.stack([first, second])
    ids = jnp.arange(COUNT, dtype=jnp.int32)[:, None, None]
    total = 0.0
    for k in range(lax.axis_size("dp")):
        theirs = both if k == 0 else shift(both, k, "dp")
        for g in range(GROUPS_DEV):
            total = total + jnp.where(ids == choices[k][g], f32(theirs[g])[None], 0.0)
    outs = []
    at = 0
    for i, w in enumerate(widths):
        w = w if i < len(shared) else w * COLS
        outs.append(total[:, :, at : at + w])
        at += w
    return outs


def body(
    hidden_in,
    out_grad,
    first_norm_gain,
    first_norm_bias,
    qkv_weight,
    qkv_bias,
    proj_weight,
    proj_bias,
    second_norm_gain,
    second_norm_bias,
    fc1_weight,
    fc1_bias,
    fc2_weight,
    second_feed_bias,
    qkv_reduce,
    qkv_expand,
    proj_reduce,
    proj_expand,
    fc1_reduce,
    fc1_expand,
    fc2_reduce,
    fc2_expand,
    adapter_choice,
    cont_prompt,
):
    r = lax.axis_index("row")
    col = lax.axis_index("col")
    dp = lax.axis_index("dp")
    y = col // 2
    c = lax.rem(col, 2)
    zl = lax.rem(r, 2)
    group = r // 2
    info = jnp.stack([r, y, c, dp * GROUPS_DEV, zl, group, col, dp]).astype(jnp.int32)
    slopes = jnp.exp2(
        -8.0 * (col * 4 + 1 + jnp.arange(4, dtype=jnp.int32)).astype(F32) / HEADS
    )
    adapter = jnp.where(group == 0, adapter_choice[0], adapter_choice[1])
    choices = [adapter_choice] + [
        shift(adapter_choice, k, "dp") for k in range(1, lax.axis_size("dp"))
    ]

    def route(v):
        other = lax.ppermute(v, "col", CORE_SWAP)
        pieces = call(
            route_body,
            [out((TOK, TOK), BF)] * 4,
            [info, cont_prompt, v, other],
            [pltpu.SMEM((GROUPS_DEV * NCONT,), jnp.int32)],
            smem=2,
            name="route",
        )
        return [pieces[0]] + [shift(pieces[k], k) for k in range(1, ROWS)]

    def unroute(pieces, dtype):
        got = to_cols(pieces)
        other = [lax.ppermute(v, "col", CORE_SWAP) for v in got]
        return call(
            unroute_body,
            [out((1024, TOK), dtype)],
            [info, cont_prompt, *got, *other],
            [pltpu.SMEM((GROUPS_DEV * NCONT,), jnp.int32)],
            smem=2,
            name="unroute",
        )[0]

    xs = route(hidden_in)
    gs = route(out_grad)

    def pack_for(k):
        which = lax.rem(r + k, ROWS) // 2
        a = jnp.where(which == 0, adapter_choice[0], adapter_choice[1])

        def one(v, flip):
            v = lax.dynamic_index_in_dim(v, a, 0, keepdims=False)
            return v.T if flip else v

        head = jnp.stack(
            [
                first_norm_gain,
                first_norm_bias,
                proj_bias,
                second_norm_gain,
                second_norm_bias,
                second_feed_bias,
            ]
        )
        return jnp.concatenate(
            [
                jnp.pad(head, ((0, 10), (0, 0))),
                one(qkv_reduce, True),
                one(fc1_reduce, True),
                one(proj_expand, False),
                one(fc2_expand, False),
            ],
            axis=0,
        )

    packs = [pack_for(0)] + [shift(pack_for(k), k) for k in range(1, ROWS)]

    def chosen(v):
        return lax.dynamic_index_in_dim(v, adapter, 0, keepdims=False)

    qkv_e = lax.dynamic_slice(qkv_expand, (adapter, 0, col * 768), (1, RANK, 768))[0]
    fc1_e = lax.dynamic_slice(fc1_expand, (adapter, 0, col * 1024), (1, RANK, 1024))[0]
    proj_r = chosen(proj_reduce).T
    fc2_r = chosen(fc2_reduce).T
    qkv_b = lax.dynamic_slice_in_dim(qkv_bias, col * 768, 768, 0)[None, :]
    fc1_b = lax.dynamic_slice_in_dim(fc1_bias, col * 1024, 1024, 0)[None, :]

    wq = gather_row(qkv_weight)
    wp = gather_row(proj_weight)
    w1 = gather_row(fc1_weight)
    w2 = gather_row(fc2_weight)

    big = out((TOK, D), BF)
    (xn1,) = call(norm1_body, [big], [*xs, *packs], smem=0, name="norm1")
    xn1s = gather_col(xn1)
    q, kvp, kvc = call(
        qkv_body,
        [out((1024, 256), BF), out((512, 512), BF), out((512, 512), BF)],
        [info, *xn1s, *wq, *packs, qkv_b, qkv_e],
        flops=2 * 1024 * 1024 * 768,
        name="qkv",
    )
    kvo = lax.ppermute(kvp, "row", Z_SWAP)
    heads, lse = call(
        attend_body,
        [out((1024, 256), BF), out((16, 256), F32)],
        [info, slopes, q, kvp, kvo, kvc],
        [pltpu.VMEM((PROMPT, 512), BF)],
        smem=2,
        flops=2 * 2 * 4 * 64 * 1000000,
        name="attend",
    )
    parts = call(
        proj_body,
        [big] * 4,
        [info, heads, *wp, proj_r, *packs],
        flops=2 * 1024 * 256 * 1024,
        name="proj",
    )
    mid, xn2 = call(
        norm2_body,
        [out((TOK, D), F32), big],
        [*reduce_col(parts), *xs, *packs],
        smem=0,
        name="norm2",
    )
    xn2s = gather_col(xn2)
    g_all = gather_col(jnp.concatenate(gs, axis=1))
    small = out((RANK, D), F32)
    res = call(
        mlp_body,
        [big] * 8 + [small] * 4,
        [info, *xn2s, *g_all, *w1, *w2, *packs, fc1_b, fc1_e, fc2_r],
        [pltpu.VMEM((RANK, D), F32)] * 2,
        flops=2 * 4 * 1024 * 1024 * 1024,
        name="mlp",
    )
    d_parts, m_parts = res[:4], res[4:8]
    fc1_rg, fc1_eg, fc2_rg, fc2_eg = res[8:]
    d_mid, g_attn = call(
        norm2_back_body,
        [out((TOK, D), F32), big],
        [*reduce_col(d_parts), mid, *gs, *packs],
        smem=0,
        name="norm2_back",
    )
    hidden = call(
        hidden_body,
        [out((TOK, TOK), BF)] * 4,
        [*reduce_col(m_parts), mid, *packs],
        smem=0,
        name="hidden",
    )
    hidden_out = unroute(hidden, BF)
    ga = gather_col(g_attn)
    d_heads, proj_rg, proj_eg = call(
        d_heads_body,
        [out((1024, 256), BF), out((RANK, 256), F32), small],
        [info, *ga, *wp, *packs, proj_r, heads],
        [pltpu.VMEM((RANK, D), F32)],
        flops=2 * 1024 * 256 * 1024,
        name="d_heads",
    )
    dq, dkp, dko, dkc = call(
        attend_back_body,
        [out((1024, 256), BF), out((512, 512), F32), out((512, 512), BF), out((512, 512), BF)],
        [info, slopes, q, kvp, kvo, kvc, heads, d_heads, lse],
        [pltpu.VMEM((PROMPT, 512), BF), pltpu.VMEM((PROMPT, 512), F32)],
        smem=2,
        flops=2 * 5 * 4 * 64 * 1000000,
        name="attend_back",
    )
    dkr = lax.ppermute(dko, "row", Z_SWAP)
    res = call(
        qkv_back_body,
        [big] * 4 + [small, out((RANK, 768), F32)],
        [info, dq, dkp, dkr, dkc, *xn1s, *wq, *packs, qkv_e],
        [pltpu.VMEM((RANK, D), F32)],
        flops=2 * 1024 * 1024 * 768,
        name="qkv_back",
    )
    q_parts = res[:4]
    qkv_rg, qkv_eg = res[4:]
    ins = call(
        norm1_back_body,
        [out((TOK, TOK), BF)] * 4,
        [*reduce_col(q_parts), d_mid, *xs, *packs],
        smem=0,
        name="norm1_back",
    )
    input_gradient = unroute(ins, F32)
    o_fc1r, o_pe, o_f2e, o_f1e, o_f2r, o_pr = spread_grads(
        [fc1_rg, proj_eg, fc2_eg], [fc1_eg, fc2_rg, proj_rg], col, group, choices
    )
    o_qr, o_qe = spread_grads([qkv_rg], [qkv_eg], col, group, choices)

    def flip(v):
        return jnp.transpose(v, (0, 2, 1))

    return (
        hidden_out,
        input_gradient,
        flip(o_qr),
        o_qe,
        flip(o_pr),
        o_pe,
        flip(o_fc1r),
        o_f1e,
        flip(o_f2r),
        o_f2e,
    )


def solution(mesh):
    placed = (
        P(("dp", "col"), "row"),
        P(("dp", "col"), "row"),
        P("row"),
        P("row"),
        P("row", "col"),
        P(),
        P("col", "row"),
        P("row"),
        P("row"),
        P("row"),
        P("row", "col"),
        P(),
        P("col", "row"),
        P("row"),
        P(None, "row", None),
        P(),
        P(None, "col", None),
        P(None, None, "row"),
        P(None, "row", None),
        P(),
        P(None, "col", None),
        P(None, None, "row"),
        P("dp"),
        P("dp"),
    )
    return jax.shard_map(
        body,
        mesh=mesh,
        in_specs=placed,
        out_specs=(P(("dp", "col"), "row"), P(("dp", "col"), "row")) + (P(),) * 8,
        check_vma=False,
    )
```

```python
import functools

import jax
import jax.numpy as jnp
from jax import lax
from jax.experimental import pallas as pl
from jax.experimental.pallas import tpu as pltpu
from jax.sharding import PartitionSpec as P

D = 1024
HEADS = 16
HEAD = 64
FF = 4096
RANK = 16
COUNT = 8
PROMPT = 1024
CONT = 128
NCONT = 8
GROUPS_DEV = 2

EPSILON = 1e-05
SCALE = 2.0
GELU_A = 0.7978845608028654
GELU_B = 0.044715
ROWS = 4
COLS = 4
TOK = 256
BLOCK = 128
LOW = -1e30

BF = jnp.bfloat16
F32 = jnp.float32

VM = pl.BlockSpec(memory_space=pltpu.VMEM)
SM = pl.BlockSpec(memory_space=pltpu.SMEM)
HB = pl.BlockSpec(memory_space=pl.ANY)

CORE_SWAP = [(0, 1), (1, 0), (2, 3), (3, 2)]
Y_SWAP = [(0, 2), (2, 0), (1, 3), (3, 1)]
Z_SWAP = [(0, 1), (1, 0), (2, 3), (3, 2)]


def nn(a, b):
    return lax.dot_general(a, b, (((1,), (0,)), ((), ())), preferred_element_type=F32)


def nt(a, b):
    return lax.dot_general(a, b, (((1,), (1,)), ((), ())), preferred_element_type=F32)


def tn(a, b):
    return lax.dot_general(a, b, (((0,), (0,)), ((), ())), preferred_element_type=F32)


def f32(v):
    return v.astype(F32)


def bf(v):
    return v.astype(BF)


def call(body, outs, ins, scratch=(), smem=1, limit=48, us=1, anys=(), name=None):
    nbytes = sum(v.size * v.dtype.itemsize for v in ins)
    nbytes += sum(o.size * o.dtype.itemsize for o in outs)
    specs = [SM] * smem + [HB if i in anys else VM for i in range(smem, len(ins))]
    return pl.pallas_call(
        body,
        out_shape=tuple(outs),
        in_specs=specs,
        out_specs=tuple([VM] * len(outs)),
        scratch_shapes=list(scratch),
        compiler_params=pltpu.CompilerParams(vmem_limit_bytes=limit << 20),
        cost_estimate=pl.CostEstimate(flops=int(us * 1e9), bytes_accessed=nbytes, transcendentals=0),
        name=name,
    )(*ins)


def out(shape, dtype):
    return jax.ShapeDtypeStruct(shape, dtype)


def block_at(zl, c, j):
    return c * 4 + zl + j * (3 - 2 * zl)


def fill_order(cont, base, order):
    first = jnp.int32(0)
    second = jnp.int32(NCONT)
    for j in range(GROUPS_DEV * NCONT):
        own = cont[j] == base
        slot = jnp.where(own, first, second)
        order[slot] = jnp.int32(j)
        first = first + jnp.where(own, 1, 0)
        second = second + jnp.where(own, 0, 1)


def place_of(info, order, z, core, j):
    prompt = (z // 2) * 8 + block_at(lax.rem(z, 2), core, j)
    cont = order[4 * z + 2 * core + j]
    return jnp.where(info[1] == 0, prompt, cont)


def route_body(info, cont, own, oth, o0, o1, o2, o3, order):
    fill_order(cont, info[3], order)
    c = info[2]
    for s, dst in enumerate((o0, o1, o2, o3)):
        z = lax.rem(info[0] + s, ROWS)
        for j in range(2):
            src = place_of(info, order, z, c, j)
            at = pl.ds(pl.multiple_of(lax.rem(src, 8) * BLOCK, BLOCK), BLOCK)
            mine = src // 8 == c

            @pl.when(mine)
            def _():
                dst[pl.ds(j * BLOCK, BLOCK), :] = own[at, :]

            @pl.when(jnp.logical_not(mine))
            def _():
                dst[pl.ds(j * BLOCK, BLOCK), :] = oth[at, :]


def route_pack_body(
    info, cont, choice, own, oth, g1, c1, pb, g2, c2, fb, qr, fr, pe, fe,
    o0, o1, o2, o3, order, v0, v1, v2, v3, v4, v5, mats, sem,
):
    vecs = (v0, v1, v2, v3, v4, v5)
    pairs = list(zip((g1, c1, pb, g2, c2, fb), vecs))
    for k in range(ROWS):
        which = lax.rem(info[0] + k, ROWS) // 2
        a = jnp.where(which == 0, choice[0], choice[1])
        pairs += [(v.at[a], mats.at[4 * k + i]) for i, v in enumerate((qr, fr, pe, fe))]
    copies = [pltpu.make_async_copy(a, b, sem.at[i]) for i, (a, b) in enumerate(pairs)]
    for copy in copies:
        copy.start()
    route_body(info, cont, own, oth, o0, o1, o2, o3, order)
    for copy in copies:
        copy.wait()
    for k, dst in enumerate((o0, o1, o2, o3)):
        head = [f32(v[...]).reshape(1, TOK) for v in vecs]
        dst[256:272, :] = bf(jnp.concatenate(head + [jnp.zeros((10, TOK), F32)], axis=0))
        for i in range(4):
            dst[272 + 16 * i : 288 + 16 * i, :] = mats[4 * k + i]


def unroute_body(info, cont, a0, a1, a2, a3, b0, b1, b2, b3, dst, order):
    fill_order(cont, info[3], order)
    c = info[2]
    for s in range(ROWS):
        z = lax.rem(info[0] + s, ROWS)
        for other, src in ((0, (a0, a1, a2, a3)[s]), (1, (b0, b1, b2, b3)[s])):
            core = c if other == 0 else 1 - c
            for j in range(2):
                at = place_of(info, order, z, core, j)

                @pl.when(at // 8 == c)
                def _():
                    rows = pl.ds(pl.multiple_of(lax.rem(at, 8) * BLOCK, BLOCK), BLOCK)
                    dst[rows, :] = src[pl.ds(j * BLOCK, BLOCK), :].astype(dst.dtype)


def cols(k, width=TOK):
    return pl.ds(k * width, width)


def row_stats(parts):
    total = sum(jnp.sum(v, axis=1, keepdims=True) for v in parts)
    mean = total * (1.0 / D)
    dev = [v - mean for v in parts]
    var = sum(jnp.sum(v * v, axis=1, keepdims=True) for v in dev) * (1.0 / D)
    rstd = lax.rsqrt(var + EPSILON)
    return [v * rstd for v in dev], rstd


def norm1_body(x0, x1, x2, x3, xn):
    for t in range(2):
        rows = pl.ds(t * 128, 128)
        hat, _ = row_stats([f32(v[rows, :]) for v in (x0, x1, x2, x3)])
        for k, pack in enumerate((x0, x1, x2, x3)):
            xn[rows, cols(k)] = bf(hat[k] * f32(pack[256:257, :]) + f32(pack[257:258, :]))


def three(k0, rc, ry, rows, k):
    return f32(k0[rows, cols(k)]) + f32(rc[rows, cols(k)]) + f32(ry[rows, cols(k)])


def norm2_body(k0, rc, ry, x0, x1, x2, x3, mid, xn):
    for t in range(2):
        rows = pl.ds(t * 128, 128)
        parts = []
        for k, x in enumerate((x0, x1, x2, x3)):
            v = f32(x[rows, :]) + three(k0, rc, ry, rows, k) + f32(x[258:259, :])
            mid[rows, cols(k)] = v
            parts.append(v)
        hat, _ = row_stats(parts)
        for k, pack in enumerate((x0, x1, x2, x3)):
            xn[rows, cols(k)] = bf(hat[k] * f32(pack[259:260, :]) + f32(pack[260:261, :]))


def norm_back(hat, rstd, grads):
    total = sum(jnp.sum(g, axis=1, keepdims=True) for g in grads) * (1.0 / D)
    along = sum(jnp.sum(g * h, axis=1, keepdims=True) for g, h in zip(grads, hat)) * (1.0 / D)
    return [rstd * (g - total - h * along) for g, h in zip(grads, hat)]


def norm2_back_body(k0, rc, ry, mid, g0, g1, g2, g3, x0, x1, x2, x3, d_mid, g_attn):
    for t in range(2):
        rows = pl.ds(t * 128, 128)
        hat, rstd = row_stats([mid[rows, cols(k)] for k in range(4)])
        grads = []
        for k, pack in enumerate((x0, x1, x2, x3)):
            grads.append(three(k0, rc, ry, rows, k) * f32(pack[259:260, :]))
        back = norm_back(hat, rstd, grads)
        for k, g in enumerate((g0, g1, g2, g3)):
            v = f32(g[rows, :]) + back[k]
            d_mid[rows, cols(k)] = v
            g_attn[rows, cols(k)] = bf(v)


def norm1_back_body(k0, rc, ry, d_mid, x0, x1, x2, x3, i0, i1, i2, i3):
    for t in range(2):
        rows = pl.ds(t * 128, 128)
        hat, rstd = row_stats([f32(v[rows, :]) for v in (x0, x1, x2, x3)])
        grads = []
        for k, pack in enumerate((x0, x1, x2, x3)):
            grads.append(three(k0, rc, ry, rows, k) * f32(pack[256:257, :]))
        back = norm_back(hat, rstd, grads)
        for k, dst in enumerate((i0, i1, i2, i3)):
            dst[rows, :] = bf(d_mid[rows, cols(k)] + back[k])


def hidden_body(k0, rc, ry, mid, x0, x1, x2, x3, h0, h1, h2, h3):
    for t in range(2):
        rows = pl.ds(t * 128, 128)
        for k, (pack, dst) in enumerate(zip((x0, x1, x2, x3), (h0, h1, h2, h3))):
            v = three(k0, rc, ry, rows, k)
            dst[rows, :] = bf(mid[rows, cols(k)] + v + f32(pack[261:262, :]))


def join_body(a0, a1, a2, a3, dst):
    for k, v in enumerate((a0, a1, a2, a3)):
        dst[:, cols(k)] = v[...]


def slab_rows(info, b):
    y = jnp.bitwise_xor(info[1], b // 2)
    c = jnp.bitwise_xor(info[2], b % 2)
    return y, c


def low_lanes(rows):
    return lax.broadcasted_iota(jnp.int32, (rows, 128), 1) < HEAD


def rel(info, k):
    return lax.rem(info[0] - k + ROWS, ROWS)


def rel_cols(info, k):
    return pl.ds(pl.multiple_of(rel(info, k) * TOK, TOK), TOK)


def rows_at(i, size):
    return pl.ds(pl.multiple_of(i * size, size), size)


def qkv_body(
    info, x0, x1, x2, x3, own_w, z1, z2, z3, s1, s2, s3, p0, p1, p2, p3, bias, expand,
    q, kvp, kvc, ws,
):
    ps = (p0, p1, p2, p3)
    low = low_lanes(TOK)
    half = info[8]
    ws[0] = own_w[...]
    for k, (zv, sv) in enumerate(((z1, s1), (z2, s2), (z3, s3))):
        ws[k + 1, rows_at(half, 128), :] = zv[...]
        ws[k + 1, rows_at(1 - half, 128), :] = sv[...]
    for b, x in enumerate((x0, x1, x2, x3)):
        y, c = slab_rows(info, b)
        acc = sum(nn(x[:, cols(k)], ws[k]) for k in range(4))
        u = bf(sum(nt(x[:, cols(k)], ps[k][272:288, :]) for k in range(4)))
        acc = acc + f32(bias[...]) + SCALE * nn(u, expand[...])
        kv = []
        for pair in range(2):
            at = 384 * pair
            g0, g1, g2 = (acc[:, at + 128 * i : at + 128 * i + 128] for i in range(3))
            q[rows_at(y * 2 + c, TOK), cols(pair, 128)] = bf(
                bf(jnp.where(low, g0, g1)) * BF(0.125)
            )
            kv.append((bf(pltpu.roll(jnp.where(low, g2, g0), 64, 1)), bf(jnp.where(low, g1, g2))))
        rows = rows_at(c, TOK)

        @pl.when(y == 0)
        def _():
            for pair in range(2):
                kvp[rows, cols(pair, 128)] = kv[pair][0]
                kvp[rows, cols(2 + pair, 128)] = kv[pair][1]

        @pl.when(y == 1)
        def _():
            for pair in range(2):
                kvc[rows, cols(pair, 128)] = kv[pair][0]
                kvc[rows, cols(2 + pair, 128)] = kv[pair][1]


WIDE = 256


def stacked(v, low):
    zero = jnp.zeros_like(v)
    return jnp.concatenate([jnp.where(low, v, zero), jnp.where(low, zero, v)], axis=0)


def split_id(shape, axis):
    lane = lax.broadcasted_iota(jnp.int32, shape, axis)
    return lane, jnp.where(lane < BLOCK, lane, lane - BLOCK)


def chunk_place(shape, axis, side, n):
    lane, within = split_id(shape, axis)
    first = block_at(side, n, 0) * BLOCK
    second = block_at(side, n, 1) * BLOCK
    return within + jnp.where(lane < BLOCK, first, second)


def keep_state(state, low):
    top, total, acc = state
    lane = lax.broadcasted_iota(jnp.int32, (2 * BLOCK, 128), 1)
    spot = lax.rem(lane, HEAD)
    row = lax.broadcasted_iota(jnp.int32, (2 * BLOCK, 128), 0)
    own = (lane < HEAD) == (row < BLOCK)
    return jnp.where(own, acc, jnp.where(spot == 0, top, total))


def load_state(v):
    top = jnp.concatenate([v[:BLOCK, HEAD : HEAD + 1], v[BLOCK:, 0:1]], axis=0)
    total = jnp.concatenate([v[:BLOCK, HEAD + 1 : HEAD + 2], v[BLOCK:, 1:2]], axis=0)
    return top, total, v


def soft_update(state, s, v):
    if state is None:
        top = jnp.max(s, axis=1, keepdims=True)
        p = jnp.exp(s - top)
        return top, jnp.sum(p, axis=1, keepdims=True), nn(bf(p), v)
    top, total, acc = state
    new = jnp.maximum(top, jnp.max(s, axis=1, keepdims=True))
    p = jnp.exp(s - new)
    shrink = jnp.exp(top - new)
    total = total * shrink + jnp.sum(p, axis=1, keepdims=True)
    return new, total, acc * shrink + nn(bf(p), v)


def head_slopes(slopes, shape, axis):
    lane = lax.broadcasted_iota(jnp.int32, shape, axis)
    return [
        jnp.where(lane < BLOCK, slopes[2 * pair], slopes[2 * pair + 1]) for pair in range(2)
    ]


def attend_chunk(q2, states, kv, rows, place, base, slope, spot, masked):
    res = []
    away = place - base
    for pair in range(2):
        s = nt(q2[pair], kv[rows, cols(pair, 128)]) + slope[pair] * away.astype(F32)
        if masked:
            s = jnp.where(away <= spot, s, LOW)
        res.append(soft_update(states[pair], s, kv[rows, cols(2 + pair, 128)]))
    return res


def attend_first_body(info, slopes, q, kvp, kvc, state):
    zl = info[4]
    low = low_lanes(BLOCK)
    _, spot = split_id((2 * BLOCK, 1), 0)
    slope = head_slopes(slopes, (2 * BLOCK, 1), 0)
    places = [chunk_place((1, WIDE), 1, zl, n) for n in range(2)]

    def load(i):
        return [stacked(q[rows_at(i, BLOCK), cols(pair, 128)], low) for pair in range(2)]

    def save(states, i):
        for pair in range(2):
            state[rows_at(i, WIDE), cols(pair, 128)] = keep_state(states[pair], low)

    def prompt_block(j, _):
        for n in range(2):
            i = 2 * n + j
            base = block_at(zl, n, j) * BLOCK
            q2 = load(i)
            states = [None, None]
            for m in range(n, -1, -1):
                states = attend_chunk(
                    q2, states, kvp, pl.ds(m * WIDE, WIDE), places[m], base, slope, spot, m == n
                )
            save(states, i)
        return 0

    lax.fori_loop(0, 2, prompt_block, 0)

    def cont_block(j, _):
        q2 = load(4 + j)
        own_place = lax.broadcasted_iota(jnp.int32, (1, BLOCK), 1)
        states = attend_chunk(
            q2, [None, None], kvc, rows_at(j, BLOCK), own_place, 0, slope, spot, True
        )
        for m in range(2):
            states = attend_chunk(
                q2, states, kvp, pl.ds(m * WIDE, WIDE), places[m], PROMPT, slope, spot, False
            )
        save(states, 4 + j)
        return 0

    lax.fori_loop(0, 4, cont_block, 0)


def attend_rest_body(
    which, info, slopes, q, kvo, state, wa, wb, reduce, p0, p1, p2, p3, heads, lse, o0, o1, wp
):
    zl = info[4]
    y = info[1] if which == 0 else 1 - info[1]
    low = low_lanes(BLOCK)
    _, spot = split_id((2 * BLOCK, 1), 0)
    slope = head_slopes(slopes, (2 * BLOCK, 1), 0)
    places = [chunk_place((1, WIDE), 1, 1 - zl, n) for n in range(2)]
    proj_load(info, wa, wb, wp)

    def load(i):
        q2 = [stacked(q[rows_at(i, BLOCK), cols(pair, 128)], low) for pair in range(2)]
        states = [load_state(state[rows_at(i, WIDE), cols(pair, 128)]) for pair in range(2)]
        return q2, states

    def finish(states, j):
        for pair in range(2):
            top, total, acc = states[pair]
            res = acc / total
            heads[rows_at(j, BLOCK), cols(pair, 128)] = bf(
                jnp.where(low, res[:BLOCK], res[BLOCK:])
            )
            kept = jnp.transpose(jnp.broadcast_to(top + jnp.log(total), (2 * BLOCK, 128)))
            lse[pl.ds(pair * 4 + j, 1), :] = kept[0:1, :]

    @pl.when(y == 0)
    def _():
        def prompt_block(j, _):
            for n in range(2):
                i = 2 * n + j
                base = block_at(zl, n, j) * BLOCK
                q2, states = load(i)
                for m in range(n + 1):
                    states = attend_chunk(
                        q2, states, kvo, pl.ds(m * WIDE, WIDE), places[m], base, slope, spot, m == n
                    )
                finish(states, i)
            return 0

        lax.fori_loop(0, 2, prompt_block, 0)

    @pl.when(y == 1)
    def _():
        def cont_block(j, _):
            q2, states = load(4 + j)
            for m in range(2):
                states = attend_chunk(
                    q2, states, kvo, pl.ds(m * WIDE, WIDE), places[m], PROMPT, slope, spot, False
                )
            finish(states, j)
            return 0

        lax.fori_loop(0, 4, cont_block, 0)

    ps = (p0, p1, p2, p3)
    for b, dst in enumerate((o0, o1)):
        c = jnp.bitwise_xor(info[2], b)
        h = heads[rows_at(c, TOK), :]
        u = bf(nt(h, reduce[...]))
        for k in range(4):
            dst[:, cols(k)] = bf(nn(h, wp[rel(info, k)]) + SCALE * nn(u, ps[k][304:320, :]))


def proj_load(info, wa, wb, wp):
    for src, at in ((wa, info[8]), (wb, 1 - info[8])):
        for j in range(ROWS):
            wp[j, rows_at(at, 128), :] = src[j, :, 1024:1280]


def d_act_body(info, g0, g1, g2, g3, wa, wb, reduce, p0, p1, p2, p3, d_act, w2):
    ps = (p0, p1, p2, p3)
    for src, at in ((wa, info[8]), (wb, 1 - info[8])):
        for j in range(ROWS):
            w2[j, rows_at(at, 512), :] = src[j]
    for b, g in enumerate((g0, g1, g2, g3)):
        du = bf(SCALE * sum(nt(g[:, cols(k)], ps[k][320:336, :]) for k in range(4)))
        v = sum(nt(g[:, cols(k)], w2[rel(info, k)]) for k in range(4)) + nn(du, reduce[...])
        d_act[b] = bf(v)


def mlp_body(
    first, info, x0, x1, d_act, wa, wb, p0, p1, p2, p3, bias, expand, r_in, e_in,
    d0, d1, act, r_out, e_out, w1,
):
    ps = (p0, p1, p2, p3)
    for src, at in ((wa, info[8]), (wb, 1 - info[8])):
        for j in range(ROWS):
            w1[j, rows_at(at, 128), :] = src[j, :, :1024]
    rv, ev = r_in[...], e_in[...]
    for b, (x, dx) in enumerate(((x0, d0), (x1, d1))):
        u = bf(sum(nt(x[:, cols(k)], ps[k][288:304, :]) for k in range(4)))
        pre = sum(nn(x[:, cols(k)], w1[rel(info, k)]) for k in range(4))
        pre = pre + f32(bias[...]) + SCALE * nn(u, expand[...])
        sq = pre * pre
        t = jnp.tanh(pre * (GELU_A + (GELU_A * GELU_B) * sq))
        half = 0.5 + 0.5 * t
        act[b] = bf(pre * half)
        slope = half + (0.5 * pre) * (1.0 - t * t) * (GELU_A + (3.0 * GELU_A * GELU_B) * sq)
        d_pre = bf(f32(d_act[2 * first + b]) * slope)
        du = bf(SCALE * nt(d_pre, expand[...]))
        for k in range(4):
            dx[:, cols(k)] = bf(nt(d_pre, w1[rel(info, k)]) + nn(du, ps[k][288:304, :]))
        rv = rv + tn(du, x[...])
        ev = ev + tn(u, d_pre)
    r_out[...] = rv
    e_out[...] = ev


def fc2_body(
    info, a0, a1, g0, g1, g2, g3, wa, wb, reduce, p0, p1, p2, p3, r1, e1,
    m0, m1, m2, m3, grads, w2,
):
    ps = (p0, p1, p2, p3)
    for src, at in ((wa, info[8]), (wb, 1 - info[8])):
        for j in range(ROWS):
            w2[j, rows_at(at, 512), :] = src[j]
    rv = ev = 0.0
    for b, (g, m) in enumerate(zip((g0, g1, g2, g3), (m0, m1, m2, m3))):
        act = a0[b] if b < 2 else a1[b - 2]
        du = bf(SCALE * sum(nt(g[:, cols(k)], ps[k][320:336, :]) for k in range(4)))
        u = bf(nt(act, reduce[...]))
        for k in range(4):
            m[:, cols(k)] = bf(nn(act, w2[rel(info, k)]) + SCALE * nn(u, ps[k][320:336, :]))
        rv = rv + tn(du, act)
        ev = ev + SCALE * tn(u, g[...])
    for k in range(4):
        at = rel(info, k) * TOK
        grads[:, pl.ds(pl.multiple_of(at, TOK), TOK)] = bf(r1[:, cols(k)])
        grads[:, pl.ds(pl.multiple_of(at + 1024, TOK), TOK)] = bf(ev[:, k * TOK : k * TOK + TOK])
    grads[:, 2048:3072] = bf(SCALE * e1[...])
    grads[:, 3072:4096] = bf(rv)


def d_heads_body(
    info, g0, g1, wa, wb, p0, p1, p2, p3, reduce, heads, r_in, e_in, dh, r_out, e_out, wp
):
    ps = (p0, p1, p2, p3)
    proj_load(info, wa, wb, wp)
    rv, ev = r_in[...], e_in[...]
    for b, g in enumerate((g0, g1)):
        rows = rows_at(jnp.bitwise_xor(info[2], b), TOK)
        h = heads[rows, :]
        u = bf(nt(h, reduce[...]))
        du = bf(SCALE * sum(nt(g[:, cols(k)], ps[k][304:320, :]) for k in range(4)))
        v = sum(nt(g[:, cols(k)], wp[rel(info, k)]) for k in range(4)) + nn(du, reduce[...])
        dh[rows, :] = bf(v)
        rv = rv + tn(du, h)
        ev = ev + SCALE * tn(u, g[...])
    r_out[...] = rv
    e_out[...] = ev


def proj_grads_body(info, r, e, grads):
    for k in range(4):
        grads[:, rel_cols(info, k)] = bf(e[:, cols(k)])
    grads[:, 1024:1280] = bf(r[...])


def back_load(heads, d_heads, lse, q, qi, j, low):
    res = []
    for pair in range(2):
        lane = cols(pair, 128)
        q2 = stacked(q[rows_at(qi, BLOCK), lane], low)
        do = d_heads[rows_at(j, BLOCK), lane]
        both = jnp.transpose(f32(do) * f32(heads[rows_at(j, BLOCK), lane]))
        delta = jnp.concatenate(
            [
                jnp.sum(both[:HEAD], axis=0, keepdims=True),
                jnp.sum(both[HEAD:], axis=0, keepdims=True),
            ],
            axis=1,
        )
        res.append((q2, stacked(do, low), delta, lse[pl.ds(pair * 4 + j, 1), :]))
    return res


def back_chunk(args, kv, d_kv, d_at, rows, place, base, slope, spot, masked, store, d_qs):
    away = place - base
    res = []
    for pair in range(2):
        q2, do2, delta, kept = args[pair]
        lane = cols(pair, 128)
        vlane = cols(2 + pair, 128)
        k = kv[rows, lane]
        s = nt(k, q2) + (away.astype(F32) * slope[pair] - kept)
        p = jnp.exp(s)
        if masked:
            p = jnp.where(away <= spot, p, 0.0)
        ds = bf(p * (nt(kv[rows, vlane], do2) - delta))
        dk = nn(ds, q2)
        dv = nn(bf(p), do2)
        if store:
            d_kv[d_at, lane] = bf(dk)
            d_kv[d_at, vlane] = bf(dv)
        else:
            d_kv[d_at, lane] += dk
            d_kv[d_at, vlane] += dv
        d_q = tn(ds, k)
        res.append(d_q if d_qs is None else d_qs[pair] + d_q)
    return res


def back_common(info, slopes):
    low = low_lanes(BLOCK)
    _, spot = split_id((1, 2 * BLOCK), 1)
    slope = head_slopes(slopes, (1, 2 * BLOCK), 1)
    zl = info[4]
    own = [chunk_place((WIDE, 1), 0, zl, n) for n in range(2)]
    oth = [chunk_place((WIDE, 1), 0, 1 - zl, n) for n in range(2)]
    return zl, low, spot, slope, own, oth


def fold(d_q, low):
    return jnp.where(low, d_q[:BLOCK], d_q[BLOCK:]) * 0.125


def back_sweep(info, slopes, y, q, heads, d_heads, lse, sides, kvc, dkc, finish):
    zl, low, spot, slope, own, oth = back_common(info, slopes)
    place_sets = {"own": own, "oth": oth}

    @pl.when(y == 0)
    def _():
        def prompt_block(j, _):
            for n in range(2):
                i = 2 * n + j
                args = back_load(heads, d_heads, lse, q, i, i, low)
                base = block_at(zl, n, j) * BLOCK
                d_qs = None
                for side, kv, d_kv in sides:
                    for m in range(n + 1):
                        rows = pl.ds(m * WIDE, WIDE)
                        d_qs = back_chunk(
                            args, kv, d_kv, rows, rows, place_sets[side][m], base, slope, spot,
                            m == n, False, d_qs,
                        )
                finish(d_qs, i, low)
            return 0

        lax.fori_loop(0, 2, prompt_block, 0)

    @pl.when(y == 1)
    def _():
        def cont_block(j, _):
            args = back_load(heads, d_heads, lse, q, 4 + j, j, low)
            d_qs = None
            if kvc is not None:
                mine = rows_at(j, BLOCK)
                own_place = lax.broadcasted_iota(jnp.int32, (BLOCK, 1), 0)
                d_qs = back_chunk(
                    args, kvc, dkc, mine, mine, own_place, 0, slope, spot, True, True, d_qs
                )
            for side, kv, d_kv in sides:
                for m in range(2):
                    rows = pl.ds(m * WIDE, WIDE)
                    d_qs = back_chunk(
                        args, kv, d_kv, rows, rows, place_sets[side][m], PROMPT, slope, spot,
                        False, False, d_qs,
                    )
            finish(d_qs, j, low)
            return 0

        lax.fori_loop(0, 4, cont_block, 0)


def attend_back_a_body(
    info, slopes, q, kvp, kvo, kvc, heads, d_heads, lse, dq, dkp, dko, dkc
):
    dkp[...] = jnp.zeros_like(dkp)
    dko[...] = jnp.zeros_like(dko)
    dkc[...] = jnp.zeros_like(dkc)

    def finish(d_qs, j, low):
        for pair in range(2):
            dq[rows_at(j, BLOCK), cols(pair, 128)] = bf(fold(d_qs[pair], low))

    back_sweep(
        info, slopes, info[1], q, heads, d_heads, lse,
        (("own", kvp, dkp), ("oth", kvo, dko)), kvc, dkc, finish,
    )


def attend_back_b_body(info, slopes, q, kvo, heads, d_heads, lse, dko_in, dq, dko, acc):
    acc[...] = dko_in[...]

    def finish(d_qs, j, low):
        for pair in range(2):
            dq[rows_at(j, BLOCK), cols(pair, 128)] = fold(d_qs[pair], low)

    back_sweep(
        info, slopes, 1 - info[1], q, heads, d_heads, lse,
        (("oth", kvo, acc),), None, None, finish,
    )
    dko[...] = bf(acc[...])


def attend_back_c_body(
    info, slopes, q, kvp, kvc, heads, d_heads, lse, dkp_in, dkc_in, dq_in, dq, dkp, dkc
):
    dkp[...] = dkp_in[...]
    dkc[...] = dkc_in[...]

    def finish(d_qs, j, low):
        for pair in range(2):
            lane = cols(pair, 128)
            rows = rows_at(j, BLOCK)
            dq[rows, lane] = bf(dq_in[rows, lane] + fold(d_qs[pair], low))

    back_sweep(
        info, slopes, 1 - info[1], q, heads, d_heads, lse,
        (("own", kvp, dkp),), kvc, dkc, finish,
    )


def qkv_back_body(
    info, dq0, dq1, dkp, dkr, dkc, x0, x1, x2, x3, ws, p0, p1, p2, p3, expand,
    o0, o1, o2, o3, grads,
):
    ps = (p0, p1, p2, p3)
    low = low_lanes(TOK)
    sr = se = 0.0
    for b, (x, dst) in enumerate(zip((x0, x1, x2, x3), (o0, o1, o2, o3))):
        y, c = slab_rows(info, b)
        half = rows_at(c, TOK)
        groups = []
        dq = dq0 if b < 2 else dq1
        for pair in range(2):
            vq = f32(dq[half, cols(pair, 128)])
            got = []
            for lane in (cols(pair, 128), cols(2 + pair, 128)):
                prompt = dkp[half, lane] + f32(dkr[half, lane])
                got.append(jnp.where(y == 0, prompt, f32(dkc[half, lane])))
            vk = pltpu.roll(got[0], 64, 1)
            vv = got[1]
            groups += [jnp.where(low, vq, vk), jnp.where(low, vv, vq), jnp.where(low, vk, vv)]
        d = bf(jnp.concatenate(groups, axis=1))
        u = bf(sum(nt(x[:, cols(k)], ps[k][272:288, :]) for k in range(4)))
        du = bf(SCALE * nt(d, expand[...]))
        for k in range(4):
            dst[:, cols(k)] = bf(nt(d, ws[k]) + nn(du, ps[k][272:288, :]))
        sr = sr + tn(du, x[...])
        se = se + SCALE * tn(u, d)
    for k in range(4):
        grads[:, rel_cols(info, k)] = bf(sr[:, k * TOK : k * TOK + TOK])
    grads[:, 1024:1792] = bf(se)


def add_body(a, b, dst):
    dst[...] = bf(f32(a[...]) + f32(b[...]))


def add_two_body(a0, b0, a1, b1, dst):
    n = a0.shape[1]
    dst[:, :n] = bf(f32(a0[...]) + f32(b0[...]))
    dst[:, n:] = bf(f32(a1[...]) + f32(b1[...]))


def merge_body(parts, info, v0, v1, v2, v3, dst):
    four = (v0, v1, v2, v3)
    at = to = 0
    for width, shared in parts:
        if shared:
            total = sum(f32(v[:, at : at + width]) for v in four)
            dst[:, to : to + width] = bf(total)
        else:
            for b, v in enumerate(four):
                j = jnp.bitwise_xor(info[6], b) * width
                lanes = pl.ds(pl.multiple_of(to + j, 128), width)
                dst[:, lanes] = v[:, at : at + width]
        at += width
        to += width if shared else width * COLS


def expand_body(widths, info, choices, *refs):
    n = len(refs) - len(widths)
    groups = refs[:n]
    outs = refs[n:]
    for a in range(COUNT):
        at = 0
        for width, dst in zip(widths, outs):
            total = 0.0
            for k in range(n):
                pair = k // 2
                spot = info[5] if k % 2 == 0 else 1 - info[5]
                hit = jnp.where(choices[2 * pair + spot] == a, 1.0, 0.0)
                total = total + hit * f32(groups[k][:, at : at + width])
            dst[a] = total
            at += width


def shift(v, k, axis="row"):
    size = lax.axis_size(axis)
    return lax.ppermute(v, axis, [(s, (s + k) % size) for s in range(size)])


def gather_row(v):
    return [v] + [shift(v, k) for k in range(1, ROWS)]


def gather_col(v):
    core = lax.ppermute(v, "col", CORE_SWAP)
    side = lax.ppermute(v, "col", Y_SWAP)
    return [v, core, side, lax.ppermute(side, "col", CORE_SWAP)]


def reduce_col(parts):
    far = lax.ppermute(parts[3], "col", CORE_SWAP)
    side = bf(f32(parts[2]) + f32(far))
    side = lax.ppermute(side, "col", Y_SWAP)
    core = lax.ppermute(parts[1], "col", CORE_SWAP)
    return [parts[0], core, side]


def to_cols(pieces):
    return [pieces[0]] + [shift(pieces[k], ROWS - k) for k in range(1, ROWS)]


def spread_grads(pack, parts, info, choices):
    four = gather_col(pack)
    total = sum(w if shared else w * COLS for w, shared in parts)
    whole = out((RANK, total), BF)
    (mine,) = call(
        functools.partial(merge_body, parts), [whole], [info, *four], name="merge"
    )
    other = shift(mine, 2)
    groups = []
    for k in range(lax.axis_size("dp")):
        groups += [mine, other] if k == 0 else [shift(mine, k, "dp"), shift(other, k, "dp")]
    widths = [w if shared else w * COLS for w, shared in parts]
    return call(
        functools.partial(expand_body, widths),
        [out((COUNT, RANK, w), F32) for w in widths],
        [info, choices, *groups],
        smem=2,
        name="expand",
    )

def body(
    hidden_in,
    out_grad,
    first_norm_gain,
    first_norm_bias,
    qkv_weight,
    qkv_bias,
    proj_weight,
    proj_bias,
    second_norm_gain,
    second_norm_bias,
    fc1_weight,
    fc1_bias,
    fc2_weight,
    second_feed_bias,
    qkv_reduce,
    qkv_expand,
    proj_reduce,
    proj_expand,
    fc1_reduce,
    fc1_expand,
    fc2_reduce,
    fc2_expand,
    adapter_choice,
    cont_prompt,
):
    r = lax.axis_index("row")
    col = lax.axis_index("col")
    dp = lax.axis_index("dp")
    y = col // 2
    c = lax.rem(col, 2)
    zl = lax.rem(r, 2)
    group = r // 2
    half = lax.rem(dp, 2)
    dp_swap = [(k, k ^ 1) for k in range(lax.axis_size("dp"))]
    info = jnp.stack([r, y, c, dp * GROUPS_DEV, zl, group, col, dp, half]).astype(jnp.int32)
    slopes = jnp.exp2(
        -8.0 * (col * 4 + 1 + jnp.arange(4, dtype=jnp.int32)).astype(F32) / HEADS
    )
    adapter = jnp.where(group == 0, adapter_choice[0], adapter_choice[1])
    choices = jnp.concatenate(
        [adapter_choice]
        + [shift(adapter_choice, k, "dp") for k in range(1, lax.axis_size("dp"))]
    )
    order = pltpu.SMEM((GROUPS_DEV * NCONT,), jnp.int32)
    flip = functools.partial(jnp.transpose, axes=(0, 2, 1))

    def part(v):
        n = v.shape[0] // 2
        return lax.dynamic_slice_in_dim(v, half * n, n, 0)

    wfa = lax.all_gather(jnp.concatenate([part(fc1_weight), part(proj_weight)], axis=1), "row")
    w2a = lax.all_gather(part(fc2_weight), "row")
    qkv_half = part(qkv_weight)

    other = lax.ppermute(hidden_in, "col", CORE_SWAP)
    pieces = call(
        route_pack_body,
        [out((336, TOK), BF)] * 4,
        [
            info, cont_prompt, adapter_choice, hidden_in, other,
            first_norm_gain, first_norm_bias, proj_bias,
            second_norm_gain, second_norm_bias, second_feed_bias,
            flip(qkv_reduce), flip(fc1_reduce), proj_expand, fc2_expand,
        ],
        [
            order,
            *[pltpu.VMEM((TOK,), BF)] * 6,
            pltpu.VMEM((16, RANK, TOK), BF),
            pltpu.SemaphoreType.DMA((22,)),
        ],
        smem=3,
        anys=range(5, 15),
        us=1.5,
        name="route_x",
    )
    xs = [pieces[0]] + [shift(pieces[k], k) for k in range(1, ROWS)]
    z_parts = [shift(qkv_half, k) for k in range(1, ROWS)]
    s_parts = [lax.ppermute(v, "dp", dp_swap) for v in z_parts]

    def unroute(parts, dtype):
        got = to_cols(parts)
        far = [lax.ppermute(v, "col", CORE_SWAP) for v in got]
        return call(
            unroute_body,
            [out((1024, TOK), dtype)],
            [info, cont_prompt, *got, *far],
            [order],
            smem=2,
            us=2,
            name="unroute",
        )[0]

    def chosen(v):
        return lax.dynamic_index_in_dim(v, adapter, 0, keepdims=False)

    qkv_e = lax.dynamic_slice(qkv_expand, (adapter, 0, col * 768), (1, RANK, 768))[0]
    fc1_e = lax.dynamic_slice(fc1_expand, (adapter, 0, col * 1024), (1, RANK, 1024))[0]
    proj_r = chosen(proj_reduce).T
    fc2_r = chosen(fc2_reduce).T
    qkv_b = lax.dynamic_slice_in_dim(qkv_bias, col * 768, 768, 0)[None, :]
    fc1_b = lax.dynamic_slice_in_dim(fc1_bias, col * 1024, 1024, 0)[None, :]

    big = out((TOK, D), BF)
    small = out((RANK, D), F32)
    (xn1,) = call(norm1_body, [big], xs, smem=0, us=1, name="norm1")
    xn1s = gather_col(xn1)
    q, kvp, kvc, wq = call(
        qkv_body,
        [
            out((1024, 256), BF),
            out((512, 512), BF),
            out((512, 512), BF),
            out((ROWS, TOK, 768), BF),
        ],
        [info, *xn1s, qkv_weight, *z_parts, *s_parts, *xs, qkv_b, qkv_e],
        us=6.5,
        name="qkv",
    )
    kvo = lax.ppermute(kvp, "row", Z_SWAP)
    (state,) = call(
        attend_first_body,
        [out((2048, 256), F32)],
        [info, slopes, q, kvp, kvc],
        smem=2,
        us=9,
        name="attend_first",
    )
    wfb = lax.ppermute(wfa, "dp", dp_swap)
    w2b = lax.ppermute(w2a, "dp", dp_swap)

    def attend_rest(which):
        return call(
            functools.partial(attend_rest_body, which),
            [out((512, 256), BF), out((8, 256), F32), big, big],
            [info, slopes, q, kvo, state, wfa, wfb, proj_r, *xs],
            [pltpu.VMEM((ROWS, TOK, TOK), BF)],
            smem=2,
            us=5,
            name="attend_rest",
        )

    heads1, lse1, p2, p3 = attend_rest(1)
    heads0, lse0, p0, p1 = attend_rest(0)
    mid, xn2 = call(
        norm2_body,
        [out((TOK, D), F32), big],
        [*reduce_col([p0, p1, p2, p3]), *xs],
        smem=0,
        us=1.5,
        name="norm2",
    )
    xn2s = gather_col(xn2)

    g_other = lax.ppermute(out_grad, "col", CORE_SWAP)
    pieces = call(
        route_body,
        [out((TOK, TOK), BF)] * 4,
        [info, cont_prompt, out_grad, g_other],
        [order],
        smem=2,
        us=1,
        name="route_g",
    )
    gs = [pieces[0]] + [shift(pieces[k], k) for k in range(1, ROWS)]
    (g_own,) = call(join_body, [big], gs, smem=0, us=0.5, name="join")
    g_all = gather_col(g_own)
    (d_act,) = call(
        d_act_body,
        [out((4, TOK, D), BF)],
        [info, *g_all, w2a, w2b, fc2_r, *xs],
        [pltpu.VMEM((ROWS, D, TOK), BF)],
        us=5,
        name="d_act",
    )

    zero = jnp.zeros((RANK, D), F32)

    def mlp(first, blocks, r_in, e_in):
        return call(
            functools.partial(mlp_body, first),
            [big, big, out((2, TOK, D), BF), small, small],
            [info, *blocks, d_act, wfa, wfb, *xs, fc1_b, fc1_e, r_in, e_in],
            [pltpu.VMEM((ROWS, TOK, D), BF)],
            us=8,
            name="mlp",
        )

    d0, d1, act0, r1, e1 = mlp(0, xn2s[:2], zero, zero)
    d2, d3, act1, r1, e1 = mlp(1, xn2s[2:], r1, e1)
    res = call(
        fc2_body,
        [big] * 4 + [out((RANK, 4096), BF)],
        [info, act0, act1, *g_all, w2a, w2b, fc2_r, *xs, r1, e1],
        [pltpu.VMEM((ROWS, D, TOK), BF)],
        us=6,
        name="fc2",
    )
    m_parts, mlp_pack = res[:4], res[4]
    d_mid, g_attn = call(
        norm2_back_body,
        [out((TOK, D), F32), big],
        [*reduce_col([d0, d1, d2, d3]), mid, *gs, *xs],
        smem=0,
        us=1.5,
        name="norm2_back",
    )
    ga = gather_col(g_attn)

    def d_heads(blocks, heads, r_in, e_in):
        return call(
            d_heads_body,
            [out((512, 256), BF), out((RANK, TOK), F32), small],
            [info, *blocks, wfa, wfb, *xs, proj_r, heads, r_in, e_in],
            [pltpu.VMEM((ROWS, TOK, TOK), BF)],
            us=1.5,
            name="d_heads",
        )

    dh0, pr, pe = d_heads(ga[:2], heads0, jnp.zeros((RANK, TOK), F32), zero)
    dq0, dkp, dko, dkc = call(
        attend_back_a_body,
        [out((512, 256), BF), out((512, 512), F32), out((512, 512), F32), out((512, 512), BF)],
        [info, slopes, q, kvp, kvo, kvc, heads0, dh0, lse0],
        smem=2,
        us=16,
        name="attend_back_a",
    )
    dh1, pr, pe = d_heads(ga[2:], heads1, pr, pe)
    (proj_pack,) = call(
        proj_grads_body, [out((RANK, 1280), BF)], [info, pr, pe], us=0.5, name="proj_grads"
    )
    dq1, dko = call(
        attend_back_b_body,
        [out((512, 256), F32), out((512, 512), BF)],
        [info, slopes, q, kvo, heads1, dh1, lse1, dko],
        [pltpu.VMEM((512, 512), F32)],
        smem=2,
        us=8,
        name="attend_back_b",
    )
    dkr = lax.ppermute(dko, "row", Z_SWAP)
    dq1, dkp, dkc = call(
        attend_back_c_body,
        [out((512, 256), BF), out((512, 512), F32), out((512, 512), BF)],
        [info, slopes, q, kvp, kvc, heads1, dh1, lse1, dkp, dkc, dq1],
        smem=2,
        us=8,
        name="attend_back_c",
    )
    hidden = call(
        hidden_body,
        [out((TOK, TOK), BF)] * 4,
        [*reduce_col(m_parts), mid, *xs],
        smem=0,
        us=1,
        name="hidden",
    )
    hidden_out = unroute(hidden, BF)
    res = call(
        qkv_back_body,
        [big] * 4 + [out((RANK, 1792), BF)],
        [info, dq0, dq1, dkp, dkr, dkc, *xn1s, wq, *xs, qkv_e],
        us=6,
        name="qkv_back",
    )
    q_parts, qkv_pack = res[:4], res[4]
    ins = call(
        norm1_back_body,
        [out((TOK, TOK), BF)] * 4,
        [*reduce_col(q_parts), d_mid, *xs],
        smem=0,
        us=1,
        name="norm1_back",
    )
    input_gradient = unroute(ins, F32)
    early = call(
        add_two_body,
        [out((RANK, 5376), BF)],
        [
            mlp_pack, lax.ppermute(mlp_pack, "row", Z_SWAP),
            proj_pack, lax.ppermute(proj_pack, "row", Z_SWAP),
        ],
        smem=0,
        us=0.5,
        name="add_early",
    )[0]
    o_fc1r, o_f2e, o_f1e, o_f2r, o_pe, o_pr = spread_grads(
        early,
        [(1024, True), (1024, True), (1024, False), (1024, False), (1024, True), (256, False)],
        info,
        choices,
    )
    late = call(
        add_body,
        [out((RANK, 1792), BF)],
        [qkv_pack, lax.ppermute(qkv_pack, "row", Z_SWAP)],
        smem=0,
        us=0.5,
        name="add_late",
    )[0]
    o_qr, o_qe = spread_grads(late, [(1024, True), (768, False)], info, choices)
    return (
        hidden_out,
        input_gradient,
        flip(o_qr),
        o_qe,
        flip(o_pr),
        o_pe,
        flip(o_fc1r),
        o_f1e,
        flip(o_f2r),
        o_f2e,
    )


def solution(mesh):
    placed = (
        P(("dp", "col"), "row"),
        P(("dp", "col"), "row"),
        P("row"),
        P("row"),
        P("row", "col"),
        P(),
        P("col", "row"),
        P("row"),
        P("row"),
        P("row"),
        P("row", "col"),
        P(),
        P("col", "row"),
        P("row"),
        P(None, "row", None),
        P(),
        P(None, "col", None),
        P(None, None, "row"),
        P(None, "row", None),
        P(),
        P(None, "col", None),
        P(None, None, "row"),
        P("dp"),
        P("dp"),
    )
    return jax.shard_map(
        body,
        mesh=mesh,
        in_specs=placed,
        out_specs=(P(("dp", "col"), "row"), P(("dp", "col"), "row")) + (P(),) * 8,
        check_vma=False,
    )
```

```python
import functools

import jax
import jax.numpy as jnp
from jax import lax
from jax.experimental import pallas as pl
from jax.experimental.pallas import tpu as pltpu
from jax.sharding import PartitionSpec as P

D = 1024
HEADS = 16
HEAD = 64
FF = 4096
RANK = 16
COUNT = 8
PROMPT = 1024
CONT = 128
NCONT = 8
GROUPS_DEV = 2

EPSILON = 1e-05
SCALE = 2.0
GELU_A = 0.7978845608028654
GELU_B = 0.044715
ROWS = 4
COLS = 4
TOK = 256
BLOCK = 128
LOW = -1e30
W_SMALL = 5e8
W_BIG = 5e8

BF = jnp.bfloat16
F32 = jnp.float32

VM = pl.BlockSpec(memory_space=pltpu.VMEM)
SM = pl.BlockSpec(memory_space=pltpu.SMEM)
HB = pl.BlockSpec(memory_space=pltpu.HBM)

CORE_SWAP = [(0, 1), (1, 0), (2, 3), (3, 2)]
Y_SWAP = [(0, 2), (2, 0), (1, 3), (3, 1)]
Z_SWAP = [(0, 1), (1, 0), (2, 3), (3, 2)]


def nn(a, b):
    return lax.dot_general(a, b, (((1,), (0,)), ((), ())), preferred_element_type=F32)


def nt(a, b):
    return lax.dot_general(a, b, (((1,), (1,)), ((), ())), preferred_element_type=F32)


def tn(a, b):
    return lax.dot_general(a, b, (((0,), (0,)), ((), ())), preferred_element_type=F32)


def f32(v):
    return v.astype(F32)


def bf(v):
    return v.astype(BF)


class Far:
    def __init__(self, value):
        self.value = value


def far(values):
    return [Far(v) for v in values]


def call(
    body, outs, ins, scratch=(), smem=1, limit=40, us=1, raw=(), weight=W_SMALL, name=None
):
    values = [
        pltpu.with_memory_space_constraint(v.value, pltpu.HBM) if isinstance(v, Far) else v
        for v in ins
    ]
    fetched = [i for i, v in enumerate(ins) if isinstance(v, Far) and i not in raw]
    specs = [SM] * smem
    for v in ins[smem:]:
        specs.append(HB if isinstance(v, Far) else VM)
    nbytes = sum(v.size * v.dtype.itemsize for v in values)
    nbytes += sum(o.size * o.dtype.itemsize for o in outs)
    extra = [pltpu.VMEM(values[i].shape, values[i].dtype) for i in fetched]
    if fetched:
        extra.append(pltpu.SemaphoreType.DMA((len(fetched),)))

    def whole(*refs):
        refs = list(refs)
        if fetched:
            sem = refs[-1]
            buffers = refs[-1 - len(fetched) : -1]
            refs = refs[: -1 - len(fetched)]
            copies = []
            for n, (i, buffer) in enumerate(zip(fetched, buffers)):
                copies.append(pltpu.make_async_copy(refs[i], buffer, sem.at[n]))
                copies[-1].start()
                refs[i] = buffer
            for copy in copies:
                copy.wait()
        body(*refs)

    return pl.pallas_call(
        whole,
        out_shape=tuple(outs),
        in_specs=specs,
        out_specs=tuple([VM] * len(outs)),
        scratch_shapes=list(scratch) + extra,
        compiler_params=pltpu.CompilerParams(vmem_limit_bytes=limit << 20),
        cost_estimate=pl.CostEstimate(
            flops=int(us * weight), bytes_accessed=nbytes // 8, transcendentals=0
        ),
        name=name,
    )(*values)


def after(value, *others):
    res = lax.optimization_barrier((value, others))
    return res[0]


def out(shape, dtype):
    return jax.ShapeDtypeStruct(shape, dtype)


def block_at(zl, c, j):
    return c * 4 + zl + j * (3 - 2 * zl)


def fill_order(info, order):
    base = info[3]
    first = jnp.int32(0)
    second = jnp.int32(NCONT)
    for j in range(GROUPS_DEV * NCONT):
        own = info[16 + j] == base
        slot = jnp.where(own, first, second)
        order[slot] = jnp.int32(j)
        first = first + jnp.where(own, 1, 0)
        second = second + jnp.where(own, 0, 1)


def place_of(info, order, z, core, j):
    prompt = (z // 2) * 8 + block_at(lax.rem(z, 2), core, j)
    cont = order[4 * z + 2 * core + j]
    return jnp.where(info[1] == 0, prompt, cont)


def route_body(info, own, oth, o0, o1, o2, o3, order):
    fill_order(info, order)
    c = info[2]
    for s, dst in enumerate((o0, o1, o2, o3)):
        z = lax.rem(info[0] + s, ROWS)
        for j in range(2):
            src = place_of(info, order, z, c, j)
            at = pl.ds(pl.multiple_of(lax.rem(src, 8) * BLOCK, BLOCK), BLOCK)
            mine = src // 8 == c

            @pl.when(mine)
            def _():
                dst[pl.ds(j * BLOCK, BLOCK), :] = own[at, :]

            @pl.when(jnp.logical_not(mine))
            def _():
                dst[pl.ds(j * BLOCK, BLOCK), :] = oth[at, :]


def route_pack_body(
    info, own, oth, g1, c1, pb, g2, c2, fb, qr, fr, pe, fe,
    o0, o1, o2, o3, order, v0, v1, v2, v3, v4, v5, mats, sem,
):
    vecs = (v0, v1, v2, v3, v4, v5)
    pairs = list(zip((g1, c1, pb, g2, c2, fb), vecs))
    for k in range(ROWS):
        which = lax.rem(info[0] + k, ROWS) // 2
        a = jnp.where(which == 0, info[32], info[33])
        pairs += [(v.at[a], mats.at[4 * k + i]) for i, v in enumerate((qr, fr, pe, fe))]
    copies = [pltpu.make_async_copy(a, b, sem.at[i]) for i, (a, b) in enumerate(pairs)]
    for copy in copies:
        copy.start()
    route_body(info, own, oth, o0, o1, o2, o3, order)
    for copy in copies:
        copy.wait()
    for k, dst in enumerate((o0, o1, o2, o3)):
        head = [f32(v[...]).reshape(1, TOK) for v in vecs]
        dst[256:272, :] = bf(jnp.concatenate(head + [jnp.zeros((10, TOK), F32)], axis=0))
        for i in range(4):
            dst[272 + 16 * i : 288 + 16 * i, :] = mats[4 * k + i]


def stack_body(a0, a1, a2, a3, dst):
    for k, v in enumerate((a0, a1, a2, a3)):
        dst[k * TOK : (k + 1) * TOK, :] = v[...]


def route_all_body(info, own, oth, dst, order):
    fill_order(info, order)
    c = info[2]
    for z in range(ROWS):
        for j in range(2):
            src = place_of(info, order, z, c, j)
            at = pl.ds(pl.multiple_of(lax.rem(src, 8) * BLOCK, BLOCK), BLOCK)
            mine = src // 8 == c

            @pl.when(mine)
            def _():
                dst[z, pl.ds(j * BLOCK, BLOCK), :] = own[at, :]

            @pl.when(jnp.logical_not(mine))
            def _():
                dst[z, pl.ds(j * BLOCK, BLOCK), :] = oth[at, :]


def unroute_body(relative, info, a, b, dst, order):
    fill_order(info, order)
    c = info[2]
    for s in range(ROWS):
        z = lax.rem(info[0] + s, ROWS) if relative else s
        for other, src in ((0, a), (1, b)):
            core = c if other == 0 else 1 - c
            for j in range(2):
                at = place_of(info, order, z, core, j)

                @pl.when(at // 8 == c)
                def _():
                    rows = pl.ds(pl.multiple_of(lax.rem(at, 8) * BLOCK, BLOCK), BLOCK)
                    dst[rows, :] = src[pl.ds(s * TOK + j * BLOCK, BLOCK), :].astype(dst.dtype)


def cols(k, width=TOK):
    return pl.ds(k * width, width)


def row_stats(parts):
    total = sum(jnp.sum(v, axis=1, keepdims=True) for v in parts)
    mean = total * (1.0 / D)
    dev = [v - mean for v in parts]
    var = sum(jnp.sum(v * v, axis=1, keepdims=True) for v in dev) * (1.0 / D)
    rstd = lax.rsqrt(var + EPSILON)
    return [v * rstd for v in dev], rstd


def norm1_body(x0, x1, x2, x3, xn):
    for t in range(2):
        rows = pl.ds(t * 128, 128)
        hat, _ = row_stats([f32(v[rows, :]) for v in (x0, x1, x2, x3)])
        for k, pack in enumerate((x0, x1, x2, x3)):
            xn[rows, cols(k)] = bf(hat[k] * f32(pack[256:257, :]) + f32(pack[257:258, :]))


def both(a, b, rows, k):
    return f32(a[rows, cols(k)]) + f32(b[rows, cols(k)])


def norm2_body(a, b, x0, x1, x2, x3, mid, xn):
    for t in range(2):
        rows = pl.ds(t * 128, 128)
        parts = []
        for k, x in enumerate((x0, x1, x2, x3)):
            v = f32(x[rows, :]) + both(a, b, rows, k) + f32(x[258:259, :])
            mid[rows, cols(k)] = v
            parts.append(v)
        hat, _ = row_stats(parts)
        for k, pack in enumerate((x0, x1, x2, x3)):
            xn[rows, cols(k)] = bf(hat[k] * f32(pack[259:260, :]) + f32(pack[260:261, :]))


def norm_back(hat, rstd, grads):
    total = sum(jnp.sum(g, axis=1, keepdims=True) for g in grads) * (1.0 / D)
    along = sum(jnp.sum(g * h, axis=1, keepdims=True) for g, h in zip(grads, hat)) * (1.0 / D)
    return [rstd * (g - total - h * along) for g, h in zip(grads, hat)]


def norm2_back_body(
    a, b, pack, mid, g, x0, x1, x2, x3, d_mid, g_attn
):
    g_attn[256:320, :] = pack[...]
    for t in range(2):
        rows = pl.ds(t * 128, 128)
        hat, rstd = row_stats([mid[rows, cols(k)] for k in range(4)])
        grads = []
        for k, pack in enumerate((x0, x1, x2, x3)):
            grads.append(both(a, b, rows, k) * f32(pack[259:260, :]))
        back = norm_back(hat, rstd, grads)
        for k in range(4):
            v = f32(g[rows, cols(k)]) + back[k]
            d_mid[rows, cols(k)] = v
            g_attn[rows, cols(k)] = bf(v)


def norm1_back_body(a, b, d_mid, x0, x1, x2, x3, i0, i1, i2, i3):
    for t in range(2):
        rows = pl.ds(t * 128, 128)
        hat, rstd = row_stats([f32(v[rows, :]) for v in (x0, x1, x2, x3)])
        grads = []
        for k, pack in enumerate((x0, x1, x2, x3)):
            grads.append(both(a, b, rows, k) * f32(pack[256:257, :]))
        back = norm_back(hat, rstd, grads)
        for k, dst in enumerate((i0, i1, i2, i3)):
            dst[rows, :] = bf(d_mid[rows, cols(k)] + back[k])


def hidden_body(info, a, b, mid, x0, x1, x2, x3, dst):
    for t in range(2):
        rows = pl.ds(t * 128, 128)
        for k, pack in enumerate((x0, x1, x2, x3)):
            v = mid[rows, cols(k)] + both(a, b, rows, k) + f32(pack[261:262, :])
            dst[rel(info, k), rows, :] = bf(v)


def join_body(info, v, dst):
    for k in range(ROWS):
        dst[:, cols(k)] = v[rel(info, k)]


def slab_rows(info, b):
    y = jnp.bitwise_xor(info[1], b // 2)
    c = jnp.bitwise_xor(info[2], b % 2)
    return y, c


def low_lanes(rows):
    return lax.broadcasted_iota(jnp.int32, (rows, 128), 1) < HEAD


def rel(info, k):
    return lax.rem(info[0] - k + ROWS, ROWS)


def rel_cols(info, k):
    return pl.ds(pl.multiple_of(rel(info, k) * TOK, TOK), TOK)


def lanes_at(at, size):
    return pl.ds(pl.multiple_of(at, 128), size)


def rows_at(i, size):
    return pl.ds(pl.multiple_of(i * size, size), size)


def prepare_body(
    info, wq, wp, w1, w2, qe, fe, pr, fr, first, c1, c2, o_qe, o_fe, o_pr, o_fr, sem
):
    half = info[8]
    a = jnp.where(info[5] == 0, info[32], info[33])
    rows = rows_at(half, 128)
    pairs = [(wq.at[rows], first.at[:, 0:768]), (wp.at[rows], first.at[:, 768:1024])]
    pairs += [(qe.at[a, :, lanes_at(info[6] * 768, 768)], o_qe)]
    pairs += [(fe.at[a, :, lanes_at(info[6] * 1024, 1024)], o_fe)]
    pairs += [(pr.at[a], o_pr), (fr.at[a], o_fr)]
    for j in range(ROWS):
        pairs += [(w1.at[rows], c1.at[j]), (w2.at[rows_at(half, 512)], c2.at[j])]
    copies = [pltpu.make_async_copy(x, y, sem.at[i]) for i, (x, y) in enumerate(pairs)]
    for copy in copies:
        copy.start()
    for copy in copies:
        copy.wait()


def assemble_body(info, own_q, own_p, z1, z2, z3, s1, s2, s3, ws, wp, sem):
    half = info[8]
    copies = [
        pltpu.make_async_copy(own_q, ws.at[0], sem.at[0]),
        pltpu.make_async_copy(own_p, wp.at[0], sem.at[1]),
    ]
    for k, (zv, sv) in enumerate(((z1, s1), (z2, s2), (z3, s3))):
        for n, (v, at) in enumerate(((zv, half), (sv, 1 - half))):
            rows = rows_at(at, 128)
            at = 2 + 4 * k + 2 * n
            copies.append(
                pltpu.make_async_copy(v.at[:, 0:768], ws.at[k + 1, rows], sem.at[at])
            )
            copies.append(
                pltpu.make_async_copy(v.at[:, 768:1024], wp.at[k + 1, rows], sem.at[at + 1])
            )
    for copy in copies:
        copy.start()
    for copy in copies:
        copy.wait()


def qkv_body(
    info, x0, x1, x2, x3, ws, p0, p1, p2, p3, bias, expand, q, kvp, kvc
):
    ps = (p0, p1, p2, p3)
    low = low_lanes(TOK)
    for b, x in enumerate((x0, x1, x2, x3)):
        y, c = slab_rows(info, b)
        acc = sum(nn(x[:, cols(k)], ws[k]) for k in range(4))
        u = bf(sum(nt(x[:, cols(k)], ps[k][272:288, :]) for k in range(4)))
        acc = acc + f32(bias[...]) + SCALE * nn(u, expand[...])
        kv = []
        for pair in range(2):
            at = 384 * pair
            g0, g1, g2 = (acc[:, at + 128 * i : at + 128 * i + 128] for i in range(3))
            q[rows_at(y * 2 + c, TOK), cols(pair, 128)] = bf(
                bf(jnp.where(low, g0, g1)) * BF(0.125)
            )
            kv.append((bf(pltpu.roll(jnp.where(low, g2, g0), 64, 1)), bf(jnp.where(low, g1, g2))))
        rows = rows_at(c, TOK)

        @pl.when(y == 0)
        def _():
            for pair in range(2):
                kvp[rows, cols(pair, 128)] = kv[pair][0]
                kvp[rows, cols(2 + pair, 128)] = kv[pair][1]

        @pl.when(y == 1)
        def _():
            for pair in range(2):
                kvc[rows, cols(pair, 128)] = kv[pair][0]
                kvc[rows, cols(2 + pair, 128)] = kv[pair][1]


WIDE = 256


def stacked(v, low):
    zero = jnp.zeros_like(v)
    return jnp.concatenate([jnp.where(low, v, zero), jnp.where(low, zero, v)], axis=0)


def split_id(shape, axis):
    lane = lax.broadcasted_iota(jnp.int32, shape, axis)
    return lane, jnp.where(lane < BLOCK, lane, lane - BLOCK)


def chunk_place(shape, axis, side, n):
    lane, within = split_id(shape, axis)
    first = block_at(side, n, 0) * BLOCK
    second = block_at(side, n, 1) * BLOCK
    return within + jnp.where(lane < BLOCK, first, second)


def keep_state(state, low):
    top, total, acc = state
    lane = lax.broadcasted_iota(jnp.int32, (2 * BLOCK, 128), 1)
    spot = lax.rem(lane, HEAD)
    row = lax.broadcasted_iota(jnp.int32, (2 * BLOCK, 128), 0)
    own = (lane < HEAD) == (row < BLOCK)
    return jnp.where(own, acc, jnp.where(spot == 0, top, total))


def load_state(v):
    lane = lax.broadcasted_iota(jnp.int32, (2 * BLOCK, 128), 1)
    row = lax.broadcasted_iota(jnp.int32, (2 * BLOCK, 128), 0)
    spot = jnp.where(row < BLOCK, HEAD, 0)
    top = jnp.max(jnp.where(lane == spot, v, LOW), axis=1, keepdims=True)
    total = jnp.sum(jnp.where(lane == spot + 1, v, 0.0), axis=1, keepdims=True)
    return top, total, v


def soft_update(state, s, v):
    if state is None:
        top = jnp.max(s, axis=1, keepdims=True)
        p = jnp.exp(s - top)
        return top, jnp.sum(p, axis=1, keepdims=True), nn(bf(p), v)
    top, total, acc = state
    new = jnp.maximum(top, jnp.max(s, axis=1, keepdims=True))
    p = jnp.exp(s - new)
    shrink = jnp.exp(top - new)
    total = total * shrink + jnp.sum(p, axis=1, keepdims=True)
    return new, total, acc * shrink + nn(bf(p), v)


def head_slopes(slopes, shape, axis):
    lane = lax.broadcasted_iota(jnp.int32, shape, axis)
    return [
        jnp.where(lane < BLOCK, slopes[2 * pair], slopes[2 * pair + 1]) for pair in range(2)
    ]


def attend_chunk(q2, states, kv, rows, place, base, slope, spot, masked):
    res = []
    away = place - base
    for pair in range(2):
        s = nt(q2[pair], kv[rows, cols(pair, 128)]) + slope[pair] * away.astype(F32)
        if masked:
            s = jnp.where(away <= spot, s, LOW)
        res.append(soft_update(states[pair], s, kv[rows, cols(2 + pair, 128)]))
    return res


def attend_first_body(info, slopes, q, kvp, kvc, state):
    zl = info[4]
    low = low_lanes(BLOCK)
    _, spot = split_id((2 * BLOCK, 1), 0)
    slope = head_slopes(slopes, (2 * BLOCK, 1), 0)
    places = [chunk_place((1, WIDE), 1, zl, n) for n in range(2)]

    def load(i):
        return [stacked(q[rows_at(i, BLOCK), cols(pair, 128)], low) for pair in range(2)]

    def save(states, i):
        for pair in range(2):
            state[rows_at(i, WIDE), cols(pair, 128)] = keep_state(states[pair], low)

    def prompt_block(j, _):
        for n in range(2):
            i = 2 * n + j
            base = block_at(zl, n, j) * BLOCK
            q2 = load(i)
            states = [None, None]
            for m in range(n, -1, -1):
                states = attend_chunk(
                    q2, states, kvp, pl.ds(m * WIDE, WIDE), places[m], base, slope, spot, m == n
                )
            save(states, i)
        return 0

    lax.fori_loop(0, 2, prompt_block, 0)

    def cont_block(j, _):
        q2 = load(4 + j)
        own_place = lax.broadcasted_iota(jnp.int32, (1, BLOCK), 1)
        states = attend_chunk(
            q2, [None, None], kvc, rows_at(j, BLOCK), own_place, 0, slope, spot, True
        )
        for m in range(2):
            states = attend_chunk(
                q2, states, kvp, pl.ds(m * WIDE, WIDE), places[m], PROMPT, slope, spot, False
            )
        save(states, 4 + j)
        return 0

    lax.fori_loop(0, 4, cont_block, 0)


def attend_rest_body(
    which, info, slopes, q, kvo, state, ws, reduce, p0, p1, p2, p3, heads, lse, o0, o1
):
    zl = info[4]
    y = info[1] if which == 0 else 1 - info[1]
    low = low_lanes(BLOCK)
    _, spot = split_id((2 * BLOCK, 1), 0)
    slope = head_slopes(slopes, (2 * BLOCK, 1), 0)
    places = [chunk_place((1, WIDE), 1, 1 - zl, n) for n in range(2)]

    def load(i):
        q2 = [stacked(q[rows_at(i, BLOCK), cols(pair, 128)], low) for pair in range(2)]
        states = [load_state(state[rows_at(i, WIDE), cols(pair, 128)]) for pair in range(2)]
        return q2, states

    def finish(states, j):
        for pair in range(2):
            top, total, acc = states[pair]
            res = acc / total
            heads[rows_at(j, BLOCK), cols(pair, 128)] = bf(
                jnp.where(low, res[:BLOCK], res[BLOCK:])
            )
            kept = jnp.transpose(jnp.broadcast_to(top + jnp.log(total), (2 * BLOCK, 128)))
            lse[pl.ds(pair * 4 + j, 1), :] = kept[0:1, :]

    @pl.when(y == 0)
    def _():
        def prompt_block(j, _):
            for n in range(2):
                i = 2 * n + j
                base = block_at(zl, n, j) * BLOCK
                q2, states = load(i)
                for m in range(n + 1):
                    states = attend_chunk(
                        q2, states, kvo, pl.ds(m * WIDE, WIDE), places[m], base, slope, spot, m == n
                    )
                finish(states, i)
            return 0

        lax.fori_loop(0, 2, prompt_block, 0)

    @pl.when(y == 1)
    def _():
        def cont_block(j, _):
            q2, states = load(4 + j)
            for m in range(2):
                states = attend_chunk(
                    q2, states, kvo, pl.ds(m * WIDE, WIDE), places[m], PROMPT, slope, spot, False
                )
            finish(states, j)
            return 0

        lax.fori_loop(0, 4, cont_block, 0)

    ps = (p0, p1, p2, p3)
    for b, dst in enumerate((o0, o1)):
        c = jnp.bitwise_xor(info[2], b)
        h = heads[rows_at(c, TOK), :]
        u = bf(nt(h, reduce[...]))
        for k in range(4):
            dst[:, cols(k)] = bf(nn(h, ws[k]) + SCALE * nn(u, ps[k][304:320, :]))


def mlp_pre_body(info, x0, x1, w1, p0, p1, p2, p3, bias, expand, act, slope):
    ps = (p0, p1, p2, p3)
    for b, x in enumerate((x0, x1)):
        u = bf(sum(nt(x[:, cols(k)], ps[k][288:304, :]) for k in range(4)))
        pre = sum(nn(x[:, cols(k)], w1[rel(info, k)]) for k in range(4))
        pre = pre + f32(bias[...]) + SCALE * nn(u, expand[...])
        sq = pre * pre
        t = jnp.tanh(pre * (GELU_A + (GELU_A * GELU_B) * sq))
        half = 0.5 + 0.5 * t
        act[b] = bf(pre * half)
        slope[b] = bf(
            half + (0.5 * pre) * (1.0 - t * t) * (GELU_A + (3.0 * GELU_A * GELU_B) * sq)
        )


def mlp_back_body(
    info, x0, x1, g0, g1, slope, w1, w2, p0, p1, p2, p3, expand, reduce, r_in, e_in,
    d0, d1, r_out, e_out,
):
    ps = (p0, p1, p2, p3)
    rv, ev = r_in[...], e_in[...]
    for b, (x, g, dx) in enumerate(((x0, g0, d0), (x1, g1, d1))):
        u = bf(sum(nt(x[:, cols(k)], ps[k][288:304, :]) for k in range(4)))
        du2 = bf(SCALE * sum(nt(g[:, cols(k)], ps[k][320:336, :]) for k in range(4)))
        d_act = sum(nt(g[:, cols(k)], w2[rel(info, k)]) for k in range(4)) + nn(du2, reduce[...])
        d_pre = bf(d_act * f32(slope[b]))
        du = bf(SCALE * nt(d_pre, expand[...]))
        for k in range(4):
            dx[:, cols(k)] = bf(nt(d_pre, w1[rel(info, k)]) + nn(du, ps[k][288:304, :]))
        rv = rv + tn(du, x[...])
        ev = ev + tn(u, d_pre)
    r_out[...] = rv
    e_out[...] = ev


def fc2_body(
    info, a0, a1, g0, g1, g2, g3, w2, reduce, p0, p1, p2, p3, r1, e1,
    m0, m1, m2, m3, grads,
):
    ps = (p0, p1, p2, p3)
    rv = ev = 0.0
    for b, (g, m) in enumerate(zip((g0, g1, g2, g3), (m0, m1, m2, m3))):
        act = a0[b] if b < 2 else a1[b - 2]
        du = bf(SCALE * sum(nt(g[:, cols(k)], ps[k][320:336, :]) for k in range(4)))
        u = bf(nt(act, reduce[...]))
        for k in range(4):
            m[:, cols(k)] = bf(nn(act, w2[rel(info, k)]) + SCALE * nn(u, ps[k][320:336, :]))
        rv = rv + tn(du, act)
        ev = ev + SCALE * tn(u, g[...])
    for k in range(4):
        grads[0:16, rel_cols(info, k)] = bf(r1[:, cols(k)])
        grads[16:32, rel_cols(info, k)] = bf(ev[:, k * TOK : k * TOK + TOK])
    grads[32:48, :] = bf(SCALE * e1[...])
    grads[48:64, :] = bf(rv)


def d_heads_body(
    info, g0, g1, ws, p0, p1, p2, p3, reduce, heads, r_in, e_in, dh, r_out, e_out
):
    ps = (p0, p1, p2, p3)
    rv, ev = r_in[...], e_in[...]
    for b, g in enumerate((g0, g1)):
        rows = rows_at(jnp.bitwise_xor(info[2], b), TOK)
        h = heads[rows, :]
        u = bf(nt(h, reduce[...]))
        du = bf(SCALE * sum(nt(g[0:256, cols(k)], ps[k][304:320, :]) for k in range(4)))
        v = sum(nt(g[0:256, cols(k)], ws[k]) for k in range(4)) + nn(du, reduce[...])
        dh[rows, :] = bf(v)
        rv = rv + tn(du, h)
        ev = ev + SCALE * tn(u, g[0:256, :])
    r_out[...] = rv
    e_out[...] = ev


def back_load(heads, d_heads, lse, q, qi, j, low):
    res = []
    for pair in range(2):
        lane = cols(pair, 128)
        q2 = stacked(q[rows_at(qi, BLOCK), lane], low)
        do = d_heads[rows_at(j, BLOCK), lane]
        both = jnp.transpose(f32(do) * f32(heads[rows_at(j, BLOCK), lane]))
        delta = jnp.concatenate(
            [
                jnp.sum(both[:HEAD], axis=0, keepdims=True),
                jnp.sum(both[HEAD:], axis=0, keepdims=True),
            ],
            axis=1,
        )
        res.append((q2, stacked(do, low), delta, lse[pl.ds(pair * 4 + j, 1), :]))
    return res


def back_chunk(args, kv, d_kv, d_at, rows, place, base, slope, spot, masked, store, d_qs):
    away = place - base
    res = []
    for pair in range(2):
        q2, do2, delta, kept = args[pair]
        lane = cols(pair, 128)
        vlane = cols(2 + pair, 128)
        k = kv[rows, lane]
        s = nt(k, q2) + (away.astype(F32) * slope[pair] - kept)
        p = jnp.exp(s)
        if masked:
            p = jnp.where(away <= spot, p, 0.0)
        ds = bf(p * (nt(kv[rows, vlane], do2) - delta))
        dk = nn(ds, q2)
        dv = nn(bf(p), do2)
        if store:
            d_kv[d_at, lane] = bf(dk)
            d_kv[d_at, vlane] = bf(dv)
        else:
            d_kv[d_at, lane] += dk
            d_kv[d_at, vlane] += dv
        d_q = tn(ds, k)
        res.append(d_q if d_qs is None else d_qs[pair] + d_q)
    return res


def back_common(info, slopes):
    low = low_lanes(BLOCK)
    _, spot = split_id((1, 2 * BLOCK), 1)
    slope = head_slopes(slopes, (1, 2 * BLOCK), 1)
    zl = info[4]
    own = [chunk_place((WIDE, 1), 0, zl, n) for n in range(2)]
    oth = [chunk_place((WIDE, 1), 0, 1 - zl, n) for n in range(2)]
    return zl, low, spot, slope, own, oth


def fold(d_q, low):
    return jnp.where(low, d_q[:BLOCK], d_q[BLOCK:]) * 0.125


def back_sweep(info, slopes, y, q, heads, d_heads, lse, sides, kvc, dkc, finish):
    zl, low, spot, slope, own, oth = back_common(info, slopes)
    place_sets = {"own": own, "oth": oth}

    @pl.when(y == 0)
    def _():
        def prompt_block(j, _):
            for n in range(2):
                i = 2 * n + j
                args = back_load(heads, d_heads, lse, q, i, i, low)
                base = block_at(zl, n, j) * BLOCK
                d_qs = None
                for side, kv, d_kv in sides:
                    for m in range(n + 1):
                        rows = pl.ds(m * WIDE, WIDE)
                        d_qs = back_chunk(
                            args, kv, d_kv, rows, rows, place_sets[side][m], base, slope, spot,
                            m == n, False, d_qs,
                        )
                finish(d_qs, i, low)
            return 0

        lax.fori_loop(0, 2, prompt_block, 0)

    @pl.when(y == 1)
    def _():
        def cont_block(j, _):
            args = back_load(heads, d_heads, lse, q, 4 + j, j, low)
            d_qs = None
            if kvc is not None:
                mine = rows_at(j, BLOCK)
                own_place = lax.broadcasted_iota(jnp.int32, (BLOCK, 1), 0)
                d_qs = back_chunk(
                    args, kvc, dkc, mine, mine, own_place, 0, slope, spot, True, True, d_qs
                )
            for side, kv, d_kv in sides:
                for m in range(2):
                    rows = pl.ds(m * WIDE, WIDE)
                    d_qs = back_chunk(
                        args, kv, d_kv, rows, rows, place_sets[side][m], PROMPT, slope, spot,
                        False, False, d_qs,
                    )
            finish(d_qs, j, low)
            return 0

        lax.fori_loop(0, 4, cont_block, 0)


def attend_back_a_body(
    info, slopes, q, kvp, kvo, kvc, heads, d_heads, lse, dq, dkp, dko, dkc
):
    dkp[...] = jnp.zeros_like(dkp)
    dko[...] = jnp.zeros_like(dko)
    dkc[...] = jnp.zeros_like(dkc)

    def finish(d_qs, j, low):
        for pair in range(2):
            dq[rows_at(j, BLOCK), cols(pair, 128)] = bf(fold(d_qs[pair], low))

    back_sweep(
        info, slopes, info[1], q, heads, d_heads, lse,
        (("own", kvp, dkp), ("oth", kvo, dko)), kvc, dkc, finish,
    )


def attend_back_b_body(info, slopes, q, kvo, heads, d_heads, lse, dko_in, dq, dko, acc):
    acc[...] = dko_in[...]

    def finish(d_qs, j, low):
        for pair in range(2):
            dq[rows_at(j, BLOCK), cols(pair, 128)] = fold(d_qs[pair], low)

    back_sweep(
        info, slopes, 1 - info[1], q, heads, d_heads, lse,
        (("oth", kvo, acc),), None, None, finish,
    )
    dko[...] = bf(acc[...])


def attend_back_c_body(
    info, slopes, q, kvp, kvc, heads, d_heads, lse, dkp_in, dkc_in, dq_in, dq, dkp, dkc
):
    dkp[...] = dkp_in[...]
    dkc[...] = dkc_in[...]

    def finish(d_qs, j, low):
        for pair in range(2):
            lane = cols(pair, 128)
            rows = rows_at(j, BLOCK)
            dq[rows, lane] = bf(dq_in[rows, lane] + fold(d_qs[pair], low))

    back_sweep(
        info, slopes, 1 - info[1], q, heads, d_heads, lse,
        (("own", kvp, dkp),), kvc, dkc, finish,
    )


def qkv_back_body(
    info, dq0, dq1, dkp, dkr, dkc, x0, x1, x2, x3, ws, p0, p1, p2, p3, expand, pr, pe,
    o0, o1, o2, o3, grads,
):
    ps = (p0, p1, p2, p3)
    low = low_lanes(TOK)
    sr = se = 0.0
    for b, (x, dst) in enumerate(zip((x0, x1, x2, x3), (o0, o1, o2, o3))):
        y, c = slab_rows(info, b)
        half = rows_at(c, TOK)
        groups = []
        dq = dq0 if b < 2 else dq1
        for pair in range(2):
            vq = f32(dq[half, cols(pair, 128)])
            got = []
            for lane in (cols(pair, 128), cols(2 + pair, 128)):
                prompt = dkp[half, lane] + f32(dkr[half, lane])
                got.append(jnp.where(y == 0, prompt, f32(dkc[half, lane])))
            vk = pltpu.roll(got[0], 64, 1)
            vv = got[1]
            groups += [jnp.where(low, vq, vk), jnp.where(low, vv, vq), jnp.where(low, vk, vv)]
        d = bf(jnp.concatenate(groups, axis=1))
        u = bf(sum(nt(x[:, cols(k)], ps[k][272:288, :]) for k in range(4)))
        du = bf(SCALE * nt(d, expand[...]))
        for k in range(4):
            dst[:, cols(k)] = bf(nt(d, ws[k]) + nn(du, ps[k][272:288, :]))
        sr = sr + tn(du, x[...])
        se = se + SCALE * tn(u, d)
    for k in range(4):
        grads[0:16, rel_cols(info, k)] = bf(sr[:, k * TOK : k * TOK + TOK])
        grads[16:32, rel_cols(info, k)] = bf(pe[:, cols(k)])
    grads[32:48, 0:768] = bf(se)
    grads[32:48, 768:1024] = bf(pr[...])


def add_body(a, b, dst):
    dst[...] = bf(f32(a[...]) + f32(b[...]))


def add(a, b):
    return call(add_body, [out(a.shape, BF)], [a, b], smem=0, us=0.01, name="add")[0]


def add32_body(a, b, dst):
    dst[...] = f32(a[...]) + f32(b[...])


def add32(a, b, us=8):
    return call(add32_body, [out(a.shape, F32)], [a, b], smem=0, us=us, name="add32")[0]


def stage_body(*refs):
    n = len(refs) // 2
    for src, dst in zip(refs[:n], refs[n:]):
        dst[...] = src[...]


def stage(values):
    return call(
        stage_body, [out(v.shape, v.dtype) for v in values], far(values), smem=0, us=0.01, name="stage"
    )


def stage_weight_body(size, info, wa, wb, w, sem):
    copies = []
    for n, (src, at) in enumerate(((wa, info[8]), (wb, 1 - info[8]))):
        for j in range(ROWS):
            copies.append(
                pltpu.make_async_copy(src.at[j], w.at[j, rows_at(at, size)], sem.at[4 * n + j])
            )
    for copy in copies:
        copy.start()
    for copy in copies:
        copy.wait()


def merge_body(info, v0, v1, v2, v3, dst):
    four = (v0, v1, v2, v3)

    def fill(c):
        total = sum(f32(v[256 + 16 * c : 272 + 16 * c, :]) for v in four)
        dst[0:16, :] = bf(total)
        for b, v in enumerate(four):
            rows = pl.ds(pl.multiple_of(16 + 16 * jnp.bitwise_xor(info[6], b), 16), 16)
            dst[rows, :] = v[288 + 16 * c : 304 + 16 * c, :]

    @pl.when(info[2] == 0)
    def _():
        fill(0)

    @pl.when(info[2] == 1)
    def _():
        fill(1)


def pile_body(*refs):
    dst = refs[-1]
    for n, src in enumerate(refs[:-1]):
        dst[n] = src[...]


def expand_early_body(info, own, oth, r1, e2, e1, r2):
    for v in (r1, e2, e1, r2):
        v[...] = jnp.zeros_like(v)

    def fill(src, shared, split):
        for n in range(own.shape[0]):
            there = lax.rem(info[7] + info[10] - n // ROWS, info[10])
            a = info[40 + there * GROUPS_DEV + n % ROWS // 2]
            shared[a] += f32(src[n, 0:16, :])
            for j in range(COLS):
                at = 16 + 16 * j
                split[a, :, cols(j, 1024)] += f32(src[n, at : at + 16, :])

    @pl.when(info[2] == 0)
    def _():
        fill(own, r1, e1)
        fill(oth, e2, r2)

    @pl.when(info[2] == 1)
    def _():
        fill(oth, r1, e1)
        fill(own, e2, r2)


def expand_late_body(info, v0, v1, v2, v3, qr, pe, qe, pr):
    four = (v0, v1, v2, v3)
    for v in (qr, pe, qe, pr):
        v[...] = jnp.zeros_like(v)
    for k in range(v0.shape[0]):
        group = info[5] if k % 2 == 0 else 1 - info[5]
        a = info[40 + k // 2 * GROUPS_DEV + group]
        qr[a] += sum(f32(v[k, 0:16, :]) for v in four)
        pe[a] += sum(f32(v[k, 16:32, :]) for v in four)
        for b, v in enumerate(four):
            j = jnp.bitwise_xor(info[6], b)
            qe[a, :, lanes_at(j * 768, 768)] += f32(v[k, 32:48, :768])
            pr[a, :, lanes_at(j * 256, 256)] += f32(v[k, 32:48, 768:])


def shift(v, k, axis="row"):
    if k == 0:
        return v
    size = lax.axis_size(axis)
    return lax.ppermute(v, axis, [(s, (s + k) % size) for s in range(size)])


def gather_row(v):
    return [v] + [shift(v, k) for k in range(1, ROWS)]


def gather_col(v):
    core = lax.ppermute(v, "col", CORE_SWAP)
    side = lax.ppermute(v, "col", Y_SWAP)
    return [v, core, side, lax.ppermute(side, "col", CORE_SWAP)]


def to_cols(pieces):
    return [pieces[0]] + [shift(pieces[k], ROWS - k) for k in range(1, ROWS)]


def spread(mine, other):
    groups = [mine, other]
    for k in range(1, lax.axis_size("dp")):
        groups += [shift(v, k, "dp") for v in groups[:2]]
    return call(
        pile_body, [out((len(groups), *mine.shape), BF)], groups, smem=0, us=0.01, name="pile"
    )[0]

def body(
    hidden_in,
    out_grad,
    first_norm_gain,
    first_norm_bias,
    qkv_weight,
    qkv_bias,
    proj_weight,
    proj_bias,
    second_norm_gain,
    second_norm_bias,
    fc1_weight,
    fc1_bias,
    fc2_weight,
    second_feed_bias,
    qkv_reduce,
    qkv_expand,
    proj_reduce,
    proj_expand,
    fc1_reduce,
    fc1_expand,
    fc2_reduce,
    fc2_expand,
    adapter_choice,
    cont_prompt,
):
    r = lax.axis_index("row")
    col = lax.axis_index("col")
    dp = lax.axis_index("dp")
    y = col // 2
    c = lax.rem(col, 2)
    zl = lax.rem(r, 2)
    group = r // 2
    half = lax.rem(dp, 2)
    dp_swap = [(k, k ^ 1) for k in range(lax.axis_size("dp"))]
    slopes = jnp.exp2(
        -8.0 * (col * 4 + 1 + jnp.arange(4, dtype=jnp.int32)).astype(F32) / HEADS
    )
    adapter = jnp.where(group == 0, adapter_choice[0], adapter_choice[1])
    n_dp = jnp.int32(lax.axis_size("dp"))
    info = jnp.stack([r, y, c, dp * GROUPS_DEV, zl, group, col, dp, half] + [half, n_dp] + [half] * 5)
    info = jnp.concatenate([info.astype(jnp.int32), cont_prompt, adapter_choice])
    order = pltpu.SMEM((GROUPS_DEV * NCONT,), jnp.int32)
    flip = functools.partial(jnp.transpose, axes=(0, 2, 1))
    big = out((TOK, D), BF)
    small = out((RANK, D), F32)

    other = lax.ppermute(hidden_in, "col", CORE_SWAP)
    vectors = [
        first_norm_gain, first_norm_bias, proj_bias,
        second_norm_gain, second_norm_bias, second_feed_bias,
    ]
    factors = [flip(qkv_reduce), flip(fc1_reduce), proj_expand, fc2_expand]
    pieces = call(
        route_pack_body,
        [out((336, TOK), BF)] * 4,
        [info, Far(hidden_in), Far(other), *far(vectors), *far(factors)],
        [
            order,
            *[pltpu.VMEM((TOK,), BF)] * 6,
            pltpu.VMEM((16, RANK, TOK), BF),
            pltpu.SemaphoreType.DMA((22,)),
        ],
        raw=range(3, 13),
        us=1.5,
        name="route_x",
    )
    xs = [pieces[0]] + [shift(pieces[k], k) for k in range(1, ROWS)]
    packs = far(xs)
    first_half, w1_copies, w2_copies, qkv_e, fc1_e, proj_r, fc2_r = call(
        prepare_body,
        [
            out((128, D), BF), out((ROWS, 128, D), BF), out((ROWS, 512, TOK), BF),
            out((RANK, 768), BF), out((RANK, D), BF), out((RANK, TOK), BF), out((RANK, D), BF),
        ],
        [
            after(info, pieces[0]),
            *far([qkv_weight, proj_weight, fc1_weight, fc2_weight, qkv_expand, fc1_expand]),
            *far([flip(proj_reduce), flip(fc2_reduce)]),
        ],
        [pltpu.SemaphoreType.DMA((14,))],
        raw=range(1, 9),
        us=3,
        name="prepare",
    )
    first_half = after(first_half, xs[1])
    z_parts = [shift(first_half, k) for k in range(1, ROWS)]
    s_parts = [lax.ppermute(v, "dp", dp_swap) for v in z_parts]
    w1a = lax.all_to_all(after(w1_copies, *z_parts), "row", 0, 0)
    wq, wp = call(
        assemble_body,
        [out((ROWS, TOK, 768), BF), out((ROWS, TOK, TOK), BF)],
        [info, *far([qkv_weight, proj_weight, *z_parts, *s_parts])],
        [pltpu.SemaphoreType.DMA((14,))],
        raw=range(1, 9),
        us=15,
        name="assemble",
    )

    def unroute(parts, dtype, *done):
        if isinstance(parts, tuple):
            (joined,) = call(
                stack_body, [out((1024, TOK), BF)], [after(v, *done) for v in to_cols(parts)], smem=0, us=0.5, name="stack"
            )
        else:
            joined = lax.all_to_all(parts, "row", 0, 0).reshape(1024, TOK)
        return call(
            functools.partial(unroute_body, isinstance(parts, tuple)),
            [out((1024, TOK), dtype)],
            [info, joined, lax.ppermute(joined, "col", CORE_SWAP)],
            [order],
            us=2,
            weight=W_BIG,
            name="unroute",
        )[0]

    qkv_b = lax.dynamic_slice_in_dim(qkv_bias, col * 768, 768, 0)[None, :]
    fc1_b = lax.dynamic_slice_in_dim(fc1_bias, col * 1024, 1024, 0)[None, :]

    choices = [adapter_choice] + [
        shift(adapter_choice, k, "dp") for k in range(1, lax.axis_size("dp"))
    ]
    first = after(xs[0], qkv_b, fc1_b, w1_copies, w2_copies, *choices)
    (xn1,) = call(norm1_body, [big], [first, *xs[1:]], smem=0, us=8, name="norm1")
    xn1s = gather_col(xn1)
    q, kvp, kvc = call(
        qkv_body,
        [out((1024, 256), BF), out((512, 512), BF), out((512, 512), BF)],
        [info, *xn1s, Far(wq), *packs, Far(qkv_b), Far(qkv_e)],
        us=6.5,
        name="qkv",
    )
    kvo = lax.ppermute(kvp, "row", Z_SWAP)

    g_other = lax.ppermute(after(out_grad, *z_parts), "col", CORE_SWAP)
    (pieces,) = call(
        route_all_body,
        [out((ROWS, TOK, TOK), BF)],
        [info, Far(out_grad), Far(g_other)],
        [order],
        us=1,
        name="route_g",
    )
    (g_own,) = call(
        join_body, [big], [info, lax.all_to_all(pieces, "row", 0, 0)], us=0.5, name="join"
    )
    g_side = lax.ppermute(g_own, "col", Y_SWAP)
    w1b = lax.ppermute(after(w1a, kvp), "dp", dp_swap)
    (state,) = call(
        attend_first_body,
        [out((2048, 256), F32)],
        [info, slopes, after(q, g_own), kvp, kvc],
        smem=2,
        us=9,
        name="attend_first",
    )
    w2a = lax.all_to_all(after(w2_copies, state, kvo), "row", 0, 0)
    w2b = lax.ppermute(w2a, "dp", dp_swap)

    def attend_rest(which, q, state):
        return call(
            functools.partial(attend_rest_body, which),
            [out((512, 256), BF), out((8, 256), F32), big, big],
            [info, slopes, Far(q), kvo, state, Far(wp), Far(proj_r), *packs],
            smem=2,
            us=20 if which else 0.01,
            name="attend_rest",
        )

    heads1, lse1, p2, p3 = attend_rest(1, q, after(state, g_side))
    g_core = lax.ppermute(after(g_own, p3), "col", CORE_SWAP)
    g_all = [g_own, g_core, g_side, lax.ppermute(after(g_side, p3), "col", CORE_SWAP)]
    p_far = lax.ppermute(p3, "col", CORE_SWAP)
    p_side = add(p2, p_far)
    heads0, lse0, p0, p1 = attend_rest(0, q, Far(after(state, p_side)))
    p_side = lax.ppermute(p_side, "col", Y_SWAP)
    p_core = lax.ppermute(p1, "col", CORE_SWAP)
    staged = stage([after(xs[0], p0), *xs[1:]])
    mid, xn2 = call(
        norm2_body,
        [out((TOK, D), F32), big],
        [add32(p0, p_side), p_core, *staged],
        smem=0,
        us=1.5,
        name="norm2",
    )
    (w1,) = call(
        functools.partial(stage_weight_body, 128),
        [out((ROWS, TOK, D), BF)],
        [info, Far(after(w1a, p0)), Far(w1b)],
        [pltpu.SemaphoreType.DMA((8,))],
        raw=(1, 2),
        us=2,
        name="stage_w1",
    )
    zero = jnp.zeros((RANK, D), F32)
    xn2_core = lax.ppermute(xn2, "col", CORE_SWAP)
    xn2_side = lax.ppermute(xn2, "col", Y_SWAP)

    def mlp_pre(first, blocks):
        return call(
            mlp_pre_body,
            [out((2, TOK, D), BF)] * 2,
            [info, *blocks, w1, *staged, Far(fc1_b), Far(fc1_e)],
            us=5,
            name="mlp_pre",
        )

    act0, slope0 = mlp_pre(0, [xn2, xn2_core])
    xn2_far = lax.ppermute(after(xn2_side, act0), "col", CORE_SWAP)
    xn2s = [xn2, xn2_core, xn2_side, xn2_far]
    act1, slope1 = mlp_pre(1, xn2s[2:])
    (w2,) = call(
        functools.partial(stage_weight_body, 512),
        [out((ROWS, D, TOK), BF)],
        [info, Far(after(w2a, act0)), Far(w2b)],
        [pltpu.SemaphoreType.DMA((8,))],
        raw=(1, 2),
        us=2,
        name="stage_w2",
    )

    def mlp_back(blocks, slope, r_in, e_in):
        xa, xb = (xn2s[b] for b in blocks)
        ga, gb = (g_all[b] for b in blocks)
        return call(
            mlp_back_body,
            [big, big, small, small],
            [info, xa, xb, ga, gb, slope, w1, w2, *staged, Far(fc1_e), Far(fc2_r), r_in, e_in],
            us=0.01,
            name="mlp_back",
        )

    d2, d3, r1, e1 = mlp_back((2, 3), slope1, zero, zero)
    d_far = lax.ppermute(d3, "col", CORE_SWAP)
    d_side = add(d2, d_far)
    d0, d1, r1, e1 = mlp_back((0, 1), slope0, after(r1, d_side), e1)
    d_side = lax.ppermute(d_side, "col", Y_SWAP)
    d_core = lax.ppermute(d1, "col", CORE_SWAP)
    res = call(
        fc2_body,
        [big] * 4 + [out((64, D), BF)],
        [info, act0, act1, *g_all, w2, Far(fc2_r), *staged, r1, e1],
        us=0.01,
        name="fc2",
    )
    m_parts, mlp_pack = res[:4], res[4]
    staged_back = stage([after(mid, mlp_pack), g_own, *xs])
    d_mid, g_attn = call(
        norm2_back_body,
        [out((TOK, D), F32), out((320, D), BF)],
        [add32(d0, d_side), d_core, mlp_pack, *staged_back],
        smem=0,
        us=1.5,
        name="norm2_back",
    )
    ga_core = lax.ppermute(g_attn, "col", CORE_SWAP)
    ga_side = lax.ppermute(g_attn, "col", Y_SWAP)
    shared = far([q, kvp, kvo, kvc])

    def d_heads(blocks, heads, r_in, e_in):
        return call(
            d_heads_body,
            [out((512, 256), BF), out((RANK, TOK), F32), small],
            [info, *blocks, Far(wp), *packs, Far(proj_r), Far(heads), r_in, e_in],
            us=1.5,
            name="d_heads",
        )

    dh0, pr, pe = d_heads([g_attn, ga_core], heads0, jnp.zeros((RANK, TOK), F32), zero)
    dq0, dkp, dko, dkc = call(
        attend_back_a_body,
        [out((512, 256), BF), out((512, 512), F32), out((512, 512), F32), out((512, 512), BF)],
        [info, slopes, *shared, Far(heads0), dh0, Far(lse0)],
        smem=2,
        us=16,
        weight=W_BIG,
        name="attend_back_a",
    )
    ga_side = after(ga_side, dq0)
    ga_far = lax.ppermute(ga_side, "col", CORE_SWAP)
    (early_half,) = call(
        merge_body,
        [out((80, D), BF)],
        [info, g_attn, ga_core, ga_side, ga_far],
        us=0.7,
        name="merge",
    )
    dh1, pr, pe = d_heads([ga_side, ga_far], heads1, pr, pe)
    dq1_part, dko = call(
        attend_back_b_body,
        [out((512, 256), F32), out((512, 512), BF)],
        [info, slopes, Far(q), Far(kvo), Far(heads1), dh1, Far(lse1), after(dko, early_half)],
        [pltpu.VMEM((512, 512), F32)],
        smem=2,
        us=8,
        name="attend_back_b",
    )
    dkr = lax.ppermute(dko, "row", Z_SWAP)
    dq1, dkp, dkc = call(
        attend_back_c_body,
        [out((512, 256), BF), out((512, 512), F32), out((512, 512), BF)],
        [info, slopes, Far(q), Far(kvp), Far(kvc), Far(heads1), dh1, Far(lse1), dkp, dkc, dq1_part],
        smem=2,
        us=8,
        name="attend_back_c",
    )
    early_all = lax.all_gather(early_half, ("dp", "row"))
    m_far = lax.ppermute(after(m_parts[3], dq0), "col", CORE_SWAP)
    m_core = lax.ppermute(after(m_parts[1], dq0), "col", CORE_SWAP)
    m_sum = add(after(m_parts[2], dko), m_far)
    m_side = lax.ppermute(m_sum, "col", Y_SWAP)
    res = call(
        qkv_back_body,
        [big] * 4 + [out((48, D), BF)],
        [
            info, dq0, dq1, dkp, dkr, dkc,
            *far(xn1s), Far(wq), *packs, Far(qkv_e), pr, pe,
        ],
        us=20,
        name="qkv_back",
    )
    q_parts, late_pack = res[:4], res[4]
    q_sum = add(q_parts[2], lax.ppermute(after(q_parts[3], m_side), "col", CORE_SWAP))
    (hidden,) = call(
        hidden_body,
        [out((ROWS, TOK, TOK), BF)],
        [info, add32(m_parts[0], after(m_side, q_sum), 0.01), m_core, Far(mid), *packs],
        us=0.01,
        name="hidden",
    )
    k0, rc = q_parts[0], lax.ppermute(q_parts[1], "col", CORE_SWAP)
    ry = lax.ppermute(q_sum, "col", Y_SWAP)
    late_sum = add(late_pack, lax.ppermute(after(late_pack, q_sum), "row", Z_SWAP))
    late_next = shift(late_sum, 2)
    late_four = spread(late_sum, late_next)
    staged_last = stage([after(d_mid, k0), *xs])
    ins = call(
        norm1_back_body,
        [out((TOK, TOK), BF)] * 4,
        [add32(after(k0, hidden, late_four), ry), rc, *staged_last],
        smem=0,
        us=1,
        name="norm1_back",
    )
    early_far = lax.ppermute(after(early_all, ins[0]), "col", CORE_SWAP)
    table = jnp.concatenate([info, jnp.zeros((40 - 34,), jnp.int32), *choices])
    o_fc1r, o_f2e, o_f1e, o_f2r = call(
        expand_early_body,
        [out((COUNT, RANK, w), F32) for w in (1024, 1024, 4096, 4096)],
        [table, Far(early_all), Far(early_far)],
        us=3,
        name="expand_early",
    )
    input_gradient = unroute(tuple(ins), F32, o_fc1r)
    late_all = gather_col(late_four)
    hidden_out = unroute(after(hidden, late_next), BF)
    o_qr, o_pe, o_qe, o_pr = call(
        expand_late_body,
        [out((COUNT, RANK, w), F32) for w in (1024, 1024, 3072, 1024)],
        [table, *late_all],
        us=3,
        name="expand_late",
    )
    return (
        hidden_out,
        input_gradient,
        flip(o_qr),
        o_qe,
        flip(o_pr),
        o_pe,
        flip(o_fc1r),
        o_f1e,
        flip(o_f2r),
        o_f2e,
    )


def solution(mesh):
    placed = (
        P(("dp", "col"), "row"),
        P(("dp", "col"), "row"),
        P("row"),
        P("row"),
        P("row", "col"),
        P(),
        P("col", "row"),
        P("row"),
        P("row"),
        P("row"),
        P("row", "col"),
        P(),
        P("col", "row"),
        P("row"),
        P(None, "row", None),
        P(),
        P(None, "col", None),
        P(None, None, "row"),
        P(None, "row", None),
        P(),
        P(None, "col", None),
        P(None, None, "row"),
        P("dp"),
        P("dp"),
    )
    return jax.shard_map(
        body,
        mesh=mesh,
        in_specs=placed,
        out_specs=(P(("dp", "col"), "row"), P(("dp", "col"), "row")) + (P(),) * 8,
        check_vma=False,
    )
```

```python
import functools

import jax
import jax.numpy as jnp
from jax import lax
from jax.experimental import pallas as pl
from jax.experimental.pallas import tpu as pltpu
from jax.sharding import PartitionSpec as P

D = 1024
HEADS = 16
HEAD = 64
FF = 4096
RANK = 16
COUNT = 8
PROMPT = 1024
CONT = 128
NCONT = 8
GROUPS_DEV = 2

EPSILON = 1e-05
SCALE = 2.0
GELU_A = 0.7978845608028654
GELU_B = 0.044715
ROWS = 4
COLS = 4
TOK = 256
BLOCK = 128
LOW = -1e30
W_SMALL = 5e8
W_BIG = 5e8

BF = jnp.bfloat16
F32 = jnp.float32

VM = pl.BlockSpec(memory_space=pltpu.VMEM)
SM = pl.BlockSpec(memory_space=pltpu.SMEM)
HB = pl.BlockSpec(memory_space=pltpu.HBM)

CORE_SWAP = [(0, 1), (1, 0), (2, 3), (3, 2)]
Y_SWAP = [(0, 2), (2, 0), (1, 3), (3, 1)]
Z_SWAP = [(0, 1), (1, 0), (2, 3), (3, 2)]


def nn(a, b):
    return lax.dot_general(a, b, (((1,), (0,)), ((), ())), preferred_element_type=F32)


def nt(a, b):
    return lax.dot_general(a, b, (((1,), (1,)), ((), ())), preferred_element_type=F32)


def tn(a, b):
    return lax.dot_general(a, b, (((0,), (0,)), ((), ())), preferred_element_type=F32)


def f32(v):
    return v.astype(F32)


def bf(v):
    return v.astype(BF)


class Far:
    def __init__(self, value):
        self.value = value


def far(values):
    return [Far(v) for v in values]


def call(
    body, outs, ins, scratch=(), smem=1, limit=40, us=1, raw=(), weight=W_SMALL, name=None
):
    values = [
        pltpu.with_memory_space_constraint(v.value, pltpu.HBM) if isinstance(v, Far) else v
        for v in ins
    ]
    fetched = [i for i, v in enumerate(ins) if isinstance(v, Far) and i not in raw]
    specs = [SM] * smem
    for v in ins[smem:]:
        specs.append(HB if isinstance(v, Far) else VM)
    nbytes = sum(v.size * v.dtype.itemsize for v in values)
    nbytes += sum(o.size * o.dtype.itemsize for o in outs)
    extra = [pltpu.VMEM(values[i].shape, values[i].dtype) for i in fetched]
    if fetched:
        extra.append(pltpu.SemaphoreType.DMA((len(fetched),)))

    def whole(*refs):
        refs = list(refs)
        if fetched:
            sem = refs[-1]
            buffers = refs[-1 - len(fetched) : -1]
            refs = refs[: -1 - len(fetched)]
            copies = []
            for n, (i, buffer) in enumerate(zip(fetched, buffers)):
                copies.append(pltpu.make_async_copy(refs[i], buffer, sem.at[n]))
                copies[-1].start()
                refs[i] = buffer
            for copy in copies:
                copy.wait()
        body(*refs)

    return pl.pallas_call(
        whole,
        out_shape=tuple(outs),
        in_specs=specs,
        out_specs=tuple([VM] * len(outs)),
        scratch_shapes=list(scratch) + extra,
        compiler_params=pltpu.CompilerParams(vmem_limit_bytes=limit << 20),
        cost_estimate=pl.CostEstimate(
            flops=int(us * weight), bytes_accessed=nbytes // 8, transcendentals=0
        ),
        name=name,
    )(*values)


def after(value, *others):
    res = lax.optimization_barrier((value, others))
    return res[0]


def out(shape, dtype):
    return jax.ShapeDtypeStruct(shape, dtype)


def block_at(zl, c, j):
    return c * 4 + zl + j * (3 - 2 * zl)


def fill_order(info, order):
    base = info[3]
    first = jnp.int32(0)
    second = jnp.int32(NCONT)
    for j in range(GROUPS_DEV * NCONT):
        own = info[16 + j] == base
        slot = jnp.where(own, first, second)
        order[slot] = jnp.int32(j)
        first = first + jnp.where(own, 1, 0)
        second = second + jnp.where(own, 0, 1)


def place_of(info, order, z, core, j):
    prompt = (z // 2) * 8 + block_at(lax.rem(z, 2), core, j)
    cont = order[4 * z + 2 * core + j]
    return jnp.where(info[1] == 0, prompt, cont)


def route_body(info, own, oth, o0, o1, o2, o3, order):
    fill_order(info, order)
    c = info[2]
    for s, dst in enumerate((o0, o1, o2, o3)):
        z = lax.rem(info[0] + s, ROWS)
        for j in range(2):
            src = place_of(info, order, z, c, j)
            at = pl.ds(pl.multiple_of(lax.rem(src, 8) * BLOCK, BLOCK), BLOCK)
            mine = src // 8 == c

            @pl.when(mine)
            def _():
                dst[pl.ds(j * BLOCK, BLOCK), :] = own[at, :]

            @pl.when(jnp.logical_not(mine))
            def _():
                dst[pl.ds(j * BLOCK, BLOCK), :] = oth[at, :]


def route_pack_body(
    info, own, oth, g1, c1, pb, g2, c2, fb, qr, fr, pe, fe,
    o0, o1, o2, o3, order, v0, v1, v2, v3, v4, v5, mats, sem,
):
    vecs = (v0, v1, v2, v3, v4, v5)
    pairs = list(zip((g1, c1, pb, g2, c2, fb), vecs))
    for k in range(ROWS):
        which = lax.rem(info[0] + k, ROWS) // 2
        a = jnp.where(which == 0, info[32], info[33])
        pairs += [(v.at[a], mats.at[4 * k + i]) for i, v in enumerate((qr, fr, pe, fe))]
    copies = [pltpu.make_async_copy(a, b, sem.at[i]) for i, (a, b) in enumerate(pairs)]
    for copy in copies:
        copy.start()
    route_body(info, own, oth, o0, o1, o2, o3, order)
    for copy in copies:
        copy.wait()
    for k, dst in enumerate((o0, o1, o2, o3)):
        head = [f32(v[...]).reshape(1, TOK) for v in vecs]
        dst[256:272, :] = bf(jnp.concatenate(head + [jnp.zeros((10, TOK), F32)], axis=0))
        for i in range(4):
            dst[272 + 16 * i : 288 + 16 * i, :] = mats[4 * k + i]


def stack_body(a0, a1, a2, a3, dst):
    n = a0.shape[0]
    for k, v in enumerate((a0, a1, a2, a3)):
        dst[k * n : (k + 1) * n, :] = v[...]


def route_all_body(info, own, oth, w1, dst, order, sem):
    rows = pl.ds(pl.multiple_of(info[8] * 128, 128), 128)
    copies = []
    for z in range(ROWS):
        for b in range(ROWS):
            to = dst.at[z, pl.ds(TOK + 128 * b, 128)]
            copies.append(
                pltpu.make_async_copy(w1.at[rows, cols(b)], to, sem.at[ROWS * z + b])
            )
    for copy in copies:
        copy.start()
    fill_order(info, order)
    c = info[2]
    for z in range(ROWS):
        for j in range(2):
            src = place_of(info, order, z, c, j)
            at = pl.ds(pl.multiple_of(lax.rem(src, 8) * BLOCK, BLOCK), BLOCK)
            mine = src // 8 == c

            @pl.when(mine)
            def _():
                dst[z, pl.ds(j * BLOCK, BLOCK), :] = own[at, :]

            @pl.when(jnp.logical_not(mine))
            def _():
                dst[z, pl.ds(j * BLOCK, BLOCK), :] = oth[at, :]
    for copy in copies:
        copy.wait()


def unroute_body(info, a, b, grad, hidden, order):
    fill_order(info, order)
    c = info[2]
    for s in range(ROWS):
        z = lax.rem(info[0] + s, ROWS)
        for other, src in ((0, a), (1, b)):
            core = c if other == 0 else 1 - c
            for j in range(2):
                at = place_of(info, order, z, core, j)

                @pl.when(at // 8 == c)
                def _():
                    rows = pl.ds(pl.multiple_of(lax.rem(at, 8) * BLOCK, BLOCK), BLOCK)
                    start = 2 * s * TOK + j * BLOCK
                    grad[rows, :] = f32(src[pl.ds(start, BLOCK), :])
                    hidden[rows, :] = src[pl.ds(start + TOK, BLOCK), :]


def cols(k, width=TOK):
    return pl.ds(k * width, width)


def row_stats(parts):
    total = sum(jnp.sum(v, axis=1, keepdims=True) for v in parts)
    mean = total * (1.0 / D)
    dev = [v - mean for v in parts]
    var = sum(jnp.sum(v * v, axis=1, keepdims=True) for v in dev) * (1.0 / D)
    rstd = lax.rsqrt(var + EPSILON)
    return [v * rstd for v in dev], rstd


def norm1_body(x0, x1, x2, x3, xn):
    for t in range(2):
        rows = pl.ds(t * 128, 128)
        hat, _ = row_stats([f32(v[rows, :]) for v in (x0, x1, x2, x3)])
        for k, pack in enumerate((x0, x1, x2, x3)):
            xn[rows, cols(k)] = bf(hat[k] * f32(pack[256:257, :]) + f32(pack[257:258, :]))


def both(a, b, rows, k):
    return f32(a[rows, cols(k)]) + f32(b[rows, cols(k)])


def norm2_body(a, b, x0, x1, x2, x3, mid, xn):
    for t in range(2):
        rows = pl.ds(t * 128, 128)
        parts = []
        for k, x in enumerate((x0, x1, x2, x3)):
            v = f32(x[rows, :]) + both(a, b, rows, k) + f32(x[258:259, :])
            mid[rows, cols(k)] = v
            parts.append(v)
        hat, _ = row_stats(parts)
        for k, pack in enumerate((x0, x1, x2, x3)):
            xn[rows, cols(k)] = bf(hat[k] * f32(pack[259:260, :]) + f32(pack[260:261, :]))


def norm_back(hat, rstd, grads):
    total = sum(jnp.sum(g, axis=1, keepdims=True) for g in grads) * (1.0 / D)
    along = sum(jnp.sum(g * h, axis=1, keepdims=True) for g, h in zip(grads, hat)) * (1.0 / D)
    return [rstd * (g - total - h * along) for g, h in zip(grads, hat)]


def norm2_back_body(
    a, b, pack, mid, g, x0, x1, x2, x3, d_mid, g_attn
):
    g_attn[256:320, :] = pack[...]
    for t in range(2):
        rows = pl.ds(t * 128, 128)
        hat, rstd = row_stats([mid[rows, cols(k)] for k in range(4)])
        grads = []
        for k, pack in enumerate((x0, x1, x2, x3)):
            grads.append(both(a, b, rows, k) * f32(pack[259:260, :]))
        back = norm_back(hat, rstd, grads)
        for k in range(4):
            v = f32(g[rows, cols(k)]) + back[k]
            d_mid[rows, cols(k)] = v
            g_attn[rows, cols(k)] = bf(v)


def norm1_back_body(
    a, b, d_mid, x0, x1, x2, x3, h0, h1, h2, h3, i0, i1, i2, i3
):
    for src, dst in zip((h0, h1, h2, h3), (i0, i1, i2, i3)):
        dst[256:512, :] = src[...]
    for t in range(2):
        rows = pl.ds(t * 128, 128)
        hat, rstd = row_stats([f32(v[rows, :]) for v in (x0, x1, x2, x3)])
        grads = []
        for k, pack in enumerate((x0, x1, x2, x3)):
            grads.append(both(a, b, rows, k) * f32(pack[256:257, :]))
        back = norm_back(hat, rstd, grads)
        for k, dst in enumerate((i0, i1, i2, i3)):
            dst[rows, :] = bf(d_mid[rows, cols(k)] + back[k])


def hidden_body(a, b, mid, x0, x1, x2, x3, h0, h1, h2, h3):
    for t in range(2):
        rows = pl.ds(t * 128, 128)
        for k, (pack, dst) in enumerate(zip((x0, x1, x2, x3), (h0, h1, h2, h3))):
            v = mid[rows, cols(k)] + both(a, b, rows, k) + f32(pack[261:262, :])
            dst[rows, :] = bf(v)


def join_body(info, v, dst, w1):
    for k in range(ROWS):
        dst[:, cols(k)] = v[rel(info, k), 0:TOK, :]
        for b in range(ROWS):
            w1[k, :, cols(b)] = v[k, TOK + 128 * b : TOK + 128 * b + 128, :]


def slab_rows(info, b):
    y = jnp.bitwise_xor(info[1], b // 2)
    c = jnp.bitwise_xor(info[2], b % 2)
    return y, c


def low_lanes(rows):
    return lax.broadcasted_iota(jnp.int32, (rows, 128), 1) < HEAD


def rel(info, k):
    return lax.rem(info[0] - k + ROWS, ROWS)


def rel_cols(info, k):
    return pl.ds(pl.multiple_of(rel(info, k) * TOK, TOK), TOK)


def lanes_at(at, size):
    return pl.ds(pl.multiple_of(at, 128), size)


def rows_at(i, size):
    return pl.ds(pl.multiple_of(i * size, size), size)


def prepare_body(
    info, wq, wp, w2, qe, fe, pr, fr, first, c2, o_qe, o_fe, o_pr, o_fr, sem
):
    half = info[8]
    a = jnp.where(info[5] == 0, info[32], info[33])
    rows = rows_at(half, 128)
    pairs = [(wq.at[rows], first.at[:, 0:768]), (wp.at[rows], first.at[:, 768:1024])]
    pairs += [(qe.at[a, :, lanes_at(info[6] * 768, 768)], o_qe)]
    pairs += [(fe.at[a, :, lanes_at(info[6] * 1024, 1024)], o_fe)]
    pairs += [(pr.at[a], o_pr), (fr.at[a], o_fr)]
    for j in range(ROWS):
        pairs += [(w2.at[rows_at(half, 512)], c2.at[j])]
    copies = [pltpu.make_async_copy(x, y, sem.at[i]) for i, (x, y) in enumerate(pairs)]
    for copy in copies:
        copy.start()
    for copy in copies:
        copy.wait()


def assemble_body(info, own_q, own_p, z1, z2, z3, s1, s2, s3, ws, wp, sem):
    half = info[8]
    copies = [
        pltpu.make_async_copy(own_q, ws.at[0], sem.at[0]),
        pltpu.make_async_copy(own_p, wp.at[0], sem.at[1]),
    ]
    for k, (zv, sv) in enumerate(((z1, s1), (z2, s2), (z3, s3))):
        for n, (v, at) in enumerate(((zv, half), (sv, 1 - half))):
            rows = rows_at(at, 128)
            at = 2 + 4 * k + 2 * n
            copies.append(
                pltpu.make_async_copy(v.at[:, 0:768], ws.at[k + 1, rows], sem.at[at])
            )
            copies.append(
                pltpu.make_async_copy(v.at[:, 768:1024], wp.at[k + 1, rows], sem.at[at + 1])
            )
    for copy in copies:
        copy.start()
    for copy in copies:
        copy.wait()


def qkv_body(
    info, x0, x1, x2, x3, ws, p0, p1, p2, p3, bias, expand, q, kvp, kvc
):
    ps = (p0, p1, p2, p3)
    low = low_lanes(TOK)
    for b, x in enumerate((x0, x1, x2, x3)):
        y, c = slab_rows(info, b)
        acc = sum(nn(x[:, cols(k)], ws[k]) for k in range(4))
        u = bf(sum(nt(x[:, cols(k)], ps[k][272:288, :]) for k in range(4)))
        acc = acc + f32(bias[...]) + SCALE * nn(u, expand[...])
        kv = []
        for pair in range(2):
            at = 384 * pair
            g0, g1, g2 = (acc[:, at + 128 * i : at + 128 * i + 128] for i in range(3))
            q[rows_at(y * 2 + c, TOK), cols(pair, 128)] = bf(
                bf(jnp.where(low, g0, g1)) * BF(0.125)
            )
            kv.append((bf(pltpu.roll(jnp.where(low, g2, g0), 64, 1)), bf(jnp.where(low, g1, g2))))
        rows = rows_at(c, TOK)

        @pl.when(y == 0)
        def _():
            for pair in range(2):
                kvp[rows, cols(pair, 128)] = kv[pair][0]
                kvp[rows, cols(2 + pair, 128)] = kv[pair][1]

        @pl.when(y == 1)
        def _():
            for pair in range(2):
                kvc[rows, cols(pair, 128)] = kv[pair][0]
                kvc[rows, cols(2 + pair, 128)] = kv[pair][1]


WIDE = 256


def stacked(v, low):
    zero = jnp.zeros_like(v)
    return jnp.concatenate([jnp.where(low, v, zero), jnp.where(low, zero, v)], axis=0)


def split_id(shape, axis):
    lane = lax.broadcasted_iota(jnp.int32, shape, axis)
    return lane, jnp.where(lane < BLOCK, lane, lane - BLOCK)


def chunk_place(shape, axis, side, n):
    lane, within = split_id(shape, axis)
    first = block_at(side, n, 0) * BLOCK
    second = block_at(side, n, 1) * BLOCK
    return within + jnp.where(lane < BLOCK, first, second)


def keep_state(state, low):
    top, total, acc = state
    lane = lax.broadcasted_iota(jnp.int32, (2 * BLOCK, 128), 1)
    spot = lax.rem(lane, HEAD)
    row = lax.broadcasted_iota(jnp.int32, (2 * BLOCK, 128), 0)
    own = (lane < HEAD) == (row < BLOCK)
    return jnp.where(own, acc, jnp.where(spot == 0, top, total))


def load_state(v):
    lane = lax.broadcasted_iota(jnp.int32, (2 * BLOCK, 128), 1)
    row = lax.broadcasted_iota(jnp.int32, (2 * BLOCK, 128), 0)
    spot = jnp.where(row < BLOCK, HEAD, 0)
    top = jnp.max(jnp.where(lane == spot, v, LOW), axis=1, keepdims=True)
    total = jnp.sum(jnp.where(lane == spot + 1, v, 0.0), axis=1, keepdims=True)
    return top, total, v


def soft_update(state, s, v):
    if state is None:
        top = jnp.max(s, axis=1, keepdims=True)
        p = jnp.exp(s - top)
        return top, jnp.sum(p, axis=1, keepdims=True), nn(bf(p), v)
    top, total, acc = state
    new = jnp.maximum(top, jnp.max(s, axis=1, keepdims=True))
    p = jnp.exp(s - new)
    shrink = jnp.exp(top - new)
    total = total * shrink + jnp.sum(p, axis=1, keepdims=True)
    return new, total, acc * shrink + nn(bf(p), v)


def head_slopes(slopes, shape, axis):
    lane = lax.broadcasted_iota(jnp.int32, shape, axis)
    return [
        jnp.where(lane < BLOCK, slopes[2 * pair], slopes[2 * pair + 1]) for pair in range(2)
    ]


def attend_chunk(q2, states, kv, rows, place, base, slope, spot, masked):
    res = []
    away = place - base
    for pair in range(2):
        s = nt(q2[pair], kv[rows, cols(pair, 128)]) + slope[pair] * away.astype(F32)
        if masked:
            s = jnp.where(away <= spot, s, LOW)
        res.append(soft_update(states[pair], s, kv[rows, cols(2 + pair, 128)]))
    return res


def attend_first_body(info, slopes, q, kvp, kvc, state):
    zl = info[4]
    low = low_lanes(BLOCK)
    _, spot = split_id((2 * BLOCK, 1), 0)
    slope = head_slopes(slopes, (2 * BLOCK, 1), 0)
    places = [chunk_place((1, WIDE), 1, zl, n) for n in range(2)]

    def load(i):
        return [stacked(q[rows_at(i, BLOCK), cols(pair, 128)], low) for pair in range(2)]

    def save(states, i):
        for pair in range(2):
            state[rows_at(i, WIDE), cols(pair, 128)] = keep_state(states[pair], low)

    def prompt_block(j, _):
        for n in range(2):
            i = 2 * n + j
            base = block_at(zl, n, j) * BLOCK
            q2 = load(i)
            states = [None, None]
            for m in range(n, -1, -1):
                states = attend_chunk(
                    q2, states, kvp, pl.ds(m * WIDE, WIDE), places[m], base, slope, spot, m == n
                )
            save(states, i)
        return 0

    lax.fori_loop(0, 2, prompt_block, 0)

    def cont_block(j, _):
        q2 = load(4 + j)
        own_place = lax.broadcasted_iota(jnp.int32, (1, BLOCK), 1)
        states = attend_chunk(
            q2, [None, None], kvc, rows_at(j, BLOCK), own_place, 0, slope, spot, True
        )
        for m in range(2):
            states = attend_chunk(
                q2, states, kvp, pl.ds(m * WIDE, WIDE), places[m], PROMPT, slope, spot, False
            )
        save(states, 4 + j)
        return 0

    lax.fori_loop(0, 4, cont_block, 0)


def attend_rest_body(
    which, info, slopes, q, kvo, state, ws, reduce, p0, p1, p2, p3, heads, lse, o0, o1
):
    zl = info[4]
    y = info[1] if which == 0 else 1 - info[1]
    low = low_lanes(BLOCK)
    _, spot = split_id((2 * BLOCK, 1), 0)
    slope = head_slopes(slopes, (2 * BLOCK, 1), 0)
    places = [chunk_place((1, WIDE), 1, 1 - zl, n) for n in range(2)]

    def load(i):
        q2 = [stacked(q[rows_at(i, BLOCK), cols(pair, 128)], low) for pair in range(2)]
        states = [load_state(state[rows_at(i, WIDE), cols(pair, 128)]) for pair in range(2)]
        return q2, states

    def finish(states, j):
        for pair in range(2):
            top, total, acc = states[pair]
            res = acc / total
            heads[rows_at(j, BLOCK), cols(pair, 128)] = bf(
                jnp.where(low, res[:BLOCK], res[BLOCK:])
            )
            kept = jnp.transpose(jnp.broadcast_to(top + jnp.log(total), (2 * BLOCK, 128)))
            lse[pl.ds(pair * 4 + j, 1), :] = kept[0:1, :]

    @pl.when(y == 0)
    def _():
        def prompt_block(j, _):
            for n in range(2):
                i = 2 * n + j
                base = block_at(zl, n, j) * BLOCK
                q2, states = load(i)
                for m in range(n + 1):
                    states = attend_chunk(
                        q2, states, kvo, pl.ds(m * WIDE, WIDE), places[m], base, slope, spot, m == n
                    )
                finish(states, i)
            return 0

        lax.fori_loop(0, 2, prompt_block, 0)

    @pl.when(y == 1)
    def _():
        def cont_block(j, _):
            q2, states = load(4 + j)
            for m in range(2):
                states = attend_chunk(
                    q2, states, kvo, pl.ds(m * WIDE, WIDE), places[m], PROMPT, slope, spot, False
                )
            finish(states, j)
            return 0

        lax.fori_loop(0, 4, cont_block, 0)

    ps = (p0, p1, p2, p3)
    for b, dst in enumerate((o0, o1)):
        c = jnp.bitwise_xor(info[2], b)
        h = heads[rows_at(c, TOK), :]
        u = bf(nt(h, reduce[...]))
        for k in range(4):
            dst[:, cols(k)] = bf(nn(h, ws[k]) + SCALE * nn(u, ps[k][304:320, :]))


def mlp_pre_body(info, x0, x1, w1, p0, p1, p2, p3, bias, expand, act, slope):
    ps = (p0, p1, p2, p3)
    for b, x in enumerate((x0, x1)):
        u = bf(sum(nt(x[:, cols(k)], ps[k][288:304, :]) for k in range(4)))
        pre = sum(nn(x[:, cols(k)], w1[rel(info, k)]) for k in range(4))
        pre = pre + f32(bias[...]) + SCALE * nn(u, expand[...])
        sq = pre * pre
        t = jnp.tanh(pre * (GELU_A + (GELU_A * GELU_B) * sq))
        half = 0.5 + 0.5 * t
        act[b] = bf(pre * half)
        slope[b] = bf(
            half + (0.5 * pre) * (1.0 - t * t) * (GELU_A + (3.0 * GELU_A * GELU_B) * sq)
        )


def mlp_back_body(
    info, x0, x1, g0, g1, slope, w1, w2, p0, p1, p2, p3, expand, reduce, r_in, e_in,
    d0, d1, r_out, e_out,
):
    ps = (p0, p1, p2, p3)
    rv, ev = r_in[...], e_in[...]
    for b, (x, g, dx) in enumerate(((x0, g0, d0), (x1, g1, d1))):
        u = bf(sum(nt(x[:, cols(k)], ps[k][288:304, :]) for k in range(4)))
        du2 = bf(SCALE * sum(nt(g[:, cols(k)], ps[k][320:336, :]) for k in range(4)))
        d_act = sum(nt(g[:, cols(k)], w2[rel(info, k)]) for k in range(4)) + nn(du2, reduce[...])
        d_pre = bf(d_act * f32(slope[b]))
        du = bf(SCALE * nt(d_pre, expand[...]))
        for k in range(4):
            dx[:, cols(k)] = bf(nt(d_pre, w1[rel(info, k)]) + nn(du, ps[k][288:304, :]))
        rv = rv + tn(du, x[...])
        ev = ev + tn(u, d_pre)
    r_out[...] = rv
    e_out[...] = ev


def fc2_body(
    info, a0, a1, g0, g1, g2, g3, w2, reduce, p0, p1, p2, p3, r1, e1,
    m0, m1, m2, m3, grads,
):
    ps = (p0, p1, p2, p3)
    rv = ev = 0.0
    for b, (g, m) in enumerate(zip((g0, g1, g2, g3), (m0, m1, m2, m3))):
        act = a0[b] if b < 2 else a1[b - 2]
        du = bf(SCALE * sum(nt(g[:, cols(k)], ps[k][320:336, :]) for k in range(4)))
        u = bf(nt(act, reduce[...]))
        for k in range(4):
            m[:, cols(k)] = bf(nn(act, w2[rel(info, k)]) + SCALE * nn(u, ps[k][320:336, :]))
        rv = rv + tn(du, act)
        ev = ev + SCALE * tn(u, g[...])
    for k in range(4):
        grads[0:16, rel_cols(info, k)] = bf(r1[:, cols(k)])
        grads[16:32, rel_cols(info, k)] = bf(ev[:, k * TOK : k * TOK + TOK])
    grads[32:48, :] = bf(SCALE * e1[...])
    grads[48:64, :] = bf(rv)


def d_heads_body(
    info, g0, g1, ws, p0, p1, p2, p3, reduce, heads, r_in, e_in, dh, r_out, e_out
):
    ps = (p0, p1, p2, p3)
    rv, ev = r_in[...], e_in[...]
    for b, g in enumerate((g0, g1)):
        rows = rows_at(jnp.bitwise_xor(info[2], b), TOK)
        h = heads[rows, :]
        u = bf(nt(h, reduce[...]))
        du = bf(SCALE * sum(nt(g[0:256, cols(k)], ps[k][304:320, :]) for k in range(4)))
        v = sum(nt(g[0:256, cols(k)], ws[k]) for k in range(4)) + nn(du, reduce[...])
        dh[rows, :] = bf(v)
        rv = rv + tn(du, h)
        ev = ev + SCALE * tn(u, g[0:256, :])
    r_out[...] = rv
    e_out[...] = ev


def back_load(heads, d_heads, lse, q, qi, j, low):
    res = []
    for pair in range(2):
        lane = cols(pair, 128)
        q2 = stacked(q[rows_at(qi, BLOCK), lane], low)
        do = d_heads[rows_at(j, BLOCK), lane]
        both = jnp.transpose(f32(do) * f32(heads[rows_at(j, BLOCK), lane]))
        delta = jnp.concatenate(
            [
                jnp.sum(both[:HEAD], axis=0, keepdims=True),
                jnp.sum(both[HEAD:], axis=0, keepdims=True),
            ],
            axis=1,
        )
        res.append((q2, stacked(do, low), delta, lse[pl.ds(pair * 4 + j, 1), :]))
    return res


def back_chunk(args, kv, d_kv, d_at, rows, place, base, slope, spot, masked, store, d_qs):
    away = place - base
    res = []
    for pair in range(2):
        q2, do2, delta, kept = args[pair]
        lane = cols(pair, 128)
        vlane = cols(2 + pair, 128)
        k = kv[rows, lane]
        s = nt(k, q2) + (away.astype(F32) * slope[pair] - kept)
        p = jnp.exp(s)
        if masked:
            p = jnp.where(away <= spot, p, 0.0)
        ds = bf(p * (nt(kv[rows, vlane], do2) - delta))
        dk = nn(ds, q2)
        dv = nn(bf(p), do2)
        if store:
            d_kv[d_at, lane] = bf(dk)
            d_kv[d_at, vlane] = bf(dv)
        else:
            d_kv[d_at, lane] += dk
            d_kv[d_at, vlane] += dv
        d_q = tn(ds, k)
        res.append(d_q if d_qs is None else d_qs[pair] + d_q)
    return res


def back_common(info, slopes):
    low = low_lanes(BLOCK)
    _, spot = split_id((1, 2 * BLOCK), 1)
    slope = head_slopes(slopes, (1, 2 * BLOCK), 1)
    zl = info[4]
    own = [chunk_place((WIDE, 1), 0, zl, n) for n in range(2)]
    oth = [chunk_place((WIDE, 1), 0, 1 - zl, n) for n in range(2)]
    return zl, low, spot, slope, own, oth


def fold(d_q, low):
    return jnp.where(low, d_q[:BLOCK], d_q[BLOCK:]) * 0.125


def back_sweep(info, slopes, y, q, heads, d_heads, lse, sides, kvc, dkc, finish):
    zl, low, spot, slope, own, oth = back_common(info, slopes)
    place_sets = {"own": own, "oth": oth}

    @pl.when(y == 0)
    def _():
        def prompt_block(j, _):
            for n in range(2):
                i = 2 * n + j
                args = back_load(heads, d_heads, lse, q, i, i, low)
                base = block_at(zl, n, j) * BLOCK
                d_qs = None
                for side, kv, d_kv in sides:
                    for m in range(n + 1):
                        rows = pl.ds(m * WIDE, WIDE)
                        d_qs = back_chunk(
                            args, kv, d_kv, rows, rows, place_sets[side][m], base, slope, spot,
                            m == n, False, d_qs,
                        )
                finish(d_qs, i, low)
            return 0

        lax.fori_loop(0, 2, prompt_block, 0)

    @pl.when(y == 1)
    def _():
        def cont_block(j, _):
            args = back_load(heads, d_heads, lse, q, 4 + j, j, low)
            d_qs = None
            if kvc is not None:
                mine = rows_at(j, BLOCK)
                own_place = lax.broadcasted_iota(jnp.int32, (BLOCK, 1), 0)
                d_qs = back_chunk(
                    args, kvc, dkc, mine, mine, own_place, 0, slope, spot, True, True, d_qs
                )
            for side, kv, d_kv in sides:
                for m in range(2):
                    rows = pl.ds(m * WIDE, WIDE)
                    d_qs = back_chunk(
                        args, kv, d_kv, rows, rows, place_sets[side][m], PROMPT, slope, spot,
                        False, False, d_qs,
                    )
            finish(d_qs, j, low)
            return 0

        lax.fori_loop(0, 4, cont_block, 0)


def attend_back_a_body(
    info, slopes, q, kvp, kvo, kvc, heads, d_heads, lse, dq, dkp, dko, dkc
):
    dkp[...] = jnp.zeros_like(dkp)
    dko[...] = jnp.zeros_like(dko)
    dkc[...] = jnp.zeros_like(dkc)

    def finish(d_qs, j, low):
        for pair in range(2):
            dq[rows_at(j, BLOCK), cols(pair, 128)] = bf(fold(d_qs[pair], low))

    back_sweep(
        info, slopes, info[1], q, heads, d_heads, lse,
        (("own", kvp, dkp), ("oth", kvo, dko)), kvc, dkc, finish,
    )


def attend_back_b_body(
    info, slopes, q, kvo, heads, d_heads, lse, dko_in, early, dq, dko, acc
):
    acc[...] = dko_in[...]

    def finish(d_qs, j, low):
        for pair in range(2):
            dq[rows_at(j, BLOCK), cols(pair, 128)] = fold(d_qs[pair], low)

    back_sweep(
        info, slopes, 1 - info[1], q, heads, d_heads, lse,
        (("oth", kvo, acc),), None, None, finish,
    )
    dko[0:512, :] = bf(acc[...])
    dko[512:592, :] = early[:, 0:512]
    dko[592:672, :] = early[:, 512:1024]


def early_sum_body(own, other, dst):
    dst[:, 0:512] = bf(f32(own[:, 0:512]) + f32(other[512:592, :]))
    dst[:, 512:1024] = bf(f32(own[:, 512:1024]) + f32(other[592:672, :]))


def attend_back_c_body(
    info, slopes, q, kvp, kvc, heads, d_heads, lse, dkp_in, dkc_in, dq_in, dq, dkp, dkc
):
    dkp[...] = dkp_in[...]
    dkc[...] = dkc_in[...]

    def finish(d_qs, j, low):
        for pair in range(2):
            lane = cols(pair, 128)
            rows = rows_at(j, BLOCK)
            dq[rows, lane] = bf(dq_in[rows, lane] + fold(d_qs[pair], low))

    back_sweep(
        info, slopes, 1 - info[1], q, heads, d_heads, lse,
        (("own", kvp, dkp),), kvc, dkc, finish,
    )


def qkv_back_body(
    info, dq0, dq1, dkp, dkr, dkc, x0, x1, x2, x3, ws, p0, p1, p2, p3, expand, pr, pe,
    o0, o1, o2, o3, grads,
):
    ps = (p0, p1, p2, p3)
    low = low_lanes(TOK)
    sr = se = 0.0
    for b, (x, dst) in enumerate(zip((x0, x1, x2, x3), (o0, o1, o2, o3))):
        y, c = slab_rows(info, b)
        half = rows_at(c, TOK)
        groups = []
        dq = dq0 if b < 2 else dq1
        for pair in range(2):
            vq = f32(dq[half, cols(pair, 128)])
            got = []
            for lane in (cols(pair, 128), cols(2 + pair, 128)):
                prompt = dkp[half, lane] + f32(dkr[half, lane])
                got.append(jnp.where(y == 0, prompt, f32(dkc[half, lane])))
            vk = pltpu.roll(got[0], 64, 1)
            vv = got[1]
            groups += [jnp.where(low, vq, vk), jnp.where(low, vv, vq), jnp.where(low, vk, vv)]
        d = bf(jnp.concatenate(groups, axis=1))
        u = bf(sum(nt(x[:, cols(k)], ps[k][272:288, :]) for k in range(4)))
        du = bf(SCALE * nt(d, expand[...]))
        for k in range(4):
            dst[:, cols(k)] = bf(nt(d, ws[k]) + nn(du, ps[k][272:288, :]))
        sr = sr + tn(du, x[...])
        se = se + SCALE * tn(u, d)
    for k in range(4):
        grads[0:16, rel_cols(info, k)] = bf(sr[:, k * TOK : k * TOK + TOK])
        grads[16:32, rel_cols(info, k)] = bf(pe[:, cols(k)])
    grads[32:48, 0:768] = bf(se)
    grads[32:48, 768:1024] = bf(pr[...])


def add_body(a, b, dst):
    dst[...] = bf(f32(a[...]) + f32(b[...]))


def add(a, b):
    return call(add_body, [out(a.shape, BF)], [a, b], smem=0, us=0.01, name="add")[0]


def add32_body(a, b, dst):
    dst[...] = f32(a[...]) + f32(b[...])


def add32(a, b, us=8):
    return call(add32_body, [out(a.shape, F32)], [a, b], smem=0, us=us, name="add32")[0]


def stage_body(*refs):
    n = len(refs) // 2
    for src, dst in zip(refs[:n], refs[n:]):
        dst[...] = src[...]


def stage(values):
    return call(
        stage_body, [out(v.shape, v.dtype) for v in values], far(values), smem=0, us=0.01, name="stage"
    )


def stage_weight_body(size, info, wa, wb, w, sem):
    copies = []
    for n, (src, at) in enumerate(((wa, info[8]), (wb, 1 - info[8]))):
        for j in range(ROWS):
            copies.append(
                pltpu.make_async_copy(src.at[j], w.at[j, rows_at(at, size)], sem.at[4 * n + j])
            )
    for copy in copies:
        copy.start()
    for copy in copies:
        copy.wait()


def merge_body(info, v0, v1, v2, v3, dst):
    four = (v0, v1, v2, v3)

    def fill(c):
        total = sum(f32(v[256 + 16 * c : 272 + 16 * c, :]) for v in four)
        dst[0:16, :] = bf(total)
        for b, v in enumerate(four):
            rows = pl.ds(pl.multiple_of(16 + 16 * jnp.bitwise_xor(info[6], b), 16), 16)
            dst[rows, :] = v[288 + 16 * c : 304 + 16 * c, :]

    @pl.when(info[2] == 0)
    def _():
        fill(0)

    @pl.when(info[2] == 1)
    def _():
        fill(1)


def pile_body(*refs):
    dst = refs[-1]
    for n, src in enumerate(refs[:-1]):
        dst[n] = src[...]


def expand_early_body(info, own, oth, r1, e2, e1, r2):
    for v in (r1, e2, e1, r2):
        v[...] = jnp.zeros_like(v)

    def fill(src, shared, split):
        for n in range(own.shape[0]):
            group = info[5] if n % 2 == 0 else 1 - info[5]
            a = info[40 + n // 2 * GROUPS_DEV + group]
            shared[a] += f32(src[n, 0:16, :])
            for j in range(COLS):
                at = 16 + 16 * j
                split[a, :, cols(j, 1024)] += f32(src[n, at : at + 16, :])

    @pl.when(info[2] == 0)
    def _():
        fill(own, r1, e1)
        fill(oth, e2, r2)

    @pl.when(info[2] == 1)
    def _():
        fill(oth, r1, e1)
        fill(own, e2, r2)


def expand_late_body(info, v0, v1, v2, v3, qr, pe, qe, pr):
    four = (v0, v1, v2, v3)
    for v in (qr, pe, qe, pr):
        v[...] = jnp.zeros_like(v)
    for k in range(v0.shape[0]):
        group = info[5] if k % 2 == 0 else 1 - info[5]
        a = info[40 + k // 2 * GROUPS_DEV + group]
        qr[a] += sum(f32(v[k, 0:16, :]) for v in four)
        pe[a] += sum(f32(v[k, 16:32, :]) for v in four)
        for b, v in enumerate(four):
            j = jnp.bitwise_xor(info[6], b)
            qe[a, :, lanes_at(j * 768, 768)] += f32(v[k, 32:48, :768])
            pr[a, :, lanes_at(j * 256, 256)] += f32(v[k, 32:48, 768:])


def shift(v, k, axis="row"):
    if k == 0:
        return v
    size = lax.axis_size(axis)
    return lax.ppermute(v, axis, [(s, (s + k) % size) for s in range(size)])


def gather_row(v):
    return [v] + [shift(v, k) for k in range(1, ROWS)]


def gather_col(v):
    core = lax.ppermute(v, "col", CORE_SWAP)
    side = lax.ppermute(v, "col", Y_SWAP)
    return [v, core, side, lax.ppermute(side, "col", CORE_SWAP)]


def to_cols(pieces):
    return [pieces[0]] + [shift(pieces[k], ROWS - k) for k in range(1, ROWS)]


def spread(mine, other):
    return [mine, other] + [
        shift(v, k, "dp") for k in range(1, lax.axis_size("dp")) for v in (mine, other)
    ]


def pile(parts):
    shape = (len(parts), *parts[0].shape)
    return call(pile_body, [out(shape, BF)], parts, smem=0, us=0.01, name="pile")[0]

def body(
    hidden_in,
    out_grad,
    first_norm_gain,
    first_norm_bias,
    qkv_weight,
    qkv_bias,
    proj_weight,
    proj_bias,
    second_norm_gain,
    second_norm_bias,
    fc1_weight,
    fc1_bias,
    fc2_weight,
    second_feed_bias,
    qkv_reduce,
    qkv_expand,
    proj_reduce,
    proj_expand,
    fc1_reduce,
    fc1_expand,
    fc2_reduce,
    fc2_expand,
    adapter_choice,
    cont_prompt,
):
    r = lax.axis_index("row")
    col = lax.axis_index("col")
    dp = lax.axis_index("dp")
    y = col // 2
    c = lax.rem(col, 2)
    zl = lax.rem(r, 2)
    group = r // 2
    half = lax.rem(dp, 2)
    dp_swap = [(k, k ^ 1) for k in range(lax.axis_size("dp"))]
    slopes = jnp.exp2(
        -8.0 * (col * 4 + 1 + jnp.arange(4, dtype=jnp.int32)).astype(F32) / HEADS
    )
    adapter = jnp.where(group == 0, adapter_choice[0], adapter_choice[1])
    n_dp = jnp.int32(lax.axis_size("dp"))
    info = jnp.stack([r, y, c, dp * GROUPS_DEV, zl, group, col, dp, half] + [half, n_dp] + [half] * 5)
    info = jnp.concatenate([info.astype(jnp.int32), cont_prompt, adapter_choice])
    order = pltpu.SMEM((GROUPS_DEV * NCONT,), jnp.int32)
    flip = functools.partial(jnp.transpose, axes=(0, 2, 1))
    big = out((TOK, D), BF)
    small = out((RANK, D), F32)

    other = lax.ppermute(hidden_in, "col", CORE_SWAP)
    vectors = [
        first_norm_gain, first_norm_bias, proj_bias,
        second_norm_gain, second_norm_bias, second_feed_bias,
    ]
    factors = [flip(qkv_reduce), flip(fc1_reduce), proj_expand, fc2_expand]
    pieces = call(
        route_pack_body,
        [out((336, TOK), BF)] * 4,
        [info, Far(hidden_in), Far(other), *far(vectors), *far(factors)],
        [
            order,
            *[pltpu.VMEM((TOK,), BF)] * 6,
            pltpu.VMEM((16, RANK, TOK), BF),
            pltpu.SemaphoreType.DMA((22,)),
        ],
        raw=range(3, 13),
        us=1.5,
        name="route_x",
    )
    xs = [pieces[0]] + [shift(pieces[k], k) for k in range(1, ROWS)]
    packs = far(xs)
    first_half, w2_copies, qkv_e, fc1_e, proj_r, fc2_r = call(
        prepare_body,
        [
            out((128, D), BF), out((ROWS, 512, TOK), BF),
            out((RANK, 768), BF), out((RANK, D), BF), out((RANK, TOK), BF), out((RANK, D), BF),
        ],
        [
            after(info, pieces[0]),
            *far([qkv_weight, proj_weight, fc2_weight, qkv_expand, fc1_expand]),
            *far([flip(proj_reduce), flip(fc2_reduce)]),
        ],
        [pltpu.SemaphoreType.DMA((10,))],
        raw=range(1, 8),
        us=3,
        name="prepare",
    )
    first_half = after(first_half, xs[1])
    z_parts = [shift(first_half, k) for k in range(1, ROWS)]
    s_parts = [lax.ppermute(v, "dp", dp_swap) for v in z_parts]
    wq, wp = call(
        assemble_body,
        [out((ROWS, TOK, 768), BF), out((ROWS, TOK, TOK), BF)],
        [info, *far([qkv_weight, proj_weight, *z_parts, *s_parts])],
        [pltpu.SemaphoreType.DMA((14,))],
        raw=range(1, 9),
        us=15,
        name="assemble",
    )

    qkv_b = lax.dynamic_slice_in_dim(qkv_bias, col * 768, 768, 0)[None, :]
    fc1_b = lax.dynamic_slice_in_dim(fc1_bias, col * 1024, 1024, 0)[None, :]

    choices = [adapter_choice] + [
        shift(adapter_choice, k, "dp") for k in range(1, lax.axis_size("dp"))
    ]
    first = after(xs[0], qkv_b, fc1_b, w2_copies, *choices)
    (xn1,) = call(norm1_body, [big], [first, *xs[1:]], smem=0, us=8, name="norm1")
    xn1s = gather_col(xn1)
    q, kvp, kvc = call(
        qkv_body,
        [out((1024, 256), BF), out((512, 512), BF), out((512, 512), BF)],
        [info, *xn1s, wq, *packs, Far(qkv_b), Far(qkv_e)],
        us=6.5,
        name="qkv",
    )
    kvo = lax.ppermute(kvp, "row", Z_SWAP)

    g_other = lax.ppermute(after(out_grad, *z_parts), "col", CORE_SWAP)
    (pieces,) = call(
        route_all_body,
        [out((ROWS, 3 * TOK, TOK), BF)],
        [info, Far(out_grad), Far(g_other), Far(fc1_weight)],
        [order, pltpu.SemaphoreType.DMA((16,))],
        raw=(3,),
        us=1,
        name="route_g",
    )
    (state,) = call(
        attend_first_body,
        [out((2048, 256), F32)],
        [info, slopes, q, kvp, kvc],
        smem=2,
        us=9,
        name="attend_first",
    )
    g_own, w1a = call(
        join_body,
        [big, out((ROWS, 128, D), BF)],
        [info, after(lax.all_to_all(pieces, "row", 0, 0), state)],
        us=0.5,
        name="join",
    )
    g_side = lax.ppermute(g_own, "col", Y_SWAP)
    w1b = lax.ppermute(w1a, "dp", dp_swap)
    w2a = lax.all_to_all(after(w2_copies, state, kvo), "row", 0, 0)
    w2b = lax.ppermute(w2a, "dp", dp_swap)

    def attend_rest(which, q, state):
        return call(
            functools.partial(attend_rest_body, which),
            [out((512, 256), BF), out((8, 256), F32), big, big],
            [info, slopes, Far(q), kvo, state, Far(wp), Far(proj_r), *packs],
            smem=2,
            us=20 if which else 0.01,
            name="attend_rest",
        )

    heads1, lse1, p2, p3 = attend_rest(1, q, state)
    g_core = lax.ppermute(after(g_own, p3), "col", CORE_SWAP)
    g_all = [g_own, g_core, g_side, lax.ppermute(after(g_side, p3), "col", CORE_SWAP)]
    p_far = lax.ppermute(p3, "col", CORE_SWAP)
    p_side = add(p2, p_far)
    heads0, lse0, p0, p1 = attend_rest(0, q, Far(after(state, p_side)))
    p_side = lax.ppermute(p_side, "col", Y_SWAP)
    p_core = lax.ppermute(p1, "col", CORE_SWAP)
    staged = stage([after(xs[0], p0), *xs[1:]])
    mid, xn2 = call(
        norm2_body,
        [out((TOK, D), F32), big],
        [add32(p0, p_side), p_core, *staged],
        smem=0,
        us=1.5,
        name="norm2",
    )
    (w1,) = call(
        functools.partial(stage_weight_body, 128),
        [out((ROWS, TOK, D), BF)],
        [info, Far(after(w1a, p0)), Far(w1b)],
        [pltpu.SemaphoreType.DMA((8,))],
        raw=(1, 2),
        us=2,
        name="stage_w1",
    )
    zero = jnp.zeros((RANK, D), F32)
    xn2_core = lax.ppermute(xn2, "col", CORE_SWAP)
    xn2_side = lax.ppermute(xn2, "col", Y_SWAP)

    def mlp_pre(first, blocks):
        return call(
            mlp_pre_body,
            [out((2, TOK, D), BF)] * 2,
            [info, *blocks, w1, *staged, Far(fc1_b), Far(fc1_e)],
            us=5,
            name="mlp_pre",
        )

    act0, slope0 = mlp_pre(0, [xn2, xn2_core])
    xn2_far = lax.ppermute(after(xn2_side, act0), "col", CORE_SWAP)
    xn2s = [xn2, xn2_core, xn2_side, xn2_far]
    act1, slope1 = mlp_pre(1, xn2s[2:])
    (w2,) = call(
        functools.partial(stage_weight_body, 512),
        [out((ROWS, D, TOK), BF)],
        [info, Far(after(w2a, act0)), Far(w2b)],
        [pltpu.SemaphoreType.DMA((8,))],
        raw=(1, 2),
        us=2,
        name="stage_w2",
    )

    def mlp_back(blocks, slope, r_in, e_in):
        xa, xb = (xn2s[b] for b in blocks)
        ga, gb = (g_all[b] for b in blocks)
        return call(
            mlp_back_body,
            [big, big, small, small],
            [info, xa, xb, ga, gb, slope, w1, w2, *staged, Far(fc1_e), Far(fc2_r), r_in, e_in],
            us=0.01,
            name="mlp_back",
        )

    d2, d3, r1, e1 = mlp_back((2, 3), slope1, zero, zero)
    d_far = lax.ppermute(d3, "col", CORE_SWAP)
    d_side = add(d2, d_far)
    d0, d1, r1, e1 = mlp_back((0, 1), slope0, after(r1, d_side), e1)
    d_side = lax.ppermute(d_side, "col", Y_SWAP)
    d_core = lax.ppermute(d1, "col", CORE_SWAP)
    res = call(
        fc2_body,
        [big] * 4 + [out((64, D), BF)],
        [info, act0, act1, *g_all, w2, Far(fc2_r), *staged, r1, e1],
        us=0.01,
        name="fc2",
    )
    m_parts, mlp_pack = res[:4], res[4]
    staged_back = stage([after(mid, mlp_pack), g_own, *xs])
    d_mid, g_attn = call(
        norm2_back_body,
        [out((TOK, D), F32), out((320, D), BF)],
        [add32(d0, d_side), d_core, mlp_pack, *staged_back],
        smem=0,
        us=1.5,
        name="norm2_back",
    )
    ga_core = lax.ppermute(g_attn, "col", CORE_SWAP)
    ga_side = lax.ppermute(g_attn, "col", Y_SWAP)
    shared = far([q, kvp, kvo, kvc])

    def d_heads(blocks, heads, r_in, e_in):
        return call(
            d_heads_body,
            [out((512, 256), BF), out((RANK, TOK), F32), small],
            [info, *blocks, Far(wp), *packs, Far(proj_r), Far(heads), r_in, e_in],
            us=1.5,
            name="d_heads",
        )

    dh0, pr, pe = d_heads([g_attn, ga_core], heads0, jnp.zeros((RANK, TOK), F32), zero)
    dq0, dkp, dko, dkc = call(
        attend_back_a_body,
        [out((512, 256), BF), out((512, 512), F32), out((512, 512), F32), out((512, 512), BF)],
        [info, slopes, *shared, Far(heads0), dh0, Far(lse0)],
        smem=2,
        us=16,
        weight=W_BIG,
        name="attend_back_a",
    )
    ga_side = after(ga_side, dq0)
    ga_far = lax.ppermute(ga_side, "col", CORE_SWAP)
    (early_half,) = call(
        merge_body,
        [out((80, D), BF)],
        [info, g_attn, ga_core, ga_side, ga_far],
        us=0.7,
        name="merge",
    )
    dh1, pr, pe = d_heads([ga_side, ga_far], heads1, pr, pe)
    dq1_part, dko = call(
        attend_back_b_body,
        [out((512, 256), F32), out((672, 512), BF)],
        [info, slopes, Far(q), Far(kvo), Far(heads1), dh1, Far(lse1), Far(dko), early_half],
        [pltpu.VMEM((512, 512), F32)],
        smem=2,
        us=8,
        name="attend_back_b",
    )
    dkr = lax.ppermute(dko, "row", Z_SWAP)
    dq1, dkp, dkc = call(
        attend_back_c_body,
        [out((512, 256), BF), out((512, 512), F32), out((512, 512), BF)],
        [info, slopes, Far(q), Far(kvp), Far(kvc), Far(heads1), dh1, Far(lse1), *far([dkp, dkc, dq1_part])],
        smem=2,
        us=8,
        name="attend_back_c",
    )
    (early_sum,) = call(
        early_sum_body, [out((80, D), BF)], [early_half, dkr], smem=0, us=0.01, name="early_sum"
    )
    m_far = lax.ppermute(after(m_parts[3], dq0), "col", CORE_SWAP)
    m_core = lax.ppermute(after(m_parts[1], dq0), "col", CORE_SWAP)
    m_sum = add(after(m_parts[2], dko), m_far)
    m_side = lax.ppermute(m_sum, "col", Y_SWAP)
    res = call(
        qkv_back_body,
        [big] * 4 + [out((48, D), BF)],
        [
            info, dq0, dq1, dkp, after(dkr, early_sum), Far(dkc),
            *far(xn1s), Far(wq), *packs, Far(qkv_e), pr, pe,
        ],
        us=20,
        name="qkv_back",
    )
    q_parts, late_pack = res[:4], res[4]
    early_parts = spread(early_sum, shift(early_sum, 2))
    ready = after(q_parts[3], m_side, *early_parts[1:3])
    q_sum = add(q_parts[2], lax.ppermute(ready, "col", CORE_SWAP))
    hidden = call(
        hidden_body,
        [out((TOK, TOK), BF)] * 4,
        [add32(m_parts[0], after(m_side, q_sum), 0.01), m_core, Far(mid), *packs],
        smem=0,
        us=0.01,
        name="hidden",
    )
    k0, rc = q_parts[0], lax.ppermute(q_parts[1], "col", CORE_SWAP)
    ry = lax.ppermute(q_sum, "col", Y_SWAP)
    late_sum = add(late_pack, lax.ppermute(after(late_pack, q_sum), "row", Z_SWAP))
    late_next = shift(late_sum, 2)
    late_four = pile(spread(late_sum, late_next))
    late_all = gather_col(late_four)
    staged_last = stage([after(d_mid, k0), *xs])
    ins = call(
        norm1_back_body,
        [out((2 * TOK, TOK), BF)] * 4,
        [add32(after(k0, late_next), ry), rc, *staged_last, *hidden],
        smem=0,
        us=1,
        name="norm1_back",
    )
    early_all = pile(early_parts)
    early_far = lax.ppermute(after(early_all, ins[0]), "col", CORE_SWAP)
    table = jnp.concatenate([info, jnp.zeros((40 - 34,), jnp.int32), *choices])
    o_fc1r, o_f2e, o_f1e, o_f2r = call(
        expand_early_body,
        [out((COUNT, RANK, w), F32) for w in (1024, 1024, 4096, 4096)],
        [table, Far(early_all), Far(early_far)],
        us=3,
        name="expand_early",
    )
    (joined,) = call(
        stack_body,
        [out((8 * TOK, TOK), BF)],
        [after(v, o_fc1r, late_all[2]) for v in to_cols(ins)],
        smem=0,
        us=0.01,
        name="stack",
    )
    input_gradient, hidden_out = call(
        unroute_body,
        [out((1024, TOK), F32), out((1024, TOK), BF)],
        [info, joined, lax.ppermute(joined, "col", CORE_SWAP)],
        [order],
        us=2,
        name="unroute",
    )
    o_qr, o_pe, o_qe, o_pr = call(
        expand_late_body,
        [out((COUNT, RANK, w), F32) for w in (1024, 1024, 3072, 1024)],
        [table, *late_all],
        us=3,
        name="expand_late",
    )
    return (
        hidden_out,
        input_gradient,
        flip(o_qr),
        o_qe,
        flip(o_pr),
        o_pe,
        flip(o_fc1r),
        o_f1e,
        flip(o_f2r),
        o_f2e,
    )


def solution(mesh):
    placed = (
        P(("dp", "col"), "row"),
        P(("dp", "col"), "row"),
        P("row"),
        P("row"),
        P("row", "col"),
        P(),
        P("col", "row"),
        P("row"),
        P("row"),
        P("row"),
        P("row", "col"),
        P(),
        P("col", "row"),
        P("row"),
        P(None, "row", None),
        P(),
        P(None, "col", None),
        P(None, None, "row"),
        P(None, "row", None),
        P(),
        P(None, "col", None),
        P(None, None, "row"),
        P("dp"),
        P("dp"),
    )
    return jax.shard_map(
        body,
        mesh=mesh,
        in_specs=placed,
        out_specs=(P(("dp", "col"), "row"), P(("dp", "col"), "row")) + (P(),) * 8,
        check_vma=False,
    )
```

```python
import functools

import jax
import jax.numpy as jnp
from jax import lax
from jax.experimental import pallas as pl
from jax.experimental.pallas import tpu as pltpu
from jax.sharding import PartitionSpec as P

D = 1024
HEADS = 16
HEAD = 64
FF = 4096
RANK = 16
COUNT = 8
PROMPT = 1024
CONT = 128
NCONT = 8
GROUPS_DEV = 2

EPSILON = 1e-05
SCALE = 2.0
GELU_A = 0.7978845608028654
GELU_B = 0.044715
ROWS = 4
COLS = 4
TOK = 256
BLOCK = 128
LOW = -1e30
W_SMALL = 5e8
W_BIG = 5e8

BF = jnp.bfloat16
F32 = jnp.float32

VM = pl.BlockSpec(memory_space=pltpu.VMEM)
SM = pl.BlockSpec(memory_space=pltpu.SMEM)
HB = pl.BlockSpec(memory_space=pltpu.HBM)

CORE_SWAP = [(0, 1), (1, 0), (2, 3), (3, 2)]
Y_SWAP = [(0, 2), (2, 0), (1, 3), (3, 1)]
Z_SWAP = [(0, 1), (1, 0), (2, 3), (3, 2)]


def nn(a, b):
    return lax.dot_general(a, b, (((1,), (0,)), ((), ())), preferred_element_type=F32)


def nt(a, b):
    return lax.dot_general(a, b, (((1,), (1,)), ((), ())), preferred_element_type=F32)


def tn(a, b):
    return lax.dot_general(a, b, (((0,), (0,)), ((), ())), preferred_element_type=F32)


def f32(v):
    return v.astype(F32)


def bf(v):
    return v.astype(BF)


class Far:
    def __init__(self, value):
        self.value = value


def far(values):
    return [Far(v) for v in values]


def call(
    body, outs, ins, scratch=(), smem=1, limit=40, us=1, raw=(), weight=W_SMALL, name=None
):
    values = [
        pltpu.with_memory_space_constraint(v.value, pltpu.HBM) if isinstance(v, Far) else v
        for v in ins
    ]
    fetched = [i for i, v in enumerate(ins) if isinstance(v, Far) and i not in raw]
    specs = [SM] * smem
    for v in ins[smem:]:
        specs.append(HB if isinstance(v, Far) else VM)
    nbytes = sum(v.size * v.dtype.itemsize for v in values)
    nbytes += sum(o.size * o.dtype.itemsize for o in outs)
    extra = [pltpu.VMEM(values[i].shape, values[i].dtype) for i in fetched]
    if fetched:
        extra.append(pltpu.SemaphoreType.DMA((len(fetched),)))

    def whole(*refs):
        refs = list(refs)
        if fetched:
            sem = refs[-1]
            buffers = refs[-1 - len(fetched) : -1]
            refs = refs[: -1 - len(fetched)]
            copies = []
            for n, (i, buffer) in enumerate(zip(fetched, buffers)):
                copies.append(pltpu.make_async_copy(refs[i], buffer, sem.at[n]))
                copies[-1].start()
                refs[i] = buffer
            for copy in copies:
                copy.wait()
        body(*refs)

    return pl.pallas_call(
        whole,
        out_shape=tuple(outs),
        in_specs=specs,
        out_specs=tuple([VM] * len(outs)),
        scratch_shapes=list(scratch) + extra,
        compiler_params=pltpu.CompilerParams(vmem_limit_bytes=limit << 20),
        cost_estimate=pl.CostEstimate(
            flops=int(us * weight), bytes_accessed=nbytes // 8, transcendentals=0
        ),
        name=name,
    )(*values)


def after(value, *others):
    res = lax.optimization_barrier((value, others))
    return res[0]


def out(shape, dtype):
    return jax.ShapeDtypeStruct(shape, dtype)


def block_at(zl, c, j):
    return c * 4 + zl + j * (3 - 2 * zl)


def fill_order(info, order):
    base = info[3]
    first = jnp.int32(0)
    second = jnp.int32(NCONT)
    for j in range(GROUPS_DEV * NCONT):
        own = info[16 + j] == base
        slot = jnp.where(own, first, second)
        order[slot] = jnp.int32(j)
        first = first + jnp.where(own, 1, 0)
        second = second + jnp.where(own, 0, 1)


def place_of(info, order, z, core, j):
    prompt = (z // 2) * 8 + block_at(lax.rem(z, 2), core, j)
    cont = order[4 * z + 2 * core + j]
    return jnp.where(info[1] == 0, prompt, cont)


def route_body(info, own, oth, o0, o1, o2, o3, order):
    fill_order(info, order)
    c = info[2]
    for s, dst in enumerate((o0, o1, o2, o3)):
        z = lax.rem(info[0] + s, ROWS)
        for j in range(2):
            src = place_of(info, order, z, c, j)
            at = pl.ds(pl.multiple_of(lax.rem(src, 8) * BLOCK, BLOCK), BLOCK)
            mine = src // 8 == c

            @pl.when(mine)
            def _():
                dst[pl.ds(j * BLOCK, BLOCK), :] = own[at, :]

            @pl.when(jnp.logical_not(mine))
            def _():
                dst[pl.ds(j * BLOCK, BLOCK), :] = oth[at, :]


def route_pack_body(
    info, own, oth, g1, c1, pb, g2, c2, fb, qr, fr, pe, fe,
    o0, o1, o2, o3, order, v0, v1, v2, v3, v4, v5, mats, sem,
):
    vecs = (v0, v1, v2, v3, v4, v5)
    pairs = list(zip((g1, c1, pb, g2, c2, fb), vecs))
    for k in range(ROWS):
        which = lax.rem(info[0] + k, ROWS) // 2
        a = jnp.where(which == 0, info[32], info[33])
        pairs += [(v.at[a], mats.at[4 * k + i]) for i, v in enumerate((qr, fr, pe, fe))]
    copies = [pltpu.make_async_copy(a, b, sem.at[i]) for i, (a, b) in enumerate(pairs)]
    for copy in copies:
        copy.start()
    route_body(info, own, oth, o0, o1, o2, o3, order)
    for copy in copies:
        copy.wait()
    for k, dst in enumerate((o0, o1, o2, o3)):
        head = [f32(v[...]).reshape(1, TOK) for v in vecs]
        dst[256:272, :] = bf(jnp.concatenate(head + [jnp.zeros((10, TOK), F32)], axis=0))
        for i in range(4):
            dst[272 + 16 * i : 288 + 16 * i, :] = mats[4 * k + i]


def stack_body(a0, a1, a2, a3, h0, h1, h2, h3, dst):
    for k, (a, h) in enumerate(((a0, h0), (a1, h1), (a2, h2), (a3, h3))):
        dst[2 * k * TOK : (2 * k + 1) * TOK, :] = a[...]
        dst[(2 * k + 1) * TOK : (2 * k + 2) * TOK, :] = h[...]


def route_all_body(info, own, oth, w2, dst, order, sem):
    copies = []
    for z in range(ROWS):
        to = dst.at[z, pl.ds(TOK, 512)]
        copies.append(pltpu.make_async_copy(w2.at[rows_at(info[8], 512)], to, sem.at[z]))
    for copy in copies:
        copy.start()
    fill_order(info, order)
    c = info[2]
    for z in range(ROWS):
        for j in range(2):
            src = place_of(info, order, z, c, j)
            at = pl.ds(pl.multiple_of(lax.rem(src, 8) * BLOCK, BLOCK), BLOCK)
            mine = src // 8 == c

            @pl.when(mine)
            def _():
                dst[z, pl.ds(j * BLOCK, BLOCK), :] = own[at, :]

            @pl.when(jnp.logical_not(mine))
            def _():
                dst[z, pl.ds(j * BLOCK, BLOCK), :] = oth[at, :]
    for copy in copies:
        copy.wait()


def unroute_body(info, a, b, grad, hidden, order):
    fill_order(info, order)
    c = info[2]
    for s in range(ROWS):
        z = lax.rem(info[0] + s, ROWS)
        for other, src in ((0, a), (1, b)):
            core = c if other == 0 else 1 - c
            for j in range(2):
                at = place_of(info, order, z, core, j)

                @pl.when(at // 8 == c)
                def _():
                    rows = pl.ds(pl.multiple_of(lax.rem(at, 8) * BLOCK, BLOCK), BLOCK)
                    start = 2 * s * TOK + j * BLOCK
                    grad[rows, :] = f32(src[pl.ds(start, BLOCK), :])
                    hidden[rows, :] = src[pl.ds(start + TOK, BLOCK), :]


def cols(k, width=TOK):
    return pl.ds(k * width, width)


def row_stats(parts):
    total = sum(jnp.sum(v, axis=1, keepdims=True) for v in parts)
    mean = total * (1.0 / D)
    dev = [v - mean for v in parts]
    var = sum(jnp.sum(v * v, axis=1, keepdims=True) for v in dev) * (1.0 / D)
    rstd = lax.rsqrt(var + EPSILON)
    return [v * rstd for v in dev], rstd


def norm1_body(x0, x1, x2, x3, xn):
    for t in range(2):
        rows = pl.ds(t * 128, 128)
        hat, _ = row_stats([f32(v[rows, :]) for v in (x0, x1, x2, x3)])
        for k, pack in enumerate((x0, x1, x2, x3)):
            xn[rows, cols(k)] = bf(hat[k] * f32(pack[256:257, :]) + f32(pack[257:258, :]))


def both(a, b, rows, k):
    return f32(a[rows, cols(k)]) + f32(b[rows, cols(k)])


def norm2_body(a, b, x0, x1, x2, x3, mid, xn):
    for t in range(2):
        rows = pl.ds(t * 128, 128)
        parts = []
        for k, x in enumerate((x0, x1, x2, x3)):
            v = f32(x[rows, :]) + both(a, b, rows, k) + f32(x[258:259, :])
            mid[rows, cols(k)] = v
            parts.append(v)
        hat, _ = row_stats(parts)
        for k, pack in enumerate((x0, x1, x2, x3)):
            xn[rows, cols(k)] = bf(hat[k] * f32(pack[259:260, :]) + f32(pack[260:261, :]))


def norm_back(hat, rstd, grads):
    total = sum(jnp.sum(g, axis=1, keepdims=True) for g in grads) * (1.0 / D)
    along = sum(jnp.sum(g * h, axis=1, keepdims=True) for g, h in zip(grads, hat)) * (1.0 / D)
    return [rstd * (g - total - h * along) for g, h in zip(grads, hat)]


def norm2_back_body(
    a, b, pack, mid, g, x0, x1, x2, x3, d_mid, g_attn
):
    g_attn[256:320, :] = pack[...]
    for t in range(2):
        rows = pl.ds(t * 128, 128)
        hat, rstd = row_stats([mid[rows, cols(k)] for k in range(4)])
        grads = []
        for k, pack in enumerate((x0, x1, x2, x3)):
            grads.append(both(a, b, rows, k) * f32(pack[259:260, :]))
        back = norm_back(hat, rstd, grads)
        for k in range(4):
            v = f32(g[rows, cols(k)]) + back[k]
            d_mid[rows, cols(k)] = v
            g_attn[rows, cols(k)] = bf(v)


def norm1_back_body(a, b, d_mid, x0, x1, x2, x3, i0, i1, i2, i3):
    for t in range(2):
        rows = pl.ds(t * 128, 128)
        hat, rstd = row_stats([f32(v[rows, :]) for v in (x0, x1, x2, x3)])
        grads = []
        for k, pack in enumerate((x0, x1, x2, x3)):
            grads.append(both(a, b, rows, k) * f32(pack[256:257, :]))
        back = norm_back(hat, rstd, grads)
        for k, dst in enumerate((i0, i1, i2, i3)):
            dst[rows, :] = bf(d_mid[rows, cols(k)] + back[k])


def hidden_body(a, b, mid, x0, x1, x2, x3, h0, h1, h2, h3):
    for t in range(2):
        rows = pl.ds(t * 128, 128)
        for k, (pack, dst) in enumerate(zip((x0, x1, x2, x3), (h0, h1, h2, h3))):
            v = mid[rows, cols(k)] + both(a, b, rows, k) + f32(pack[261:262, :])
            dst[rows, :] = bf(v)


def join_body(info, v, dst, w2):
    for k in range(ROWS):
        dst[:, cols(k)] = v[rel(info, k), 0:TOK, :]
    for k in range(1, ROWS):
        w2[k - 1] = v[rel(info, k), TOK:, :]


def rest_body(info, v, dst):
    for k in range(1, ROWS):
        dst[k - 1] = v[rel(info, k)]


def slab_rows(info, b):
    y = jnp.bitwise_xor(info[1], b // 2)
    c = jnp.bitwise_xor(info[2], b % 2)
    return y, c


def low_lanes(rows):
    return lax.broadcasted_iota(jnp.int32, (rows, 128), 1) < HEAD


def rel(info, k):
    return lax.rem(info[0] - k + ROWS, ROWS)


def rel_cols(info, k):
    return pl.ds(pl.multiple_of(rel(info, k) * TOK, TOK), TOK)


def lanes_at(at, size):
    return pl.ds(pl.multiple_of(at, 128), size)


def rows_at(i, size):
    return pl.ds(pl.multiple_of(i * size, size), size)


def prepare_body(
    info, wq, wp, w1, qe, fe, pr, fr, first, c1, o_qe, o_fe, o_pr, o_fr, sem
):
    half = info[8]
    a = jnp.where(info[5] == 0, info[32], info[33])
    rows = rows_at(half, 128)
    pairs = [(wq.at[rows], first.at[:, 0:768]), (wp.at[rows], first.at[:, 768:1024])]
    pairs += [(qe.at[a, :, lanes_at(info[6] * 768, 768)], o_qe)]
    pairs += [(fe.at[a, :, lanes_at(info[6] * 1024, 1024)], o_fe)]
    pairs += [(pr.at[a], o_pr), (fr.at[a], o_fr)]
    for j in range(ROWS):
        pairs += [(w1.at[rows], c1.at[j])]
    copies = [pltpu.make_async_copy(x, y, sem.at[i]) for i, (x, y) in enumerate(pairs)]
    for copy in copies:
        copy.start()
    for copy in copies:
        copy.wait()


def assemble_body(info, own_q, own_p, z1, z2, z3, s1, s2, s3, ws, wp, sem):
    half = info[8]
    copies = [
        pltpu.make_async_copy(own_q, ws.at[0], sem.at[0]),
        pltpu.make_async_copy(own_p, wp.at[0], sem.at[1]),
    ]
    for k, (zv, sv) in enumerate(((z1, s1), (z2, s2), (z3, s3))):
        for n, (v, at) in enumerate(((zv, half), (sv, 1 - half))):
            rows = rows_at(at, 128)
            at = 2 + 4 * k + 2 * n
            copies.append(
                pltpu.make_async_copy(v.at[:, 0:768], ws.at[k + 1, rows], sem.at[at])
            )
            copies.append(
                pltpu.make_async_copy(v.at[:, 768:1024], wp.at[k + 1, rows], sem.at[at + 1])
            )
    for copy in copies:
        copy.start()
    for copy in copies:
        copy.wait()


def qkv_body(
    info, x0, x1, x2, x3, ws, p0, p1, p2, p3, bias, expand, q, kvp, kvc
):
    ps = (p0, p1, p2, p3)
    low = low_lanes(TOK)
    for b, x in enumerate((x0, x1, x2, x3)):
        y, c = slab_rows(info, b)
        acc = sum(nn(x[:, cols(k)], ws[k]) for k in range(4))
        u = bf(sum(nt(x[:, cols(k)], ps[k][272:288, :]) for k in range(4)))
        acc = acc + f32(bias[...]) + SCALE * nn(u, expand[...])
        kv = []
        for pair in range(2):
            at = 384 * pair
            g0, g1, g2 = (acc[:, at + 128 * i : at + 128 * i + 128] for i in range(3))
            q[rows_at(y * 2 + c, TOK), cols(pair, 128)] = bf(
                bf(jnp.where(low, g0, g1)) * BF(0.125)
            )
            kv.append((bf(pltpu.roll(jnp.where(low, g2, g0), 64, 1)), bf(jnp.where(low, g1, g2))))
        rows = rows_at(c, TOK)

        @pl.when(y == 0)
        def _():
            for pair in range(2):
                kvp[rows, cols(pair, 128)] = kv[pair][0]
                kvp[rows, cols(2 + pair, 128)] = kv[pair][1]

        @pl.when(y == 1)
        def _():
            for pair in range(2):
                kvc[rows, cols(pair, 128)] = kv[pair][0]
                kvc[rows, cols(2 + pair, 128)] = kv[pair][1]


WIDE = 256


def stacked(v, low):
    zero = jnp.zeros_like(v)
    return jnp.concatenate([jnp.where(low, v, zero), jnp.where(low, zero, v)], axis=0)


def split_id(shape, axis):
    lane = lax.broadcasted_iota(jnp.int32, shape, axis)
    return lane, jnp.where(lane < BLOCK, lane, lane - BLOCK)


def chunk_place(shape, axis, side, n):
    lane, within = split_id(shape, axis)
    first = block_at(side, n, 0) * BLOCK
    second = block_at(side, n, 1) * BLOCK
    return within + jnp.where(lane < BLOCK, first, second)


def keep_state(state, low):
    top, total, acc = state
    lane = lax.broadcasted_iota(jnp.int32, (2 * BLOCK, 128), 1)
    spot = lax.rem(lane, HEAD)
    row = lax.broadcasted_iota(jnp.int32, (2 * BLOCK, 128), 0)
    own = (lane < HEAD) == (row < BLOCK)
    return jnp.where(own, acc, jnp.where(spot == 0, top, total))


def load_state(v):
    lane = lax.broadcasted_iota(jnp.int32, (2 * BLOCK, 128), 1)
    row = lax.broadcasted_iota(jnp.int32, (2 * BLOCK, 128), 0)
    spot = jnp.where(row < BLOCK, HEAD, 0)
    top = jnp.max(jnp.where(lane == spot, v, LOW), axis=1, keepdims=True)
    total = jnp.sum(jnp.where(lane == spot + 1, v, 0.0), axis=1, keepdims=True)
    return top, total, v


def soft_update(state, s, v):
    if state is None:
        top = jnp.max(s, axis=1, keepdims=True)
        p = jnp.exp(s - top)
        return top, jnp.sum(p, axis=1, keepdims=True), nn(bf(p), v)
    top, total, acc = state
    new = jnp.maximum(top, jnp.max(s, axis=1, keepdims=True))
    p = jnp.exp(s - new)
    shrink = jnp.exp(top - new)
    total = total * shrink + jnp.sum(p, axis=1, keepdims=True)
    return new, total, acc * shrink + nn(bf(p), v)


def head_slopes(slopes, shape, axis):
    lane = lax.broadcasted_iota(jnp.int32, shape, axis)
    return [
        jnp.where(lane < BLOCK, slopes[2 * pair], slopes[2 * pair + 1]) for pair in range(2)
    ]


def attend_chunk(q2, states, kv, rows, place, base, slope, spot, masked):
    res = []
    away = place - base
    for pair in range(2):
        s = nt(q2[pair], kv[rows, cols(pair, 128)]) + slope[pair] * away.astype(F32)
        if masked:
            s = jnp.where(away <= spot, s, LOW)
        res.append(soft_update(states[pair], s, kv[rows, cols(2 + pair, 128)]))
    return res


def attend_first_body(info, slopes, q, kvp, kvc, state):
    zl = info[4]
    low = low_lanes(BLOCK)
    _, spot = split_id((2 * BLOCK, 1), 0)
    slope = head_slopes(slopes, (2 * BLOCK, 1), 0)
    places = [chunk_place((1, WIDE), 1, zl, n) for n in range(2)]

    def load(i):
        return [stacked(q[rows_at(i, BLOCK), cols(pair, 128)], low) for pair in range(2)]

    def save(states, i):
        for pair in range(2):
            state[rows_at(i, WIDE), cols(pair, 128)] = keep_state(states[pair], low)

    def prompt_block(j, _):
        for n in range(2):
            i = 2 * n + j
            base = block_at(zl, n, j) * BLOCK
            q2 = load(i)
            states = [None, None]
            for m in range(n, -1, -1):
                states = attend_chunk(
                    q2, states, kvp, pl.ds(m * WIDE, WIDE), places[m], base, slope, spot, m == n
                )
            save(states, i)
        return 0

    lax.fori_loop(0, 2, prompt_block, 0)

    def cont_block(j, _):
        q2 = load(4 + j)
        own_place = lax.broadcasted_iota(jnp.int32, (1, BLOCK), 1)
        states = attend_chunk(
            q2, [None, None], kvc, rows_at(j, BLOCK), own_place, 0, slope, spot, True
        )
        for m in range(2):
            states = attend_chunk(
                q2, states, kvp, pl.ds(m * WIDE, WIDE), places[m], PROMPT, slope, spot, False
            )
        save(states, 4 + j)
        return 0

    lax.fori_loop(0, 4, cont_block, 0)


def attend_rest_body(
    which, info, slopes, q, kvo, state, ws, reduce, p0, p1, p2, p3, heads, lse, o0, o1
):
    zl = info[4]
    y = info[1] if which == 0 else 1 - info[1]
    low = low_lanes(BLOCK)
    _, spot = split_id((2 * BLOCK, 1), 0)
    slope = head_slopes(slopes, (2 * BLOCK, 1), 0)
    places = [chunk_place((1, WIDE), 1, 1 - zl, n) for n in range(2)]

    def load(i):
        q2 = [stacked(q[rows_at(i, BLOCK), cols(pair, 128)], low) for pair in range(2)]
        states = [load_state(state[rows_at(i, WIDE), cols(pair, 128)]) for pair in range(2)]
        return q2, states

    def finish(states, j):
        for pair in range(2):
            top, total, acc = states[pair]
            res = acc / total
            heads[rows_at(j, BLOCK), cols(pair, 128)] = bf(
                jnp.where(low, res[:BLOCK], res[BLOCK:])
            )
            kept = jnp.transpose(jnp.broadcast_to(top + jnp.log(total), (2 * BLOCK, 128)))
            lse[pl.ds(pair * 4 + j, 1), :] = kept[0:1, :]

    @pl.when(y == 0)
    def _():
        def prompt_block(j, _):
            for n in range(2):
                i = 2 * n + j
                base = block_at(zl, n, j) * BLOCK
                q2, states = load(i)
                for m in range(n + 1):
                    states = attend_chunk(
                        q2, states, kvo, pl.ds(m * WIDE, WIDE), places[m], base, slope, spot, m == n
                    )
                finish(states, i)
            return 0

        lax.fori_loop(0, 2, prompt_block, 0)

    @pl.when(y == 1)
    def _():
        def cont_block(j, _):
            q2, states = load(4 + j)
            for m in range(2):
                states = attend_chunk(
                    q2, states, kvo, pl.ds(m * WIDE, WIDE), places[m], PROMPT, slope, spot, False
                )
            finish(states, j)
            return 0

        lax.fori_loop(0, 4, cont_block, 0)

    ps = (p0, p1, p2, p3)
    for b, dst in enumerate((o0, o1)):
        c = jnp.bitwise_xor(info[2], b)
        h = heads[rows_at(c, TOK), :]
        u = bf(nt(h, reduce[...]))
        for k in range(4):
            dst[:, cols(k)] = bf(nn(h, ws[k]) + SCALE * nn(u, ps[k][304:320, :]))


def mlp_pre_body(info, x0, x1, w1, p0, p1, p2, p3, bias, expand, act, slope):
    ps = (p0, p1, p2, p3)
    for b, x in enumerate((x0, x1)):
        u = bf(sum(nt(x[:, cols(k)], ps[k][288:304, :]) for k in range(4)))
        pre = sum(nn(x[:, cols(k)], w1[rel(info, k)]) for k in range(4))
        pre = pre + f32(bias[...]) + SCALE * nn(u, expand[...])
        sq = pre * pre
        t = jnp.tanh(pre * (GELU_A + (GELU_A * GELU_B) * sq))
        half = 0.5 + 0.5 * t
        act[b] = bf(pre * half)
        slope[b] = bf(
            half + (0.5 * pre) * (1.0 - t * t) * (GELU_A + (3.0 * GELU_A * GELU_B) * sq)
        )


def mlp_back_body(
    info, x0, x1, g0, g1, slope, w1, w2, p0, p1, p2, p3, expand, reduce, r_in, e_in,
    d0, d1, r_out, e_out,
):
    ps = (p0, p1, p2, p3)
    rv, ev = r_in[...], e_in[...]
    for b, (x, g, dx) in enumerate(((x0, g0, d0), (x1, g1, d1))):
        u = bf(sum(nt(x[:, cols(k)], ps[k][288:304, :]) for k in range(4)))
        du2 = bf(SCALE * sum(nt(g[:, cols(k)], ps[k][320:336, :]) for k in range(4)))
        d_act = sum(nt(g[:, cols(k)], w2[rel(info, k)]) for k in range(4)) + nn(du2, reduce[...])
        d_pre = bf(d_act * f32(slope[b]))
        du = bf(SCALE * nt(d_pre, expand[...]))
        for k in range(4):
            dx[:, cols(k)] = bf(nt(d_pre, w1[rel(info, k)]) + nn(du, ps[k][288:304, :]))
        rv = rv + tn(du, x[...])
        ev = ev + tn(u, d_pre)
    r_out[...] = rv
    e_out[...] = ev


def fc2_body(
    info, a0, a1, g0, g1, g2, g3, w2, reduce, p0, p1, p2, p3, r1, e1,
    m0, m1, m2, m3, grads,
):
    ps = (p0, p1, p2, p3)
    rv = ev = 0.0
    for b, (g, m) in enumerate(zip((g0, g1, g2, g3), (m0, m1, m2, m3))):
        act = a0[b] if b < 2 else a1[b - 2]
        du = bf(SCALE * sum(nt(g[:, cols(k)], ps[k][320:336, :]) for k in range(4)))
        u = bf(nt(act, reduce[...]))
        for k in range(4):
            m[:, cols(k)] = bf(nn(act, w2[rel(info, k)]) + SCALE * nn(u, ps[k][320:336, :]))
        rv = rv + tn(du, act)
        ev = ev + SCALE * tn(u, g[...])
    for k in range(4):
        grads[0:16, rel_cols(info, k)] = bf(r1[:, cols(k)])
        grads[16:32, rel_cols(info, k)] = bf(ev[:, k * TOK : k * TOK + TOK])
    grads[32:48, :] = bf(SCALE * e1[...])
    grads[48:64, :] = bf(rv)


def d_heads_body(
    info, g0, g1, ws, p0, p1, p2, p3, reduce, heads, r_in, e_in, dh, r_out, e_out
):
    ps = (p0, p1, p2, p3)
    rv, ev = r_in[...], e_in[...]
    for b, g in enumerate((g0, g1)):
        rows = rows_at(jnp.bitwise_xor(info[2], b), TOK)
        h = heads[rows, :]
        u = bf(nt(h, reduce[...]))
        du = bf(SCALE * sum(nt(g[0:256, cols(k)], ps[k][304:320, :]) for k in range(4)))
        v = sum(nt(g[0:256, cols(k)], ws[k]) for k in range(4)) + nn(du, reduce[...])
        dh[rows, :] = bf(v)
        rv = rv + tn(du, h)
        ev = ev + SCALE * tn(u, g[0:256, :])
    r_out[...] = rv
    e_out[...] = ev


def back_load(heads, d_heads, lse, q, qi, j, low):
    res = []
    for pair in range(2):
        lane = cols(pair, 128)
        q2 = stacked(q[rows_at(qi, BLOCK), lane], low)
        do = d_heads[rows_at(j, BLOCK), lane]
        both = jnp.transpose(f32(do) * f32(heads[rows_at(j, BLOCK), lane]))
        delta = jnp.concatenate(
            [
                jnp.sum(both[:HEAD], axis=0, keepdims=True),
                jnp.sum(both[HEAD:], axis=0, keepdims=True),
            ],
            axis=1,
        )
        res.append((q2, stacked(do, low), delta, lse[pl.ds(pair * 4 + j, 1), :]))
    return res


def back_chunk(args, kv, d_kv, d_at, rows, place, base, slope, spot, masked, store, d_qs):
    away = place - base
    res = []
    for pair in range(2):
        q2, do2, delta, kept = args[pair]
        lane = cols(pair, 128)
        vlane = cols(2 + pair, 128)
        k = kv[rows, lane]
        s = nt(k, q2) + (away.astype(F32) * slope[pair] - kept)
        p = jnp.exp(s)
        if masked:
            p = jnp.where(away <= spot, p, 0.0)
        ds = bf(p * (nt(kv[rows, vlane], do2) - delta))
        dk = nn(ds, q2)
        dv = nn(bf(p), do2)
        if store:
            d_kv[d_at, lane] = bf(dk)
            d_kv[d_at, vlane] = bf(dv)
        else:
            d_kv[d_at, lane] += dk
            d_kv[d_at, vlane] += dv
        d_q = tn(ds, k)
        res.append(d_q if d_qs is None else d_qs[pair] + d_q)
    return res


def back_common(info, slopes):
    low = low_lanes(BLOCK)
    _, spot = split_id((1, 2 * BLOCK), 1)
    slope = head_slopes(slopes, (1, 2 * BLOCK), 1)
    zl = info[4]
    own = [chunk_place((WIDE, 1), 0, zl, n) for n in range(2)]
    oth = [chunk_place((WIDE, 1), 0, 1 - zl, n) for n in range(2)]
    return zl, low, spot, slope, own, oth


def fold(d_q, low):
    return jnp.where(low, d_q[:BLOCK], d_q[BLOCK:]) * 0.125


def back_sweep(info, slopes, y, q, heads, d_heads, lse, sides, kvc, dkc, finish):
    zl, low, spot, slope, own, oth = back_common(info, slopes)
    place_sets = {"own": own, "oth": oth}

    @pl.when(y == 0)
    def _():
        def prompt_block(j, _):
            for n in range(2):
                i = 2 * n + j
                args = back_load(heads, d_heads, lse, q, i, i, low)
                base = block_at(zl, n, j) * BLOCK
                d_qs = None
                for side, kv, d_kv in sides:
                    for m in range(n + 1):
                        rows = pl.ds(m * WIDE, WIDE)
                        d_qs = back_chunk(
                            args, kv, d_kv, rows, rows, place_sets[side][m], base, slope, spot,
                            m == n, False, d_qs,
                        )
                finish(d_qs, i, low)
            return 0

        lax.fori_loop(0, 2, prompt_block, 0)

    @pl.when(y == 1)
    def _():
        def cont_block(j, _):
            args = back_load(heads, d_heads, lse, q, 4 + j, j, low)
            d_qs = None
            if kvc is not None:
                mine = rows_at(j, BLOCK)
                own_place = lax.broadcasted_iota(jnp.int32, (BLOCK, 1), 0)
                d_qs = back_chunk(
                    args, kvc, dkc, mine, mine, own_place, 0, slope, spot, True, True, d_qs
                )
            for side, kv, d_kv in sides:
                for m in range(2):
                    rows = pl.ds(m * WIDE, WIDE)
                    d_qs = back_chunk(
                        args, kv, d_kv, rows, rows, place_sets[side][m], PROMPT, slope, spot,
                        False, False, d_qs,
                    )
            finish(d_qs, j, low)
            return 0

        lax.fori_loop(0, 4, cont_block, 0)


def attend_back_a_body(
    info, slopes, q, kvp, kvo, kvc, heads, d_heads, lse, dq, dkp, dko, dkc
):
    dkp[...] = jnp.zeros_like(dkp)
    dko[...] = jnp.zeros_like(dko)
    dkc[...] = jnp.zeros_like(dkc)

    def finish(d_qs, j, low):
        for pair in range(2):
            dq[rows_at(j, BLOCK), cols(pair, 128)] = bf(fold(d_qs[pair], low))

    back_sweep(
        info, slopes, info[1], q, heads, d_heads, lse,
        (("own", kvp, dkp), ("oth", kvo, dko)), kvc, dkc, finish,
    )


def attend_back_b_body(
    info, slopes, q, kvo, heads, d_heads, lse, dko_in, early, dq, dko, acc
):
    acc[...] = dko_in[...]

    def finish(d_qs, j, low):
        for pair in range(2):
            dq[rows_at(j, BLOCK), cols(pair, 128)] = fold(d_qs[pair], low)

    back_sweep(
        info, slopes, 1 - info[1], q, heads, d_heads, lse,
        (("oth", kvo, acc),), None, None, finish,
    )
    dko[0:512, :] = bf(acc[...])
    dko[512:592, :] = early[:, 0:512]
    dko[592:672, :] = early[:, 512:1024]


def early_sum_body(own, other, dst):
    dst[:, 0:512] = bf(f32(own[:, 0:512]) + f32(other[512:592, :]))
    dst[:, 512:1024] = bf(f32(own[:, 512:1024]) + f32(other[592:672, :]))


def attend_back_c_body(
    info, slopes, q, kvp, kvc, heads, d_heads, lse, dkp_in, dkc_in, dq_in, dq, dkp, dkc
):
    dkp[...] = dkp_in[...]
    dkc[...] = dkc_in[...]

    def finish(d_qs, j, low):
        for pair in range(2):
            lane = cols(pair, 128)
            rows = rows_at(j, BLOCK)
            dq[rows, lane] = bf(dq_in[rows, lane] + fold(d_qs[pair], low))

    back_sweep(
        info, slopes, 1 - info[1], q, heads, d_heads, lse,
        (("own", kvp, dkp),), kvc, dkc, finish,
    )


def qkv_back_body(
    info, dq0, dq1, dkp, dkr, dkc, x0, x1, x2, x3, ws, p0, p1, p2, p3, expand, pr, pe,
    o0, o1, o2, o3, grads,
):
    ps = (p0, p1, p2, p3)
    low = low_lanes(TOK)
    sr = se = 0.0
    for b, (x, dst) in enumerate(zip((x0, x1, x2, x3), (o0, o1, o2, o3))):
        y, c = slab_rows(info, b)
        half = rows_at(c, TOK)
        groups = []
        dq = dq0 if b < 2 else dq1
        for pair in range(2):
            vq = f32(dq[half, cols(pair, 128)])
            got = []
            for lane in (cols(pair, 128), cols(2 + pair, 128)):
                prompt = dkp[half, lane] + f32(dkr[half, lane])
                got.append(jnp.where(y == 0, prompt, f32(dkc[half, lane])))
            vk = pltpu.roll(got[0], 64, 1)
            vv = got[1]
            groups += [jnp.where(low, vq, vk), jnp.where(low, vv, vq), jnp.where(low, vk, vv)]
        d = bf(jnp.concatenate(groups, axis=1))
        u = bf(sum(nt(x[:, cols(k)], ps[k][272:288, :]) for k in range(4)))
        du = bf(SCALE * nt(d, expand[...]))
        for k in range(4):
            dst[:, cols(k)] = bf(nt(d, ws[k]) + nn(du, ps[k][272:288, :]))
        sr = sr + tn(du, x[...])
        se = se + SCALE * tn(u, d)
    for k in range(4):
        grads[0:16, rel_cols(info, k)] = bf(sr[:, k * TOK : k * TOK + TOK])
        grads[16:32, rel_cols(info, k)] = bf(pe[:, cols(k)])
    grads[32:48, 0:768] = bf(se)
    grads[32:48, 768:1024] = bf(pr[...])


def add_body(a, b, dst):
    dst[...] = bf(f32(a[...]) + f32(b[...]))


def add(a, b):
    return call(add_body, [out(a.shape, BF)], [a, b], smem=0, us=0.01, name="add")[0]


def add32_body(a, b, dst):
    dst[...] = f32(a[...]) + f32(b[...])


def add32(a, b, us=8):
    return call(add32_body, [out(a.shape, F32)], [a, b], smem=0, us=us, name="add32")[0]


def stage_body(*refs):
    n = len(refs) // 2
    for src, dst in zip(refs[:n], refs[n:]):
        dst[...] = src[...]


def stage(values):
    return call(
        stage_body, [out(v.shape, v.dtype) for v in values], far(values), smem=0, us=0.01, name="stage"
    )


def stage_weight_body(size, info, own, wr, ws, w, sem):
    copies = [pltpu.make_async_copy(own, w.at[info[0]], sem.at[6])]
    for n, (src, at) in enumerate(((wr, info[8]), (ws, 1 - info[8]))):
        for k in range(1, ROWS):
            to = w.at[rel(info, k), rows_at(at, size)]
            copies.append(pltpu.make_async_copy(src.at[k - 1], to, sem.at[3 * n + k - 1]))
    for copy in copies:
        copy.start()
    for copy in copies:
        copy.wait()


def merge_body(info, v0, v1, v2, v3, dst):
    four = (v0, v1, v2, v3)

    def fill(c):
        total = sum(f32(v[256 + 16 * c : 272 + 16 * c, :]) for v in four)
        dst[0:16, :] = bf(total)
        for b, v in enumerate(four):
            rows = pl.ds(pl.multiple_of(16 + 16 * jnp.bitwise_xor(info[6], b), 16), 16)
            dst[rows, :] = v[288 + 16 * c : 304 + 16 * c, :]

    @pl.when(info[2] == 0)
    def _():
        fill(0)

    @pl.when(info[2] == 1)
    def _():
        fill(1)


def pile_body(*refs):
    dst = refs[-1]
    for n, src in enumerate(refs[:-1]):
        dst[n] = src[...]


def expand_early_body(info, own, oth, r1, e2, e1, r2):
    for v in (r1, e2, e1, r2):
        v[...] = jnp.zeros_like(v)

    def fill(src, shared, split):
        for n in range(own.shape[0]):
            group = info[5] if n % 2 == 0 else 1 - info[5]
            a = info[40 + n // 2 * GROUPS_DEV + group]
            shared[a] += f32(src[n, 0:16, :])
            for j in range(COLS):
                at = 16 + 16 * j
                split[a, :, cols(j, 1024)] += f32(src[n, at : at + 16, :])

    @pl.when(info[2] == 0)
    def _():
        fill(own, r1, e1)
        fill(oth, e2, r2)

    @pl.when(info[2] == 1)
    def _():
        fill(oth, r1, e1)
        fill(own, e2, r2)


def expand_late_body(info, v0, v1, v2, v3, qr, pe, qe, pr):
    four = (v0, v1, v2, v3)
    for v in (qr, pe, qe, pr):
        v[...] = jnp.zeros_like(v)
    for k in range(v0.shape[0]):
        group = info[5] if k % 2 == 0 else 1 - info[5]
        a = info[40 + k // 2 * GROUPS_DEV + group]
        qr[a] += sum(f32(v[k, 0:16, :]) for v in four)
        pe[a] += sum(f32(v[k, 16:32, :]) for v in four)
        for b, v in enumerate(four):
            j = jnp.bitwise_xor(info[6], b)
            qe[a, :, lanes_at(j * 768, 768)] += f32(v[k, 32:48, :768])
            pr[a, :, lanes_at(j * 256, 256)] += f32(v[k, 32:48, 768:])


def shift(v, k, axis="row"):
    if k == 0:
        return v
    size = lax.axis_size(axis)
    return lax.ppermute(v, axis, [(s, (s + k) % size) for s in range(size)])


def gather_row(v):
    return [v] + [shift(v, k) for k in range(1, ROWS)]


def gather_col(v):
    core = lax.ppermute(v, "col", CORE_SWAP)
    side = lax.ppermute(v, "col", Y_SWAP)
    return [v, core, side, lax.ppermute(side, "col", CORE_SWAP)]


def to_cols(pieces):
    return [pieces[0]] + [shift(pieces[k], ROWS - k) for k in range(1, ROWS)]


def spread(mine, other):
    return [mine, other] + [
        shift(v, k, "dp") for k in range(1, lax.axis_size("dp")) for v in (mine, other)
    ]


def pile(parts):
    shape = (len(parts), *parts[0].shape)
    return call(pile_body, [out(shape, BF)], parts, smem=0, us=0.01, name="pile")[0]

def body(
    hidden_in,
    out_grad,
    first_norm_gain,
    first_norm_bias,
    qkv_weight,
    qkv_bias,
    proj_weight,
    proj_bias,
    second_norm_gain,
    second_norm_bias,
    fc1_weight,
    fc1_bias,
    fc2_weight,
    second_feed_bias,
    qkv_reduce,
    qkv_expand,
    proj_reduce,
    proj_expand,
    fc1_reduce,
    fc1_expand,
    fc2_reduce,
    fc2_expand,
    adapter_choice,
    cont_prompt,
):
    r = lax.axis_index("row")
    col = lax.axis_index("col")
    dp = lax.axis_index("dp")
    y = col // 2
    c = lax.rem(col, 2)
    zl = lax.rem(r, 2)
    group = r // 2
    half = lax.rem(dp, 2)
    dp_swap = [(k, k ^ 1) for k in range(lax.axis_size("dp"))]
    slopes = jnp.exp2(
        -8.0 * (col * 4 + 1 + jnp.arange(4, dtype=jnp.int32)).astype(F32) / HEADS
    )
    adapter = jnp.where(group == 0, adapter_choice[0], adapter_choice[1])
    n_dp = jnp.int32(lax.axis_size("dp"))
    info = jnp.stack([r, y, c, dp * GROUPS_DEV, zl, group, col, dp, half] + [half, n_dp] + [half] * 5)
    info = jnp.concatenate([info.astype(jnp.int32), cont_prompt, adapter_choice])
    order = pltpu.SMEM((GROUPS_DEV * NCONT,), jnp.int32)
    flip = functools.partial(jnp.transpose, axes=(0, 2, 1))
    big = out((TOK, D), BF)
    small = out((RANK, D), F32)

    other = lax.ppermute(hidden_in, "col", CORE_SWAP)
    vectors = [
        first_norm_gain, first_norm_bias, proj_bias,
        second_norm_gain, second_norm_bias, second_feed_bias,
    ]
    factors = [flip(qkv_reduce), flip(fc1_reduce), proj_expand, fc2_expand]
    pieces = call(
        route_pack_body,
        [out((336, TOK), BF)] * 4,
        [info, Far(hidden_in), Far(other), *far(vectors), *far(factors)],
        [
            order,
            *[pltpu.VMEM((TOK,), BF)] * 6,
            pltpu.VMEM((16, RANK, TOK), BF),
            pltpu.SemaphoreType.DMA((22,)),
        ],
        raw=range(3, 13),
        us=1.5,
        name="route_x",
    )
    xs = [pieces[0]] + [shift(pieces[k], k) for k in range(1, ROWS)]
    packs = far(xs)
    first_half, w1_copies, qkv_e, fc1_e, proj_r, fc2_r = call(
        prepare_body,
        [
            out((128, D), BF), out((ROWS, 128, D), BF),
            out((RANK, 768), BF), out((RANK, D), BF), out((RANK, TOK), BF), out((RANK, D), BF),
        ],
        [
            after(info, pieces[0]),
            *far([qkv_weight, proj_weight, fc1_weight, qkv_expand, fc1_expand]),
            *far([flip(proj_reduce), flip(fc2_reduce)]),
        ],
        [pltpu.SemaphoreType.DMA((10,))],
        raw=range(1, 8),
        us=3,
        name="prepare",
    )
    first_half = after(first_half, xs[1])
    z_parts = [shift(first_half, k) for k in range(1, ROWS)]
    s_parts = [lax.ppermute(v, "dp", dp_swap) for v in z_parts]
    wq, wp = call(
        assemble_body,
        [out((ROWS, TOK, 768), BF), out((ROWS, TOK, TOK), BF)],
        [info, *far([qkv_weight, proj_weight, *z_parts, *s_parts])],
        [pltpu.SemaphoreType.DMA((14,))],
        raw=range(1, 9),
        us=15,
        name="assemble",
    )

    qkv_b = lax.dynamic_slice_in_dim(qkv_bias, col * 768, 768, 0)[None, :]
    fc1_b = lax.dynamic_slice_in_dim(fc1_bias, col * 1024, 1024, 0)[None, :]

    choices = [adapter_choice] + [
        shift(adapter_choice, k, "dp") for k in range(1, lax.axis_size("dp"))
    ]
    first = after(xs[0], qkv_b, fc1_b, w1_copies, *choices)
    (xn1,) = call(norm1_body, [big], [first, *xs[1:]], smem=0, us=8, name="norm1")
    xn1s = gather_col(xn1)
    q, kvp, kvc = call(
        qkv_body,
        [out((1024, 256), BF), out((512, 512), BF), out((512, 512), BF)],
        [info, *xn1s, wq, *packs, Far(qkv_b), Far(qkv_e)],
        us=6.5,
        name="qkv",
    )
    kvo = lax.ppermute(kvp, "row", Z_SWAP)

    g_other = lax.ppermute(after(out_grad, kvp), "col", CORE_SWAP)
    (pieces,) = call(
        route_all_body,
        [out((ROWS, 3 * TOK, TOK), BF)],
        [info, Far(out_grad), Far(g_other), Far(fc2_weight)],
        [order, pltpu.SemaphoreType.DMA((4,))],
        raw=(3,),
        us=1,
        name="route_g",
    )
    (state,) = call(
        attend_first_body,
        [out((2048, 256), F32)],
        [info, slopes, q, kvp, kvc],
        smem=2,
        us=9,
        name="attend_first",
    )
    (w1r,) = call(
        rest_body,
        [out((3, 128, D), BF)],
        [info, after(lax.all_to_all(after(w1_copies, *z_parts), "row", 0, 0), state)],
        us=0.01,
        name="rest",
    )
    w1s = lax.ppermute(w1r, "dp", dp_swap)
    pieces = after(pieces, state, kvo)
    g_own, w2r = call(
        join_body,
        [big, out((3, 512, TOK), BF)],
        [info, lax.all_to_all(pieces, "row", 0, 0)],
        us=0.01,
        name="join",
    )
    g_side = lax.ppermute(g_own, "col", Y_SWAP)
    w2s = lax.ppermute(w2r, "dp", dp_swap)

    def attend_rest(which, q, state):
        return call(
            functools.partial(attend_rest_body, which),
            [out((512, 256), BF), out((8, 256), F32), big, big],
            [info, slopes, Far(q), kvo, state, Far(wp), Far(proj_r), *packs],
            smem=2,
            us=20 if which else 0.01,
            name="attend_rest",
        )

    heads1, lse1, p2, p3 = attend_rest(1, q, after(state, w1r))
    g_core = lax.ppermute(g_own, "col", CORE_SWAP)
    g_all = [g_own, g_core, g_side, lax.ppermute(g_side, "col", CORE_SWAP)]
    p_far = lax.ppermute(p3, "col", CORE_SWAP)
    p_side = add(p2, p_far)
    heads0, lse0, p0, p1 = attend_rest(0, q, Far(after(state, p_side)))
    p_side = lax.ppermute(p_side, "col", Y_SWAP)
    p_core = lax.ppermute(p1, "col", CORE_SWAP)
    staged = stage([after(xs[0], p0), *xs[1:]])
    mid, xn2 = call(
        norm2_body,
        [out((TOK, D), F32), big],
        [add32(after(p0, w1s), p_side), p_core, *staged],
        smem=0,
        us=1.5,
        name="norm2",
    )
    (w1,) = call(
        functools.partial(stage_weight_body, 128),
        [out((ROWS, TOK, D), BF)],
        [info, Far(fc1_weight), Far(after(w1r, p0)), Far(w1s)],
        [pltpu.SemaphoreType.DMA((7,))],
        raw=(1, 2, 3),
        us=2,
        name="stage_w1",
    )
    zero = jnp.zeros((RANK, D), F32)
    xn2_core = lax.ppermute(xn2, "col", CORE_SWAP)
    xn2_side = lax.ppermute(xn2, "col", Y_SWAP)

    def mlp_pre(first, blocks):
        return call(
            mlp_pre_body,
            [out((2, TOK, D), BF)] * 2,
            [info, *blocks, w1, *staged, Far(fc1_b), Far(fc1_e)],
            us=5,
            name="mlp_pre",
        )

    act0, slope0 = mlp_pre(0, [xn2, xn2_core])
    xn2_far = lax.ppermute(after(xn2_side, act0), "col", CORE_SWAP)
    xn2s = [xn2, xn2_core, xn2_side, xn2_far]
    act1, slope1 = mlp_pre(1, xn2s[2:])
    (w2,) = call(
        functools.partial(stage_weight_body, 512),
        [out((ROWS, D, TOK), BF)],
        [info, Far(fc2_weight), Far(after(w2r, act0)), Far(w2s)],
        [pltpu.SemaphoreType.DMA((7,))],
        raw=(1, 2, 3),
        us=2,
        name="stage_w2",
    )

    def mlp_back(blocks, slope, r_in, e_in):
        xa, xb = (xn2s[b] for b in blocks)
        ga, gb = (g_all[b] for b in blocks)
        return call(
            mlp_back_body,
            [big, big, small, small],
            [info, xa, xb, ga, gb, slope, w1, w2, *staged, Far(fc1_e), Far(fc2_r), r_in, e_in],
            us=0.01,
            name="mlp_back",
        )

    d2, d3, r1, e1 = mlp_back((2, 3), slope1, zero, zero)
    d_far = lax.ppermute(d3, "col", CORE_SWAP)
    d_side = add(d2, d_far)
    d0, d1, r1, e1 = mlp_back((0, 1), slope0, after(r1, d_side), e1)
    d_side = lax.ppermute(d_side, "col", Y_SWAP)
    d_core = lax.ppermute(d1, "col", CORE_SWAP)
    res = call(
        fc2_body,
        [big] * 4 + [out((64, D), BF)],
        [info, act0, act1, *g_all, w2, Far(fc2_r), *staged, r1, e1],
        us=0.01,
        name="fc2",
    )
    m_parts, mlp_pack = res[:4], res[4]
    staged_back = stage([after(mid, mlp_pack), g_own, *xs])
    d_mid, g_attn = call(
        norm2_back_body,
        [out((TOK, D), F32), out((320, D), BF)],
        [add32(d0, d_side), d_core, mlp_pack, *staged_back],
        smem=0,
        us=1.5,
        name="norm2_back",
    )
    ga_core = lax.ppermute(g_attn, "col", CORE_SWAP)
    ga_side = lax.ppermute(g_attn, "col", Y_SWAP)
    shared = far([q, kvp, kvo, kvc])

    def d_heads(blocks, heads, r_in, e_in):
        return call(
            d_heads_body,
            [out((512, 256), BF), out((RANK, TOK), F32), small],
            [info, *blocks, Far(wp), *packs, Far(proj_r), Far(heads), r_in, e_in],
            us=1.5,
            name="d_heads",
        )

    dh0, pr, pe = d_heads([g_attn, ga_core], heads0, jnp.zeros((RANK, TOK), F32), zero)
    dq0, dkp, dko, dkc = call(
        attend_back_a_body,
        [out((512, 256), BF), out((512, 512), F32), out((512, 512), F32), out((512, 512), BF)],
        [info, slopes, *shared, Far(heads0), dh0, Far(lse0)],
        smem=2,
        us=16,
        weight=W_BIG,
        name="attend_back_a",
    )
    ga_side = after(ga_side, dq0)
    ga_far = lax.ppermute(ga_side, "col", CORE_SWAP)
    (early_half,) = call(
        merge_body,
        [out((80, D), BF)],
        [info, g_attn, ga_core, ga_side, ga_far],
        us=0.7,
        name="merge",
    )
    dh1, pr, pe = d_heads([ga_side, ga_far], heads1, pr, pe)
    dq1_part, dko = call(
        attend_back_b_body,
        [out((512, 256), F32), out((672, 512), BF)],
        [info, slopes, Far(q), Far(kvo), Far(heads1), dh1, Far(lse1), Far(dko), early_half],
        [pltpu.VMEM((512, 512), F32)],
        smem=2,
        us=8,
        name="attend_back_b",
    )
    dkr = lax.ppermute(dko, "row", Z_SWAP)
    dq1, dkp, dkc = call(
        attend_back_c_body,
        [out((512, 256), BF), out((512, 512), F32), out((512, 512), BF)],
        [info, slopes, Far(q), Far(kvp), Far(kvc), Far(heads1), dh1, Far(lse1), *far([dkp, dkc, dq1_part])],
        smem=2,
        us=8,
        name="attend_back_c",
    )
    (early_sum,) = call(
        early_sum_body, [out((80, D), BF)], [early_half, dkr], smem=0, us=0.01, name="early_sum"
    )
    m_far = lax.ppermute(after(m_parts[3], dq0), "col", CORE_SWAP)
    m_core = lax.ppermute(after(m_parts[1], dq0), "col", CORE_SWAP)
    m_sum = add(after(m_parts[2], dko), m_far)
    m_side = lax.ppermute(m_sum, "col", Y_SWAP)
    res = call(
        qkv_back_body,
        [big] * 4 + [out((48, D), BF)],
        [
            info, dq0, dq1, dkp, after(dkr, early_sum), Far(dkc),
            *far(xn1s), Far(wq), *packs, Far(qkv_e), pr, pe,
        ],
        us=20,
        name="qkv_back",
    )
    q_parts, late_pack = res[:4], res[4]
    early_parts = spread(early_sum, shift(early_sum, 2))
    ready = after(q_parts[3], m_side, *early_parts[1:3])
    q_sum = add(q_parts[2], lax.ppermute(ready, "col", CORE_SWAP))
    hidden = call(
        hidden_body,
        [out((TOK, TOK), BF)] * 4,
        [add32(m_parts[0], after(m_side, q_sum), 0.01), m_core, Far(mid), *packs],
        smem=0,
        us=0.01,
        name="hidden",
    )
    hidden_got = to_cols(hidden)
    k0, rc = q_parts[0], lax.ppermute(q_parts[1], "col", CORE_SWAP)
    ry = lax.ppermute(q_sum, "col", Y_SWAP)
    late_sum = add(late_pack, lax.ppermute(after(late_pack, q_sum), "row", Z_SWAP))
    late_next = shift(late_sum, 2)
    late_four = pile(spread(late_sum, late_next))
    late_all = gather_col(late_four)
    staged_last = stage([after(d_mid, k0), *xs])
    ins = call(
        norm1_back_body,
        [out((TOK, TOK), BF)] * 4,
        [add32(after(k0, late_next, *hidden_got), ry), rc, *staged_last],
        smem=0,
        us=1,
        name="norm1_back",
    )
    early_all = pile(early_parts)
    early_far = lax.ppermute(after(early_all, ins[0]), "col", CORE_SWAP)
    table = jnp.concatenate([info, jnp.zeros((40 - 34,), jnp.int32), *choices])
    o_fc1r, o_f2e, o_f1e, o_f2r = call(
        expand_early_body,
        [out((COUNT, RANK, w), F32) for w in (1024, 1024, 4096, 4096)],
        [table, Far(early_all), Far(early_far)],
        us=0.01,
        name="expand_early",
    )
    (joined,) = call(
        stack_body,
        [out((8 * TOK, TOK), BF)],
        [*[after(v, o_fc1r, late_all[2]) for v in to_cols(ins)], *hidden_got],
        smem=0,
        us=0.01,
        name="stack",
    )
    input_gradient, hidden_out = call(
        unroute_body,
        [out((1024, TOK), F32), out((1024, TOK), BF)],
        [info, joined, lax.ppermute(joined, "col", CORE_SWAP)],
        [order],
        us=2,
        name="unroute",
    )
    o_qr, o_pe, o_qe, o_pr = call(
        expand_late_body,
        [out((COUNT, RANK, w), F32) for w in (1024, 1024, 3072, 1024)],
        [table, *late_all],
        us=0.01,
        name="expand_late",
    )
    return (
        hidden_out,
        input_gradient,
        flip(o_qr),
        o_qe,
        flip(o_pr),
        o_pe,
        flip(o_fc1r),
        o_f1e,
        flip(o_f2r),
        o_f2e,
    )


def solution(mesh):
    placed = (
        P(("dp", "col"), "row"),
        P(("dp", "col"), "row"),
        P("row"),
        P("row"),
        P("row", "col"),
        P(),
        P("col", "row"),
        P("row"),
        P("row"),
        P("row"),
        P("row", "col"),
        P(),
        P("col", "row"),
        P("row"),
        P(None, "row", None),
        P(),
        P(None, "col", None),
        P(None, None, "row"),
        P(None, "row", None),
        P(),
        P(None, "col", None),
        P(None, None, "row"),
        P("dp"),
        P("dp"),
    )
    return jax.shard_map(
        body,
        mesh=mesh,
        in_specs=placed,
        out_specs=(P(("dp", "col"), "row"), P(("dp", "col"), "row")) + (P(),) * 8,
        check_vma=False,
    )
```

```python
import functools

import jax
import jax.numpy as jnp
from jax import lax
from jax.experimental import pallas as pl
from jax.experimental.pallas import tpu as pltpu
from jax.sharding import PartitionSpec as P

D = 1024
HEADS = 16
HEAD = 64
FF = 4096
RANK = 16
COUNT = 8
PROMPT = 1024
CONT = 128
NCONT = 8
GROUPS_DEV = 2

EPSILON = 1e-05
SCALE = 2.0
GELU_A = 0.7978845608028654
GELU_B = 0.044715
ROWS = 4
COLS = 4
TOK = 256
BLOCK = 128
LOW = -1e30
W_SMALL = 5e8
W_BIG = 5e8

BF = jnp.bfloat16
F32 = jnp.float32

VM = pl.BlockSpec(memory_space=pltpu.VMEM)
SM = pl.BlockSpec(memory_space=pltpu.SMEM)
HB = pl.BlockSpec(memory_space=pltpu.HBM)

CORE_SWAP = [(0, 1), (1, 0), (2, 3), (3, 2)]
Y_SWAP = [(0, 2), (2, 0), (1, 3), (3, 1)]
Z_SWAP = [(0, 1), (1, 0), (2, 3), (3, 2)]


def nn(a, b):
    return lax.dot_general(a, b, (((1,), (0,)), ((), ())), preferred_element_type=F32)


def nt(a, b):
    return lax.dot_general(a, b, (((1,), (1,)), ((), ())), preferred_element_type=F32)


def tn(a, b):
    return lax.dot_general(a, b, (((0,), (0,)), ((), ())), preferred_element_type=F32)


def f32(v):
    return v.astype(F32)


def bf(v):
    return v.astype(BF)


class Far:
    def __init__(self, value):
        self.value = value


def far(values):
    return [Far(v) for v in values]


def call(
    body, outs, ins, scratch=(), smem=1, limit=40, us=1, raw=(), weight=W_SMALL, hbm=(), name=None
):
    values = [
        pltpu.with_memory_space_constraint(v.value, pltpu.HBM) if isinstance(v, Far) else v
        for v in ins
    ]
    fetched = [i for i, v in enumerate(ins) if isinstance(v, Far) and i not in raw]
    specs = [SM] * smem
    for v in ins[smem:]:
        specs.append(HB if isinstance(v, Far) else VM)
    nbytes = sum(v.size * v.dtype.itemsize for v in values)
    nbytes += sum(o.size * o.dtype.itemsize for o in outs)
    extra = [pltpu.VMEM(values[i].shape, values[i].dtype) for i in fetched]
    extra += [pltpu.VMEM(outs[i].shape, outs[i].dtype) for i in hbm]
    moved = len(extra)
    if moved:
        extra.append(pltpu.SemaphoreType.DMA((moved,)))

    def whole(*refs):
        refs = list(refs)
        stores = []
        if moved:
            sem = refs[-1]
            buffers = refs[-1 - moved : -1]
            refs = refs[: -1 - moved]
            copies = []
            for n, i in enumerate(fetched):
                copies.append(pltpu.make_async_copy(refs[i], buffers[n], sem.at[n]))
                copies[-1].start()
                refs[i] = buffers[n]
            for n, i in enumerate(hbm, len(fetched)):
                at = len(values) + i
                stores.append(pltpu.make_async_copy(buffers[n], refs[at], sem.at[n]))
                refs[at] = buffers[n]
            for copy in copies:
                copy.wait()
        body(*refs)
        for copy in stores:
            copy.start()
        for copy in stores:
            copy.wait()

    return pl.pallas_call(
        whole,
        out_shape=tuple(
            pltpu.HBM(o.shape, o.dtype) if i in hbm else o for i, o in enumerate(outs)
        ),
        in_specs=specs,
        out_specs=tuple(HB if i in hbm else VM for i in range(len(outs))),
        scratch_shapes=list(scratch) + extra,
        compiler_params=pltpu.CompilerParams(vmem_limit_bytes=limit << 20),
        cost_estimate=pl.CostEstimate(
            flops=int(us * weight), bytes_accessed=nbytes // 8, transcendentals=0
        ),
        name=name,
    )(*values)


def after(value, *others):
    res = lax.optimization_barrier((value, others))
    return res[0]


def out(shape, dtype):
    return jax.ShapeDtypeStruct(shape, dtype)


def block_at(zl, c, j):
    return c * 4 + zl + j * (3 - 2 * zl)


def fill_order(info, order):
    base = info[3]
    first = jnp.int32(0)
    second = jnp.int32(NCONT)
    for j in range(GROUPS_DEV * NCONT):
        own = info[16 + j] == base
        slot = jnp.where(own, first, second)
        order[slot] = jnp.int32(j)
        first = first + jnp.where(own, 1, 0)
        second = second + jnp.where(own, 0, 1)


def place_of(info, order, z, core, j):
    prompt = (z // 2) * 8 + block_at(lax.rem(z, 2), core, j)
    cont = order[4 * z + 2 * core + j]
    return jnp.where(info[1] == 0, prompt, cont)


def route_body(info, own, oth, o0, o1, o2, o3, order):
    fill_order(info, order)
    c = info[2]
    for s, dst in enumerate((o0, o1, o2, o3)):
        z = lax.rem(info[0] + s, ROWS)
        for j in range(2):
            src = place_of(info, order, z, c, j)
            at = pl.ds(pl.multiple_of(lax.rem(src, 8) * BLOCK, BLOCK), BLOCK)
            mine = src // 8 == c

            @pl.when(mine)
            def _():
                dst[pl.ds(j * BLOCK, BLOCK), :] = own[at, :]

            @pl.when(jnp.logical_not(mine))
            def _():
                dst[pl.ds(j * BLOCK, BLOCK), :] = oth[at, :]


def route_pack_body(
    info, own, oth, g1, c1, pb, g2, c2, fb, qr, fr, pe, fe,
    o0, o1, o2, o3, order, v0, v1, v2, v3, v4, v5, mats, sem,
):
    vecs = (v0, v1, v2, v3, v4, v5)
    pairs = list(zip((g1, c1, pb, g2, c2, fb), vecs))
    for k in range(ROWS):
        which = lax.rem(info[0] + k, ROWS) // 2
        a = jnp.where(which == 0, info[32], info[33])
        pairs += [(v.at[a], mats.at[4 * k + i]) for i, v in enumerate((qr, fr, pe, fe))]
    copies = [pltpu.make_async_copy(a, b, sem.at[i]) for i, (a, b) in enumerate(pairs)]
    for copy in copies:
        copy.start()
    route_body(info, own, oth, o0, o1, o2, o3, order)
    for copy in copies:
        copy.wait()
    for k, dst in enumerate((o0, o1, o2, o3)):
        head = [f32(v[...]).reshape(1, TOK) for v in vecs]
        dst[256:272, :] = bf(jnp.concatenate(head + [jnp.zeros((10, TOK), F32)], axis=0))
        for i in range(4):
            dst[272 + 16 * i : 288 + 16 * i, :] = mats[4 * k + i]


def stack_body(a0, a1, a2, a3, h0, h1, h2, h3, dst):
    for k, (a, h) in enumerate(((a0, h0), (a1, h1), (a2, h2), (a3, h3))):
        dst[2 * k * TOK : (2 * k + 1) * TOK, :] = a[...]
        dst[(2 * k + 1) * TOK : (2 * k + 2) * TOK, :] = h[...]


def route_all_body(info, own, oth, w2, dst, order, sem):
    copies = []
    for z in range(ROWS):
        to = dst.at[z, pl.ds(TOK, 512)]
        copies.append(pltpu.make_async_copy(w2.at[rows_at(info[8], 512)], to, sem.at[z]))
    for copy in copies:
        copy.start()
    fill_order(info, order)
    c = info[2]
    for z in range(ROWS):
        for j in range(2):
            src = place_of(info, order, z, c, j)
            at = pl.ds(pl.multiple_of(lax.rem(src, 8) * BLOCK, BLOCK), BLOCK)
            mine = src // 8 == c

            @pl.when(mine)
            def _():
                dst[z, pl.ds(j * BLOCK, BLOCK), :] = own[at, :]

            @pl.when(jnp.logical_not(mine))
            def _():
                dst[z, pl.ds(j * BLOCK, BLOCK), :] = oth[at, :]
    for copy in copies:
        copy.wait()


def unroute_body(info, a, b, grad, hidden, order):
    fill_order(info, order)
    c = info[2]
    for s in range(ROWS):
        z = lax.rem(info[0] + s, ROWS)
        for other, src in ((0, a), (1, b)):
            core = c if other == 0 else 1 - c
            for j in range(2):
                at = place_of(info, order, z, core, j)

                @pl.when(at // 8 == c)
                def _():
                    rows = pl.ds(pl.multiple_of(lax.rem(at, 8) * BLOCK, BLOCK), BLOCK)
                    start = 2 * s * TOK + j * BLOCK
                    grad[rows, :] = f32(src[pl.ds(start, BLOCK), :])
                    hidden[rows, :] = src[pl.ds(start + TOK, BLOCK), :]


def cols(k, width=TOK):
    return pl.ds(k * width, width)


def row_stats(parts):
    total = sum(jnp.sum(v, axis=1, keepdims=True) for v in parts)
    mean = total * (1.0 / D)
    dev = [v - mean for v in parts]
    var = sum(jnp.sum(v * v, axis=1, keepdims=True) for v in dev) * (1.0 / D)
    rstd = lax.rsqrt(var + EPSILON)
    return [v * rstd for v in dev], rstd


def norm1_body(x0, x1, x2, x3, xn):
    for t in range(2):
        rows = pl.ds(t * 128, 128)
        hat, _ = row_stats([f32(v[rows, :]) for v in (x0, x1, x2, x3)])
        for k, pack in enumerate((x0, x1, x2, x3)):
            xn[rows, cols(k)] = bf(hat[k] * f32(pack[256:257, :]) + f32(pack[257:258, :]))


def both(a, b, rows, k):
    return f32(a[rows, cols(k)]) + f32(b[rows, cols(k)])


def norm2_body(a, b, x0, x1, x2, x3, mid, xn):
    for t in range(2):
        rows = pl.ds(t * 128, 128)
        parts = []
        for k, x in enumerate((x0, x1, x2, x3)):
            v = f32(x[rows, :]) + both(a, b, rows, k) + f32(x[258:259, :])
            mid[rows, cols(k)] = v
            parts.append(v)
        hat, _ = row_stats(parts)
        for k, pack in enumerate((x0, x1, x2, x3)):
            xn[rows, cols(k)] = bf(hat[k] * f32(pack[259:260, :]) + f32(pack[260:261, :]))


def norm_back(hat, rstd, grads):
    total = sum(jnp.sum(g, axis=1, keepdims=True) for g in grads) * (1.0 / D)
    along = sum(jnp.sum(g * h, axis=1, keepdims=True) for g, h in zip(grads, hat)) * (1.0 / D)
    return [rstd * (g - total - h * along) for g, h in zip(grads, hat)]


def norm2_back_body(
    a, b, pack, mid, g, x0, x1, x2, x3, d_mid, g_attn
):
    g_attn[256:320, :] = pack[...]
    for t in range(2):
        rows = pl.ds(t * 128, 128)
        hat, rstd = row_stats([mid[rows, cols(k)] for k in range(4)])
        grads = []
        for k, pack in enumerate((x0, x1, x2, x3)):
            grads.append(both(a, b, rows, k) * f32(pack[259:260, :]))
        back = norm_back(hat, rstd, grads)
        for k in range(4):
            v = f32(g[rows, cols(k)]) + back[k]
            d_mid[rows, cols(k)] = v
            g_attn[rows, cols(k)] = bf(v)


def norm1_back_body(a, b, d_mid, x0, x1, x2, x3, i0, i1, i2, i3):
    for t in range(2):
        rows = pl.ds(t * 128, 128)
        hat, rstd = row_stats([f32(v[rows, :]) for v in (x0, x1, x2, x3)])
        grads = []
        for k, pack in enumerate((x0, x1, x2, x3)):
            grads.append(both(a, b, rows, k) * f32(pack[256:257, :]))
        back = norm_back(hat, rstd, grads)
        for k, dst in enumerate((i0, i1, i2, i3)):
            dst[rows, :] = bf(d_mid[rows, cols(k)] + back[k])


def hidden_body(a, b, mid, x0, x1, x2, x3, h0, h1, h2, h3):
    for t in range(2):
        rows = pl.ds(t * 128, 128)
        for k, (pack, dst) in enumerate(zip((x0, x1, x2, x3), (h0, h1, h2, h3))):
            v = mid[rows, cols(k)] + both(a, b, rows, k) + f32(pack[261:262, :])
            dst[rows, :] = bf(v)


def join_body(info, v, dst, w2):
    for k in range(ROWS):
        dst[:, cols(k)] = v[rel(info, k), 0:TOK, :]
    for k in range(1, ROWS):
        w2[k - 1] = v[rel(info, k), TOK:, :]


def rest_body(info, v, dst):
    for k in range(1, ROWS):
        dst[k - 1] = v[rel(info, k)]


def slab_rows(info, b):
    y = jnp.bitwise_xor(info[1], b // 2)
    c = jnp.bitwise_xor(info[2], b % 2)
    return y, c


def low_lanes(rows):
    return lax.broadcasted_iota(jnp.int32, (rows, 128), 1) < HEAD


def rel(info, k):
    return lax.rem(info[0] - k + ROWS, ROWS)


def rel_cols(info, k):
    return pl.ds(pl.multiple_of(rel(info, k) * TOK, TOK), TOK)


def lanes_at(at, size):
    return pl.ds(pl.multiple_of(at, 128), size)


def rows_at(i, size):
    return pl.ds(pl.multiple_of(i * size, size), size)


def prepare_body(
    info, wq, wp, w1, qe, fe, pr, fr, first, c1, o_qe, o_fe, o_pr, o_fr, sem
):
    half = info[8]
    a = jnp.where(info[5] == 0, info[32], info[33])
    rows = rows_at(half, 128)
    pairs = [(wq.at[rows], first.at[:, 0:768]), (wp.at[rows], first.at[:, 768:1024])]
    pairs += [(qe.at[a, :, lanes_at(info[6] * 768, 768)], o_qe)]
    pairs += [(fe.at[a, :, lanes_at(info[6] * 1024, 1024)], o_fe)]
    pairs += [(pr.at[a], o_pr), (fr.at[a], o_fr)]
    for j in range(ROWS):
        pairs += [(w1.at[rows], c1.at[j])]
    copies = [pltpu.make_async_copy(x, y, sem.at[i]) for i, (x, y) in enumerate(pairs)]
    for copy in copies:
        copy.start()
    for copy in copies:
        copy.wait()


def assemble_body(info, own_q, own_p, z1, z2, z3, s1, s2, s3, ws, wp, sem):
    half = info[8]
    copies = [
        pltpu.make_async_copy(own_q, ws.at[0], sem.at[0]),
        pltpu.make_async_copy(own_p, wp.at[0], sem.at[1]),
    ]
    for k, (zv, sv) in enumerate(((z1, s1), (z2, s2), (z3, s3))):
        for n, (v, at) in enumerate(((zv, half), (sv, 1 - half))):
            rows = rows_at(at, 128)
            at = 2 + 4 * k + 2 * n
            copies.append(
                pltpu.make_async_copy(v.at[:, 0:768], ws.at[k + 1, rows], sem.at[at])
            )
            copies.append(
                pltpu.make_async_copy(v.at[:, 768:1024], wp.at[k + 1, rows], sem.at[at + 1])
            )
    for copy in copies:
        copy.start()
    for copy in copies:
        copy.wait()


def qkv_body(
    info, x0, x1, x2, x3, ws, p0, p1, p2, p3, bias, expand, q, kvp, kvc
):
    ps = (p0, p1, p2, p3)
    low = low_lanes(TOK)
    for b, x in enumerate((x0, x1, x2, x3)):
        y, c = slab_rows(info, b)
        acc = sum(nn(x[:, cols(k)], ws[k]) for k in range(4))
        u = bf(sum(nt(x[:, cols(k)], ps[k][272:288, :]) for k in range(4)))
        acc = acc + f32(bias[...]) + SCALE * nn(u, expand[...])
        kv = []
        for pair in range(2):
            at = 384 * pair
            g0, g1, g2 = (acc[:, at + 128 * i : at + 128 * i + 128] for i in range(3))
            q[rows_at(y * 2 + c, TOK), cols(pair, 128)] = bf(
                bf(jnp.where(low, g0, g1)) * BF(0.125)
            )
            kv.append((bf(pltpu.roll(jnp.where(low, g2, g0), 64, 1)), bf(jnp.where(low, g1, g2))))
        rows = rows_at(c, TOK)

        @pl.when(y == 0)
        def _():
            for pair in range(2):
                kvp[rows, cols(pair, 128)] = kv[pair][0]
                kvp[rows, cols(2 + pair, 128)] = kv[pair][1]

        @pl.when(y == 1)
        def _():
            for pair in range(2):
                kvc[rows, cols(pair, 128)] = kv[pair][0]
                kvc[rows, cols(2 + pair, 128)] = kv[pair][1]


WIDE = 256


def stacked(v, low):
    zero = jnp.zeros_like(v)
    return jnp.concatenate([jnp.where(low, v, zero), jnp.where(low, zero, v)], axis=0)


def split_id(shape, axis):
    lane = lax.broadcasted_iota(jnp.int32, shape, axis)
    return lane, jnp.where(lane < BLOCK, lane, lane - BLOCK)


def chunk_place(shape, axis, side, n):
    lane, within = split_id(shape, axis)
    first = block_at(side, n, 0) * BLOCK
    second = block_at(side, n, 1) * BLOCK
    return within + jnp.where(lane < BLOCK, first, second)


def keep_state(state, low):
    top, total, acc = state
    lane = lax.broadcasted_iota(jnp.int32, (2 * BLOCK, 128), 1)
    spot = lax.rem(lane, HEAD)
    row = lax.broadcasted_iota(jnp.int32, (2 * BLOCK, 128), 0)
    own = (lane < HEAD) == (row < BLOCK)
    return jnp.where(own, acc, jnp.where(spot == 0, top, total))


def load_state(v):
    lane = lax.broadcasted_iota(jnp.int32, (2 * BLOCK, 128), 1)
    row = lax.broadcasted_iota(jnp.int32, (2 * BLOCK, 128), 0)
    spot = jnp.where(row < BLOCK, HEAD, 0)
    top = jnp.max(jnp.where(lane == spot, v, LOW), axis=1, keepdims=True)
    total = jnp.sum(jnp.where(lane == spot + 1, v, 0.0), axis=1, keepdims=True)
    return top, total, v


def soft_update(state, s, v):
    if state is None:
        top = jnp.max(s, axis=1, keepdims=True)
        p = jnp.exp(s - top)
        return top, jnp.sum(p, axis=1, keepdims=True), nn(bf(p), v)
    top, total, acc = state
    new = jnp.maximum(top, jnp.max(s, axis=1, keepdims=True))
    p = jnp.exp(s - new)
    shrink = jnp.exp(top - new)
    total = total * shrink + jnp.sum(p, axis=1, keepdims=True)
    return new, total, acc * shrink + nn(bf(p), v)


def head_slopes(slopes, shape, axis):
    lane = lax.broadcasted_iota(jnp.int32, shape, axis)
    return [
        jnp.where(lane < BLOCK, slopes[2 * pair], slopes[2 * pair + 1]) for pair in range(2)
    ]


def attend_chunk(q2, states, kv, rows, place, base, slope, spot, masked):
    res = []
    away = place - base
    for pair in range(2):
        s = nt(q2[pair], kv[rows, cols(pair, 128)]) + slope[pair] * away.astype(F32)
        if masked:
            s = jnp.where(away <= spot, s, LOW)
        res.append(soft_update(states[pair], s, kv[rows, cols(2 + pair, 128)]))
    return res


def attend_first_body(info, slopes, q, kvp, kvc, state):
    zl = info[4]
    low = low_lanes(BLOCK)
    _, spot = split_id((2 * BLOCK, 1), 0)
    slope = head_slopes(slopes, (2 * BLOCK, 1), 0)
    places = [chunk_place((1, WIDE), 1, zl, n) for n in range(2)]

    def load(i):
        return [stacked(q[rows_at(i, BLOCK), cols(pair, 128)], low) for pair in range(2)]

    def save(states, i):
        for pair in range(2):
            state[rows_at(i, WIDE), cols(pair, 128)] = keep_state(states[pair], low)

    def prompt_block(j, _):
        for n in range(2):
            i = 2 * n + j
            base = block_at(zl, n, j) * BLOCK
            q2 = load(i)
            states = [None, None]
            for m in range(n, -1, -1):
                states = attend_chunk(
                    q2, states, kvp, pl.ds(m * WIDE, WIDE), places[m], base, slope, spot, m == n
                )
            save(states, i)
        return 0

    lax.fori_loop(0, 2, prompt_block, 0)

    def cont_block(j, _):
        q2 = load(4 + j)
        own_place = lax.broadcasted_iota(jnp.int32, (1, BLOCK), 1)
        states = attend_chunk(
            q2, [None, None], kvc, rows_at(j, BLOCK), own_place, 0, slope, spot, True
        )
        for m in range(2):
            states = attend_chunk(
                q2, states, kvp, pl.ds(m * WIDE, WIDE), places[m], PROMPT, slope, spot, False
            )
        save(states, 4 + j)
        return 0

    lax.fori_loop(0, 4, cont_block, 0)


def attend_rest_body(
    which, info, slopes, q, kvo, state, ws, reduce, p0, p1, p2, p3, heads, lse, o0, o1
):
    zl = info[4]
    y = info[1] if which == 0 else 1 - info[1]
    low = low_lanes(BLOCK)
    _, spot = split_id((2 * BLOCK, 1), 0)
    slope = head_slopes(slopes, (2 * BLOCK, 1), 0)
    places = [chunk_place((1, WIDE), 1, 1 - zl, n) for n in range(2)]

    def load(i):
        q2 = [stacked(q[rows_at(i, BLOCK), cols(pair, 128)], low) for pair in range(2)]
        states = [load_state(state[rows_at(i, WIDE), cols(pair, 128)]) for pair in range(2)]
        return q2, states

    def finish(states, j):
        for pair in range(2):
            top, total, acc = states[pair]
            res = acc / total
            heads[rows_at(j, BLOCK), cols(pair, 128)] = bf(
                jnp.where(low, res[:BLOCK], res[BLOCK:])
            )
            kept = jnp.transpose(jnp.broadcast_to(top + jnp.log(total), (2 * BLOCK, 128)))
            lse[pl.ds(pair * 4 + j, 1), :] = kept[0:1, :]

    @pl.when(y == 0)
    def _():
        def prompt_block(j, _):
            for n in range(2):
                i = 2 * n + j
                base = block_at(zl, n, j) * BLOCK
                q2, states = load(i)
                for m in range(n + 1):
                    states = attend_chunk(
                        q2, states, kvo, pl.ds(m * WIDE, WIDE), places[m], base, slope, spot, m == n
                    )
                finish(states, i)
            return 0

        lax.fori_loop(0, 2, prompt_block, 0)

    @pl.when(y == 1)
    def _():
        def cont_block(j, _):
            q2, states = load(4 + j)
            for m in range(2):
                states = attend_chunk(
                    q2, states, kvo, pl.ds(m * WIDE, WIDE), places[m], PROMPT, slope, spot, False
                )
            finish(states, j)
            return 0

        lax.fori_loop(0, 4, cont_block, 0)

    ps = (p0, p1, p2, p3)
    for b, dst in enumerate((o0, o1)):
        c = jnp.bitwise_xor(info[2], b)
        h = heads[rows_at(c, TOK), :]
        u = bf(nt(h, reduce[...]))
        for k in range(4):
            dst[:, cols(k)] = bf(nn(h, ws[k]) + SCALE * nn(u, ps[k][304:320, :]))


def mlp_pre_body(info, x0, x1, w1, p0, p1, p2, p3, bias, expand, act, slope):
    ps = (p0, p1, p2, p3)
    for b, x in enumerate((x0, x1)):
        u = bf(sum(nt(x[:, cols(k)], ps[k][288:304, :]) for k in range(4)))
        pre = sum(nn(x[:, cols(k)], w1[rel(info, k)]) for k in range(4))
        pre = pre + f32(bias[...]) + SCALE * nn(u, expand[...])
        sq = pre * pre
        t = jnp.tanh(pre * (GELU_A + (GELU_A * GELU_B) * sq))
        half = 0.5 + 0.5 * t
        act[b] = bf(pre * half)
        slope[b] = bf(
            half + (0.5 * pre) * (1.0 - t * t) * (GELU_A + (3.0 * GELU_A * GELU_B) * sq)
        )


def mlp_back_body(
    info, x0, x1, g0, g1, slope, w1, w2, p0, p1, p2, p3, expand, reduce, r_in, e_in,
    d0, d1, r_out, e_out,
):
    ps = (p0, p1, p2, p3)
    rv, ev = r_in[...], e_in[...]
    for b, (x, g, dx) in enumerate(((x0, g0, d0), (x1, g1, d1))):
        u = bf(sum(nt(x[:, cols(k)], ps[k][288:304, :]) for k in range(4)))
        du2 = bf(SCALE * sum(nt(g[:, cols(k)], ps[k][320:336, :]) for k in range(4)))
        d_act = sum(nt(g[:, cols(k)], w2[rel(info, k)]) for k in range(4)) + nn(du2, reduce[...])
        d_pre = bf(d_act * f32(slope[b]))
        du = bf(SCALE * nt(d_pre, expand[...]))
        for k in range(4):
            dx[:, cols(k)] = bf(nt(d_pre, w1[rel(info, k)]) + nn(du, ps[k][288:304, :]))
        rv = rv + tn(du, x[...])
        ev = ev + tn(u, d_pre)
    r_out[...] = rv
    e_out[...] = ev


def fc2_body(
    info, a0, a1, g0, g1, g2, g3, w2, reduce, p0, p1, p2, p3, r1, e1,
    m0, m1, m2, m3, grads,
):
    ps = (p0, p1, p2, p3)
    rv = ev = 0.0
    for b, (g, m) in enumerate(zip((g0, g1, g2, g3), (m0, m1, m2, m3))):
        act = a0[b] if b < 2 else a1[b - 2]
        du = bf(SCALE * sum(nt(g[:, cols(k)], ps[k][320:336, :]) for k in range(4)))
        u = bf(nt(act, reduce[...]))
        for k in range(4):
            m[:, cols(k)] = bf(nn(act, w2[rel(info, k)]) + SCALE * nn(u, ps[k][320:336, :]))
        rv = rv + tn(du, act)
        ev = ev + SCALE * tn(u, g[...])
    for k in range(4):
        grads[0:16, rel_cols(info, k)] = bf(r1[:, cols(k)])
        grads[16:32, rel_cols(info, k)] = bf(ev[:, k * TOK : k * TOK + TOK])
    grads[32:48, :] = bf(SCALE * e1[...])
    grads[48:64, :] = bf(rv)


def d_heads_body(
    info, g0, g1, ws, p0, p1, p2, p3, reduce, heads, r_in, e_in, dh, r_out, e_out
):
    ps = (p0, p1, p2, p3)
    rv, ev = r_in[...], e_in[...]
    for b, g in enumerate((g0, g1)):
        rows = rows_at(jnp.bitwise_xor(info[2], b), TOK)
        h = heads[rows, :]
        u = bf(nt(h, reduce[...]))
        du = bf(SCALE * sum(nt(g[0:256, cols(k)], ps[k][304:320, :]) for k in range(4)))
        v = sum(nt(g[0:256, cols(k)], ws[k]) for k in range(4)) + nn(du, reduce[...])
        dh[rows, :] = bf(v)
        rv = rv + tn(du, h)
        ev = ev + SCALE * tn(u, g[0:256, :])
    r_out[...] = rv
    e_out[...] = ev


def back_load(heads, d_heads, lse, q, qi, j, low):
    res = []
    for pair in range(2):
        lane = cols(pair, 128)
        q2 = stacked(q[rows_at(qi, BLOCK), lane], low)
        do = d_heads[rows_at(j, BLOCK), lane]
        both = jnp.transpose(f32(do) * f32(heads[rows_at(j, BLOCK), lane]))
        delta = jnp.concatenate(
            [
                jnp.sum(both[:HEAD], axis=0, keepdims=True),
                jnp.sum(both[HEAD:], axis=0, keepdims=True),
            ],
            axis=1,
        )
        res.append((q2, stacked(do, low), delta, lse[pl.ds(pair * 4 + j, 1), :]))
    return res


def back_chunk(args, kv, d_kv, d_at, rows, place, base, slope, spot, masked, store, d_qs):
    away = place - base
    res = []
    for pair in range(2):
        q2, do2, delta, kept = args[pair]
        lane = cols(pair, 128)
        vlane = cols(2 + pair, 128)
        k = kv[rows, lane]
        s = nt(k, q2) + (away.astype(F32) * slope[pair] - kept)
        p = jnp.exp(s)
        if masked:
            p = jnp.where(away <= spot, p, 0.0)
        ds = bf(p * (nt(kv[rows, vlane], do2) - delta))
        dk = nn(ds, q2)
        dv = nn(bf(p), do2)
        if store:
            d_kv[d_at, lane] = bf(dk)
            d_kv[d_at, vlane] = bf(dv)
        else:
            d_kv[d_at, lane] += dk
            d_kv[d_at, vlane] += dv
        d_q = tn(ds, k)
        res.append(d_q if d_qs is None else d_qs[pair] + d_q)
    return res


def back_common(info, slopes):
    low = low_lanes(BLOCK)
    _, spot = split_id((1, 2 * BLOCK), 1)
    slope = head_slopes(slopes, (1, 2 * BLOCK), 1)
    zl = info[4]
    own = [chunk_place((WIDE, 1), 0, zl, n) for n in range(2)]
    oth = [chunk_place((WIDE, 1), 0, 1 - zl, n) for n in range(2)]
    return zl, low, spot, slope, own, oth


def fold(d_q, low):
    return jnp.where(low, d_q[:BLOCK], d_q[BLOCK:]) * 0.125


def back_sweep(info, slopes, y, q, heads, d_heads, lse, sides, kvc, dkc, finish):
    zl, low, spot, slope, own, oth = back_common(info, slopes)
    place_sets = {"own": own, "oth": oth}

    @pl.when(y == 0)
    def _():
        def prompt_block(j, _):
            for n in range(2):
                i = 2 * n + j
                args = back_load(heads, d_heads, lse, q, i, i, low)
                base = block_at(zl, n, j) * BLOCK
                d_qs = None
                for side, kv, d_kv in sides:
                    for m in range(n + 1):
                        rows = pl.ds(m * WIDE, WIDE)
                        d_qs = back_chunk(
                            args, kv, d_kv, rows, rows, place_sets[side][m], base, slope, spot,
                            m == n, False, d_qs,
                        )
                finish(d_qs, i, low)
            return 0

        lax.fori_loop(0, 2, prompt_block, 0)

    @pl.when(y == 1)
    def _():
        def cont_block(j, _):
            args = back_load(heads, d_heads, lse, q, 4 + j, j, low)
            d_qs = None
            if kvc is not None:
                mine = rows_at(j, BLOCK)
                own_place = lax.broadcasted_iota(jnp.int32, (BLOCK, 1), 0)
                d_qs = back_chunk(
                    args, kvc, dkc, mine, mine, own_place, 0, slope, spot, True, True, d_qs
                )
            for side, kv, d_kv in sides:
                for m in range(2):
                    rows = pl.ds(m * WIDE, WIDE)
                    d_qs = back_chunk(
                        args, kv, d_kv, rows, rows, place_sets[side][m], PROMPT, slope, spot,
                        False, False, d_qs,
                    )
            finish(d_qs, j, low)
            return 0

        lax.fori_loop(0, 4, cont_block, 0)


def attend_back_a_body(
    info, slopes, q, kvp, kvo, kvc, heads, d_heads, lse, dq, dkp, dko, dkc
):
    dkp[...] = jnp.zeros_like(dkp)
    dko[...] = jnp.zeros_like(dko)
    dkc[...] = jnp.zeros_like(dkc)

    def finish(d_qs, j, low):
        for pair in range(2):
            dq[rows_at(j, BLOCK), cols(pair, 128)] = bf(fold(d_qs[pair], low))

    back_sweep(
        info, slopes, info[1], q, heads, d_heads, lse,
        (("own", kvp, dkp), ("oth", kvo, dko)), kvc, dkc, finish,
    )


def attend_back_b_body(
    info, slopes, q, kvo, heads, d_heads, lse, dko_in, early, dq, dko, acc
):
    acc[...] = dko_in[...]

    def finish(d_qs, j, low):
        for pair in range(2):
            dq[rows_at(j, BLOCK), cols(pair, 128)] = fold(d_qs[pair], low)

    back_sweep(
        info, slopes, 1 - info[1], q, heads, d_heads, lse,
        (("oth", kvo, acc),), None, None, finish,
    )
    dko[0:512, :] = bf(acc[...])
    dko[512:592, :] = early[:, 0:512]
    dko[592:672, :] = early[:, 512:1024]


def early_sum_body(own, other, dst):
    dst[:, 0:512] = bf(f32(own[:, 0:512]) + f32(other[512:592, :]))
    dst[:, 512:1024] = bf(f32(own[:, 512:1024]) + f32(other[592:672, :]))


def attend_back_c_body(
    info, slopes, q, kvp, kvc, heads, d_heads, lse, dkp_in, dkc_in, dq_in, dq, dkp, dkc
):
    dkp[...] = dkp_in[...]
    dkc[...] = dkc_in[...]

    def finish(d_qs, j, low):
        for pair in range(2):
            lane = cols(pair, 128)
            rows = rows_at(j, BLOCK)
            dq[rows, lane] = bf(dq_in[rows, lane] + fold(d_qs[pair], low))

    back_sweep(
        info, slopes, 1 - info[1], q, heads, d_heads, lse,
        (("own", kvp, dkp),), kvc, dkc, finish,
    )


def qkv_back_body(
    info, dq0, dq1, dkp, dkr, dkc, x0, x1, x2, x3, ws, p0, p1, p2, p3, expand, pr, pe,
    o0, o1, o2, o3, grads,
):
    ps = (p0, p1, p2, p3)
    low = low_lanes(TOK)
    sr = se = 0.0
    for b, (x, dst) in enumerate(zip((x0, x1, x2, x3), (o0, o1, o2, o3))):
        y, c = slab_rows(info, b)
        half = rows_at(c, TOK)
        groups = []
        dq = dq0 if b < 2 else dq1
        for pair in range(2):
            vq = f32(dq[half, cols(pair, 128)])
            got = []
            for lane in (cols(pair, 128), cols(2 + pair, 128)):
                prompt = dkp[half, lane] + f32(dkr[half, lane])
                got.append(jnp.where(y == 0, prompt, f32(dkc[half, lane])))
            vk = pltpu.roll(got[0], 64, 1)
            vv = got[1]
            groups += [jnp.where(low, vq, vk), jnp.where(low, vv, vq), jnp.where(low, vk, vv)]
        d = bf(jnp.concatenate(groups, axis=1))
        u = bf(sum(nt(x[:, cols(k)], ps[k][272:288, :]) for k in range(4)))
        du = bf(SCALE * nt(d, expand[...]))
        for k in range(4):
            dst[:, cols(k)] = bf(nt(d, ws[k]) + nn(du, ps[k][272:288, :]))
        sr = sr + tn(du, x[...])
        se = se + SCALE * tn(u, d)
    for k in range(4):
        grads[0:16, rel_cols(info, k)] = bf(sr[:, k * TOK : k * TOK + TOK])
        grads[16:32, rel_cols(info, k)] = bf(pe[:, cols(k)])
    grads[32:48, 0:768] = bf(se)
    grads[32:48, 768:1024] = bf(pr[...])


def add_body(a, b, dst):
    dst[...] = bf(f32(a[...]) + f32(b[...]))


def add(a, b):
    return call(add_body, [out(a.shape, BF)], [a, b], smem=0, us=0.01, name="add")[0]


def add32_body(a, b, dst):
    dst[...] = f32(a[...]) + f32(b[...])


def add32(a, b, us=8):
    return call(add32_body, [out(a.shape, F32)], [a, b], smem=0, us=us, name="add32")[0]


def stage_body(*refs):
    n = len(refs) // 2
    for src, dst in zip(refs[:n], refs[n:]):
        dst[...] = src[...]


def stage(values):
    return call(
        stage_body, [out(v.shape, v.dtype) for v in values], far(values), smem=0, us=0.01, name="stage"
    )


def stage_weight_body(size, info, own, wr, ws, w, sem):
    copies = [pltpu.make_async_copy(own, w.at[info[0]], sem.at[6])]
    for n, (src, at) in enumerate(((wr, info[8]), (ws, 1 - info[8]))):
        for k in range(1, ROWS):
            to = w.at[rel(info, k), rows_at(at, size)]
            copies.append(pltpu.make_async_copy(src.at[k - 1], to, sem.at[3 * n + k - 1]))
    for copy in copies:
        copy.start()
    for copy in copies:
        copy.wait()


def merge_body(info, v0, v1, v2, v3, dst):
    four = (v0, v1, v2, v3)

    def fill(c):
        total = sum(f32(v[256 + 16 * c : 272 + 16 * c, :]) for v in four)
        dst[0:16, :] = bf(total)
        for b, v in enumerate(four):
            rows = pl.ds(pl.multiple_of(16 + 16 * jnp.bitwise_xor(info[6], b), 16), 16)
            dst[rows, :] = v[288 + 16 * c : 304 + 16 * c, :]

    @pl.when(info[2] == 0)
    def _():
        fill(0)

    @pl.when(info[2] == 1)
    def _():
        fill(1)


def pile_body(*refs):
    dst = refs[-1]
    for n, src in enumerate(refs[:-1]):
        dst[n] = src[...]


def expand_early_body(info, own, oth, r1, e2, e1, r2):
    for v in (r1, e2, e1, r2):
        v[...] = jnp.zeros_like(v)

    def fill(src, shared, split):
        for n in range(own.shape[0]):
            group = info[5] if n % 2 == 0 else 1 - info[5]
            a = info[40 + n // 2 * GROUPS_DEV + group]
            shared[a] += f32(src[n, 0:16, :])
            for j in range(COLS):
                at = 16 + 16 * j
                split[a, :, cols(j, 1024)] += f32(src[n, at : at + 16, :])

    @pl.when(info[2] == 0)
    def _():
        fill(own, r1, e1)
        fill(oth, e2, r2)

    @pl.when(info[2] == 1)
    def _():
        fill(oth, r1, e1)
        fill(own, e2, r2)


def expand_late_body(info, v0, v1, v2, v3, qr, pe, qe, pr):
    four = (v0, v1, v2, v3)
    for v in (qr, pe, qe, pr):
        v[...] = jnp.zeros_like(v)
    for k in range(v0.shape[0]):
        group = info[5] if k % 2 == 0 else 1 - info[5]
        a = info[40 + k // 2 * GROUPS_DEV + group]
        qr[a] += sum(f32(v[k, 0:16, :]) for v in four)
        pe[a] += sum(f32(v[k, 16:32, :]) for v in four)
        for b, v in enumerate(four):
            j = jnp.bitwise_xor(info[6], b)
            qe[a, :, lanes_at(j * 768, 768)] += f32(v[k, 32:48, :768])
            pr[a, :, lanes_at(j * 256, 256)] += f32(v[k, 32:48, 768:])


def shift(v, k, axis="row"):
    if k == 0:
        return v
    size = lax.axis_size(axis)
    return lax.ppermute(v, axis, [(s, (s + k) % size) for s in range(size)])


def gather_row(v):
    return [v] + [shift(v, k) for k in range(1, ROWS)]


def gather_col(v):
    core = lax.ppermute(v, "col", CORE_SWAP)
    side = lax.ppermute(v, "col", Y_SWAP)
    return [v, core, side, lax.ppermute(side, "col", CORE_SWAP)]


def to_cols(pieces):
    return [pieces[0]] + [shift(pieces[k], ROWS - k) for k in range(1, ROWS)]


def spread(mine, other):
    return [mine, other] + [
        shift(v, k, "dp") for k in range(1, lax.axis_size("dp")) for v in (mine, other)
    ]


def pile(parts):
    shape = (len(parts), *parts[0].shape)
    return call(pile_body, [out(shape, BF)], parts, smem=0, us=0.01, name="pile")[0]

def body(
    hidden_in,
    out_grad,
    first_norm_gain,
    first_norm_bias,
    qkv_weight,
    qkv_bias,
    proj_weight,
    proj_bias,
    second_norm_gain,
    second_norm_bias,
    fc1_weight,
    fc1_bias,
    fc2_weight,
    second_feed_bias,
    qkv_reduce,
    qkv_expand,
    proj_reduce,
    proj_expand,
    fc1_reduce,
    fc1_expand,
    fc2_reduce,
    fc2_expand,
    adapter_choice,
    cont_prompt,
):
    r = lax.axis_index("row")
    col = lax.axis_index("col")
    dp = lax.axis_index("dp")
    y = col // 2
    c = lax.rem(col, 2)
    zl = lax.rem(r, 2)
    group = r // 2
    half = lax.rem(dp, 2)
    dp_swap = [(k, k ^ 1) for k in range(lax.axis_size("dp"))]
    slopes = jnp.exp2(
        -8.0 * (col * 4 + 1 + jnp.arange(4, dtype=jnp.int32)).astype(F32) / HEADS
    )
    adapter = jnp.where(group == 0, adapter_choice[0], adapter_choice[1])
    n_dp = jnp.int32(lax.axis_size("dp"))
    info = jnp.stack([r, y, c, dp * GROUPS_DEV, zl, group, col, dp, half] + [half, n_dp] + [half] * 5)
    info = jnp.concatenate([info.astype(jnp.int32), cont_prompt, adapter_choice])
    order = pltpu.SMEM((GROUPS_DEV * NCONT,), jnp.int32)
    flip = functools.partial(jnp.transpose, axes=(0, 2, 1))
    big = out((TOK, D), BF)
    small = out((RANK, D), F32)

    other = lax.ppermute(hidden_in, "col", CORE_SWAP)
    vectors = [
        first_norm_gain, first_norm_bias, proj_bias,
        second_norm_gain, second_norm_bias, second_feed_bias,
    ]
    factors = [flip(qkv_reduce), flip(fc1_reduce), proj_expand, fc2_expand]
    pieces = call(
        route_pack_body,
        [out((336, TOK), BF)] * 4,
        [info, Far(hidden_in), Far(other), *far(vectors), *far(factors)],
        [
            order,
            *[pltpu.VMEM((TOK,), BF)] * 6,
            pltpu.VMEM((16, RANK, TOK), BF),
            pltpu.SemaphoreType.DMA((22,)),
        ],
        raw=range(3, 13),
        us=1.5,
        name="route_x",
    )
    xs = [pieces[0]] + [shift(pieces[k], k) for k in range(1, ROWS)]
    packs = far(xs)
    first_half, w1_copies, qkv_e, fc1_e, proj_r, fc2_r = call(
        prepare_body,
        [
            out((128, D), BF), out((ROWS, 128, D), BF),
            out((RANK, 768), BF), out((RANK, D), BF), out((RANK, TOK), BF), out((RANK, D), BF),
        ],
        [
            after(info, pieces[0]),
            *far([qkv_weight, proj_weight, fc1_weight, qkv_expand, fc1_expand]),
            *far([flip(proj_reduce), flip(fc2_reduce)]),
        ],
        [pltpu.SemaphoreType.DMA((10,))],
        raw=range(1, 8),
        us=3,
        name="prepare",
    )
    first_half = after(first_half, xs[1])
    z_parts = [shift(first_half, k) for k in range(1, ROWS)]
    s_parts = [lax.ppermute(v, "dp", dp_swap) for v in z_parts]
    wq, wp = call(
        assemble_body,
        [out((ROWS, TOK, 768), BF), out((ROWS, TOK, TOK), BF)],
        [info, *far([qkv_weight, proj_weight, *z_parts, *s_parts])],
        [pltpu.SemaphoreType.DMA((14,))],
        raw=range(1, 9),
        us=15,
        name="assemble",
    )

    qkv_b = lax.dynamic_slice_in_dim(qkv_bias, col * 768, 768, 0)[None, :]
    fc1_b = lax.dynamic_slice_in_dim(fc1_bias, col * 1024, 1024, 0)[None, :]

    choices = [adapter_choice] + [
        shift(adapter_choice, k, "dp") for k in range(1, lax.axis_size("dp"))
    ]
    first = after(xs[0], qkv_b, fc1_b, w1_copies, *choices)
    (xn1,) = call(norm1_body, [big], [first, *xs[1:]], smem=0, us=8, name="norm1")
    xn1s = gather_col(xn1)
    q, kvp, kvc = call(
        qkv_body,
        [out((1024, 256), BF), out((512, 512), BF), out((512, 512), BF)],
        [info, *xn1s, wq, *packs, Far(qkv_b), Far(qkv_e)],
        us=6.5,
        name="qkv",
    )
    kvo = lax.ppermute(kvp, "row", Z_SWAP)

    g_other = lax.ppermute(after(out_grad, kvp), "col", CORE_SWAP)
    (pieces,) = call(
        route_all_body,
        [out((ROWS, 3 * TOK, TOK), BF)],
        [info, Far(out_grad), Far(g_other), Far(fc2_weight)],
        [order, pltpu.SemaphoreType.DMA((4,))],
        raw=(3,),
        us=1,
        name="route_g",
    )
    (state,) = call(
        attend_first_body,
        [out((2048, 256), F32)],
        [info, slopes, q, kvp, kvc],
        smem=2,
        us=9,
        name="attend_first",
    )
    (w1r,) = call(
        rest_body,
        [out((3, 128, D), BF)],
        [info, after(lax.all_to_all(after(w1_copies, *z_parts), "row", 0, 0), state)],
        us=0.01,
        name="rest",
    )
    w1s = lax.ppermute(w1r, "dp", dp_swap)
    pieces = after(pieces, state, kvo)
    g_own, w2r = call(
        join_body,
        [big, out((3, 512, TOK), BF)],
        [info, lax.all_to_all(pieces, "row", 0, 0)],
        us=0.01,
        name="join",
    )
    g_side = lax.ppermute(g_own, "col", Y_SWAP)
    w2s = lax.ppermute(w2r, "dp", dp_swap)

    def attend_rest(which, q, state):
        return call(
            functools.partial(attend_rest_body, which),
            [out((512, 256), BF), out((8, 256), F32), big, big],
            [info, slopes, Far(q), kvo, state, Far(wp), Far(proj_r), *packs],
            smem=2,
            us=20 if which else 0.01,
            name="attend_rest",
        )

    heads1, lse1, p2, p3 = attend_rest(1, q, after(state, w1r))
    g_core = lax.ppermute(g_own, "col", CORE_SWAP)
    g_all = [g_own, g_core, g_side, lax.ppermute(g_side, "col", CORE_SWAP)]
    p_far = lax.ppermute(p3, "col", CORE_SWAP)
    p_side = add(p2, p_far)
    heads0, lse0, p0, p1 = attend_rest(0, q, Far(after(state, p_side)))
    p_side = lax.ppermute(p_side, "col", Y_SWAP)
    p_core = lax.ppermute(p1, "col", CORE_SWAP)
    staged = stage([after(xs[0], p0), *xs[1:]])
    mid, xn2 = call(
        norm2_body,
        [out((TOK, D), F32), big],
        [add32(after(p0, w1s), p_side), p_core, *staged],
        smem=0,
        us=1.5,
        hbm=(0,),
        name="norm2",
    )
    (w1,) = call(
        functools.partial(stage_weight_body, 128),
        [out((ROWS, TOK, D), BF)],
        [info, Far(fc1_weight), Far(after(w1r, p0)), Far(w1s)],
        [pltpu.SemaphoreType.DMA((7,))],
        raw=(1, 2, 3),
        us=2,
        name="stage_w1",
    )
    zero = jnp.zeros((RANK, D), F32)
    xn2_core = lax.ppermute(xn2, "col", CORE_SWAP)
    xn2_side = lax.ppermute(xn2, "col", Y_SWAP)

    def mlp_pre(first, blocks):
        return call(
            mlp_pre_body,
            [out((2, TOK, D), BF)] * 2,
            [info, *blocks, w1, *staged, Far(fc1_b), Far(fc1_e)],
            us=0.01,
            name="mlp_pre",
        )

    act0, slope0 = mlp_pre(0, [xn2, xn2_core])
    xn2_far = lax.ppermute(after(xn2_side, act0), "col", CORE_SWAP)
    xn2s = [xn2, xn2_core, xn2_side, xn2_far]
    act1, slope1 = mlp_pre(1, xn2s[2:])
    (w2,) = call(
        functools.partial(stage_weight_body, 512),
        [out((ROWS, D, TOK), BF)],
        [info, Far(fc2_weight), Far(after(w2r, act0)), Far(w2s)],
        [pltpu.SemaphoreType.DMA((7,))],
        raw=(1, 2, 3),
        us=20,
        name="stage_w2",
    )

    def mlp_back(blocks, slope, r_in, e_in):
        xa, xb = (xn2s[b] for b in blocks)
        ga, gb = (g_all[b] for b in blocks)
        return call(
            mlp_back_body,
            [big, big, small, small],
            [info, xa, xb, ga, gb, slope, w1, w2, *staged, Far(fc1_e), Far(fc2_r), r_in, e_in],
            us=0.01,
            name="mlp_back",
        )

    d2, d3, r1, e1 = mlp_back((2, 3), slope1, zero, zero)
    d_far = lax.ppermute(d3, "col", CORE_SWAP)
    d_side = add(d2, d_far)
    d0, d1, r1, e1 = mlp_back((0, 1), slope0, after(r1, d_side), e1)
    d_side = lax.ppermute(d_side, "col", Y_SWAP)
    d_core = lax.ppermute(d1, "col", CORE_SWAP)
    res = call(
        fc2_body,
        [big] * 4 + [out((64, D), BF)],
        [info, act0, act1, *g_all, w2, Far(fc2_r), *staged, r1, e1],
        us=0.01,
        name="fc2",
    )
    m_parts, mlp_pack = res[:4], res[4]
    staged_back = stage([after(mid, mlp_pack), g_own, *xs])
    d_mid, g_attn = call(
        norm2_back_body,
        [out((TOK, D), F32), out((320, D), BF)],
        [add32(d0, d_side), d_core, mlp_pack, *staged_back],
        smem=0,
        us=1.5,
        hbm=(0,),
        name="norm2_back",
    )
    ga_core = lax.ppermute(g_attn, "col", CORE_SWAP)
    ga_side = lax.ppermute(g_attn, "col", Y_SWAP)
    shared = far([q, kvp, kvo, kvc])

    def d_heads(blocks, heads, r_in, e_in):
        return call(
            d_heads_body,
            [out((512, 256), BF), out((RANK, TOK), F32), small],
            [info, *blocks, Far(wp), *packs, Far(proj_r), Far(heads), r_in, e_in],
            us=1.5,
            name="d_heads",
        )

    dh0, pr, pe = d_heads([g_attn, ga_core], heads0, jnp.zeros((RANK, TOK), F32), zero)
    dq0, dkp, dko, dkc = call(
        attend_back_a_body,
        [out((512, 256), BF), out((512, 512), F32), out((512, 512), F32), out((512, 512), BF)],
        [info, slopes, *shared, Far(heads0), dh0, Far(lse0)],
        smem=2,
        us=16,
        weight=W_BIG,
        hbm=(1, 2, 3),
        name="attend_back_a",
    )
    ga_side = after(ga_side, dq0)
    ga_far = lax.ppermute(ga_side, "col", CORE_SWAP)
    (early_half,) = call(
        merge_body,
        [out((80, D), BF)],
        [info, g_attn, ga_core, ga_side, ga_far],
        us=0.7,
        name="merge",
    )
    dh1, pr, pe = d_heads([ga_side, ga_far], heads1, pr, pe)
    dq1_part, dko = call(
        attend_back_b_body,
        [out((512, 256), F32), out((672, 512), BF)],
        [info, slopes, Far(q), Far(kvo), Far(heads1), dh1, Far(lse1), Far(dko), early_half],
        [pltpu.VMEM((512, 512), F32)],
        smem=2,
        us=8,
        hbm=(0,),
        name="attend_back_b",
    )
    dkr = lax.ppermute(dko, "row", Z_SWAP)
    dq1, dkp, dkc = call(
        attend_back_c_body,
        [out((512, 256), BF), out((512, 512), F32), out((512, 512), BF)],
        [info, slopes, Far(q), Far(kvp), Far(kvc), Far(heads1), dh1, Far(lse1), *far([dkp, dkc, dq1_part])],
        smem=2,
        us=8,
        hbm=(2,),
        name="attend_back_c",
    )
    (early_sum,) = call(
        early_sum_body, [out((80, D), BF)], [early_half, dkr], smem=0, us=0.01, name="early_sum"
    )
    m_far = lax.ppermute(after(m_parts[3], dq0), "col", CORE_SWAP)
    m_core = lax.ppermute(after(m_parts[1], dq0), "col", CORE_SWAP)
    m_sum = add(after(m_parts[2], dko), m_far)
    m_side = lax.ppermute(m_sum, "col", Y_SWAP)
    res = call(
        qkv_back_body,
        [big] * 4 + [out((48, D), BF)],
        [
            info, dq0, dq1, dkp, after(dkr, early_sum), Far(dkc),
            *far(xn1s), Far(wq), *packs, Far(qkv_e), pr, pe,
        ],
        us=20,
        name="qkv_back",
    )
    q_parts, late_pack = res[:4], res[4]
    early_parts = spread(early_sum, shift(early_sum, 2))
    ready = after(q_parts[3], m_side, *early_parts[1:3])
    q_sum = add(q_parts[2], lax.ppermute(ready, "col", CORE_SWAP))
    hidden = call(
        hidden_body,
        [out((TOK, TOK), BF)] * 4,
        [add32(m_parts[0], after(m_side, q_sum), 0.01), m_core, Far(mid), *packs],
        smem=0,
        us=0.01,
        name="hidden",
    )
    hidden_got = to_cols(hidden)
    k0, rc = q_parts[0], lax.ppermute(q_parts[1], "col", CORE_SWAP)
    ry = lax.ppermute(q_sum, "col", Y_SWAP)
    late_sum = add(late_pack, lax.ppermute(after(late_pack, q_sum), "row", Z_SWAP))
    late_next = shift(late_sum, 2)
    late_four = pile(spread(late_sum, late_next))
    late_all = gather_col(late_four)
    staged_last = stage([after(d_mid, k0), *xs])
    ins = call(
        norm1_back_body,
        [out((TOK, TOK), BF)] * 4,
        [add32(after(k0, late_next, *hidden_got), ry), rc, *staged_last],
        smem=0,
        us=1,
        name="norm1_back",
    )
    early_all = pile(early_parts)
    early_far = lax.ppermute(after(early_all, ins[0]), "col", CORE_SWAP)
    table = jnp.concatenate([info, jnp.zeros((40 - 34,), jnp.int32), *choices])
    o_fc1r, o_f2e, o_f1e, o_f2r = call(
        expand_early_body,
        [out((COUNT, RANK, w), F32) for w in (1024, 1024, 4096, 4096)],
        [table, Far(early_all), Far(early_far)],
        us=0.01,
        name="expand_early",
    )
    (joined,) = call(
        stack_body,
        [out((8 * TOK, TOK), BF)],
        [*[after(v, o_fc1r, late_all[2]) for v in to_cols(ins)], *hidden_got],
        smem=0,
        us=0.01,
        name="stack",
    )
    input_gradient, hidden_out = call(
        unroute_body,
        [out((1024, TOK), F32), out((1024, TOK), BF)],
        [info, joined, lax.ppermute(joined, "col", CORE_SWAP)],
        [order],
        us=2,
        name="unroute",
    )
    o_qr, o_pe, o_qe, o_pr = call(
        expand_late_body,
        [out((COUNT, RANK, w), F32) for w in (1024, 1024, 3072, 1024)],
        [table, *late_all],
        us=0.01,
        name="expand_late",
    )
    return (
        hidden_out,
        input_gradient,
        flip(o_qr),
        o_qe,
        flip(o_pr),
        o_pe,
        flip(o_fc1r),
        o_f1e,
        flip(o_f2r),
        o_f2e,
    )


def solution(mesh):
    placed = (
        P(("dp", "col"), "row"),
        P(("dp", "col"), "row"),
        P("row"),
        P("row"),
        P("row", "col"),
        P(),
        P("col", "row"),
        P("row"),
        P("row"),
        P("row"),
        P("row", "col"),
        P(),
        P("col", "row"),
        P("row"),
        P(None, "row", None),
        P(),
        P(None, "col", None),
        P(None, None, "row"),
        P(None, "row", None),
        P(),
        P(None, "col", None),
        P(None, None, "row"),
        P("dp"),
        P("dp"),
    )
    return jax.shard_map(
        body,
        mesh=mesh,
        in_specs=placed,
        out_specs=(P(("dp", "col"), "row"), P(("dp", "col"), "row")) + (P(),) * 8,
        check_vma=False,
    )
```

```python
import functools

import jax
import jax.numpy as jnp
from jax import lax
from jax.experimental import pallas as pl
from jax.experimental.pallas import tpu as pltpu
from jax.sharding import PartitionSpec as P

D = 1024
HEADS = 16
HEAD = 64
FF = 4096
RANK = 16
COUNT = 8
PROMPT = 1024
CONT = 128
NCONT = 8
GROUPS_DEV = 2

EPSILON = 1e-05
SCALE = 2.0
GELU_A = 0.7978845608028654
GELU_B = 0.044715
ROWS = 4
COLS = 4
TOK = 256
BLOCK = 128
LOW = -1e30
W_SMALL = 5e8
W_BIG = 5e8

BF = jnp.bfloat16
F32 = jnp.float32

VM = pl.BlockSpec(memory_space=pltpu.VMEM)
SM = pl.BlockSpec(memory_space=pltpu.SMEM)
HB = pl.BlockSpec(memory_space=pltpu.HBM)

CORE_SWAP = [(0, 1), (1, 0), (2, 3), (3, 2)]
Y_SWAP = [(0, 2), (2, 0), (1, 3), (3, 1)]
Z_SWAP = [(0, 1), (1, 0), (2, 3), (3, 2)]


def nn(a, b):
    return lax.dot_general(a, b, (((1,), (0,)), ((), ())), preferred_element_type=F32)


def nt(a, b):
    return lax.dot_general(a, b, (((1,), (1,)), ((), ())), preferred_element_type=F32)


def tn(a, b):
    return lax.dot_general(a, b, (((0,), (0,)), ((), ())), preferred_element_type=F32)


def f32(v):
    return v.astype(F32)


def bf(v):
    return v.astype(BF)


class Far:
    def __init__(self, value):
        self.value = value


def far(values):
    return [Far(v) for v in values]


def call(
    body, outs, ins, scratch=(), smem=1, limit=40, us=1, raw=(), weight=W_SMALL, hbm=(), name=None
):
    values = [
        pltpu.with_memory_space_constraint(v.value, pltpu.HBM) if isinstance(v, Far) else v
        for v in ins
    ]
    fetched = [i for i, v in enumerate(ins) if isinstance(v, Far) and i not in raw]
    specs = [SM] * smem
    for v in ins[smem:]:
        specs.append(HB if isinstance(v, Far) else VM)
    nbytes = sum(v.size * v.dtype.itemsize for v in values)
    nbytes += sum(o.size * o.dtype.itemsize for o in outs)
    extra = [pltpu.VMEM(values[i].shape, values[i].dtype) for i in fetched]
    extra += [pltpu.VMEM(outs[i].shape, outs[i].dtype) for i in hbm]
    moved = len(extra)
    if moved:
        extra.append(pltpu.SemaphoreType.DMA((moved,)))

    def whole(*refs):
        refs = list(refs)
        stores = []
        if moved:
            sem = refs[-1]
            buffers = refs[-1 - moved : -1]
            refs = refs[: -1 - moved]
            copies = []
            for n, i in enumerate(fetched):
                copies.append(pltpu.make_async_copy(refs[i], buffers[n], sem.at[n]))
                copies[-1].start()
                refs[i] = buffers[n]
            for n, i in enumerate(hbm, len(fetched)):
                at = len(values) + i
                stores.append(pltpu.make_async_copy(buffers[n], refs[at], sem.at[n]))
                refs[at] = buffers[n]
            for copy in copies:
                copy.wait()
        body(*refs)
        for copy in stores:
            copy.start()
        for copy in stores:
            copy.wait()

    return pl.pallas_call(
        whole,
        out_shape=tuple(
            pltpu.HBM(o.shape, o.dtype) if i in hbm else o for i, o in enumerate(outs)
        ),
        in_specs=specs,
        out_specs=tuple(HB if i in hbm else VM for i in range(len(outs))),
        scratch_shapes=list(scratch) + extra,
        compiler_params=pltpu.CompilerParams(vmem_limit_bytes=limit << 20),
        cost_estimate=pl.CostEstimate(
            flops=int(us * weight), bytes_accessed=nbytes // 8, transcendentals=0
        ),
        name=name,
    )(*values)


def after(value, *others):
    res = lax.optimization_barrier((value, others))
    return res[0]


def out(shape, dtype):
    return jax.ShapeDtypeStruct(shape, dtype)


def block_at(zl, c, j):
    return c * 4 + zl + j * (3 - 2 * zl)


def fill_order(info, order):
    base = info[3]
    first = jnp.int32(0)
    second = jnp.int32(NCONT)
    for j in range(GROUPS_DEV * NCONT):
        own = info[16 + j] == base
        slot = jnp.where(own, first, second)
        order[slot] = jnp.int32(j)
        first = first + jnp.where(own, 1, 0)
        second = second + jnp.where(own, 0, 1)


def place_of(info, order, z, core, j):
    prompt = (z // 2) * 8 + block_at(lax.rem(z, 2), core, j)
    cont = order[4 * z + 2 * core + j]
    return jnp.where(info[1] == 0, prompt, cont)


def route_body(info, own, oth, o0, o1, o2, o3, order):
    fill_order(info, order)
    c = info[2]
    for s, dst in enumerate((o0, o1, o2, o3)):
        z = lax.rem(info[0] + s, ROWS)
        for j in range(2):
            src = place_of(info, order, z, c, j)
            at = pl.ds(pl.multiple_of(lax.rem(src, 8) * BLOCK, BLOCK), BLOCK)
            mine = src // 8 == c

            @pl.when(mine)
            def _():
                dst[pl.ds(j * BLOCK, BLOCK), :] = own[at, :]

            @pl.when(jnp.logical_not(mine))
            def _():
                dst[pl.ds(j * BLOCK, BLOCK), :] = oth[at, :]


def route_pack_body(
    info, own, oth, g1, c1, pb, g2, c2, fb, qr, fr, pe, fe,
    o0, o1, o2, o3, order, v0, v1, v2, v3, v4, v5, mats, sem,
):
    vecs = (v0, v1, v2, v3, v4, v5)
    pairs = list(zip((g1, c1, pb, g2, c2, fb), vecs))
    for k in range(ROWS):
        which = lax.rem(info[0] + k, ROWS) // 2
        a = jnp.where(which == 0, info[32], info[33])
        pairs += [(v.at[a], mats.at[4 * k + i]) for i, v in enumerate((qr, fr, pe, fe))]
    copies = [pltpu.make_async_copy(a, b, sem.at[i]) for i, (a, b) in enumerate(pairs)]
    for copy in copies:
        copy.start()
    route_body(info, own, oth, o0, o1, o2, o3, order)
    for copy in copies:
        copy.wait()
    for k, dst in enumerate((o0, o1, o2, o3)):
        head = [f32(v[...]).reshape(1, TOK) for v in vecs]
        dst[256:272, :] = bf(jnp.concatenate(head + [jnp.zeros((10, TOK), F32)], axis=0))
        for i in range(4):
            dst[272 + 16 * i : 288 + 16 * i, :] = mats[4 * k + i]


def stack_body(a0, a1, a2, a3, h0, h1, h2, h3, dst):
    for k, (a, h) in enumerate(((a0, h0), (a1, h1), (a2, h2), (a3, h3))):
        dst[2 * k * TOK : (2 * k + 1) * TOK, :] = a[...]
        dst[(2 * k + 1) * TOK : (2 * k + 2) * TOK, :] = h[...]


def route_all_body(info, own, oth, w2, dst, order, sem):
    copies = []
    for z in range(ROWS):
        to = dst.at[z, pl.ds(TOK, 512)]
        copies.append(pltpu.make_async_copy(w2.at[rows_at(info[8], 512)], to, sem.at[z]))
    for copy in copies:
        copy.start()
    fill_order(info, order)
    c = info[2]
    for z in range(ROWS):
        for j in range(2):
            src = place_of(info, order, z, c, j)
            at = pl.ds(pl.multiple_of(lax.rem(src, 8) * BLOCK, BLOCK), BLOCK)
            mine = src // 8 == c

            @pl.when(mine)
            def _():
                dst[z, pl.ds(j * BLOCK, BLOCK), :] = own[at, :]

            @pl.when(jnp.logical_not(mine))
            def _():
                dst[z, pl.ds(j * BLOCK, BLOCK), :] = oth[at, :]
    for copy in copies:
        copy.wait()


def unroute_body(info, a, b, grad, hidden, order):
    fill_order(info, order)
    c = info[2]
    for s in range(ROWS):
        z = lax.rem(info[0] + s, ROWS)
        for other, src in ((0, a), (1, b)):
            core = c if other == 0 else 1 - c
            for j in range(2):
                at = place_of(info, order, z, core, j)

                @pl.when(at // 8 == c)
                def _():
                    rows = pl.ds(pl.multiple_of(lax.rem(at, 8) * BLOCK, BLOCK), BLOCK)
                    start = 2 * s * TOK + j * BLOCK
                    grad[rows, :] = f32(src[pl.ds(start, BLOCK), :])
                    hidden[rows, :] = src[pl.ds(start + TOK, BLOCK), :]


def cols(k, width=TOK):
    return pl.ds(k * width, width)


def row_stats(parts):
    total = sum(jnp.sum(v, axis=1, keepdims=True) for v in parts)
    mean = total * (1.0 / D)
    dev = [v - mean for v in parts]
    var = sum(jnp.sum(v * v, axis=1, keepdims=True) for v in dev) * (1.0 / D)
    rstd = lax.rsqrt(var + EPSILON)
    return [v * rstd for v in dev], rstd


def norm1_body(x0, x1, x2, x3, xn):
    for t in range(2):
        rows = pl.ds(t * 128, 128)
        hat, _ = row_stats([f32(v[rows, :]) for v in (x0, x1, x2, x3)])
        for k, pack in enumerate((x0, x1, x2, x3)):
            xn[rows, cols(k)] = bf(hat[k] * f32(pack[256:257, :]) + f32(pack[257:258, :]))


def both(a, b, rows, k):
    return f32(a[rows, cols(k)]) + f32(b[rows, cols(k)])


def norm2_body(a, b, x0, x1, x2, x3, mid, xn):
    for t in range(2):
        rows = pl.ds(t * 128, 128)
        parts = []
        for k, x in enumerate((x0, x1, x2, x3)):
            v = f32(x[rows, :]) + both(a, b, rows, k) + f32(x[258:259, :])
            mid[rows, cols(k)] = v
            parts.append(v)
        hat, _ = row_stats(parts)
        for k, pack in enumerate((x0, x1, x2, x3)):
            xn[rows, cols(k)] = bf(hat[k] * f32(pack[259:260, :]) + f32(pack[260:261, :]))


def norm_back(hat, rstd, grads):
    total = sum(jnp.sum(g, axis=1, keepdims=True) for g in grads) * (1.0 / D)
    along = sum(jnp.sum(g * h, axis=1, keepdims=True) for g, h in zip(grads, hat)) * (1.0 / D)
    return [rstd * (g - total - h * along) for g, h in zip(grads, hat)]


def norm2_back_body(
    a, b, pack, mid, g, x0, x1, x2, x3, d_mid, g_attn
):
    g_attn[256:320, :] = pack[...]
    for t in range(2):
        rows = pl.ds(t * 128, 128)
        hat, rstd = row_stats([mid[rows, cols(k)] for k in range(4)])
        grads = []
        for k, pack in enumerate((x0, x1, x2, x3)):
            grads.append(both(a, b, rows, k) * f32(pack[259:260, :]))
        back = norm_back(hat, rstd, grads)
        for k in range(4):
            v = f32(g[rows, cols(k)]) + back[k]
            d_mid[rows, cols(k)] = v
            g_attn[rows, cols(k)] = bf(v)


def norm1_back_body(a, b, d_mid, x0, x1, x2, x3, i0, i1, i2, i3):
    for t in range(2):
        rows = pl.ds(t * 128, 128)
        hat, rstd = row_stats([f32(v[rows, :]) for v in (x0, x1, x2, x3)])
        grads = []
        for k, pack in enumerate((x0, x1, x2, x3)):
            grads.append(both(a, b, rows, k) * f32(pack[256:257, :]))
        back = norm_back(hat, rstd, grads)
        for k, dst in enumerate((i0, i1, i2, i3)):
            dst[rows, :] = bf(d_mid[rows, cols(k)] + back[k])


def hidden_body(a, b, mid, x0, x1, x2, x3, h0, h1, h2, h3):
    for t in range(2):
        rows = pl.ds(t * 128, 128)
        for k, (pack, dst) in enumerate(zip((x0, x1, x2, x3), (h0, h1, h2, h3))):
            v = mid[rows, cols(k)] + both(a, b, rows, k) + f32(pack[261:262, :])
            dst[rows, :] = bf(v)


def join_body(info, v, dst, w2):
    for k in range(ROWS):
        dst[:, cols(k)] = v[rel(info, k), 0:TOK, :]
    for k in range(1, ROWS):
        w2[k - 1] = v[rel(info, k), TOK:, :]


def rest_body(info, v, dst):
    for k in range(1, ROWS):
        dst[k - 1] = v[rel(info, k)]


def slab_rows(info, b):
    y = jnp.bitwise_xor(info[1], b // 2)
    c = jnp.bitwise_xor(info[2], b % 2)
    return y, c


def low_lanes(rows):
    return lax.broadcasted_iota(jnp.int32, (rows, 128), 1) < HEAD


def rel(info, k):
    return lax.rem(info[0] - k + ROWS, ROWS)


def rel_cols(info, k):
    return pl.ds(pl.multiple_of(rel(info, k) * TOK, TOK), TOK)


def lanes_at(at, size):
    return pl.ds(pl.multiple_of(at, 128), size)


def rows_at(i, size):
    return pl.ds(pl.multiple_of(i * size, size), size)


def prepare_body(
    info, wq, wp, w1, qe, fe, pr, fr, first, c1, o_qe, o_fe, o_pr, o_fr, sem
):
    half = info[8]
    a = jnp.where(info[5] == 0, info[32], info[33])
    rows = rows_at(half, 128)
    pairs = [(wq.at[rows], first.at[:, 0:768]), (wp.at[rows], first.at[:, 768:1024])]
    pairs += [(qe.at[a, :, lanes_at(info[6] * 768, 768)], o_qe)]
    pairs += [(fe.at[a, :, lanes_at(info[6] * 1024, 1024)], o_fe)]
    pairs += [(pr.at[a], o_pr), (fr.at[a], o_fr)]
    for j in range(ROWS):
        pairs += [(w1.at[rows], c1.at[j])]
    copies = [pltpu.make_async_copy(x, y, sem.at[i]) for i, (x, y) in enumerate(pairs)]
    for copy in copies:
        copy.start()
    for copy in copies:
        copy.wait()


def assemble_body(info, own_q, own_p, z1, z2, z3, s1, s2, s3, ws, wp, sem):
    half = info[8]
    copies = [
        pltpu.make_async_copy(own_q, ws.at[0], sem.at[0]),
        pltpu.make_async_copy(own_p, wp.at[0], sem.at[1]),
    ]
    for k, (zv, sv) in enumerate(((z1, s1), (z2, s2), (z3, s3))):
        for n, (v, at) in enumerate(((zv, half), (sv, 1 - half))):
            rows = rows_at(at, 128)
            at = 2 + 4 * k + 2 * n
            copies.append(
                pltpu.make_async_copy(v.at[:, 0:768], ws.at[k + 1, rows], sem.at[at])
            )
            copies.append(
                pltpu.make_async_copy(v.at[:, 768:1024], wp.at[k + 1, rows], sem.at[at + 1])
            )
    for copy in copies:
        copy.start()
    for copy in copies:
        copy.wait()


def qkv_body(
    info, x0, x1, x2, x3, ws, p0, p1, p2, p3, bias, expand, q, kvp, kvc
):
    ps = (p0, p1, p2, p3)
    low = low_lanes(TOK)
    for b, x in enumerate((x0, x1, x2, x3)):
        y, c = slab_rows(info, b)
        acc = sum(nn(x[:, cols(k)], ws[k]) for k in range(4))
        u = bf(sum(nt(x[:, cols(k)], ps[k][272:288, :]) for k in range(4)))
        acc = acc + f32(bias[...]) + SCALE * nn(u, expand[...])
        kv = []
        for pair in range(2):
            at = 384 * pair
            g0, g1, g2 = (acc[:, at + 128 * i : at + 128 * i + 128] for i in range(3))
            q[rows_at(y * 2 + c, TOK), cols(pair, 128)] = bf(
                bf(jnp.where(low, g0, g1)) * BF(0.125)
            )
            kv.append((bf(pltpu.roll(jnp.where(low, g2, g0), 64, 1)), bf(jnp.where(low, g1, g2))))
        rows = rows_at(c, TOK)

        @pl.when(y == 0)
        def _():
            for pair in range(2):
                kvp[rows, cols(pair, 128)] = kv[pair][0]
                kvp[rows, cols(2 + pair, 128)] = kv[pair][1]

        @pl.when(y == 1)
        def _():
            for pair in range(2):
                kvc[rows, cols(pair, 128)] = kv[pair][0]
                kvc[rows, cols(2 + pair, 128)] = kv[pair][1]


WIDE = 256


def stacked(v, low):
    zero = jnp.zeros_like(v)
    return jnp.concatenate([jnp.where(low, v, zero), jnp.where(low, zero, v)], axis=0)


def split_id(shape, axis):
    lane = lax.broadcasted_iota(jnp.int32, shape, axis)
    return lane, jnp.where(lane < BLOCK, lane, lane - BLOCK)


def chunk_place(shape, axis, side, n):
    lane, within = split_id(shape, axis)
    first = block_at(side, n, 0) * BLOCK
    second = block_at(side, n, 1) * BLOCK
    return within + jnp.where(lane < BLOCK, first, second)


def keep_state(state, low):
    top, total, acc = state
    lane = lax.broadcasted_iota(jnp.int32, (2 * BLOCK, 128), 1)
    spot = lax.rem(lane, HEAD)
    row = lax.broadcasted_iota(jnp.int32, (2 * BLOCK, 128), 0)
    own = (lane < HEAD) == (row < BLOCK)
    return jnp.where(own, acc, jnp.where(spot == 0, top, total))


def load_state(v):
    lane = lax.broadcasted_iota(jnp.int32, (2 * BLOCK, 128), 1)
    row = lax.broadcasted_iota(jnp.int32, (2 * BLOCK, 128), 0)
    spot = jnp.where(row < BLOCK, HEAD, 0)
    top = jnp.max(jnp.where(lane == spot, v, LOW), axis=1, keepdims=True)
    total = jnp.sum(jnp.where(lane == spot + 1, v, 0.0), axis=1, keepdims=True)
    return top, total, v


def soft_update(state, s, v):
    if state is None:
        top = jnp.max(s, axis=1, keepdims=True)
        p = jnp.exp(s - top)
        return top, jnp.sum(p, axis=1, keepdims=True), nn(bf(p), v)
    top, total, acc = state
    new = jnp.maximum(top, jnp.max(s, axis=1, keepdims=True))
    p = jnp.exp(s - new)
    shrink = jnp.exp(top - new)
    total = total * shrink + jnp.sum(p, axis=1, keepdims=True)
    return new, total, acc * shrink + nn(bf(p), v)


def head_slopes(slopes, shape, axis):
    lane = lax.broadcasted_iota(jnp.int32, shape, axis)
    return [
        jnp.where(lane < BLOCK, slopes[2 * pair], slopes[2 * pair + 1]) for pair in range(2)
    ]


def attend_chunk(q2, states, kv, rows, place, base, slope, spot, masked):
    res = []
    away = place - base
    for pair in range(2):
        s = nt(q2[pair], kv[rows, cols(pair, 128)]) + slope[pair] * away.astype(F32)
        if masked:
            s = jnp.where(away <= spot, s, LOW)
        res.append(soft_update(states[pair], s, kv[rows, cols(2 + pair, 128)]))
    return res


def attend_first_body(info, slopes, q, kvp, kvc, state):
    zl = info[4]
    low = low_lanes(BLOCK)
    _, spot = split_id((2 * BLOCK, 1), 0)
    slope = head_slopes(slopes, (2 * BLOCK, 1), 0)
    places = [chunk_place((1, WIDE), 1, zl, n) for n in range(2)]

    def load(i):
        return [stacked(q[rows_at(i, BLOCK), cols(pair, 128)], low) for pair in range(2)]

    def save(states, i):
        for pair in range(2):
            state[rows_at(i, WIDE), cols(pair, 128)] = keep_state(states[pair], low)

    def prompt_block(j, _):
        for n in range(2):
            i = 2 * n + j
            base = block_at(zl, n, j) * BLOCK
            q2 = load(i)
            states = [None, None]
            for m in range(n, -1, -1):
                states = attend_chunk(
                    q2, states, kvp, pl.ds(m * WIDE, WIDE), places[m], base, slope, spot, m == n
                )
            save(states, i)
        return 0

    lax.fori_loop(0, 2, prompt_block, 0)

    def cont_block(j, _):
        q2 = load(4 + j)
        own_place = lax.broadcasted_iota(jnp.int32, (1, BLOCK), 1)
        states = attend_chunk(
            q2, [None, None], kvc, rows_at(j, BLOCK), own_place, 0, slope, spot, True
        )
        for m in range(2):
            states = attend_chunk(
                q2, states, kvp, pl.ds(m * WIDE, WIDE), places[m], PROMPT, slope, spot, False
            )
        save(states, 4 + j)
        return 0

    lax.fori_loop(0, 4, cont_block, 0)


def attend_rest_body(
    which, info, slopes, q, kvo, state, ws, reduce, p0, p1, p2, p3, heads, lse, o0, o1
):
    zl = info[4]
    y = info[1] if which == 0 else 1 - info[1]
    low = low_lanes(BLOCK)
    _, spot = split_id((2 * BLOCK, 1), 0)
    slope = head_slopes(slopes, (2 * BLOCK, 1), 0)
    places = [chunk_place((1, WIDE), 1, 1 - zl, n) for n in range(2)]

    def load(i):
        q2 = [stacked(q[rows_at(i, BLOCK), cols(pair, 128)], low) for pair in range(2)]
        states = [load_state(state[rows_at(i, WIDE), cols(pair, 128)]) for pair in range(2)]
        return q2, states

    def finish(states, j):
        for pair in range(2):
            top, total, acc = states[pair]
            res = acc / total
            heads[rows_at(j, BLOCK), cols(pair, 128)] = bf(
                jnp.where(low, res[:BLOCK], res[BLOCK:])
            )
            kept = jnp.transpose(jnp.broadcast_to(top + jnp.log(total), (2 * BLOCK, 128)))
            lse[pl.ds(pair * 4 + j, 1), :] = kept[0:1, :]

    @pl.when(y == 0)
    def _():
        def prompt_block(j, _):
            for n in range(2):
                i = 2 * n + j
                base = block_at(zl, n, j) * BLOCK
                q2, states = load(i)
                for m in range(n + 1):
                    states = attend_chunk(
                        q2, states, kvo, pl.ds(m * WIDE, WIDE), places[m], base, slope, spot, m == n
                    )
                finish(states, i)
            return 0

        lax.fori_loop(0, 2, prompt_block, 0)

    @pl.when(y == 1)
    def _():
        def cont_block(j, _):
            q2, states = load(4 + j)
            for m in range(2):
                states = attend_chunk(
                    q2, states, kvo, pl.ds(m * WIDE, WIDE), places[m], PROMPT, slope, spot, False
                )
            finish(states, j)
            return 0

        lax.fori_loop(0, 4, cont_block, 0)

    ps = (p0, p1, p2, p3)
    for b, dst in enumerate((o0, o1)):
        c = jnp.bitwise_xor(info[2], b)
        h = heads[rows_at(c, TOK), :]
        u = bf(nt(h, reduce[...]))
        for k in range(4):
            dst[:, cols(k)] = bf(nn(h, ws[k]) + SCALE * nn(u, ps[k][304:320, :]))


def mlp_pre_body(info, x0, x1, w1, p0, p1, p2, p3, bias, expand, act, slope):
    ps = (p0, p1, p2, p3)
    for b, x in enumerate((x0, x1)):
        u = bf(sum(nt(x[:, cols(k)], ps[k][288:304, :]) for k in range(4)))
        pre = sum(nn(x[:, cols(k)], w1[rel(info, k)]) for k in range(4))
        pre = pre + f32(bias[...]) + SCALE * nn(u, expand[...])
        sq = pre * pre
        t = jnp.tanh(pre * (GELU_A + (GELU_A * GELU_B) * sq))
        half = 0.5 + 0.5 * t
        act[b] = bf(pre * half)
        slope[b] = bf(
            half + (0.5 * pre) * (1.0 - t * t) * (GELU_A + (3.0 * GELU_A * GELU_B) * sq)
        )


def mlp_back_body(
    info, x0, x1, g0, g1, slope, w1, w2, p0, p1, p2, p3, expand, reduce, r_in, e_in,
    d0, d1, r_out, e_out,
):
    ps = (p0, p1, p2, p3)
    rv, ev = r_in[...], e_in[...]
    for b, (x, g, dx) in enumerate(((x0, g0, d0), (x1, g1, d1))):
        u = bf(sum(nt(x[:, cols(k)], ps[k][288:304, :]) for k in range(4)))
        du2 = bf(SCALE * sum(nt(g[:, cols(k)], ps[k][320:336, :]) for k in range(4)))
        d_act = sum(nt(g[:, cols(k)], w2[rel(info, k)]) for k in range(4)) + nn(du2, reduce[...])
        d_pre = bf(d_act * f32(slope[b]))
        du = bf(SCALE * nt(d_pre, expand[...]))
        for k in range(4):
            dx[:, cols(k)] = bf(nt(d_pre, w1[rel(info, k)]) + nn(du, ps[k][288:304, :]))
        rv = rv + tn(du, x[...])
        ev = ev + tn(u, d_pre)
    r_out[...] = rv
    e_out[...] = ev


def fc2_body(
    info, a0, a1, g0, g1, g2, g3, w2, reduce, p0, p1, p2, p3, r1, e1,
    m0, m1, m2, m3, grads,
):
    ps = (p0, p1, p2, p3)
    rv = ev = 0.0
    for b, (g, m) in enumerate(zip((g0, g1, g2, g3), (m0, m1, m2, m3))):
        act = a0[b] if b < 2 else a1[b - 2]
        du = bf(SCALE * sum(nt(g[:, cols(k)], ps[k][320:336, :]) for k in range(4)))
        u = bf(nt(act, reduce[...]))
        for k in range(4):
            m[:, cols(k)] = bf(nn(act, w2[rel(info, k)]) + SCALE * nn(u, ps[k][320:336, :]))
        rv = rv + tn(du, act)
        ev = ev + SCALE * tn(u, g[...])
    for k in range(4):
        grads[0:16, rel_cols(info, k)] = bf(r1[:, cols(k)])
        grads[16:32, rel_cols(info, k)] = bf(ev[:, k * TOK : k * TOK + TOK])
    grads[32:48, :] = bf(SCALE * e1[...])
    grads[48:64, :] = bf(rv)


def d_heads_body(
    info, g0, g1, ws, p0, p1, p2, p3, reduce, heads, r_in, e_in, dh, r_out, e_out
):
    ps = (p0, p1, p2, p3)
    rv, ev = r_in[...], e_in[...]
    for b, g in enumerate((g0, g1)):
        rows = rows_at(jnp.bitwise_xor(info[2], b), TOK)
        h = heads[rows, :]
        u = bf(nt(h, reduce[...]))
        du = bf(SCALE * sum(nt(g[0:256, cols(k)], ps[k][304:320, :]) for k in range(4)))
        v = sum(nt(g[0:256, cols(k)], ws[k]) for k in range(4)) + nn(du, reduce[...])
        dh[rows, :] = bf(v)
        rv = rv + tn(du, h)
        ev = ev + SCALE * tn(u, g[0:256, :])
    r_out[...] = rv
    e_out[...] = ev


def back_load(heads, d_heads, lse, q, qi, j, low):
    res = []
    for pair in range(2):
        lane = cols(pair, 128)
        q2 = stacked(q[rows_at(qi, BLOCK), lane], low)
        do = d_heads[rows_at(j, BLOCK), lane]
        both = jnp.transpose(f32(do) * f32(heads[rows_at(j, BLOCK), lane]))
        delta = jnp.concatenate(
            [
                jnp.sum(both[:HEAD], axis=0, keepdims=True),
                jnp.sum(both[HEAD:], axis=0, keepdims=True),
            ],
            axis=1,
        )
        res.append((q2, stacked(do, low), delta, lse[pl.ds(pair * 4 + j, 1), :]))
    return res


def back_chunk(args, kv, d_kv, d_at, rows, place, base, slope, spot, masked, store, d_qs):
    away = place - base
    res = []
    for pair in range(2):
        q2, do2, delta, kept = args[pair]
        lane = cols(pair, 128)
        vlane = cols(2 + pair, 128)
        k = kv[rows, lane]
        s = nt(k, q2) + (away.astype(F32) * slope[pair] - kept)
        p = jnp.exp(s)
        if masked:
            p = jnp.where(away <= spot, p, 0.0)
        ds = bf(p * (nt(kv[rows, vlane], do2) - delta))
        dk = nn(ds, q2)
        dv = nn(bf(p), do2)
        if store:
            d_kv[d_at, lane] = bf(dk)
            d_kv[d_at, vlane] = bf(dv)
        else:
            d_kv[d_at, lane] += dk
            d_kv[d_at, vlane] += dv
        d_q = tn(ds, k)
        res.append(d_q if d_qs is None else d_qs[pair] + d_q)
    return res


def back_common(info, slopes):
    low = low_lanes(BLOCK)
    _, spot = split_id((1, 2 * BLOCK), 1)
    slope = head_slopes(slopes, (1, 2 * BLOCK), 1)
    zl = info[4]
    own = [chunk_place((WIDE, 1), 0, zl, n) for n in range(2)]
    oth = [chunk_place((WIDE, 1), 0, 1 - zl, n) for n in range(2)]
    return zl, low, spot, slope, own, oth


def fold(d_q, low):
    return jnp.where(low, d_q[:BLOCK], d_q[BLOCK:]) * 0.125


def back_sweep(info, slopes, y, q, heads, d_heads, lse, sides, kvc, dkc, finish):
    zl, low, spot, slope, own, oth = back_common(info, slopes)
    place_sets = {"own": own, "oth": oth}

    @pl.when(y == 0)
    def _():
        def prompt_block(j, _):
            for n in range(2):
                i = 2 * n + j
                args = back_load(heads, d_heads, lse, q, i, i, low)
                base = block_at(zl, n, j) * BLOCK
                d_qs = None
                for side, kv, d_kv in sides:
                    for m in range(n + 1):
                        rows = pl.ds(m * WIDE, WIDE)
                        d_qs = back_chunk(
                            args, kv, d_kv, rows, rows, place_sets[side][m], base, slope, spot,
                            m == n, False, d_qs,
                        )
                finish(d_qs, i, low)
            return 0

        lax.fori_loop(0, 2, prompt_block, 0)

    @pl.when(y == 1)
    def _():
        def cont_block(j, _):
            args = back_load(heads, d_heads, lse, q, 4 + j, j, low)
            d_qs = None
            if kvc is not None:
                mine = rows_at(j, BLOCK)
                own_place = lax.broadcasted_iota(jnp.int32, (BLOCK, 1), 0)
                d_qs = back_chunk(
                    args, kvc, dkc, mine, mine, own_place, 0, slope, spot, True, True, d_qs
                )
            for side, kv, d_kv in sides:
                for m in range(2):
                    rows = pl.ds(m * WIDE, WIDE)
                    d_qs = back_chunk(
                        args, kv, d_kv, rows, rows, place_sets[side][m], PROMPT, slope, spot,
                        False, False, d_qs,
                    )
            finish(d_qs, j, low)
            return 0

        lax.fori_loop(0, 4, cont_block, 0)


def attend_back_a_body(
    info, slopes, q, kvp, kvo, kvc, heads, d_heads, lse, dq, dkp, dko, dkc
):
    dkp[...] = jnp.zeros_like(dkp)
    dko[...] = jnp.zeros_like(dko)
    dkc[...] = jnp.zeros_like(dkc)

    def finish(d_qs, j, low):
        for pair in range(2):
            dq[rows_at(j, BLOCK), cols(pair, 128)] = bf(fold(d_qs[pair], low))

    back_sweep(
        info, slopes, info[1], q, heads, d_heads, lse,
        (("own", kvp, dkp), ("oth", kvo, dko)), kvc, dkc, finish,
    )


def attend_back_b_body(
    info, slopes, q, kvo, heads, d_heads, lse, dko_in, early, dq, dko, acc
):
    acc[...] = dko_in[...]

    def finish(d_qs, j, low):
        for pair in range(2):
            dq[rows_at(j, BLOCK), cols(pair, 128)] = fold(d_qs[pair], low)

    back_sweep(
        info, slopes, 1 - info[1], q, heads, d_heads, lse,
        (("oth", kvo, acc),), None, None, finish,
    )
    dko[0:512, :] = bf(acc[...])
    dko[512:592, :] = early[:, 0:512]
    dko[592:672, :] = early[:, 512:1024]


def early_sum_body(own, other, dst):
    dst[:, 0:512] = bf(f32(own[:, 0:512]) + f32(other[512:592, :]))
    dst[:, 512:1024] = bf(f32(own[:, 512:1024]) + f32(other[592:672, :]))


def attend_back_c_body(
    info, slopes, q, kvp, kvc, heads, d_heads, lse, dkp_in, dkc_in, dq_in, dq, dkp, dkc
):
    dkp[...] = dkp_in[...]
    dkc[...] = dkc_in[...]

    def finish(d_qs, j, low):
        for pair in range(2):
            lane = cols(pair, 128)
            rows = rows_at(j, BLOCK)
            dq[rows, lane] = bf(dq_in[rows, lane] + fold(d_qs[pair], low))

    back_sweep(
        info, slopes, 1 - info[1], q, heads, d_heads, lse,
        (("own", kvp, dkp),), kvc, dkc, finish,
    )


def qkv_back_body(
    info, dq0, dq1, dkp, dkr, dkc, x0, x1, x2, x3, ws, p0, p1, p2, p3, expand, pr, pe,
    o0, o1, o2, o3, grads,
):
    ps = (p0, p1, p2, p3)
    low = low_lanes(TOK)
    sr = se = 0.0
    for b, (x, dst) in enumerate(zip((x0, x1, x2, x3), (o0, o1, o2, o3))):
        y, c = slab_rows(info, b)
        half = rows_at(c, TOK)
        groups = []
        dq = dq0 if b < 2 else dq1
        for pair in range(2):
            vq = f32(dq[half, cols(pair, 128)])
            got = []
            for lane in (cols(pair, 128), cols(2 + pair, 128)):
                prompt = dkp[half, lane] + f32(dkr[half, lane])
                got.append(jnp.where(y == 0, prompt, f32(dkc[half, lane])))
            vk = pltpu.roll(got[0], 64, 1)
            vv = got[1]
            groups += [jnp.where(low, vq, vk), jnp.where(low, vv, vq), jnp.where(low, vk, vv)]
        d = bf(jnp.concatenate(groups, axis=1))
        u = bf(sum(nt(x[:, cols(k)], ps[k][272:288, :]) for k in range(4)))
        du = bf(SCALE * nt(d, expand[...]))
        for k in range(4):
            dst[:, cols(k)] = bf(nt(d, ws[k]) + nn(du, ps[k][272:288, :]))
        sr = sr + tn(du, x[...])
        se = se + SCALE * tn(u, d)
    for k in range(4):
        grads[0:16, rel_cols(info, k)] = bf(sr[:, k * TOK : k * TOK + TOK])
        grads[16:32, rel_cols(info, k)] = bf(pe[:, cols(k)])
    grads[32:48, 0:768] = bf(se)
    grads[32:48, 768:1024] = bf(pr[...])


def add_body(a, b, dst):
    dst[...] = bf(f32(a[...]) + f32(b[...]))


def add(a, b):
    return call(add_body, [out(a.shape, BF)], [a, b], smem=0, us=0.01, name="add")[0]


def add32_body(a, b, dst):
    dst[...] = f32(a[...]) + f32(b[...])


def add32(a, b, us=8):
    return call(add32_body, [out(a.shape, F32)], [a, b], smem=0, us=us, name="add32")[0]


def stage_body(*refs):
    n = len(refs) // 2
    for src, dst in zip(refs[:n], refs[n:]):
        dst[...] = src[...]


def stage(values):
    return call(
        stage_body, [out(v.shape, v.dtype) for v in values], far(values), smem=0, us=0.01, name="stage"
    )


def stage_weight_body(size, info, own, wr, ws, w, sem):
    copies = [pltpu.make_async_copy(own, w.at[info[0]], sem.at[6])]
    for n, (src, at) in enumerate(((wr, info[8]), (ws, 1 - info[8]))):
        for k in range(1, ROWS):
            to = w.at[rel(info, k), rows_at(at, size)]
            copies.append(pltpu.make_async_copy(src.at[k - 1], to, sem.at[3 * n + k - 1]))
    for copy in copies:
        copy.start()
    for copy in copies:
        copy.wait()


def merge_body(info, v0, v1, v2, v3, dst):
    four = (v0, v1, v2, v3)

    def fill(c):
        total = sum(f32(v[256 + 16 * c : 272 + 16 * c, :]) for v in four)
        dst[0:16, :] = bf(total)
        for b, v in enumerate(four):
            rows = pl.ds(pl.multiple_of(16 + 16 * jnp.bitwise_xor(info[6], b), 16), 16)
            dst[rows, :] = v[288 + 16 * c : 304 + 16 * c, :]

    @pl.when(info[2] == 0)
    def _():
        fill(0)

    @pl.when(info[2] == 1)
    def _():
        fill(1)


def pile_body(*refs):
    dst = refs[-1]
    for n, src in enumerate(refs[:-1]):
        dst[n] = src[...]


def expand_early_body(info, own, oth, r1, e2, e1, r2):
    for v in (r1, e2, e1, r2):
        v[...] = jnp.zeros_like(v)

    def fill(src, shared, split):
        for n in range(own.shape[0]):
            group = info[5] if n % 2 == 0 else 1 - info[5]
            a = info[40 + n // 2 * GROUPS_DEV + group]
            shared[a] += f32(src[n, 0:16, :])
            for j in range(COLS):
                at = 16 + 16 * j
                split[a, :, cols(j, 1024)] += f32(src[n, at : at + 16, :])

    @pl.when(info[2] == 0)
    def _():
        fill(own, r1, e1)
        fill(oth, e2, r2)

    @pl.when(info[2] == 1)
    def _():
        fill(oth, r1, e1)
        fill(own, e2, r2)


def expand_late_body(info, v0, v1, v2, v3, qr, pe, qe, pr):
    four = (v0, v1, v2, v3)
    for v in (qr, pe, qe, pr):
        v[...] = jnp.zeros_like(v)
    for k in range(v0.shape[0]):
        group = info[5] if k % 2 == 0 else 1 - info[5]
        a = info[40 + k // 2 * GROUPS_DEV + group]
        qr[a] += sum(f32(v[k, 0:16, :]) for v in four)
        pe[a] += sum(f32(v[k, 16:32, :]) for v in four)
        for b, v in enumerate(four):
            j = jnp.bitwise_xor(info[6], b)
            qe[a, :, lanes_at(j * 768, 768)] += f32(v[k, 32:48, :768])
            pr[a, :, lanes_at(j * 256, 256)] += f32(v[k, 32:48, 768:])


def shift(v, k, axis="row"):
    if k == 0:
        return v
    size = lax.axis_size(axis)
    return lax.ppermute(v, axis, [(s, (s + k) % size) for s in range(size)])


def gather_row(v):
    return [v] + [shift(v, k) for k in range(1, ROWS)]


def gather_col(v):
    core = lax.ppermute(v, "col", CORE_SWAP)
    side = lax.ppermute(v, "col", Y_SWAP)
    return [v, core, side, lax.ppermute(side, "col", CORE_SWAP)]


def to_cols(pieces):
    return [pieces[0]] + [shift(pieces[k], ROWS - k) for k in range(1, ROWS)]


def spread(mine, other):
    return [mine, other] + [
        shift(v, k, "dp") for k in range(1, lax.axis_size("dp")) for v in (mine, other)
    ]


def pile(parts):
    shape = (len(parts), *parts[0].shape)
    return call(pile_body, [out(shape, BF)], parts, smem=0, us=0.01, name="pile")[0]

def body(
    hidden_in,
    out_grad,
    first_norm_gain,
    first_norm_bias,
    qkv_weight,
    qkv_bias,
    proj_weight,
    proj_bias,
    second_norm_gain,
    second_norm_bias,
    fc1_weight,
    fc1_bias,
    fc2_weight,
    second_feed_bias,
    qkv_reduce,
    qkv_expand,
    proj_reduce,
    proj_expand,
    fc1_reduce,
    fc1_expand,
    fc2_reduce,
    fc2_expand,
    adapter_choice,
    cont_prompt,
):
    r = lax.axis_index("row")
    col = lax.axis_index("col")
    dp = lax.axis_index("dp")
    y = col // 2
    c = lax.rem(col, 2)
    zl = lax.rem(r, 2)
    group = r // 2
    half = lax.rem(dp, 2)
    dp_swap = [(k, k ^ 1) for k in range(lax.axis_size("dp"))]
    slopes = jnp.exp2(
        -8.0 * (col * 4 + 1 + jnp.arange(4, dtype=jnp.int32)).astype(F32) / HEADS
    )
    adapter = jnp.where(group == 0, adapter_choice[0], adapter_choice[1])
    dp_size = jnp.int32(lax.axis_size("dp"))
    info = jnp.stack([r, y, c, dp * GROUPS_DEV, zl, group, col, dp, half] + [half, dp_size] + [half] * 5)
    info = jnp.concatenate([info.astype(jnp.int32), cont_prompt, adapter_choice])
    order = pltpu.SMEM((GROUPS_DEV * NCONT,), jnp.int32)
    flip = functools.partial(jnp.transpose, axes=(0, 2, 1))
    big = out((TOK, D), BF)
    small = out((RANK, D), F32)

    other = lax.ppermute(hidden_in, "col", CORE_SWAP)
    vectors = [
        first_norm_gain, first_norm_bias, proj_bias,
        second_norm_gain, second_norm_bias, second_feed_bias,
    ]
    factors = [flip(qkv_reduce), flip(fc1_reduce), proj_expand, fc2_expand]
    pieces = call(
        route_pack_body,
        [out((336, TOK), BF)] * 4,
        [info, Far(hidden_in), Far(other), *far(vectors), *far(factors)],
        [
            order,
            *[pltpu.VMEM((TOK,), BF)] * 6,
            pltpu.VMEM((16, RANK, TOK), BF),
            pltpu.SemaphoreType.DMA((22,)),
        ],
        raw=range(3, 13),
        us=1.5,
        name="route_x",
    )
    xs = [pieces[0]] + [shift(pieces[k], k) for k in range(1, ROWS)]
    packs = far(xs)
    first_half, w1_copies, qkv_e, fc1_e, proj_r, fc2_r = call(
        prepare_body,
        [
            out((128, D), BF), out((ROWS, 128, D), BF),
            out((RANK, 768), BF), out((RANK, D), BF), out((RANK, TOK), BF), out((RANK, D), BF),
        ],
        [
            after(info, pieces[0]),
            *far([qkv_weight, proj_weight, fc1_weight, qkv_expand, fc1_expand]),
            *far([flip(proj_reduce), flip(fc2_reduce)]),
        ],
        [pltpu.SemaphoreType.DMA((10,))],
        raw=range(1, 8),
        us=3,
        name="prepare",
    )
    first_half = after(first_half, xs[1])
    z_parts = [shift(first_half, k) for k in range(1, ROWS)]
    s_parts = [lax.ppermute(v, "dp", dp_swap) for v in z_parts]
    wq, wp = call(
        assemble_body,
        [out((ROWS, TOK, 768), BF), out((ROWS, TOK, TOK), BF)],
        [info, *far([qkv_weight, proj_weight, *z_parts, *s_parts])],
        [pltpu.SemaphoreType.DMA((14,))],
        raw=range(1, 9),
        us=15,
        name="assemble",
    )

    qkv_b = lax.dynamic_slice_in_dim(qkv_bias, col * 768, 768, 0)[None, :]
    fc1_b = lax.dynamic_slice_in_dim(fc1_bias, col * 1024, 1024, 0)[None, :]

    choices = [adapter_choice] + [
        shift(adapter_choice, k, "dp") for k in range(1, lax.axis_size("dp"))
    ]
    first = after(xs[0], qkv_b, fc1_b, w1_copies, *choices)
    (xn1,) = call(norm1_body, [big], [first, *xs[1:]], smem=0, us=8, name="norm1")
    xn1s = gather_col(xn1)
    q, kvp, kvc = call(
        qkv_body,
        [out((1024, 256), BF), out((512, 512), BF), out((512, 512), BF)],
        [info, *xn1s, wq, *packs, Far(qkv_b), Far(qkv_e)],
        us=6.5,
        name="qkv",
    )
    kvo = lax.ppermute(kvp, "row", Z_SWAP)

    g_other = lax.ppermute(after(out_grad, kvp), "col", CORE_SWAP)
    (pieces,) = call(
        route_all_body,
        [out((ROWS, 3 * TOK, TOK), BF)],
        [info, Far(out_grad), Far(g_other), Far(fc2_weight)],
        [order, pltpu.SemaphoreType.DMA((4,))],
        raw=(3,),
        us=1,
        name="route_g",
    )
    (state,) = call(
        attend_first_body,
        [out((2048, 256), F32)],
        [info, slopes, q, kvp, kvc],
        smem=2,
        us=9,
        name="attend_first",
    )
    (w1r,) = call(
        rest_body,
        [out((3, 128, D), BF)],
        [info, after(lax.all_to_all(after(w1_copies, *z_parts), "row", 0, 0), state)],
        us=0.01,
        name="rest",
    )
    w1s = lax.ppermute(w1r, "dp", dp_swap)
    pieces = after(pieces, state, kvo)
    g_own, w2r = call(
        join_body,
        [big, out((3, 512, TOK), BF)],
        [info, lax.all_to_all(pieces, "row", 0, 0)],
        us=0.01,
        name="join",
    )
    g_side = lax.ppermute(g_own, "col", Y_SWAP)
    w2s = lax.ppermute(w2r, "dp", dp_swap)

    def attend_rest(which, q, state):
        return call(
            functools.partial(attend_rest_body, which),
            [out((512, 256), BF), out((8, 256), F32), big, big],
            [info, slopes, Far(q), kvo, state, Far(wp), Far(proj_r), *packs],
            smem=2,
            us=20 if which else 0.01,
            name="attend_rest",
        )

    heads1, lse1, p2, p3 = attend_rest(1, q, after(state, w1r))
    g_core = lax.ppermute(g_own, "col", CORE_SWAP)
    g_all = [g_own, g_core, g_side, lax.ppermute(g_side, "col", CORE_SWAP)]
    p_far = lax.ppermute(p3, "col", CORE_SWAP)
    p_side = add(p2, p_far)
    heads0, lse0, p0, p1 = attend_rest(0, q, Far(after(state, p_side)))
    p_side = lax.ppermute(p_side, "col", Y_SWAP)
    p_core = lax.ppermute(p1, "col", CORE_SWAP)
    staged = stage([after(xs[0], p0), *xs[1:]])
    mid, xn2 = call(
        norm2_body,
        [out((TOK, D), F32), big],
        [add32(after(p0, w1s), p_side), p_core, *staged],
        smem=0,
        us=1.5,
        hbm=(0,),
        name="norm2",
    )
    (w1,) = call(
        functools.partial(stage_weight_body, 128),
        [out((ROWS, TOK, D), BF)],
        [info, Far(fc1_weight), Far(after(w1r, p0)), Far(w1s)],
        [pltpu.SemaphoreType.DMA((7,))],
        raw=(1, 2, 3),
        us=2,
        name="stage_w1",
    )
    zero = jnp.zeros((RANK, D), F32)
    xn2_core = lax.ppermute(xn2, "col", CORE_SWAP)
    xn2_side = lax.ppermute(xn2, "col", Y_SWAP)

    def mlp_pre(first, blocks):
        return call(
            mlp_pre_body,
            [out((2, TOK, D), BF)] * 2,
            [info, *blocks, w1, *staged, Far(fc1_b), Far(fc1_e)],
            us=0.01,
            name="mlp_pre",
        )

    act0, slope0 = mlp_pre(0, [xn2, xn2_core])
    xn2_far = lax.ppermute(after(xn2_side, act0), "col", CORE_SWAP)
    xn2s = [xn2, xn2_core, xn2_side, xn2_far]
    act1, slope1 = mlp_pre(1, xn2s[2:])
    (w2,) = call(
        functools.partial(stage_weight_body, 512),
        [out((ROWS, D, TOK), BF)],
        [info, Far(fc2_weight), Far(after(w2r, act0)), Far(w2s)],
        [pltpu.SemaphoreType.DMA((7,))],
        raw=(1, 2, 3),
        us=20,
        name="stage_w2",
    )

    def mlp_back(blocks, slope, r_in, e_in):
        xa, xb = (xn2s[b] for b in blocks)
        ga, gb = (g_all[b] for b in blocks)
        return call(
            mlp_back_body,
            [big, big, small, small],
            [info, xa, xb, ga, gb, slope, w1, w2, *staged, Far(fc1_e), Far(fc2_r), r_in, e_in],
            us=0.01,
            name="mlp_back",
        )

    d2, d3, r1, e1 = mlp_back((2, 3), slope1, zero, zero)
    d_far = lax.ppermute(d3, "col", CORE_SWAP)
    d_side = add(d2, d_far)
    d0, d1, r1, e1 = mlp_back((0, 1), slope0, after(r1, d_side), e1)
    d_side = lax.ppermute(d_side, "col", Y_SWAP)
    d_core = lax.ppermute(d1, "col", CORE_SWAP)
    res = call(
        fc2_body,
        [big] * 4 + [out((64, D), BF)],
        [info, act0, act1, *g_all, w2, Far(fc2_r), *staged, r1, e1],
        us=0.01,
        name="fc2",
    )
    m_parts, mlp_pack = res[:4], res[4]
    staged_back = stage([after(mid, mlp_pack), g_own, *xs])
    d_mid, g_attn = call(
        norm2_back_body,
        [out((TOK, D), F32), out((320, D), BF)],
        [add32(d0, d_side), d_core, mlp_pack, *staged_back],
        smem=0,
        us=1.5,
        hbm=(0,),
        name="norm2_back",
    )
    ga_core = lax.ppermute(g_attn, "col", CORE_SWAP)
    ga_side = lax.ppermute(g_attn, "col", Y_SWAP)
    shared = far([q, kvp, kvo, kvc])

    def d_heads(blocks, heads, r_in, e_in):
        return call(
            d_heads_body,
            [out((512, 256), BF), out((RANK, TOK), F32), small],
            [info, *blocks, Far(wp), *packs, Far(proj_r), Far(heads), r_in, e_in],
            us=1.5,
            name="d_heads",
        )

    dh0, pr, pe = d_heads([g_attn, ga_core], heads0, jnp.zeros((RANK, TOK), F32), zero)
    dq0, dkp, dko, dkc = call(
        attend_back_a_body,
        [out((512, 256), BF), out((512, 512), F32), out((512, 512), F32), out((512, 512), BF)],
        [info, slopes, *shared, Far(heads0), dh0, Far(lse0)],
        smem=2,
        us=16,
        weight=W_BIG,
        hbm=(1, 2, 3),
        name="attend_back_a",
    )
    ga_side = after(ga_side, dq0)
    ga_far = lax.ppermute(ga_side, "col", CORE_SWAP)
    (early_half,) = call(
        merge_body,
        [out((80, D), BF)],
        [info, g_attn, ga_core, ga_side, ga_far],
        us=0.7,
        name="merge",
    )
    dh1, pr, pe = d_heads([ga_side, ga_far], heads1, pr, pe)
    dq1_part, dko = call(
        attend_back_b_body,
        [out((512, 256), F32), out((672, 512), BF)],
        [info, slopes, Far(q), Far(kvo), Far(heads1), dh1, Far(lse1), Far(dko), early_half],
        [pltpu.VMEM((512, 512), F32)],
        smem=2,
        us=8,
        hbm=(0,),
        name="attend_back_b",
    )
    dkr = lax.ppermute(dko, "row", Z_SWAP)
    dq1, dkp, dkc = call(
        attend_back_c_body,
        [out((512, 256), BF), out((512, 512), F32), out((512, 512), BF)],
        [info, slopes, Far(q), Far(kvp), Far(kvc), Far(heads1), dh1, Far(lse1), *far([dkp, dkc, dq1_part])],
        smem=2,
        us=8,
        hbm=(2,),
        name="attend_back_c",
    )
    (early_sum,) = call(
        early_sum_body, [out((80, D), BF)], [early_half, dkr], smem=0, us=0.01, name="early_sum"
    )
    m_far = lax.ppermute(after(m_parts[3], dq0), "col", CORE_SWAP)
    m_core = lax.ppermute(after(m_parts[1], dq0), "col", CORE_SWAP)
    m_sum = add(after(m_parts[2], dko), m_far)
    m_side = lax.ppermute(m_sum, "col", Y_SWAP)
    hidden = call(
        hidden_body,
        [out((TOK, TOK), BF)] * 4,
        [add32(m_parts[0], m_side, 0.01), m_core, Far(mid), *packs],
        smem=0,
        us=0.01,
        name="hidden",
    )
    res = call(
        qkv_back_body,
        [big] * 4 + [out((48, D), BF)],
        [
            info, dq0, dq1, dkp, after(dkr, early_sum, hidden[0]), Far(dkc),
            *far(xn1s), Far(wq), *packs, Far(qkv_e), pr, pe,
        ],
        us=20,
        name="qkv_back",
    )
    q_parts, late_pack = res[:4], res[4]
    early_next = shift(early_sum, 2)
    n_dp = lax.axis_size("dp")
    early_mine = [early_sum] + [shift(early_sum, k, "dp") for k in range(1, n_dp)]
    ready = after(q_parts[3], m_side, early_next, *early_mine)
    q_sum = add(q_parts[2], lax.ppermute(ready, "col", CORE_SWAP))
    hidden_got = to_cols(hidden)
    k0, rc = q_parts[0], lax.ppermute(q_parts[1], "col", CORE_SWAP)
    ry = lax.ppermute(q_sum, "col", Y_SWAP)
    late_sum = add(late_pack, lax.ppermute(after(late_pack, q_sum), "row", Z_SWAP))
    late_next = shift(late_sum, 2)
    early_rest = after(early_next, late_sum)
    early_rest = [early_next] + [shift(early_rest, k, "dp") for k in range(1, n_dp)]
    early_parts = [v for pair in zip(early_mine, early_rest) for v in pair]
    late_four = pile(spread(late_sum, late_next))
    late_all = gather_col(late_four)
    staged_last = stage([after(d_mid, k0, rc), *xs])
    ins = call(
        norm1_back_body,
        [out((TOK, TOK), BF)] * 4,
        [add32(after(k0, late_next, *hidden_got), ry), rc, *staged_last],
        smem=0,
        us=1,
        name="norm1_back",
    )
    early_all = pile(early_parts)
    early_far = lax.ppermute(after(early_all, ins[0]), "col", CORE_SWAP)
    table = jnp.concatenate([info, jnp.zeros((40 - 34,), jnp.int32), *choices])
    o_fc1r, o_f2e, o_f1e, o_f2r = call(
        expand_early_body,
        [out((COUNT, RANK, w), F32) for w in (1024, 1024, 4096, 4096)],
        [table, Far(early_all), Far(early_far)],
        us=0.01,
        name="expand_early",
    )
    (joined,) = call(
        stack_body,
        [out((8 * TOK, TOK), BF)],
        [*[after(v, o_fc1r, late_all[2]) for v in to_cols(ins)], *hidden_got],
        smem=0,
        us=0.01,
        name="stack",
    )
    input_gradient, hidden_out = call(
        unroute_body,
        [out((1024, TOK), F32), out((1024, TOK), BF)],
        [info, joined, lax.ppermute(joined, "col", CORE_SWAP)],
        [order],
        us=2,
        name="unroute",
    )
    o_qr, o_pe, o_qe, o_pr = call(
        expand_late_body,
        [out((COUNT, RANK, w), F32) for w in (1024, 1024, 3072, 1024)],
        [table, *late_all],
        us=0.01,
        name="expand_late",
    )
    return (
        hidden_out,
        input_gradient,
        flip(o_qr),
        o_qe,
        flip(o_pr),
        o_pe,
        flip(o_fc1r),
        o_f1e,
        flip(o_f2r),
        o_f2e,
    )


def solution(mesh):
    placed = (
        P(("dp", "col"), "row"),
        P(("dp", "col"), "row"),
        P("row"),
        P("row"),
        P("row", "col"),
        P(),
        P("col", "row"),
        P("row"),
        P("row"),
        P("row"),
        P("row", "col"),
        P(),
        P("col", "row"),
        P("row"),
        P(None, "row", None),
        P(),
        P(None, "col", None),
        P(None, None, "row"),
        P(None, "row", None),
        P(),
        P(None, "col", None),
        P(None, None, "row"),
        P("dp"),
        P("dp"),
    )
    return jax.shard_map(
        body,
        mesh=mesh,
        in_specs=placed,
        out_specs=(P(("dp", "col"), "row"), P(("dp", "col"), "row")) + (P(),) * 8,
        check_vma=False,
    )
```

```python
import functools

import jax
import jax.numpy as jnp
from jax import lax
from jax.experimental import pallas as pl
from jax.experimental.pallas import tpu as pltpu
from jax.sharding import PartitionSpec as P

D = 1024
HEADS = 16
HEAD = 64
FF = 4096
RANK = 16
COUNT = 8
PROMPT = 1024
CONT = 128
NCONT = 8
GROUPS_DEV = 2

EPSILON = 1e-05
SCALE = 2.0
GELU_A = 0.7978845608028654
GELU_B = 0.044715
ROWS = 4
COLS = 4
TOK = 256
BLOCK = 128
LOW = -1e30
W_SMALL = 5e8
W_BIG = 5e8

BF = jnp.bfloat16
F32 = jnp.float32

VM = pl.BlockSpec(memory_space=pltpu.VMEM)
SM = pl.BlockSpec(memory_space=pltpu.SMEM)
HB = pl.BlockSpec(memory_space=pltpu.HBM)

CORE_SWAP = [(0, 1), (1, 0), (2, 3), (3, 2)]
Y_SWAP = [(0, 2), (2, 0), (1, 3), (3, 1)]
Z_SWAP = [(0, 1), (1, 0), (2, 3), (3, 2)]


def nn(a, b):
    return lax.dot_general(a, b, (((1,), (0,)), ((), ())), preferred_element_type=F32)


def nt(a, b):
    return lax.dot_general(a, b, (((1,), (1,)), ((), ())), preferred_element_type=F32)


def tn(a, b):
    return lax.dot_general(a, b, (((0,), (0,)), ((), ())), preferred_element_type=F32)


def f32(v):
    return v.astype(F32)


def bf(v):
    return v.astype(BF)


class Far:
    def __init__(self, value):
        self.value = value


def far(values):
    return [Far(v) for v in values]


def call(
    body, outs, ins, scratch=(), smem=1, limit=40, us=1, raw=(), weight=W_SMALL, hbm=(), name=None
):
    values = [
        pltpu.with_memory_space_constraint(v.value, pltpu.HBM) if isinstance(v, Far) else v
        for v in ins
    ]
    fetched = [i for i, v in enumerate(ins) if isinstance(v, Far) and i not in raw]
    specs = [SM] * smem
    for v in ins[smem:]:
        specs.append(HB if isinstance(v, Far) else VM)
    nbytes = sum(v.size * v.dtype.itemsize for v in values)
    nbytes += sum(o.size * o.dtype.itemsize for o in outs)
    extra = [pltpu.VMEM(values[i].shape, values[i].dtype) for i in fetched]
    extra += [pltpu.VMEM(outs[i].shape, outs[i].dtype) for i in hbm]
    moved = len(extra)
    if moved:
        extra.append(pltpu.SemaphoreType.DMA((moved,)))

    def whole(*refs):
        refs = list(refs)
        stores = []
        if moved:
            sem = refs[-1]
            buffers = refs[-1 - moved : -1]
            refs = refs[: -1 - moved]
            copies = []
            for n, i in enumerate(fetched):
                copies.append(pltpu.make_async_copy(refs[i], buffers[n], sem.at[n]))
                copies[-1].start()
                refs[i] = buffers[n]
            for n, i in enumerate(hbm, len(fetched)):
                at = len(values) + i
                stores.append(pltpu.make_async_copy(buffers[n], refs[at], sem.at[n]))
                refs[at] = buffers[n]
            for copy in copies:
                copy.wait()
        body(*refs)
        for copy in stores:
            copy.start()
        for copy in stores:
            copy.wait()

    return pl.pallas_call(
        whole,
        out_shape=tuple(
            pltpu.HBM(o.shape, o.dtype) if i in hbm else o for i, o in enumerate(outs)
        ),
        in_specs=specs,
        out_specs=tuple(HB if i in hbm else VM for i in range(len(outs))),
        scratch_shapes=list(scratch) + extra,
        compiler_params=pltpu.CompilerParams(vmem_limit_bytes=limit << 20),
        cost_estimate=pl.CostEstimate(
            flops=int(us * weight), bytes_accessed=nbytes // 8, transcendentals=0
        ),
        name=name,
    )(*values)


def after(value, *others):
    res = lax.optimization_barrier((value, others))
    return res[0]


def out(shape, dtype):
    return jax.ShapeDtypeStruct(shape, dtype)


def block_at(zl, c, j):
    return c * 4 + zl + j * (3 - 2 * zl)


def fill_order(info, order):
    base = info[3]
    first = jnp.int32(0)
    second = jnp.int32(NCONT)
    for j in range(GROUPS_DEV * NCONT):
        own = info[16 + j] == base
        slot = jnp.where(own, first, second)
        order[slot] = jnp.int32(j)
        first = first + jnp.where(own, 1, 0)
        second = second + jnp.where(own, 0, 1)


def place_of(info, order, z, core, j):
    prompt = (z // 2) * 8 + block_at(lax.rem(z, 2), core, j)
    cont = order[4 * z + 2 * core + j]
    return jnp.where(info[1] == 0, prompt, cont)


def route_body(info, own, oth, o0, o1, o2, o3, order):
    fill_order(info, order)
    c = info[2]
    for s, dst in enumerate((o0, o1, o2, o3)):
        z = lax.rem(info[0] + s, ROWS)
        for j in range(2):
            src = place_of(info, order, z, c, j)
            at = pl.ds(pl.multiple_of(lax.rem(src, 8) * BLOCK, BLOCK), BLOCK)
            mine = src // 8 == c

            @pl.when(mine)
            def _():
                dst[pl.ds(j * BLOCK, BLOCK), :] = own[at, :]

            @pl.when(jnp.logical_not(mine))
            def _():
                dst[pl.ds(j * BLOCK, BLOCK), :] = oth[at, :]


def route_pack_body(
    info, own, oth, g1, c1, pb, g2, c2, fb, qr, fr, pe, fe,
    o0, o1, o2, o3, order, v0, v1, v2, v3, v4, v5, mats, sem,
):
    vecs = (v0, v1, v2, v3, v4, v5)
    pairs = list(zip((g1, c1, pb, g2, c2, fb), vecs))
    for k in range(ROWS):
        which = lax.rem(info[0] + k, ROWS) // 2
        a = jnp.where(which == 0, info[32], info[33])
        pairs += [(v.at[a], mats.at[4 * k + i]) for i, v in enumerate((qr, fr, pe, fe))]
    copies = [pltpu.make_async_copy(a, b, sem.at[i]) for i, (a, b) in enumerate(pairs)]
    for copy in copies:
        copy.start()
    route_body(info, own, oth, o0, o1, o2, o3, order)
    for copy in copies:
        copy.wait()
    for k, dst in enumerate((o0, o1, o2, o3)):
        head = [f32(v[...]).reshape(1, TOK) for v in vecs]
        dst[256:272, :] = bf(jnp.concatenate(head + [jnp.zeros((10, TOK), F32)], axis=0))
        for i in range(4):
            dst[272 + 16 * i : 288 + 16 * i, :] = mats[4 * k + i]


def stack_body(a0, a1, a2, a3, h0, h1, h2, h3, dst):
    for k, (a, h) in enumerate(((a0, h0), (a1, h1), (a2, h2), (a3, h3))):
        dst[2 * k * TOK : (2 * k + 1) * TOK, :] = a[...]
        dst[(2 * k + 1) * TOK : (2 * k + 2) * TOK, :] = h[...]


def route_all_body(info, own, oth, w2, dst, order, sem):
    copies = []
    for z in range(ROWS):
        to = dst.at[z, pl.ds(TOK, 512)]
        copies.append(pltpu.make_async_copy(w2.at[rows_at(info[8], 512)], to, sem.at[z]))
    for copy in copies:
        copy.start()
    fill_order(info, order)
    c = info[2]
    for z in range(ROWS):
        for j in range(2):
            src = place_of(info, order, z, c, j)
            at = pl.ds(pl.multiple_of(lax.rem(src, 8) * BLOCK, BLOCK), BLOCK)
            mine = src // 8 == c

            @pl.when(mine)
            def _():
                dst[z, pl.ds(j * BLOCK, BLOCK), :] = own[at, :]

            @pl.when(jnp.logical_not(mine))
            def _():
                dst[z, pl.ds(j * BLOCK, BLOCK), :] = oth[at, :]
    for copy in copies:
        copy.wait()


def unroute_body(info, a, b, grad, hidden, order):
    fill_order(info, order)
    c = info[2]
    for s in range(ROWS):
        z = lax.rem(info[0] + s, ROWS)
        for other, src in ((0, a), (1, b)):
            core = c if other == 0 else 1 - c
            for j in range(2):
                at = place_of(info, order, z, core, j)

                @pl.when(at // 8 == c)
                def _():
                    rows = pl.ds(pl.multiple_of(lax.rem(at, 8) * BLOCK, BLOCK), BLOCK)
                    start = 2 * s * TOK + j * BLOCK
                    grad[rows, :] = f32(src[pl.ds(start, BLOCK), :])
                    hidden[rows, :] = src[pl.ds(start + TOK, BLOCK), :]


def cols(k, width=TOK):
    return pl.ds(k * width, width)


def row_stats(parts):
    total = sum(jnp.sum(v, axis=1, keepdims=True) for v in parts)
    mean = total * (1.0 / D)
    dev = [v - mean for v in parts]
    var = sum(jnp.sum(v * v, axis=1, keepdims=True) for v in dev) * (1.0 / D)
    rstd = lax.rsqrt(var + EPSILON)
    return [v * rstd for v in dev], rstd


def norm1_body(x0, x1, x2, x3, xn):
    for t in range(2):
        rows = pl.ds(t * 128, 128)
        hat, _ = row_stats([f32(v[rows, :]) for v in (x0, x1, x2, x3)])
        for k, pack in enumerate((x0, x1, x2, x3)):
            xn[rows, cols(k)] = bf(hat[k] * f32(pack[256:257, :]) + f32(pack[257:258, :]))


def both(a, b, rows, k):
    return f32(a[rows, cols(k)]) + f32(b[rows, cols(k)])


def norm2_body(a, b, x0, x1, x2, x3, mid, xn):
    for t in range(2):
        rows = pl.ds(t * 128, 128)
        parts = []
        for k, x in enumerate((x0, x1, x2, x3)):
            v = f32(x[rows, :]) + both(a, b, rows, k) + f32(x[258:259, :])
            mid[rows, cols(k)] = v
            parts.append(v)
        hat, _ = row_stats(parts)
        for k, pack in enumerate((x0, x1, x2, x3)):
            xn[rows, cols(k)] = bf(hat[k] * f32(pack[259:260, :]) + f32(pack[260:261, :]))


def norm_back(hat, rstd, grads):
    total = sum(jnp.sum(g, axis=1, keepdims=True) for g in grads) * (1.0 / D)
    along = sum(jnp.sum(g * h, axis=1, keepdims=True) for g, h in zip(grads, hat)) * (1.0 / D)
    return [rstd * (g - total - h * along) for g, h in zip(grads, hat)]


def norm2_back_body(
    a, b, pack, mid, g, x0, x1, x2, x3, d_mid, g_attn
):
    g_attn[256:320, :] = pack[...]
    for t in range(2):
        rows = pl.ds(t * 128, 128)
        hat, rstd = row_stats([mid[rows, cols(k)] for k in range(4)])
        grads = []
        for k, pack in enumerate((x0, x1, x2, x3)):
            grads.append(both(a, b, rows, k) * f32(pack[259:260, :]))
        back = norm_back(hat, rstd, grads)
        for k in range(4):
            v = f32(g[rows, cols(k)]) + back[k]
            d_mid[rows, cols(k)] = v
            g_attn[rows, cols(k)] = bf(v)


def norm1_back_body(a, b, d_mid, x0, x1, x2, x3, i0, i1, i2, i3):
    for t in range(2):
        rows = pl.ds(t * 128, 128)
        hat, rstd = row_stats([f32(v[rows, :]) for v in (x0, x1, x2, x3)])
        grads = []
        for k, pack in enumerate((x0, x1, x2, x3)):
            grads.append(both(a, b, rows, k) * f32(pack[256:257, :]))
        back = norm_back(hat, rstd, grads)
        for k, dst in enumerate((i0, i1, i2, i3)):
            dst[rows, :] = bf(d_mid[rows, cols(k)] + back[k])


def hidden_body(a, b, mid, x0, x1, x2, x3, h0, h1, h2, h3):
    for t in range(2):
        rows = pl.ds(t * 128, 128)
        for k, (pack, dst) in enumerate(zip((x0, x1, x2, x3), (h0, h1, h2, h3))):
            v = mid[rows, cols(k)] + both(a, b, rows, k) + f32(pack[261:262, :])
            dst[rows, :] = bf(v)


def join_body(info, v, dst, w2):
    for k in range(ROWS):
        dst[:, cols(k)] = v[rel(info, k), 0:TOK, :]
    for k in range(1, ROWS):
        w2[k - 1] = v[rel(info, k), TOK:, :]


def rest_body(info, v, dst):
    for k in range(1, ROWS):
        dst[k - 1] = v[rel(info, k)]


def slab_rows(info, b):
    y = jnp.bitwise_xor(info[1], b // 2)
    c = jnp.bitwise_xor(info[2], b % 2)
    return y, c


def low_lanes(rows):
    return lax.broadcasted_iota(jnp.int32, (rows, 128), 1) < HEAD


def rel(info, k):
    return lax.rem(info[0] - k + ROWS, ROWS)


def rel_cols(info, k):
    return pl.ds(pl.multiple_of(rel(info, k) * TOK, TOK), TOK)


def lanes_at(at, size):
    return pl.ds(pl.multiple_of(at, 128), size)


def rows_at(i, size):
    return pl.ds(pl.multiple_of(i * size, size), size)


def prepare_body(
    info, wq, wp, w1, qe, fe, pr, fr, first, c1, o_qe, o_fe, o_pr, o_fr, sem
):
    half = info[8]
    a = jnp.where(info[5] == 0, info[32], info[33])
    rows = rows_at(half, 128)
    pairs = [(wq.at[rows], first.at[:, 0:768]), (wp.at[rows], first.at[:, 768:1024])]
    pairs += [(qe.at[a, :, lanes_at(info[6] * 768, 768)], o_qe)]
    pairs += [(fe.at[a, :, lanes_at(info[6] * 1024, 1024)], o_fe)]
    pairs += [(pr.at[a], o_pr), (fr.at[a], o_fr)]
    for j in range(ROWS):
        pairs += [(w1.at[rows], c1.at[j])]
    copies = [pltpu.make_async_copy(x, y, sem.at[i]) for i, (x, y) in enumerate(pairs)]
    for copy in copies:
        copy.start()
    for copy in copies:
        copy.wait()


def assemble_body(info, own_q, own_p, z1, z2, z3, s1, s2, s3, ws, wp, sem):
    half = info[8]
    copies = [
        pltpu.make_async_copy(own_q, ws.at[0], sem.at[0]),
        pltpu.make_async_copy(own_p, wp.at[0], sem.at[1]),
    ]
    for k, (zv, sv) in enumerate(((z1, s1), (z2, s2), (z3, s3))):
        for n, (v, at) in enumerate(((zv, half), (sv, 1 - half))):
            rows = rows_at(at, 128)
            at = 2 + 4 * k + 2 * n
            copies.append(
                pltpu.make_async_copy(v.at[:, 0:768], ws.at[k + 1, rows], sem.at[at])
            )
            copies.append(
                pltpu.make_async_copy(v.at[:, 768:1024], wp.at[k + 1, rows], sem.at[at + 1])
            )
    for copy in copies:
        copy.start()
    for copy in copies:
        copy.wait()


def qkv_body(
    info, x0, x1, x2, x3, ws, p0, p1, p2, p3, bias, expand, q, kvp, kvc
):
    ps = (p0, p1, p2, p3)
    low = low_lanes(TOK)
    for b, x in enumerate((x0, x1, x2, x3)):
        y, c = slab_rows(info, b)
        acc = sum(nn(x[:, cols(k)], ws[k]) for k in range(4))
        u = bf(sum(nt(x[:, cols(k)], ps[k][272:288, :]) for k in range(4)))
        acc = acc + f32(bias[...]) + SCALE * nn(u, expand[...])
        kv = []
        for pair in range(2):
            at = 384 * pair
            g0, g1, g2 = (acc[:, at + 128 * i : at + 128 * i + 128] for i in range(3))
            q[rows_at(y * 2 + c, TOK), cols(pair, 128)] = bf(
                bf(jnp.where(low, g0, g1)) * BF(0.125)
            )
            kv.append((bf(pltpu.roll(jnp.where(low, g2, g0), 64, 1)), bf(jnp.where(low, g1, g2))))
        rows = rows_at(c, TOK)

        @pl.when(y == 0)
        def _():
            for pair in range(2):
                kvp[rows, cols(pair, 128)] = kv[pair][0]
                kvp[rows, cols(2 + pair, 128)] = kv[pair][1]

        @pl.when(y == 1)
        def _():
            for pair in range(2):
                kvc[rows, cols(pair, 128)] = kv[pair][0]
                kvc[rows, cols(2 + pair, 128)] = kv[pair][1]


WIDE = 256


def stacked(v, low):
    zero = jnp.zeros_like(v)
    return jnp.concatenate([jnp.where(low, v, zero), jnp.where(low, zero, v)], axis=0)


def split_id(shape, axis):
    lane = lax.broadcasted_iota(jnp.int32, shape, axis)
    return lane, jnp.where(lane < BLOCK, lane, lane - BLOCK)


def chunk_place(shape, axis, side, n):
    lane, within = split_id(shape, axis)
    first = block_at(side, n, 0) * BLOCK
    second = block_at(side, n, 1) * BLOCK
    return within + jnp.where(lane < BLOCK, first, second)


def keep_state(state, low):
    top, total, acc = state
    lane = lax.broadcasted_iota(jnp.int32, (2 * BLOCK, 128), 1)
    spot = lax.rem(lane, HEAD)
    row = lax.broadcasted_iota(jnp.int32, (2 * BLOCK, 128), 0)
    own = (lane < HEAD) == (row < BLOCK)
    return jnp.where(own, acc, jnp.where(spot == 0, top, total))


def load_state(v):
    lane = lax.broadcasted_iota(jnp.int32, (2 * BLOCK, 128), 1)
    row = lax.broadcasted_iota(jnp.int32, (2 * BLOCK, 128), 0)
    spot = jnp.where(row < BLOCK, HEAD, 0)
    top = jnp.max(jnp.where(lane == spot, v, LOW), axis=1, keepdims=True)
    total = jnp.sum(jnp.where(lane == spot + 1, v, 0.0), axis=1, keepdims=True)
    return top, total, v


def soft_update(state, s, v):
    if state is None:
        top = jnp.max(s, axis=1, keepdims=True)
        p = jnp.exp(s - top)
        return top, jnp.sum(p, axis=1, keepdims=True), nn(bf(p), v)
    top, total, acc = state
    new = jnp.maximum(top, jnp.max(s, axis=1, keepdims=True))
    p = jnp.exp(s - new)
    shrink = jnp.exp(top - new)
    total = total * shrink + jnp.sum(p, axis=1, keepdims=True)
    return new, total, acc * shrink + nn(bf(p), v)


def head_slopes(slopes, shape, axis):
    lane = lax.broadcasted_iota(jnp.int32, shape, axis)
    return [
        jnp.where(lane < BLOCK, slopes[2 * pair], slopes[2 * pair + 1]) for pair in range(2)
    ]


def attend_chunk(q2, states, kv, rows, place, base, slope, spot, masked):
    res = []
    away = place - base
    for pair in range(2):
        s = nt(q2[pair], kv[rows, cols(pair, 128)]) + slope[pair] * away.astype(F32)
        if masked:
            s = jnp.where(away <= spot, s, LOW)
        res.append(soft_update(states[pair], s, kv[rows, cols(2 + pair, 128)]))
    return res


def attend_first_body(info, slopes, q, kvp, kvc, state):
    zl = info[4]
    low = low_lanes(BLOCK)
    _, spot = split_id((2 * BLOCK, 1), 0)
    slope = head_slopes(slopes, (2 * BLOCK, 1), 0)
    places = [chunk_place((1, WIDE), 1, zl, n) for n in range(2)]

    def load(i):
        return [stacked(q[rows_at(i, BLOCK), cols(pair, 128)], low) for pair in range(2)]

    def save(states, i):
        for pair in range(2):
            state[rows_at(i, WIDE), cols(pair, 128)] = keep_state(states[pair], low)

    def prompt_block(j, _):
        for n in range(2):
            i = 2 * n + j
            base = block_at(zl, n, j) * BLOCK
            q2 = load(i)
            states = [None, None]
            for m in range(n, -1, -1):
                states = attend_chunk(
                    q2, states, kvp, pl.ds(m * WIDE, WIDE), places[m], base, slope, spot, m == n
                )
            save(states, i)
        return 0

    lax.fori_loop(0, 2, prompt_block, 0)

    def cont_block(j, _):
        q2 = load(4 + j)
        own_place = lax.broadcasted_iota(jnp.int32, (1, BLOCK), 1)
        states = attend_chunk(
            q2, [None, None], kvc, rows_at(j, BLOCK), own_place, 0, slope, spot, True
        )
        for m in range(2):
            states = attend_chunk(
                q2, states, kvp, pl.ds(m * WIDE, WIDE), places[m], PROMPT, slope, spot, False
            )
        save(states, 4 + j)
        return 0

    lax.fori_loop(0, 4, cont_block, 0)


def attend_rest_body(
    which, info, slopes, q, kvo, state, ws, reduce, p0, p1, p2, p3, heads, lse, o0, o1
):
    zl = info[4]
    y = info[1] if which == 0 else 1 - info[1]
    low = low_lanes(BLOCK)
    _, spot = split_id((2 * BLOCK, 1), 0)
    slope = head_slopes(slopes, (2 * BLOCK, 1), 0)
    places = [chunk_place((1, WIDE), 1, 1 - zl, n) for n in range(2)]

    def load(i):
        q2 = [stacked(q[rows_at(i, BLOCK), cols(pair, 128)], low) for pair in range(2)]
        states = [load_state(state[rows_at(i, WIDE), cols(pair, 128)]) for pair in range(2)]
        return q2, states

    def finish(states, j):
        for pair in range(2):
            top, total, acc = states[pair]
            res = acc / total
            heads[rows_at(j, BLOCK), cols(pair, 128)] = bf(
                jnp.where(low, res[:BLOCK], res[BLOCK:])
            )
            kept = jnp.transpose(jnp.broadcast_to(top + jnp.log(total), (2 * BLOCK, 128)))
            lse[pl.ds(pair * 4 + j, 1), :] = kept[0:1, :]

    @pl.when(y == 0)
    def _():
        def prompt_block(j, _):
            for n in range(2):
                i = 2 * n + j
                base = block_at(zl, n, j) * BLOCK
                q2, states = load(i)
                for m in range(n + 1):
                    states = attend_chunk(
                        q2, states, kvo, pl.ds(m * WIDE, WIDE), places[m], base, slope, spot, m == n
                    )
                finish(states, i)
            return 0

        lax.fori_loop(0, 2, prompt_block, 0)

    @pl.when(y == 1)
    def _():
        def cont_block(j, _):
            q2, states = load(4 + j)
            for m in range(2):
                states = attend_chunk(
                    q2, states, kvo, pl.ds(m * WIDE, WIDE), places[m], PROMPT, slope, spot, False
                )
            finish(states, j)
            return 0

        lax.fori_loop(0, 4, cont_block, 0)

    ps = (p0, p1, p2, p3)
    for b, dst in enumerate((o0, o1)):
        c = jnp.bitwise_xor(info[2], b)
        h = heads[rows_at(c, TOK), :]
        u = bf(nt(h, reduce[...]))
        for k in range(4):
            dst[:, cols(k)] = bf(nn(h, ws[k]) + SCALE * nn(u, ps[k][304:320, :]))


def mlp_pre_body(info, x0, x1, w1, p0, p1, p2, p3, bias, expand, act, slope):
    ps = (p0, p1, p2, p3)
    for b, x in enumerate((x0, x1)):
        u = bf(sum(nt(x[:, cols(k)], ps[k][288:304, :]) for k in range(4)))
        pre = sum(nn(x[:, cols(k)], w1[rel(info, k)]) for k in range(4))
        pre = pre + f32(bias[...]) + SCALE * nn(u, expand[...])
        sq = pre * pre
        t = jnp.tanh(pre * (GELU_A + (GELU_A * GELU_B) * sq))
        half = 0.5 + 0.5 * t
        act[b] = bf(pre * half)
        slope[b] = bf(
            half + (0.5 * pre) * (1.0 - t * t) * (GELU_A + (3.0 * GELU_A * GELU_B) * sq)
        )


def mlp_back_body(
    info, x0, x1, g0, g1, slope, w1, w2, p0, p1, p2, p3, expand, reduce, r_in, e_in,
    d0, d1, r_out, e_out,
):
    ps = (p0, p1, p2, p3)
    rv, ev = r_in[...], e_in[...]
    for b, (x, g, dx) in enumerate(((x0, g0, d0), (x1, g1, d1))):
        u = bf(sum(nt(x[:, cols(k)], ps[k][288:304, :]) for k in range(4)))
        du2 = bf(SCALE * sum(nt(g[:, cols(k)], ps[k][320:336, :]) for k in range(4)))
        d_act = sum(nt(g[:, cols(k)], w2[rel(info, k)]) for k in range(4)) + nn(du2, reduce[...])
        d_pre = bf(d_act * f32(slope[b]))
        du = bf(SCALE * nt(d_pre, expand[...]))
        for k in range(4):
            dx[:, cols(k)] = bf(nt(d_pre, w1[rel(info, k)]) + nn(du, ps[k][288:304, :]))
        rv = rv + tn(du, x[...])
        ev = ev + tn(u, d_pre)
    r_out[...] = rv
    e_out[...] = ev


def fc2_body(
    info, a0, a1, g0, g1, g2, g3, w2, reduce, p0, p1, p2, p3, r1, e1,
    m0, m1, m2, m3, grads,
):
    ps = (p0, p1, p2, p3)
    rv = ev = 0.0
    for b, (g, m) in enumerate(zip((g0, g1, g2, g3), (m0, m1, m2, m3))):
        act = a0[b] if b < 2 else a1[b - 2]
        du = bf(SCALE * sum(nt(g[:, cols(k)], ps[k][320:336, :]) for k in range(4)))
        u = bf(nt(act, reduce[...]))
        for k in range(4):
            m[:, cols(k)] = bf(nn(act, w2[rel(info, k)]) + SCALE * nn(u, ps[k][320:336, :]))
        rv = rv + tn(du, act)
        ev = ev + SCALE * tn(u, g[...])
    for k in range(4):
        grads[0:16, rel_cols(info, k)] = bf(r1[:, cols(k)])
        grads[16:32, rel_cols(info, k)] = bf(ev[:, k * TOK : k * TOK + TOK])
    grads[32:48, :] = bf(SCALE * e1[...])
    grads[48:64, :] = bf(rv)


def d_heads_body(
    info, g0, g1, ws, p0, p1, p2, p3, reduce, heads, r_in, e_in, dh, r_out, e_out
):
    ps = (p0, p1, p2, p3)
    rv, ev = r_in[...], e_in[...]
    for b, g in enumerate((g0, g1)):
        rows = rows_at(jnp.bitwise_xor(info[2], b), TOK)
        h = heads[rows, :]
        u = bf(nt(h, reduce[...]))
        du = bf(SCALE * sum(nt(g[0:256, cols(k)], ps[k][304:320, :]) for k in range(4)))
        v = sum(nt(g[0:256, cols(k)], ws[k]) for k in range(4)) + nn(du, reduce[...])
        dh[rows, :] = bf(v)
        rv = rv + tn(du, h)
        ev = ev + SCALE * tn(u, g[0:256, :])
    r_out[...] = rv
    e_out[...] = ev


def back_load(heads, d_heads, lse, q, qi, j, low):
    res = []
    for pair in range(2):
        lane = cols(pair, 128)
        q2 = stacked(q[rows_at(qi, BLOCK), lane], low)
        do = d_heads[rows_at(j, BLOCK), lane]
        both = jnp.transpose(f32(do) * f32(heads[rows_at(j, BLOCK), lane]))
        delta = jnp.concatenate(
            [
                jnp.sum(both[:HEAD], axis=0, keepdims=True),
                jnp.sum(both[HEAD:], axis=0, keepdims=True),
            ],
            axis=1,
        )
        res.append((q2, stacked(do, low), delta, lse[pl.ds(pair * 4 + j, 1), :]))
    return res


def back_chunk(args, kv, d_kv, d_at, rows, place, base, slope, spot, masked, store, d_qs):
    away = place - base
    res = []
    for pair in range(2):
        q2, do2, delta, kept = args[pair]
        lane = cols(pair, 128)
        vlane = cols(2 + pair, 128)
        k = kv[rows, lane]
        s = nt(k, q2) + (away.astype(F32) * slope[pair] - kept)
        p = jnp.exp(s)
        if masked:
            p = jnp.where(away <= spot, p, 0.0)
        ds = bf(p * (nt(kv[rows, vlane], do2) - delta))
        dk = nn(ds, q2)
        dv = nn(bf(p), do2)
        if store:
            d_kv[d_at, lane] = bf(dk)
            d_kv[d_at, vlane] = bf(dv)
        else:
            d_kv[d_at, lane] += dk
            d_kv[d_at, vlane] += dv
        d_q = tn(ds, k)
        res.append(d_q if d_qs is None else d_qs[pair] + d_q)
    return res


def back_common(info, slopes):
    low = low_lanes(BLOCK)
    _, spot = split_id((1, 2 * BLOCK), 1)
    slope = head_slopes(slopes, (1, 2 * BLOCK), 1)
    zl = info[4]
    own = [chunk_place((WIDE, 1), 0, zl, n) for n in range(2)]
    oth = [chunk_place((WIDE, 1), 0, 1 - zl, n) for n in range(2)]
    return zl, low, spot, slope, own, oth


def fold(d_q, low):
    return jnp.where(low, d_q[:BLOCK], d_q[BLOCK:]) * 0.125


def back_sweep(info, slopes, y, q, heads, d_heads, lse, sides, kvc, dkc, finish):
    zl, low, spot, slope, own, oth = back_common(info, slopes)
    place_sets = {"own": own, "oth": oth}

    @pl.when(y == 0)
    def _():
        def prompt_block(j, _):
            for n in range(2):
                i = 2 * n + j
                args = back_load(heads, d_heads, lse, q, i, i, low)
                base = block_at(zl, n, j) * BLOCK
                d_qs = None
                for side, kv, d_kv in sides:
                    for m in range(n + 1):
                        rows = pl.ds(m * WIDE, WIDE)
                        d_qs = back_chunk(
                            args, kv, d_kv, rows, rows, place_sets[side][m], base, slope, spot,
                            m == n, False, d_qs,
                        )
                finish(d_qs, i, low)
            return 0

        lax.fori_loop(0, 2, prompt_block, 0)

    @pl.when(y == 1)
    def _():
        def cont_block(j, _):
            args = back_load(heads, d_heads, lse, q, 4 + j, j, low)
            d_qs = None
            if kvc is not None:
                mine = rows_at(j, BLOCK)
                own_place = lax.broadcasted_iota(jnp.int32, (BLOCK, 1), 0)
                d_qs = back_chunk(
                    args, kvc, dkc, mine, mine, own_place, 0, slope, spot, True, True, d_qs
                )
            for side, kv, d_kv in sides:
                for m in range(2):
                    rows = pl.ds(m * WIDE, WIDE)
                    d_qs = back_chunk(
                        args, kv, d_kv, rows, rows, place_sets[side][m], PROMPT, slope, spot,
                        False, False, d_qs,
                    )
            finish(d_qs, j, low)
            return 0

        lax.fori_loop(0, 4, cont_block, 0)


def attend_back_a_body(
    info, slopes, q, kvp, kvo, kvc, heads, d_heads, lse, dq, dkp, dko, dkc
):
    dkp[...] = jnp.zeros_like(dkp)
    dko[...] = jnp.zeros_like(dko)
    dkc[...] = jnp.zeros_like(dkc)

    def finish(d_qs, j, low):
        for pair in range(2):
            dq[rows_at(j, BLOCK), cols(pair, 128)] = bf(fold(d_qs[pair], low))

    back_sweep(
        info, slopes, info[1], q, heads, d_heads, lse,
        (("own", kvp, dkp), ("oth", kvo, dko)), kvc, dkc, finish,
    )


def attend_back_b_body(
    info, slopes, q, kvo, heads, d_heads, lse, dko_in, early, dq, dko, acc
):
    acc[...] = dko_in[...]

    def finish(d_qs, j, low):
        for pair in range(2):
            dq[rows_at(j, BLOCK), cols(pair, 128)] = fold(d_qs[pair], low)

    back_sweep(
        info, slopes, 1 - info[1], q, heads, d_heads, lse,
        (("oth", kvo, acc),), None, None, finish,
    )
    dko[0:512, :] = bf(acc[...])
    dko[512:592, :] = early[:, 0:512]
    dko[592:672, :] = early[:, 512:1024]


def early_sum_body(own, other, dst):
    dst[:, 0:512] = bf(f32(own[:, 0:512]) + f32(other[512:592, :]))
    dst[:, 512:1024] = bf(f32(own[:, 512:1024]) + f32(other[592:672, :]))


def attend_back_c_body(
    info, slopes, q, kvp, kvc, heads, d_heads, lse, dkp_in, dkc_in, dq_in, dq, dkp, dkc
):
    dkp[...] = dkp_in[...]
    dkc[...] = dkc_in[...]

    def finish(d_qs, j, low):
        for pair in range(2):
            lane = cols(pair, 128)
            rows = rows_at(j, BLOCK)
            dq[rows, lane] = bf(dq_in[rows, lane] + fold(d_qs[pair], low))

    back_sweep(
        info, slopes, 1 - info[1], q, heads, d_heads, lse,
        (("own", kvp, dkp),), kvc, dkc, finish,
    )


def qkv_back_body(
    info, dq0, dq1, dkp, dkr, dkc, x0, x1, x2, x3, ws, p0, p1, p2, p3, expand, pr, pe,
    o0, o1, o2, o3, grads,
):
    ps = (p0, p1, p2, p3)
    low = low_lanes(TOK)
    sr = se = 0.0
    for b, (x, dst) in enumerate(zip((x0, x1, x2, x3), (o0, o1, o2, o3))):
        y, c = slab_rows(info, b)
        half = rows_at(c, TOK)
        groups = []
        dq = dq0 if b < 2 else dq1
        for pair in range(2):
            vq = f32(dq[half, cols(pair, 128)])
            got = []
            for lane in (cols(pair, 128), cols(2 + pair, 128)):
                prompt = dkp[half, lane] + f32(dkr[half, lane])
                got.append(jnp.where(y == 0, prompt, f32(dkc[half, lane])))
            vk = pltpu.roll(got[0], 64, 1)
            vv = got[1]
            groups += [jnp.where(low, vq, vk), jnp.where(low, vv, vq), jnp.where(low, vk, vv)]
        d = bf(jnp.concatenate(groups, axis=1))
        u = bf(sum(nt(x[:, cols(k)], ps[k][272:288, :]) for k in range(4)))
        du = bf(SCALE * nt(d, expand[...]))
        for k in range(4):
            dst[:, cols(k)] = bf(nt(d, ws[k]) + nn(du, ps[k][272:288, :]))
        sr = sr + tn(du, x[...])
        se = se + SCALE * tn(u, d)
    for k in range(4):
        grads[0:16, rel_cols(info, k)] = bf(sr[:, k * TOK : k * TOK + TOK])
        grads[16:32, rel_cols(info, k)] = bf(pe[:, cols(k)])
    grads[32:48, 0:768] = bf(se)
    grads[32:48, 768:1024] = bf(pr[...])


def add_body(a, b, dst):
    dst[...] = bf(f32(a[...]) + f32(b[...]))


def add(a, b):
    return call(add_body, [out(a.shape, BF)], [a, b], smem=0, us=0.01, name="add")[0]


def add32_body(a, b, dst):
    dst[...] = f32(a[...]) + f32(b[...])


def add32(a, b, us=8):
    return call(add32_body, [out(a.shape, F32)], [a, b], smem=0, us=us, name="add32")[0]


def stage_body(*refs):
    n = len(refs) // 2
    for src, dst in zip(refs[:n], refs[n:]):
        dst[...] = src[...]


def stage(values):
    return call(
        stage_body, [out(v.shape, v.dtype) for v in values], far(values), smem=0, us=0.01, name="stage"
    )


def stage_weight_body(size, info, own, wr, ws, w, sem):
    copies = [pltpu.make_async_copy(own, w.at[info[0]], sem.at[6])]
    for n, (src, at) in enumerate(((wr, info[8]), (ws, 1 - info[8]))):
        for k in range(1, ROWS):
            to = w.at[rel(info, k), rows_at(at, size)]
            copies.append(pltpu.make_async_copy(src.at[k - 1], to, sem.at[3 * n + k - 1]))
    for copy in copies:
        copy.start()
    for copy in copies:
        copy.wait()


def merge_body(info, v0, v1, v2, v3, dst):
    four = (v0, v1, v2, v3)

    def fill(c):
        total = sum(f32(v[256 + 16 * c : 272 + 16 * c, :]) for v in four)
        dst[0:16, :] = bf(total)
        for b, v in enumerate(four):
            rows = pl.ds(pl.multiple_of(16 + 16 * jnp.bitwise_xor(info[6], b), 16), 16)
            dst[rows, :] = v[288 + 16 * c : 304 + 16 * c, :]

    @pl.when(info[2] == 0)
    def _():
        fill(0)

    @pl.when(info[2] == 1)
    def _():
        fill(1)


def pile_body(*refs):
    dst = refs[-1]
    for n, src in enumerate(refs[:-1]):
        dst[n] = src[...]


def expand_early_body(info, own, oth, r1, e2, e1, r2):
    for v in (r1, e2, e1, r2):
        v[...] = jnp.zeros_like(v)

    def fill(src, shared, split):
        for n in range(own.shape[0]):
            group = info[5] if n % 2 == 0 else 1 - info[5]
            a = info[40 + n // 2 * GROUPS_DEV + group]
            shared[a] += f32(src[n, 0:16, :])
            for j in range(COLS):
                at = 16 + 16 * j
                split[a, :, cols(j, 1024)] += f32(src[n, at : at + 16, :])

    @pl.when(info[2] == 0)
    def _():
        fill(own, r1, e1)
        fill(oth, e2, r2)

    @pl.when(info[2] == 1)
    def _():
        fill(oth, r1, e1)
        fill(own, e2, r2)


def expand_late_body(info, v0, v1, v2, v3, qr, pe, qe, pr):
    four = (v0, v1, v2, v3)
    for v in (qr, pe, qe, pr):
        v[...] = jnp.zeros_like(v)
    for k in range(v0.shape[0]):
        group = info[5] if k % 2 == 0 else 1 - info[5]
        a = info[40 + k // 2 * GROUPS_DEV + group]
        qr[a] += sum(f32(v[k, 0:16, :]) for v in four)
        pe[a] += sum(f32(v[k, 16:32, :]) for v in four)
        for b, v in enumerate(four):
            j = jnp.bitwise_xor(info[6], b)
            qe[a, :, lanes_at(j * 768, 768)] += f32(v[k, 32:48, :768])
            pr[a, :, lanes_at(j * 256, 256)] += f32(v[k, 32:48, 768:])


def shift(v, k, axis="row"):
    if k == 0:
        return v
    size = lax.axis_size(axis)
    return lax.ppermute(v, axis, [(s, (s + k) % size) for s in range(size)])


def gather_row(v):
    return [v] + [shift(v, k) for k in range(1, ROWS)]


def gather_col(v):
    core = lax.ppermute(v, "col", CORE_SWAP)
    side = lax.ppermute(v, "col", Y_SWAP)
    return [v, core, side, lax.ppermute(side, "col", CORE_SWAP)]


def to_cols(pieces):
    return [pieces[0]] + [shift(pieces[k], ROWS - k) for k in range(1, ROWS)]


def spread(mine, other):
    return [mine, other] + [
        shift(v, k, "dp") for k in range(1, lax.axis_size("dp")) for v in (mine, other)
    ]


def pile(parts):
    shape = (len(parts), *parts[0].shape)
    return call(pile_body, [out(shape, BF)], parts, smem=0, us=0.01, name="pile")[0]

def body(
    hidden_in,
    out_grad,
    first_norm_gain,
    first_norm_bias,
    qkv_weight,
    qkv_bias,
    proj_weight,
    proj_bias,
    second_norm_gain,
    second_norm_bias,
    fc1_weight,
    fc1_bias,
    fc2_weight,
    second_feed_bias,
    qkv_reduce,
    qkv_expand,
    proj_reduce,
    proj_expand,
    fc1_reduce,
    fc1_expand,
    fc2_reduce,
    fc2_expand,
    adapter_choice,
    cont_prompt,
):
    r = lax.axis_index("row")
    col = lax.axis_index("col")
    dp = lax.axis_index("dp")
    y = col // 2
    c = lax.rem(col, 2)
    zl = lax.rem(r, 2)
    group = r // 2
    half = lax.rem(dp, 2)
    dp_swap = [(k, k ^ 1) for k in range(lax.axis_size("dp"))]
    slopes = jnp.exp2(
        -8.0 * (col * 4 + 1 + jnp.arange(4, dtype=jnp.int32)).astype(F32) / HEADS
    )
    adapter = jnp.where(group == 0, adapter_choice[0], adapter_choice[1])
    dp_size = jnp.int32(lax.axis_size("dp"))
    info = jnp.stack([r, y, c, dp * GROUPS_DEV, zl, group, col, dp, half] + [half, dp_size] + [half] * 5)
    info = jnp.concatenate([info.astype(jnp.int32), cont_prompt, adapter_choice])
    order = pltpu.SMEM((GROUPS_DEV * NCONT,), jnp.int32)
    flip = functools.partial(jnp.transpose, axes=(0, 2, 1))
    big = out((TOK, D), BF)
    small = out((RANK, D), F32)

    other = lax.ppermute(hidden_in, "col", CORE_SWAP)
    vectors = [
        first_norm_gain, first_norm_bias, proj_bias,
        second_norm_gain, second_norm_bias, second_feed_bias,
    ]
    factors = [flip(qkv_reduce), flip(fc1_reduce), proj_expand, fc2_expand]
    pieces = call(
        route_pack_body,
        [out((336, TOK), BF)] * 4,
        [info, Far(hidden_in), Far(other), *far(vectors), *far(factors)],
        [
            order,
            *[pltpu.VMEM((TOK,), BF)] * 6,
            pltpu.VMEM((16, RANK, TOK), BF),
            pltpu.SemaphoreType.DMA((22,)),
        ],
        raw=range(3, 13),
        us=1.5,
        name="route_x",
    )
    xs = [pieces[0]] + [shift(pieces[k], k) for k in range(1, ROWS)]
    packs = far(xs)
    first_half, w1_copies, qkv_e, fc1_e, proj_r, fc2_r = call(
        prepare_body,
        [
            out((128, D), BF), out((ROWS, 128, D), BF),
            out((RANK, 768), BF), out((RANK, D), BF), out((RANK, TOK), BF), out((RANK, D), BF),
        ],
        [
            after(info, pieces[0]),
            *far([qkv_weight, proj_weight, fc1_weight, qkv_expand, fc1_expand]),
            *far([flip(proj_reduce), flip(fc2_reduce)]),
        ],
        [pltpu.SemaphoreType.DMA((10,))],
        raw=range(1, 8),
        us=3,
        name="prepare",
    )
    first_half = after(first_half, xs[1])
    z_parts = [shift(first_half, k) for k in range(1, ROWS)]
    s_parts = [lax.ppermute(v, "dp", dp_swap) for v in z_parts]
    wq, wp = call(
        assemble_body,
        [out((ROWS, TOK, 768), BF), out((ROWS, TOK, TOK), BF)],
        [info, *far([qkv_weight, proj_weight, *z_parts, *s_parts])],
        [pltpu.SemaphoreType.DMA((14,))],
        raw=range(1, 9),
        us=15,
        name="assemble",
    )

    qkv_b = lax.dynamic_slice_in_dim(qkv_bias, col * 768, 768, 0)[None, :]
    fc1_b = lax.dynamic_slice_in_dim(fc1_bias, col * 1024, 1024, 0)[None, :]

    choices = [adapter_choice] + [
        shift(adapter_choice, k, "dp") for k in range(1, lax.axis_size("dp"))
    ]
    first = after(xs[0], qkv_b, fc1_b, w1_copies, *choices)
    (xn1,) = call(norm1_body, [big], [first, *xs[1:]], smem=0, us=8, name="norm1")
    xn1s = gather_col(xn1)
    q, kvp, kvc = call(
        qkv_body,
        [out((1024, 256), BF), out((512, 512), BF), out((512, 512), BF)],
        [info, *xn1s, wq, *packs, Far(qkv_b), Far(qkv_e)],
        us=6.5,
        name="qkv",
    )
    kvo = lax.ppermute(kvp, "row", Z_SWAP)

    g_other = lax.ppermute(after(out_grad, kvp), "col", CORE_SWAP)
    (pieces,) = call(
        route_all_body,
        [out((ROWS, 3 * TOK, TOK), BF)],
        [info, Far(out_grad), Far(g_other), Far(fc2_weight)],
        [order, pltpu.SemaphoreType.DMA((4,))],
        raw=(3,),
        us=1,
        name="route_g",
    )
    (state,) = call(
        attend_first_body,
        [out((2048, 256), F32)],
        [info, slopes, q, kvp, kvc],
        smem=2,
        us=9,
        name="attend_first",
    )
    (w1r,) = call(
        rest_body,
        [out((3, 128, D), BF)],
        [info, after(lax.all_to_all(after(w1_copies, *z_parts), "row", 0, 0), state)],
        us=0.01,
        name="rest",
    )
    w1s = lax.ppermute(w1r, "dp", dp_swap)
    pieces = after(pieces, state, kvo)
    g_own, w2r = call(
        join_body,
        [big, out((3, 512, TOK), BF)],
        [info, lax.all_to_all(pieces, "row", 0, 0)],
        us=0.01,
        name="join",
    )
    g_side = lax.ppermute(g_own, "col", Y_SWAP)
    w2s = lax.ppermute(w2r, "dp", dp_swap)

    def attend_rest(which, q, state):
        return call(
            functools.partial(attend_rest_body, which),
            [out((512, 256), BF), out((8, 256), F32), big, big],
            [info, slopes, Far(q), kvo, state, Far(wp), Far(proj_r), *packs],
            smem=2,
            us=20 if which else 0.01,
            name="attend_rest",
        )

    heads1, lse1, p2, p3 = attend_rest(1, q, after(state, w1r))
    g_core = lax.ppermute(g_own, "col", CORE_SWAP)
    g_all = [g_own, g_core, g_side, lax.ppermute(g_side, "col", CORE_SWAP)]
    p_far = lax.ppermute(p3, "col", CORE_SWAP)
    p_side = add(p2, p_far)
    heads0, lse0, p0, p1 = attend_rest(0, q, Far(after(state, p_side)))
    p_side = lax.ppermute(p_side, "col", Y_SWAP)
    p_core = lax.ppermute(p1, "col", CORE_SWAP)
    staged = stage([after(xs[0], p0), *xs[1:]])
    mid, xn2 = call(
        norm2_body,
        [out((TOK, D), F32), big],
        [add32(p0, p_side), p_core, *staged],
        smem=0,
        us=1.5,
        hbm=(0,),
        name="norm2",
    )
    (w1,) = call(
        functools.partial(stage_weight_body, 128),
        [out((ROWS, TOK, D), BF)],
        [info, Far(fc1_weight), Far(after(w1r, p0)), Far(w1s)],
        [pltpu.SemaphoreType.DMA((7,))],
        raw=(1, 2, 3),
        us=2,
        name="stage_w1",
    )
    zero = jnp.zeros((RANK, D), F32)
    xn2_core = lax.ppermute(xn2, "col", CORE_SWAP)
    xn2_side = lax.ppermute(xn2, "col", Y_SWAP)

    def mlp_pre(first, blocks):
        return call(
            mlp_pre_body,
            [out((2, TOK, D), BF)] * 2,
            [info, *blocks, w1, *staged, Far(fc1_b), Far(fc1_e)],
            us=1,
            name="mlp_pre",
        )

    act0, slope0 = mlp_pre(0, [xn2, xn2_core])
    xn2_far = lax.ppermute(xn2_side, "col", CORE_SWAP)
    xn2s = [xn2, xn2_core, xn2_side, xn2_far]
    act1, slope1 = mlp_pre(1, xn2s[2:])
    (w2,) = call(
        functools.partial(stage_weight_body, 512),
        [out((ROWS, D, TOK), BF)],
        [info, Far(fc2_weight), Far(after(w2r, act0)), Far(w2s)],
        [pltpu.SemaphoreType.DMA((7,))],
        raw=(1, 2, 3),
        us=20,
        name="stage_w2",
    )

    def mlp_back(blocks, slope, r_in, e_in):
        xa, xb = (xn2s[b] for b in blocks)
        ga, gb = (g_all[b] for b in blocks)
        return call(
            mlp_back_body,
            [big, big, small, small],
            [info, xa, xb, ga, gb, slope, w1, w2, *staged, Far(fc1_e), Far(fc2_r), r_in, e_in],
            us=0.01,
            name="mlp_back",
        )

    d2, d3, r1, e1 = mlp_back((2, 3), slope1, zero, zero)
    d_far = lax.ppermute(d3, "col", CORE_SWAP)
    d_side = add(d2, d_far)
    d0, d1, r1, e1 = mlp_back((0, 1), slope0, after(r1, d_side), e1)
    d_side = lax.ppermute(d_side, "col", Y_SWAP)
    d_core = lax.ppermute(d1, "col", CORE_SWAP)
    res = call(
        fc2_body,
        [big] * 4 + [out((64, D), BF)],
        [info, act0, act1, *g_all, w2, Far(fc2_r), *staged, r1, e1],
        us=0.01,
        name="fc2",
    )
    m_parts, mlp_pack = res[:4], res[4]
    staged_back = stage([after(mid, mlp_pack), g_own, *xs])
    d_mid, g_attn = call(
        norm2_back_body,
        [out((TOK, D), F32), out((320, D), BF)],
        [add32(d0, d_side), d_core, mlp_pack, *staged_back],
        smem=0,
        us=1.5,
        hbm=(0,),
        name="norm2_back",
    )
    ga_core = lax.ppermute(g_attn, "col", CORE_SWAP)
    ga_side = lax.ppermute(g_attn, "col", Y_SWAP)
    shared = far([q, kvp, kvo, kvc])

    def d_heads(blocks, heads, r_in, e_in):
        return call(
            d_heads_body,
            [out((512, 256), BF), out((RANK, TOK), F32), small],
            [info, *blocks, Far(wp), *packs, Far(proj_r), Far(heads), r_in, e_in],
            us=1.5,
            name="d_heads",
        )

    dh0, pr, pe = d_heads([g_attn, ga_core], heads0, jnp.zeros((RANK, TOK), F32), zero)
    dq0, dkp, dko, dkc = call(
        attend_back_a_body,
        [out((512, 256), BF), out((512, 512), F32), out((512, 512), F32), out((512, 512), BF)],
        [info, slopes, *shared, Far(heads0), dh0, Far(lse0)],
        smem=2,
        us=16,
        weight=W_BIG,
        hbm=(1, 2, 3),
        name="attend_back_a",
    )
    ga_side = after(ga_side, dq0)
    ga_far = lax.ppermute(ga_side, "col", CORE_SWAP)
    (early_half,) = call(
        merge_body,
        [out((80, D), BF)],
        [info, g_attn, ga_core, ga_side, ga_far],
        us=0.7,
        name="merge",
    )
    dh1, pr, pe = d_heads([ga_side, ga_far], heads1, pr, pe)
    dq1_part, dko = call(
        attend_back_b_body,
        [out((512, 256), F32), out((672, 512), BF)],
        [info, slopes, Far(q), Far(kvo), Far(heads1), dh1, Far(lse1), Far(dko), early_half],
        [pltpu.VMEM((512, 512), F32)],
        smem=2,
        us=8,
        hbm=(0,),
        name="attend_back_b",
    )
    dkr = lax.ppermute(dko, "row", Z_SWAP)
    dq1, dkp, dkc = call(
        attend_back_c_body,
        [out((512, 256), BF), out((512, 512), F32), out((512, 512), BF)],
        [info, slopes, Far(q), Far(kvp), Far(kvc), Far(heads1), dh1, Far(lse1), *far([dkp, dkc, dq1_part])],
        smem=2,
        us=8,
        hbm=(2,),
        name="attend_back_c",
    )
    (early_sum,) = call(
        early_sum_body, [out((80, D), BF)], [early_half, dkr], smem=0, us=0.01, name="early_sum"
    )
    m_far = lax.ppermute(after(m_parts[3], dq0), "col", CORE_SWAP)
    m_core = lax.ppermute(after(m_parts[1], dq0), "col", CORE_SWAP)
    m_sum = add(after(m_parts[2], dko), m_far)
    m_side = lax.ppermute(m_sum, "col", Y_SWAP)
    hidden = call(
        hidden_body,
        [out((TOK, TOK), BF)] * 4,
        [add32(m_parts[0], m_side, 0.01), m_core, Far(mid), *packs],
        smem=0,
        us=0.01,
        name="hidden",
    )
    res = call(
        qkv_back_body,
        [big] * 4 + [out((48, D), BF)],
        [
            info, dq0, dq1, dkp, after(dkr, early_sum, hidden[0]), Far(dkc),
            *far(xn1s), Far(wq), *packs, Far(qkv_e), pr, pe,
        ],
        us=20,
        name="qkv_back",
    )
    q_parts, late_pack = res[:4], res[4]
    early_next = shift(early_sum, 2)
    n_dp = lax.axis_size("dp")
    early_mine = [early_sum] + [shift(early_sum, k, "dp") for k in range(1, n_dp)]
    ready = after(q_parts[3], m_side, early_next, *early_mine)
    q_sum = add(q_parts[2], lax.ppermute(ready, "col", CORE_SWAP))
    hidden_got = to_cols(hidden)
    k0, rc = q_parts[0], lax.ppermute(q_parts[1], "col", CORE_SWAP)
    ry = lax.ppermute(q_sum, "col", Y_SWAP)
    late_sum = add(late_pack, lax.ppermute(after(late_pack, q_sum), "row", Z_SWAP))
    late_next = shift(late_sum, 2)
    early_rest = after(early_next, late_sum)
    early_rest = [early_next] + [shift(early_rest, k, "dp") for k in range(1, n_dp)]
    early_parts = [v for pair in zip(early_mine, early_rest) for v in pair]
    late_four = pile(spread(late_sum, late_next))
    late_all = gather_col(late_four)
    staged_last = stage([after(d_mid, k0, rc), *xs])
    ins = call(
        norm1_back_body,
        [out((TOK, TOK), BF)] * 4,
        [add32(after(k0, late_next, *hidden_got), ry), rc, *staged_last],
        smem=0,
        us=1,
        name="norm1_back",
    )
    early_all = pile(early_parts)
    early_far = lax.ppermute(after(early_all, ins[0]), "col", CORE_SWAP)
    table = jnp.concatenate([info, jnp.zeros((40 - 34,), jnp.int32), *choices])
    o_fc1r, o_f2e, o_f1e, o_f2r = call(
        expand_early_body,
        [out((COUNT, RANK, w), F32) for w in (1024, 1024, 4096, 4096)],
        [table, Far(early_all), Far(early_far)],
        us=0.01,
        name="expand_early",
    )
    (joined,) = call(
        stack_body,
        [out((8 * TOK, TOK), BF)],
        [*[after(v, o_fc1r, late_all[2]) for v in to_cols(ins)], *hidden_got],
        smem=0,
        us=0.01,
        name="stack",
    )
    input_gradient, hidden_out = call(
        unroute_body,
        [out((1024, TOK), F32), out((1024, TOK), BF)],
        [info, joined, lax.ppermute(joined, "col", CORE_SWAP)],
        [order],
        us=2,
        name="unroute",
    )
    o_qr, o_pe, o_qe, o_pr = call(
        expand_late_body,
        [out((COUNT, RANK, w), F32) for w in (1024, 1024, 3072, 1024)],
        [table, *late_all],
        us=0.01,
        name="expand_late",
    )
    return (
        hidden_out,
        input_gradient,
        flip(o_qr),
        o_qe,
        flip(o_pr),
        o_pe,
        flip(o_fc1r),
        o_f1e,
        flip(o_f2r),
        o_f2e,
    )


def solution(mesh):
    placed = (
        P(("dp", "col"), "row"),
        P(("dp", "col"), "row"),
        P("row"),
        P("row"),
        P("row", "col"),
        P(),
        P("col", "row"),
        P("row"),
        P("row"),
        P("row"),
        P("row", "col"),
        P(),
        P("col", "row"),
        P("row"),
        P(None, "row", None),
        P(),
        P(None, "col", None),
        P(None, None, "row"),
        P(None, "row", None),
        P(),
        P(None, "col", None),
        P(None, None, "row"),
        P("dp"),
        P("dp"),
    )
    return jax.shard_map(
        body,
        mesh=mesh,
        in_specs=placed,
        out_specs=(P(("dp", "col"), "row"), P(("dp", "col"), "row")) + (P(),) * 8,
        check_vma=False,
    )
```

```python
import functools

import jax
import jax.numpy as jnp
from jax import lax
from jax.experimental import pallas as pl
from jax.experimental.pallas import tpu as pltpu
from jax.sharding import PartitionSpec as P

D = 1024
HEADS = 16
HEAD = 64
FF = 4096
RANK = 16
COUNT = 8
PROMPT = 1024
CONT = 128
NCONT = 8
GROUPS_DEV = 2

EPSILON = 1e-05
SCALE = 2.0
GELU_A = 0.7978845608028654
GELU_B = 0.044715
ROWS = 4
COLS = 4
TOK = 256
BLOCK = 128
LOW = -1e30
W_SMALL = 5e8
W_BIG = 5e8

BF = jnp.bfloat16
F32 = jnp.float32

VM = pl.BlockSpec(memory_space=pltpu.VMEM)
SM = pl.BlockSpec(memory_space=pltpu.SMEM)
HB = pl.BlockSpec(memory_space=pltpu.HBM)

CORE_SWAP = [(0, 1), (1, 0), (2, 3), (3, 2)]
Y_SWAP = [(0, 2), (2, 0), (1, 3), (3, 1)]
Z_SWAP = [(0, 1), (1, 0), (2, 3), (3, 2)]


def nn(a, b):
    return lax.dot_general(a, b, (((1,), (0,)), ((), ())), preferred_element_type=F32)


def nt(a, b):
    return lax.dot_general(a, b, (((1,), (1,)), ((), ())), preferred_element_type=F32)


def tn(a, b):
    return lax.dot_general(a, b, (((0,), (0,)), ((), ())), preferred_element_type=F32)


def f32(v):
    return v.astype(F32)


def bf(v):
    return v.astype(BF)


class Far:
    def __init__(self, value):
        self.value = value


def far(values):
    return [Far(v) for v in values]


def call(
    body, outs, ins, scratch=(), smem=1, limit=40, us=1, raw=(), weight=W_SMALL, hbm=(), pre=None, name=None
):
    values = [
        pltpu.with_memory_space_constraint(v.value, pltpu.HBM) if isinstance(v, Far) else v
        for v in ins
    ]
    fetched = [i for i, v in enumerate(ins) if isinstance(v, Far) and i not in raw]
    specs = [SM] * smem
    for v in ins[smem:]:
        specs.append(HB if isinstance(v, Far) else VM)
    nbytes = sum(v.size * v.dtype.itemsize for v in values)
    nbytes += sum(o.size * o.dtype.itemsize for o in outs)
    extra = [pltpu.VMEM(values[i].shape, values[i].dtype) for i in fetched]
    extra += [pltpu.VMEM(outs[i].shape, outs[i].dtype) for i in hbm]
    moved = len(extra)
    if moved:
        extra.append(pltpu.SemaphoreType.DMA((moved,)))

    def whole(*refs):
        refs = list(refs)
        stores = []
        if moved:
            sem = refs[-1]
            buffers = refs[-1 - moved : -1]
            refs = refs[: -1 - moved]
            copies = []
            for n, i in enumerate(fetched):
                copies.append(pltpu.make_async_copy(refs[i], buffers[n], sem.at[n]))
                copies[-1].start()
                refs[i] = buffers[n]
            for n, i in enumerate(hbm, len(fetched)):
                at = len(values) + i
                stores.append(pltpu.make_async_copy(buffers[n], refs[at], sem.at[n]))
                refs[at] = buffers[n]
            if pre is not None:
                pre(*refs)
            for copy in copies:
                copy.wait()
        body(*refs)
        for copy in stores:
            copy.start()
        for copy in stores:
            copy.wait()

    return pl.pallas_call(
        whole,
        out_shape=tuple(
            pltpu.HBM(o.shape, o.dtype) if i in hbm else o for i, o in enumerate(outs)
        ),
        in_specs=specs,
        out_specs=tuple(HB if i in hbm else VM for i in range(len(outs))),
        scratch_shapes=list(scratch) + extra,
        compiler_params=pltpu.CompilerParams(vmem_limit_bytes=limit << 20),
        cost_estimate=pl.CostEstimate(
            flops=int(us * weight), bytes_accessed=nbytes // 8, transcendentals=0
        ),
        name=name,
    )(*values)


def after(value, *others):
    res = lax.optimization_barrier((value, others))
    return res[0]


def out(shape, dtype):
    return jax.ShapeDtypeStruct(shape, dtype)


def block_at(zl, c, j):
    return c * 4 + zl + j * (3 - 2 * zl)


def fill_order(info, order):
    base = info[3]
    first = jnp.int32(0)
    second = jnp.int32(NCONT)
    for j in range(GROUPS_DEV * NCONT):
        own = info[16 + j] == base
        slot = jnp.where(own, first, second)
        order[slot] = jnp.int32(j)
        first = first + jnp.where(own, 1, 0)
        second = second + jnp.where(own, 0, 1)


def place_of(info, order, z, core, j):
    prompt = (z // 2) * 8 + block_at(lax.rem(z, 2), core, j)
    cont = order[4 * z + 2 * core + j]
    return jnp.where(info[1] == 0, prompt, cont)


def route_body(info, own, oth, o0, o1, o2, o3, order):
    c = info[2]
    for s, dst in enumerate((o0, o1, o2, o3)):
        z = lax.rem(info[0] + s, ROWS)
        for j in range(2):
            src = place_of(info, order, z, c, j)
            at = pl.ds(pl.multiple_of(lax.rem(src, 8) * BLOCK, BLOCK), BLOCK)
            mine = src // 8 == c

            @pl.when(mine)
            def _():
                dst[pl.ds(j * BLOCK, BLOCK), :] = own[at, :]

            @pl.when(jnp.logical_not(mine))
            def _():
                dst[pl.ds(j * BLOCK, BLOCK), :] = oth[at, :]


def route_copies(
    info, own, oth, g1, c1, pb, g2, c2, fb, qr, fr, pe, fe,
    o0, o1, o2, o3, order, v0, v1, v2, v3, v4, v5, mats, sem,
):
    pairs = list(zip((g1, c1, pb, g2, c2, fb), (v0, v1, v2, v3, v4, v5)))
    for k in range(ROWS):
        which = lax.rem(info[0] + k, ROWS) // 2
        a = jnp.where(which == 0, info[32], info[33])
        pairs += [(v.at[a], mats.at[4 * k + i]) for i, v in enumerate((qr, fr, pe, fe))]
    return [pltpu.make_async_copy(a, b, sem.at[i]) for i, (a, b) in enumerate(pairs)]


def route_pack_pre(*refs):
    for copy in route_copies(*refs):
        copy.start()
    fill_order(refs[0], refs[17])


def route_pack_body(*refs):
    info, own, oth = refs[:3]
    o0, o1, o2, o3, order, v0, v1, v2, v3, v4, v5, mats, _ = refs[13:]
    route_body(info, own, oth, o0, o1, o2, o3, order)
    for copy in route_copies(*refs):
        copy.wait()
    for k, dst in enumerate((o0, o1, o2, o3)):
        head = [f32(v[...]).reshape(1, TOK) for v in (v0, v1, v2, v3, v4, v5)]
        dst[256:272, :] = bf(jnp.concatenate(head + [jnp.zeros((10, TOK), F32)], axis=0))
        for i in range(4):
            dst[272 + 16 * i : 288 + 16 * i, :] = mats[4 * k + i]


def stack_body(a0, a1, a2, a3, h0, h1, h2, h3, dst):
    for k, (a, h) in enumerate(((a0, h0), (a1, h1), (a2, h2), (a3, h3))):
        dst[2 * k * TOK : (2 * k + 1) * TOK, :] = a[...]
        dst[(2 * k + 1) * TOK : (2 * k + 2) * TOK, :] = h[...]


def route_all_body(info, own, oth, w2, dst, order, sem):
    copies = []
    for z in range(ROWS):
        to = dst.at[z, pl.ds(TOK, 512)]
        copies.append(pltpu.make_async_copy(w2.at[rows_at(info[8], 512)], to, sem.at[z]))
    for copy in copies:
        copy.start()
    fill_order(info, order)
    c = info[2]
    for z in range(ROWS):
        for j in range(2):
            src = place_of(info, order, z, c, j)
            at = pl.ds(pl.multiple_of(lax.rem(src, 8) * BLOCK, BLOCK), BLOCK)
            mine = src // 8 == c

            @pl.when(mine)
            def _():
                dst[z, pl.ds(j * BLOCK, BLOCK), :] = own[at, :]

            @pl.when(jnp.logical_not(mine))
            def _():
                dst[z, pl.ds(j * BLOCK, BLOCK), :] = oth[at, :]
    for copy in copies:
        copy.wait()


def unroute_body(info, a, b, grad, hidden, order):
    fill_order(info, order)
    c = info[2]
    for s in range(ROWS):
        z = lax.rem(info[0] + s, ROWS)
        for other, src in ((0, a), (1, b)):
            core = c if other == 0 else 1 - c
            for j in range(2):
                at = place_of(info, order, z, core, j)

                @pl.when(at // 8 == c)
                def _():
                    rows = pl.ds(pl.multiple_of(lax.rem(at, 8) * BLOCK, BLOCK), BLOCK)
                    start = 2 * s * TOK + j * BLOCK
                    grad[rows, :] = f32(src[pl.ds(start, BLOCK), :])
                    hidden[rows, :] = src[pl.ds(start + TOK, BLOCK), :]


def cols(k, width=TOK):
    return pl.ds(k * width, width)


def row_stats(parts):
    total = sum(jnp.sum(v, axis=1, keepdims=True) for v in parts)
    mean = total * (1.0 / D)
    dev = [v - mean for v in parts]
    var = sum(jnp.sum(v * v, axis=1, keepdims=True) for v in dev) * (1.0 / D)
    rstd = lax.rsqrt(var + EPSILON)
    return [v * rstd for v in dev], rstd


def norm1_body(x0, x1, x2, x3, xn):
    for t in range(2):
        rows = pl.ds(t * 128, 128)
        hat, _ = row_stats([f32(v[rows, :]) for v in (x0, x1, x2, x3)])
        for k, pack in enumerate((x0, x1, x2, x3)):
            xn[rows, cols(k)] = bf(hat[k] * f32(pack[256:257, :]) + f32(pack[257:258, :]))


def both(a, b, rows, k):
    return f32(a[rows, cols(k)]) + f32(b[rows, cols(k)])


def norm2_body(a, b, x0, x1, x2, x3, mid, xn):
    for t in range(2):
        rows = pl.ds(t * 128, 128)
        parts = []
        for k, x in enumerate((x0, x1, x2, x3)):
            v = f32(x[rows, :]) + both(a, b, rows, k) + f32(x[258:259, :])
            mid[rows, cols(k)] = v
            parts.append(v)
        hat, _ = row_stats(parts)
        for k, pack in enumerate((x0, x1, x2, x3)):
            xn[rows, cols(k)] = bf(hat[k] * f32(pack[259:260, :]) + f32(pack[260:261, :]))


def norm_back(hat, rstd, grads):
    total = sum(jnp.sum(g, axis=1, keepdims=True) for g in grads) * (1.0 / D)
    along = sum(jnp.sum(g * h, axis=1, keepdims=True) for g, h in zip(grads, hat)) * (1.0 / D)
    return [rstd * (g - total - h * along) for g, h in zip(grads, hat)]


def norm2_back_body(
    a, b, pack, mid, g, x0, x1, x2, x3, d_mid, g_attn
):
    g_attn[256:320, :] = pack[...]
    for t in range(2):
        rows = pl.ds(t * 128, 128)
        hat, rstd = row_stats([mid[rows, cols(k)] for k in range(4)])
        grads = []
        for k, pack in enumerate((x0, x1, x2, x3)):
            grads.append(both(a, b, rows, k) * f32(pack[259:260, :]))
        back = norm_back(hat, rstd, grads)
        for k in range(4):
            v = f32(g[rows, cols(k)]) + back[k]
            d_mid[rows, cols(k)] = v
            g_attn[rows, cols(k)] = bf(v)


def norm1_back_body(a, b, d_mid, x0, x1, x2, x3, i0, i1, i2, i3):
    for t in range(2):
        rows = pl.ds(t * 128, 128)
        hat, rstd = row_stats([f32(v[rows, :]) for v in (x0, x1, x2, x3)])
        grads = []
        for k, pack in enumerate((x0, x1, x2, x3)):
            grads.append(both(a, b, rows, k) * f32(pack[256:257, :]))
        back = norm_back(hat, rstd, grads)
        for k, dst in enumerate((i0, i1, i2, i3)):
            dst[rows, :] = bf(d_mid[rows, cols(k)] + back[k])


def hidden_body(a, b, mid, x0, x1, x2, x3, h0, h1, h2, h3):
    for t in range(2):
        rows = pl.ds(t * 128, 128)
        for k, (pack, dst) in enumerate(zip((x0, x1, x2, x3), (h0, h1, h2, h3))):
            v = mid[rows, cols(k)] + both(a, b, rows, k) + f32(pack[261:262, :])
            dst[rows, :] = bf(v)


def join_body(info, v, dst, w2):
    for k in range(ROWS):
        dst[:, cols(k)] = v[rel(info, k), 0:TOK, :]
    for k in range(1, ROWS):
        w2[k - 1] = v[rel(info, k), TOK:, :]


def rest_body(info, v, dst):
    for k in range(1, ROWS):
        dst[k - 1] = v[rel(info, k)]


def slab_rows(info, b):
    y = jnp.bitwise_xor(info[1], b // 2)
    c = jnp.bitwise_xor(info[2], b % 2)
    return y, c


def low_lanes(rows):
    return lax.broadcasted_iota(jnp.int32, (rows, 128), 1) < HEAD


def rel(info, k):
    return lax.rem(info[0] - k + ROWS, ROWS)


def rel_cols(info, k):
    return pl.ds(pl.multiple_of(rel(info, k) * TOK, TOK), TOK)


def lanes_at(at, size):
    return pl.ds(pl.multiple_of(at, 128), size)


def rows_at(i, size):
    return pl.ds(pl.multiple_of(i * size, size), size)


def prepare_body(
    info, wq, wp, w1, qe, fe, pr, fr, first, c1, o_qe, o_fe, o_pr, o_fr, sem
):
    half = info[8]
    a = jnp.where(info[5] == 0, info[32], info[33])
    rows = rows_at(half, 128)
    pairs = [(wq.at[rows], first.at[:, 0:768]), (wp.at[rows], first.at[:, 768:1024])]
    pairs += [(qe.at[a, :, lanes_at(info[6] * 768, 768)], o_qe)]
    pairs += [(fe.at[a, :, lanes_at(info[6] * 1024, 1024)], o_fe)]
    pairs += [(pr.at[a], o_pr), (fr.at[a], o_fr)]
    for j in range(ROWS):
        pairs += [(w1.at[rows], c1.at[j])]
    copies = [pltpu.make_async_copy(x, y, sem.at[i]) for i, (x, y) in enumerate(pairs)]
    for copy in copies:
        copy.start()
    for copy in copies:
        copy.wait()


def assemble_body(info, own_q, own_p, z1, z2, z3, s1, s2, s3, ws, wp, sem):
    half = info[8]
    copies = [
        pltpu.make_async_copy(own_q, ws.at[0], sem.at[0]),
        pltpu.make_async_copy(own_p, wp.at[0], sem.at[1]),
    ]
    for k, (zv, sv) in enumerate(((z1, s1), (z2, s2), (z3, s3))):
        for n, (v, at) in enumerate(((zv, half), (sv, 1 - half))):
            rows = rows_at(at, 128)
            at = 2 + 4 * k + 2 * n
            copies.append(
                pltpu.make_async_copy(v.at[:, 0:768], ws.at[k + 1, rows], sem.at[at])
            )
            copies.append(
                pltpu.make_async_copy(v.at[:, 768:1024], wp.at[k + 1, rows], sem.at[at + 1])
            )
    for copy in copies:
        copy.start()
    for copy in copies:
        copy.wait()


def qkv_body(
    info, x0, x1, x2, x3, ws, p0, p1, p2, p3, bias, expand, q, kvp, kvc
):
    ps = (p0, p1, p2, p3)
    low = low_lanes(TOK)
    for b, x in enumerate((x0, x1, x2, x3)):
        y, c = slab_rows(info, b)
        acc = sum(nn(x[:, cols(k)], ws[k]) for k in range(4))
        u = bf(sum(nt(x[:, cols(k)], ps[k][272:288, :]) for k in range(4)))
        acc = acc + f32(bias[...]) + SCALE * nn(u, expand[...])
        kv = []
        for pair in range(2):
            at = 384 * pair
            g0, g1, g2 = (acc[:, at + 128 * i : at + 128 * i + 128] for i in range(3))
            q[rows_at(y * 2 + c, TOK), cols(pair, 128)] = bf(
                bf(jnp.where(low, g0, g1)) * BF(0.125)
            )
            kv.append((bf(pltpu.roll(jnp.where(low, g2, g0), 64, 1)), bf(jnp.where(low, g1, g2))))
        rows = rows_at(c, TOK)

        @pl.when(y == 0)
        def _():
            for pair in range(2):
                kvp[rows, cols(pair, 128)] = kv[pair][0]
                kvp[rows, cols(2 + pair, 128)] = kv[pair][1]

        @pl.when(y == 1)
        def _():
            for pair in range(2):
                kvc[rows, cols(pair, 128)] = kv[pair][0]
                kvc[rows, cols(2 + pair, 128)] = kv[pair][1]


WIDE = 256


def stacked(v, low):
    zero = jnp.zeros_like(v)
    return jnp.concatenate([jnp.where(low, v, zero), jnp.where(low, zero, v)], axis=0)


def split_id(shape, axis):
    lane = lax.broadcasted_iota(jnp.int32, shape, axis)
    return lane, jnp.where(lane < BLOCK, lane, lane - BLOCK)


def chunk_place(shape, axis, side, n):
    lane, within = split_id(shape, axis)
    first = block_at(side, n, 0) * BLOCK
    second = block_at(side, n, 1) * BLOCK
    return within + jnp.where(lane < BLOCK, first, second)


def keep_state(state, low):
    top, total, acc = state
    lane = lax.broadcasted_iota(jnp.int32, (2 * BLOCK, 128), 1)
    spot = lax.rem(lane, HEAD)
    row = lax.broadcasted_iota(jnp.int32, (2 * BLOCK, 128), 0)
    own = (lane < HEAD) == (row < BLOCK)
    return jnp.where(own, acc, jnp.where(spot == 0, top, total))


def load_state(v):
    lane = lax.broadcasted_iota(jnp.int32, (2 * BLOCK, 128), 1)
    row = lax.broadcasted_iota(jnp.int32, (2 * BLOCK, 128), 0)
    spot = jnp.where(row < BLOCK, HEAD, 0)
    top = jnp.max(jnp.where(lane == spot, v, LOW), axis=1, keepdims=True)
    total = jnp.sum(jnp.where(lane == spot + 1, v, 0.0), axis=1, keepdims=True)
    return top, total, v


def soft_update(state, s, v):
    if state is None:
        top = jnp.max(s, axis=1, keepdims=True)
        p = jnp.exp(s - top)
        return top, jnp.sum(p, axis=1, keepdims=True), nn(bf(p), v)
    top, total, acc = state
    new = jnp.maximum(top, jnp.max(s, axis=1, keepdims=True))
    p = jnp.exp(s - new)
    shrink = jnp.exp(top - new)
    total = total * shrink + jnp.sum(p, axis=1, keepdims=True)
    return new, total, acc * shrink + nn(bf(p), v)


def head_slopes(slopes, shape, axis):
    lane = lax.broadcasted_iota(jnp.int32, shape, axis)
    return [
        jnp.where(lane < BLOCK, slopes[2 * pair], slopes[2 * pair + 1]) for pair in range(2)
    ]


def attend_chunk(q2, states, kv, rows, place, base, slope, spot, masked):
    res = []
    away = place - base
    for pair in range(2):
        s = nt(q2[pair], kv[rows, cols(pair, 128)]) + slope[pair] * away.astype(F32)
        if masked:
            s = jnp.where(away <= spot, s, LOW)
        res.append(soft_update(states[pair], s, kv[rows, cols(2 + pair, 128)]))
    return res


def attend_first_body(info, slopes, q, kvp, kvc, state):
    zl = info[4]
    low = low_lanes(BLOCK)
    _, spot = split_id((2 * BLOCK, 1), 0)
    slope = head_slopes(slopes, (2 * BLOCK, 1), 0)
    places = [chunk_place((1, WIDE), 1, zl, n) for n in range(2)]

    def load(i):
        return [stacked(q[rows_at(i, BLOCK), cols(pair, 128)], low) for pair in range(2)]

    def save(states, i):
        for pair in range(2):
            state[rows_at(i, WIDE), cols(pair, 128)] = keep_state(states[pair], low)

    def prompt_block(j, _):
        for n in range(2):
            i = 2 * n + j
            base = block_at(zl, n, j) * BLOCK
            q2 = load(i)
            states = [None, None]
            for m in range(n, -1, -1):
                states = attend_chunk(
                    q2, states, kvp, pl.ds(m * WIDE, WIDE), places[m], base, slope, spot, m == n
                )
            save(states, i)
        return 0

    lax.fori_loop(0, 2, prompt_block, 0)

    def cont_block(j, _):
        q2 = load(4 + j)
        own_place = lax.broadcasted_iota(jnp.int32, (1, BLOCK), 1)
        states = attend_chunk(
            q2, [None, None], kvc, rows_at(j, BLOCK), own_place, 0, slope, spot, True
        )
        for m in range(2):
            states = attend_chunk(
                q2, states, kvp, pl.ds(m * WIDE, WIDE), places[m], PROMPT, slope, spot, False
            )
        save(states, 4 + j)
        return 0

    lax.fori_loop(0, 4, cont_block, 0)


def attend_rest_body(
    which, info, slopes, q, kvo, state, ws, reduce, p0, p1, p2, p3, heads, lse, o0, o1
):
    zl = info[4]
    y = info[1] if which == 0 else 1 - info[1]
    low = low_lanes(BLOCK)
    _, spot = split_id((2 * BLOCK, 1), 0)
    slope = head_slopes(slopes, (2 * BLOCK, 1), 0)
    places = [chunk_place((1, WIDE), 1, 1 - zl, n) for n in range(2)]

    def load(i):
        q2 = [stacked(q[rows_at(i, BLOCK), cols(pair, 128)], low) for pair in range(2)]
        states = [load_state(state[rows_at(i, WIDE), cols(pair, 128)]) for pair in range(2)]
        return q2, states

    def finish(states, j):
        for pair in range(2):
            top, total, acc = states[pair]
            res = acc / total
            heads[rows_at(j, BLOCK), cols(pair, 128)] = bf(
                jnp.where(low, res[:BLOCK], res[BLOCK:])
            )
            kept = jnp.transpose(jnp.broadcast_to(top + jnp.log(total), (2 * BLOCK, 128)))
            lse[pl.ds(pair * 4 + j, 1), :] = kept[0:1, :]

    @pl.when(y == 0)
    def _():
        def prompt_block(j, _):
            for n in range(2):
                i = 2 * n + j
                base = block_at(zl, n, j) * BLOCK
                q2, states = load(i)
                for m in range(n + 1):
                    states = attend_chunk(
                        q2, states, kvo, pl.ds(m * WIDE, WIDE), places[m], base, slope, spot, m == n
                    )
                finish(states, i)
            return 0

        lax.fori_loop(0, 2, prompt_block, 0)

    @pl.when(y == 1)
    def _():
        def cont_block(j, _):
            q2, states = load(4 + j)
            for m in range(2):
                states = attend_chunk(
                    q2, states, kvo, pl.ds(m * WIDE, WIDE), places[m], PROMPT, slope, spot, False
                )
            finish(states, j)
            return 0

        lax.fori_loop(0, 4, cont_block, 0)

    ps = (p0, p1, p2, p3)
    for b, dst in enumerate((o0, o1)):
        c = jnp.bitwise_xor(info[2], b)
        h = heads[rows_at(c, TOK), :]
        u = bf(nt(h, reduce[...]))
        for k in range(4):
            dst[:, cols(k)] = bf(nn(h, ws[k]) + SCALE * nn(u, ps[k][304:320, :]))


def mlp_pre_body(info, x0, x1, w1, p0, p1, p2, p3, bias, expand, act, slope):
    ps = (p0, p1, p2, p3)
    for b, x in enumerate((x0, x1)):
        u = bf(sum(nt(x[:, cols(k)], ps[k][288:304, :]) for k in range(4)))
        pre = sum(nn(x[:, cols(k)], w1[rel(info, k)]) for k in range(4))
        pre = pre + f32(bias[...]) + SCALE * nn(u, expand[...])
        sq = pre * pre
        t = jnp.tanh(pre * (GELU_A + (GELU_A * GELU_B) * sq))
        half = 0.5 + 0.5 * t
        act[b] = bf(pre * half)
        slope[b] = bf(
            half + (0.5 * pre) * (1.0 - t * t) * (GELU_A + (3.0 * GELU_A * GELU_B) * sq)
        )


def mlp_back_body(
    info, x0, x1, g0, g1, slope, w1, w2, p0, p1, p2, p3, expand, reduce, r_in, e_in,
    d0, d1, r_out, e_out,
):
    ps = (p0, p1, p2, p3)
    rv, ev = r_in[...], e_in[...]
    for b, (x, g, dx) in enumerate(((x0, g0, d0), (x1, g1, d1))):
        u = bf(sum(nt(x[:, cols(k)], ps[k][288:304, :]) for k in range(4)))
        du2 = bf(SCALE * sum(nt(g[:, cols(k)], ps[k][320:336, :]) for k in range(4)))
        d_act = sum(nt(g[:, cols(k)], w2[rel(info, k)]) for k in range(4)) + nn(du2, reduce[...])
        d_pre = bf(d_act * f32(slope[b]))
        du = bf(SCALE * nt(d_pre, expand[...]))
        for k in range(4):
            dx[:, cols(k)] = bf(nt(d_pre, w1[rel(info, k)]) + nn(du, ps[k][288:304, :]))
        rv = rv + tn(du, x[...])
        ev = ev + tn(u, d_pre)
    r_out[...] = rv
    e_out[...] = ev


def fc2_body(
    info, a0, a1, g0, g1, g2, g3, w2, reduce, p0, p1, p2, p3, r1, e1,
    m0, m1, m2, m3, grads,
):
    ps = (p0, p1, p2, p3)
    rv = ev = 0.0
    for b, (g, m) in enumerate(zip((g0, g1, g2, g3), (m0, m1, m2, m3))):
        act = a0[b] if b < 2 else a1[b - 2]
        du = bf(SCALE * sum(nt(g[:, cols(k)], ps[k][320:336, :]) for k in range(4)))
        u = bf(nt(act, reduce[...]))
        for k in range(4):
            m[:, cols(k)] = bf(nn(act, w2[rel(info, k)]) + SCALE * nn(u, ps[k][320:336, :]))
        rv = rv + tn(du, act)
        ev = ev + SCALE * tn(u, g[...])
    for k in range(4):
        grads[0:16, rel_cols(info, k)] = bf(r1[:, cols(k)])
        grads[16:32, rel_cols(info, k)] = bf(ev[:, k * TOK : k * TOK + TOK])
    grads[32:48, :] = bf(SCALE * e1[...])
    grads[48:64, :] = bf(rv)


def d_heads_body(
    info, g0, g1, ws, p0, p1, p2, p3, reduce, heads, r_in, e_in, dh, r_out, e_out
):
    ps = (p0, p1, p2, p3)
    rv, ev = r_in[...], e_in[...]
    for b, g in enumerate((g0, g1)):
        rows = rows_at(jnp.bitwise_xor(info[2], b), TOK)
        h = heads[rows, :]
        u = bf(nt(h, reduce[...]))
        du = bf(SCALE * sum(nt(g[0:256, cols(k)], ps[k][304:320, :]) for k in range(4)))
        v = sum(nt(g[0:256, cols(k)], ws[k]) for k in range(4)) + nn(du, reduce[...])
        dh[rows, :] = bf(v)
        rv = rv + tn(du, h)
        ev = ev + SCALE * tn(u, g[0:256, :])
    r_out[...] = rv
    e_out[...] = ev


def back_load(heads, d_heads, lse, q, qi, j, low):
    res = []
    for pair in range(2):
        lane = cols(pair, 128)
        q2 = stacked(q[rows_at(qi, BLOCK), lane], low)
        do = d_heads[rows_at(j, BLOCK), lane]
        both = jnp.transpose(f32(do) * f32(heads[rows_at(j, BLOCK), lane]))
        delta = jnp.concatenate(
            [
                jnp.sum(both[:HEAD], axis=0, keepdims=True),
                jnp.sum(both[HEAD:], axis=0, keepdims=True),
            ],
            axis=1,
        )
        res.append((q2, stacked(do, low), delta, lse[pl.ds(pair * 4 + j, 1), :]))
    return res


def back_chunk(args, kv, d_kv, d_at, rows, place, base, slope, spot, masked, store, d_qs):
    away = place - base
    res = []
    for pair in range(2):
        q2, do2, delta, kept = args[pair]
        lane = cols(pair, 128)
        vlane = cols(2 + pair, 128)
        k = kv[rows, lane]
        s = nt(k, q2) + (away.astype(F32) * slope[pair] - kept)
        p = jnp.exp(s)
        if masked:
            p = jnp.where(away <= spot, p, 0.0)
        ds = bf(p * (nt(kv[rows, vlane], do2) - delta))
        dk = nn(ds, q2)
        dv = nn(bf(p), do2)
        if store:
            d_kv[d_at, lane] = bf(dk)
            d_kv[d_at, vlane] = bf(dv)
        else:
            d_kv[d_at, lane] += dk
            d_kv[d_at, vlane] += dv
        d_q = tn(ds, k)
        res.append(d_q if d_qs is None else d_qs[pair] + d_q)
    return res


def back_common(info, slopes):
    low = low_lanes(BLOCK)
    _, spot = split_id((1, 2 * BLOCK), 1)
    slope = head_slopes(slopes, (1, 2 * BLOCK), 1)
    zl = info[4]
    own = [chunk_place((WIDE, 1), 0, zl, n) for n in range(2)]
    oth = [chunk_place((WIDE, 1), 0, 1 - zl, n) for n in range(2)]
    return zl, low, spot, slope, own, oth


def fold(d_q, low):
    return jnp.where(low, d_q[:BLOCK], d_q[BLOCK:]) * 0.125


def back_sweep(info, slopes, y, q, heads, d_heads, lse, sides, kvc, dkc, finish):
    zl, low, spot, slope, own, oth = back_common(info, slopes)
    place_sets = {"own": own, "oth": oth}

    @pl.when(y == 0)
    def _():
        def prompt_block(j, _):
            for n in range(2):
                i = 2 * n + j
                args = back_load(heads, d_heads, lse, q, i, i, low)
                base = block_at(zl, n, j) * BLOCK
                d_qs = None
                for side, kv, d_kv in sides:
                    for m in range(n + 1):
                        rows = pl.ds(m * WIDE, WIDE)
                        d_qs = back_chunk(
                            args, kv, d_kv, rows, rows, place_sets[side][m], base, slope, spot,
                            m == n, False, d_qs,
                        )
                finish(d_qs, i, low)
            return 0

        lax.fori_loop(0, 2, prompt_block, 0)

    @pl.when(y == 1)
    def _():
        def cont_block(j, _):
            args = back_load(heads, d_heads, lse, q, 4 + j, j, low)
            d_qs = None
            if kvc is not None:
                mine = rows_at(j, BLOCK)
                own_place = lax.broadcasted_iota(jnp.int32, (BLOCK, 1), 0)
                d_qs = back_chunk(
                    args, kvc, dkc, mine, mine, own_place, 0, slope, spot, True, True, d_qs
                )
            for side, kv, d_kv in sides:
                for m in range(2):
                    rows = pl.ds(m * WIDE, WIDE)
                    d_qs = back_chunk(
                        args, kv, d_kv, rows, rows, place_sets[side][m], PROMPT, slope, spot,
                        False, False, d_qs,
                    )
            finish(d_qs, j, low)
            return 0

        lax.fori_loop(0, 4, cont_block, 0)


def clear_back(*refs):
    for ref in refs[10:13]:
        ref[...] = jnp.zeros_like(ref)


def attend_back_a_body(
    info, slopes, q, kvp, kvo, kvc, heads, d_heads, lse, dq, dkp, dko, dkc
):

    def finish(d_qs, j, low):
        for pair in range(2):
            dq[rows_at(j, BLOCK), cols(pair, 128)] = bf(fold(d_qs[pair], low))

    back_sweep(
        info, slopes, info[1], q, heads, d_heads, lse,
        (("own", kvp, dkp), ("oth", kvo, dko)), kvc, dkc, finish,
    )


def attend_back_b_body(
    info, slopes, q, kvo, heads, d_heads, lse, dko_in, early, dq, dko, acc
):
    acc[...] = dko_in[...]

    def finish(d_qs, j, low):
        for pair in range(2):
            dq[rows_at(j, BLOCK), cols(pair, 128)] = fold(d_qs[pair], low)

    back_sweep(
        info, slopes, 1 - info[1], q, heads, d_heads, lse,
        (("oth", kvo, acc),), None, None, finish,
    )
    dko[0:512, :] = bf(acc[...])
    dko[512:592, :] = early[:, 0:512]
    dko[592:672, :] = early[:, 512:1024]


def early_sum_body(own, other, dst):
    dst[:, 0:512] = bf(f32(own[:, 0:512]) + f32(other[512:592, :]))
    dst[:, 512:1024] = bf(f32(own[:, 512:1024]) + f32(other[592:672, :]))


def attend_back_c_body(
    info, slopes, q, kvp, kvc, heads, d_heads, lse, dkp_in, dkc_in, dq_in, dq, dkp, dkc
):
    dkp[...] = dkp_in[...]
    dkc[...] = dkc_in[...]

    def finish(d_qs, j, low):
        for pair in range(2):
            lane = cols(pair, 128)
            rows = rows_at(j, BLOCK)
            dq[rows, lane] = bf(dq_in[rows, lane] + fold(d_qs[pair], low))

    back_sweep(
        info, slopes, 1 - info[1], q, heads, d_heads, lse,
        (("own", kvp, dkp),), kvc, dkc, finish,
    )


def qkv_back_body(
    info, dq0, dq1, dkp, dkr, dkc, x0, x1, x2, x3, ws, p0, p1, p2, p3, expand, pr, pe,
    o0, o1, o2, o3, grads,
):
    ps = (p0, p1, p2, p3)
    low = low_lanes(TOK)
    sr = se = 0.0
    for b, (x, dst) in enumerate(zip((x0, x1, x2, x3), (o0, o1, o2, o3))):
        y, c = slab_rows(info, b)
        half = rows_at(c, TOK)
        groups = []
        dq = dq0 if b < 2 else dq1
        for pair in range(2):
            vq = f32(dq[half, cols(pair, 128)])
            got = []
            for lane in (cols(pair, 128), cols(2 + pair, 128)):
                prompt = dkp[half, lane] + f32(dkr[half, lane])
                got.append(jnp.where(y == 0, prompt, f32(dkc[half, lane])))
            vk = pltpu.roll(got[0], 64, 1)
            vv = got[1]
            groups += [jnp.where(low, vq, vk), jnp.where(low, vv, vq), jnp.where(low, vk, vv)]
        d = bf(jnp.concatenate(groups, axis=1))
        u = bf(sum(nt(x[:, cols(k)], ps[k][272:288, :]) for k in range(4)))
        du = bf(SCALE * nt(d, expand[...]))
        for k in range(4):
            dst[:, cols(k)] = bf(nt(d, ws[k]) + nn(du, ps[k][272:288, :]))
        sr = sr + tn(du, x[...])
        se = se + SCALE * tn(u, d)
    for k in range(4):
        grads[0:16, rel_cols(info, k)] = bf(sr[:, k * TOK : k * TOK + TOK])
        grads[16:32, rel_cols(info, k)] = bf(pe[:, cols(k)])
    grads[32:48, 0:768] = bf(se)
    grads[32:48, 768:1024] = bf(pr[...])


def add_body(a, b, dst):
    dst[...] = bf(f32(a[...]) + f32(b[...]))


def add(a, b):
    return call(add_body, [out(a.shape, BF)], [a, b], smem=0, us=0.01, name="add")[0]


def add32_body(a, b, dst):
    dst[...] = f32(a[...]) + f32(b[...])


def add32(a, b, us=8):
    return call(add32_body, [out(a.shape, F32)], [a, b], smem=0, us=us, name="add32")[0]


def stage_body(*refs):
    n = len(refs) // 2
    for src, dst in zip(refs[:n], refs[n:]):
        dst[...] = src[...]


def stage(values):
    return call(
        stage_body, [out(v.shape, v.dtype) for v in values], far(values), smem=0, us=0.01, name="stage"
    )


def stage_weight_body(size, info, own, wr, ws, w, sem):
    copies = [pltpu.make_async_copy(own, w.at[info[0]], sem.at[6])]
    for n, (src, at) in enumerate(((wr, info[8]), (ws, 1 - info[8]))):
        for k in range(1, ROWS):
            to = w.at[rel(info, k), rows_at(at, size)]
            copies.append(pltpu.make_async_copy(src.at[k - 1], to, sem.at[3 * n + k - 1]))
    for copy in copies:
        copy.start()
    for copy in copies:
        copy.wait()


def merge_body(info, v0, v1, v2, v3, dst):
    four = (v0, v1, v2, v3)

    def fill(c):
        total = sum(f32(v[256 + 16 * c : 272 + 16 * c, :]) for v in four)
        dst[0:16, :] = bf(total)
        for b, v in enumerate(four):
            rows = pl.ds(pl.multiple_of(16 + 16 * jnp.bitwise_xor(info[6], b), 16), 16)
            dst[rows, :] = v[288 + 16 * c : 304 + 16 * c, :]

    @pl.when(info[2] == 0)
    def _():
        fill(0)

    @pl.when(info[2] == 1)
    def _():
        fill(1)


def pile_body(*refs):
    dst = refs[-1]
    for n, src in enumerate(refs[:-1]):
        dst[n] = src[...]


def expand_early_body(info, own, oth, r1, e2, e1, r2):
    for v in (r1, e2, e1, r2):
        v[...] = jnp.zeros_like(v)

    def fill(src, shared, split):
        for n in range(own.shape[0]):
            group = info[5] if n % 2 == 0 else 1 - info[5]
            a = info[40 + n // 2 * GROUPS_DEV + group]
            shared[a] += f32(src[n, 0:16, :])
            for j in range(COLS):
                at = 16 + 16 * j
                split[a, :, cols(j, 1024)] += f32(src[n, at : at + 16, :])

    @pl.when(info[2] == 0)
    def _():
        fill(own, r1, e1)
        fill(oth, e2, r2)

    @pl.when(info[2] == 1)
    def _():
        fill(oth, r1, e1)
        fill(own, e2, r2)


def expand_late_body(info, v0, v1, v2, v3, qr, pe, qe, pr):
    four = (v0, v1, v2, v3)
    for v in (qr, pe, qe, pr):
        v[...] = jnp.zeros_like(v)
    for k in range(v0.shape[0]):
        group = info[5] if k % 2 == 0 else 1 - info[5]
        a = info[40 + k // 2 * GROUPS_DEV + group]
        qr[a] += sum(f32(v[k, 0:16, :]) for v in four)
        pe[a] += sum(f32(v[k, 16:32, :]) for v in four)
        for b, v in enumerate(four):
            j = jnp.bitwise_xor(info[6], b)
            qe[a, :, lanes_at(j * 768, 768)] += f32(v[k, 32:48, :768])
            pr[a, :, lanes_at(j * 256, 256)] += f32(v[k, 32:48, 768:])


def shift(v, k, axis="row"):
    if k == 0:
        return v
    size = lax.axis_size(axis)
    return lax.ppermute(v, axis, [(s, (s + k) % size) for s in range(size)])


def gather_row(v):
    return [v] + [shift(v, k) for k in range(1, ROWS)]


def gather_col(v):
    core = lax.ppermute(v, "col", CORE_SWAP)
    side = lax.ppermute(v, "col", Y_SWAP)
    return [v, core, side, lax.ppermute(side, "col", CORE_SWAP)]


def to_cols(pieces):
    return [pieces[0]] + [shift(pieces[k], ROWS - k) for k in range(1, ROWS)]


def spread(mine, other):
    return [mine, other] + [
        shift(v, k, "dp") for k in range(1, lax.axis_size("dp")) for v in (mine, other)
    ]


def pile(parts):
    shape = (len(parts), *parts[0].shape)
    return call(pile_body, [out(shape, BF)], parts, smem=0, us=0.01, name="pile")[0]

def body(
    hidden_in,
    out_grad,
    first_norm_gain,
    first_norm_bias,
    qkv_weight,
    qkv_bias,
    proj_weight,
    proj_bias,
    second_norm_gain,
    second_norm_bias,
    fc1_weight,
    fc1_bias,
    fc2_weight,
    second_feed_bias,
    qkv_reduce,
    qkv_expand,
    proj_reduce,
    proj_expand,
    fc1_reduce,
    fc1_expand,
    fc2_reduce,
    fc2_expand,
    adapter_choice,
    cont_prompt,
):
    r = lax.axis_index("row")
    col = lax.axis_index("col")
    dp = lax.axis_index("dp")
    y = col // 2
    c = lax.rem(col, 2)
    zl = lax.rem(r, 2)
    group = r // 2
    half = lax.rem(dp, 2)
    dp_swap = [(k, k ^ 1) for k in range(lax.axis_size("dp"))]
    slopes = jnp.exp2(
        -8.0 * (col * 4 + 1 + jnp.arange(4, dtype=jnp.int32)).astype(F32) / HEADS
    )
    adapter = jnp.where(group == 0, adapter_choice[0], adapter_choice[1])
    dp_size = jnp.int32(lax.axis_size("dp"))
    info = jnp.stack([r, y, c, dp * GROUPS_DEV, zl, group, col, dp, half] + [half, dp_size] + [half] * 5)
    info = jnp.concatenate([info.astype(jnp.int32), cont_prompt, adapter_choice])
    order = pltpu.SMEM((GROUPS_DEV * NCONT,), jnp.int32)
    flip = functools.partial(jnp.transpose, axes=(0, 2, 1))
    big = out((TOK, D), BF)
    small = out((RANK, D), F32)

    other = lax.ppermute(hidden_in, "col", CORE_SWAP)
    vectors = [
        first_norm_gain, first_norm_bias, proj_bias,
        second_norm_gain, second_norm_bias, second_feed_bias,
    ]
    factors = [flip(qkv_reduce), flip(fc1_reduce), proj_expand, fc2_expand]
    pieces = call(
        route_pack_body,
        [out((336, TOK), BF)] * 4,
        [info, Far(hidden_in), Far(other), *far(vectors), *far(factors)],
        [
            order,
            *[pltpu.VMEM((TOK,), BF)] * 6,
            pltpu.VMEM((16, RANK, TOK), BF),
            pltpu.SemaphoreType.DMA((22,)),
        ],
        raw=range(3, 13),
        pre=route_pack_pre,
        us=1.5,
        name="route_x",
    )
    xs = [pieces[0]] + [shift(pieces[k], k) for k in range(1, ROWS)]
    packs = far(xs)
    first_half, w1_copies, qkv_e, fc1_e, proj_r, fc2_r = call(
        prepare_body,
        [
            out((128, D), BF), out((ROWS, 128, D), BF),
            out((RANK, 768), BF), out((RANK, D), BF), out((RANK, TOK), BF), out((RANK, D), BF),
        ],
        [
            after(info, pieces[0]),
            *far([qkv_weight, proj_weight, fc1_weight, qkv_expand, fc1_expand]),
            *far([flip(proj_reduce), flip(fc2_reduce)]),
        ],
        [pltpu.SemaphoreType.DMA((10,))],
        raw=range(1, 8),
        us=3,
        name="prepare",
    )
    first_half = after(first_half, xs[1])
    z_parts = [shift(first_half, k) for k in range(1, ROWS)]
    s_parts = [lax.ppermute(v, "dp", dp_swap) for v in z_parts]
    wq, wp = call(
        assemble_body,
        [out((ROWS, TOK, 768), BF), out((ROWS, TOK, TOK), BF)],
        [info, *far([qkv_weight, proj_weight, *z_parts, *s_parts])],
        [pltpu.SemaphoreType.DMA((14,))],
        raw=range(1, 9),
        us=15,
        name="assemble",
    )

    qkv_b = lax.dynamic_slice_in_dim(qkv_bias, col * 768, 768, 0)[None, :]
    fc1_b = lax.dynamic_slice_in_dim(fc1_bias, col * 1024, 1024, 0)[None, :]

    choices = [adapter_choice] + [
        shift(adapter_choice, k, "dp") for k in range(1, lax.axis_size("dp"))
    ]
    first = after(xs[0], qkv_b, fc1_b, w1_copies, *choices)
    (xn1,) = call(norm1_body, [big], [first, *xs[1:]], smem=0, us=8, name="norm1")
    xn1s = gather_col(xn1)
    q, kvp, kvc = call(
        qkv_body,
        [out((1024, 256), BF), out((512, 512), BF), out((512, 512), BF)],
        [info, *xn1s, wq, *packs, Far(qkv_b), Far(qkv_e)],
        us=6.5,
        name="qkv",
    )
    kvo = lax.ppermute(kvp, "row", Z_SWAP)

    g_other = lax.ppermute(after(out_grad, kvp), "col", CORE_SWAP)
    (pieces,) = call(
        route_all_body,
        [out((ROWS, 3 * TOK, TOK), BF)],
        [info, Far(out_grad), Far(g_other), Far(fc2_weight)],
        [order, pltpu.SemaphoreType.DMA((4,))],
        raw=(3,),
        us=1,
        name="route_g",
    )
    (state,) = call(
        attend_first_body,
        [out((2048, 256), F32)],
        [info, slopes, q, kvp, kvc],
        smem=2,
        us=9,
        name="attend_first",
    )
    (w1r,) = call(
        rest_body,
        [out((3, 128, D), BF)],
        [info, after(lax.all_to_all(after(w1_copies, *z_parts), "row", 0, 0), state)],
        us=0.01,
        name="rest",
    )
    w1s = lax.ppermute(w1r, "dp", dp_swap)
    pieces = after(pieces, state, kvo)
    g_own, w2r = call(
        join_body,
        [big, out((3, 512, TOK), BF)],
        [info, lax.all_to_all(pieces, "row", 0, 0)],
        us=0.01,
        name="join",
    )
    g_side = lax.ppermute(g_own, "col", Y_SWAP)
    w2s = lax.ppermute(w2r, "dp", dp_swap)

    def attend_rest(which, q, state):
        return call(
            functools.partial(attend_rest_body, which),
            [out((512, 256), BF), out((8, 256), F32), big, big],
            [info, slopes, Far(q), kvo, state, Far(wp), Far(proj_r), *packs],
            smem=2,
            us=20 if which else 0.01,
            name="attend_rest",
        )

    heads1, lse1, p2, p3 = attend_rest(1, q, after(state, w1r))
    g_core = lax.ppermute(g_own, "col", CORE_SWAP)
    g_all = [g_own, g_core, g_side, lax.ppermute(g_side, "col", CORE_SWAP)]
    p_far = lax.ppermute(p3, "col", CORE_SWAP)
    p_side = add(p2, p_far)
    heads0, lse0, p0, p1 = attend_rest(0, q, Far(after(state, p_side)))
    p_side = lax.ppermute(p_side, "col", Y_SWAP)
    p_core = lax.ppermute(p1, "col", CORE_SWAP)
    staged = stage([after(xs[0], p0), *xs[1:]])
    mid, xn2 = call(
        norm2_body,
        [out((TOK, D), F32), big],
        [add32(after(p0, w1s), p_side), p_core, *staged],
        smem=0,
        us=1.5,
        hbm=(0,),
        name="norm2",
    )
    (w1,) = call(
        functools.partial(stage_weight_body, 128),
        [out((ROWS, TOK, D), BF)],
        [info, Far(fc1_weight), Far(after(w1r, p0)), Far(w1s)],
        [pltpu.SemaphoreType.DMA((7,))],
        raw=(1, 2, 3),
        us=2,
        name="stage_w1",
    )
    zero = jnp.zeros((RANK, D), F32)
    xn2_core = lax.ppermute(xn2, "col", CORE_SWAP)
    xn2_side = lax.ppermute(xn2, "col", Y_SWAP)

    def mlp_pre(first, blocks):
        return call(
            mlp_pre_body,
            [out((2, TOK, D), BF)] * 2,
            [info, *blocks, w1, *staged, Far(fc1_b), Far(fc1_e)],
            us=0.01,
            name="mlp_pre",
        )

    act0, slope0 = mlp_pre(0, [xn2, xn2_core])
    xn2_far = lax.ppermute(after(xn2_side, act0), "col", CORE_SWAP)
    xn2s = [xn2, xn2_core, xn2_side, xn2_far]
    act1, slope1 = mlp_pre(1, xn2s[2:])
    (w2,) = call(
        functools.partial(stage_weight_body, 512),
        [out((ROWS, D, TOK), BF)],
        [info, Far(fc2_weight), Far(after(w2r, act0)), Far(w2s)],
        [pltpu.SemaphoreType.DMA((7,))],
        raw=(1, 2, 3),
        us=20,
        name="stage_w2",
    )

    def mlp_back(blocks, slope, r_in, e_in):
        xa, xb = (xn2s[b] for b in blocks)
        ga, gb = (g_all[b] for b in blocks)
        return call(
            mlp_back_body,
            [big, big, small, small],
            [info, xa, xb, ga, gb, slope, w1, w2, *staged, Far(fc1_e), Far(fc2_r), r_in, e_in],
            us=0.01,
            name="mlp_back",
        )

    d2, d3, r1, e1 = mlp_back((2, 3), slope1, zero, zero)
    d_far = lax.ppermute(d3, "col", CORE_SWAP)
    d_side = add(d2, d_far)
    d0, d1, r1, e1 = mlp_back((0, 1), slope0, after(r1, d_side), e1)
    d_side = lax.ppermute(d_side, "col", Y_SWAP)
    d_core = lax.ppermute(d1, "col", CORE_SWAP)
    res = call(
        fc2_body,
        [big] * 4 + [out((64, D), BF)],
        [info, act0, act1, *g_all, w2, Far(fc2_r), *staged, r1, e1],
        us=0.01,
        name="fc2",
    )
    m_parts, mlp_pack = res[:4], res[4]
    staged_back = stage([after(mid, mlp_pack), g_own, *xs])
    d_mid, g_attn = call(
        norm2_back_body,
        [out((TOK, D), F32), out((320, D), BF)],
        [add32(d0, d_side), d_core, mlp_pack, *staged_back],
        smem=0,
        us=1.5,
        hbm=(0,),
        name="norm2_back",
    )
    ga_core = lax.ppermute(g_attn, "col", CORE_SWAP)
    ga_side = lax.ppermute(g_attn, "col", Y_SWAP)
    shared = far([q, kvp, kvo, kvc])

    def d_heads(blocks, heads, r_in, e_in):
        return call(
            d_heads_body,
            [out((512, 256), BF), out((RANK, TOK), F32), small],
            [info, *blocks, Far(wp), *packs, Far(proj_r), Far(heads), r_in, e_in],
            us=1.5,
            name="d_heads",
        )

    dh0, pr, pe = d_heads([g_attn, ga_core], heads0, jnp.zeros((RANK, TOK), F32), zero)
    dq0, dkp, dko, dkc = call(
        attend_back_a_body,
        [out((512, 256), BF), out((512, 512), F32), out((512, 512), F32), out((512, 512), BF)],
        [info, slopes, *shared, Far(heads0), dh0, Far(lse0)],
        smem=2,
        us=16,
        weight=W_BIG,
        hbm=(1, 2, 3),
        pre=clear_back,
        name="attend_back_a",
    )
    ga_side = after(ga_side, dq0)
    ga_far = lax.ppermute(ga_side, "col", CORE_SWAP)
    (early_half,) = call(
        merge_body,
        [out((80, D), BF)],
        [info, g_attn, ga_core, ga_side, ga_far],
        us=0.7,
        name="merge",
    )
    dh1, pr, pe = d_heads([ga_side, ga_far], heads1, pr, pe)
    dq1_part, dko = call(
        attend_back_b_body,
        [out((512, 256), F32), out((672, 512), BF)],
        [info, slopes, Far(q), Far(kvo), Far(heads1), dh1, Far(lse1), Far(dko), early_half],
        [pltpu.VMEM((512, 512), F32)],
        smem=2,
        us=8,
        hbm=(0,),
        name="attend_back_b",
    )
    dkr = lax.ppermute(dko, "row", Z_SWAP)
    dq1, dkp, dkc = call(
        attend_back_c_body,
        [out((512, 256), BF), out((512, 512), F32), out((512, 512), BF)],
        [info, slopes, Far(q), Far(kvp), Far(kvc), Far(heads1), dh1, Far(lse1), *far([dkp, dkc, dq1_part])],
        smem=2,
        us=8,
        hbm=(2,),
        name="attend_back_c",
    )
    (early_sum,) = call(
        early_sum_body, [out((80, D), BF)], [early_half, dkr], smem=0, us=0.01, name="early_sum"
    )
    m_far = lax.ppermute(after(m_parts[3], dq0), "col", CORE_SWAP)
    m_core = lax.ppermute(after(m_parts[1], dq0), "col", CORE_SWAP)
    m_sum = add(after(m_parts[2], dko), m_far)
    m_side = lax.ppermute(m_sum, "col", Y_SWAP)
    hidden = call(
        hidden_body,
        [out((TOK, TOK), BF)] * 4,
        [add32(m_parts[0], m_side, 0.01), m_core, Far(mid), *packs],
        smem=0,
        us=0.01,
        name="hidden",
    )
    res = call(
        qkv_back_body,
        [big] * 4 + [out((48, D), BF)],
        [
            info, dq0, dq1, dkp, after(dkr, early_sum, hidden[0]), Far(dkc),
            *far(xn1s), Far(wq), *packs, Far(qkv_e), pr, pe,
        ],
        us=20,
        name="qkv_back",
    )
    q_parts, late_pack = res[:4], res[4]
    early_next = shift(early_sum, 2)
    n_dp = lax.axis_size("dp")
    early_mine = [early_sum] + [shift(early_sum, k, "dp") for k in range(1, n_dp)]
    ready = after(q_parts[3], m_side, early_next, *early_mine)
    q_sum = add(q_parts[2], lax.ppermute(ready, "col", CORE_SWAP))
    hidden_got = to_cols(hidden)
    k0, rc = q_parts[0], lax.ppermute(q_parts[1], "col", CORE_SWAP)
    ry = lax.ppermute(q_sum, "col", Y_SWAP)
    late_sum = add(late_pack, lax.ppermute(after(late_pack, q_sum), "row", Z_SWAP))
    late_next = shift(late_sum, 2)
    early_rest = after(early_next, late_sum)
    early_rest = [early_next] + [shift(early_rest, k, "dp") for k in range(1, n_dp)]
    early_parts = [v for pair in zip(early_mine, early_rest) for v in pair]
    late_four = pile(spread(late_sum, late_next))
    late_all = gather_col(late_four)
    staged_last = stage([after(d_mid, k0, rc), *xs])
    ins = call(
        norm1_back_body,
        [out((TOK, TOK), BF)] * 4,
        [add32(after(k0, late_next, *hidden_got), ry), rc, *staged_last],
        smem=0,
        us=1,
        name="norm1_back",
    )
    early_all = pile(early_parts)
    early_far = lax.ppermute(after(early_all, ins[0]), "col", CORE_SWAP)
    table = jnp.concatenate([info, jnp.zeros((40 - 34,), jnp.int32), *choices])
    o_fc1r, o_f2e, o_f1e, o_f2r = call(
        expand_early_body,
        [out((COUNT, RANK, w), F32) for w in (1024, 1024, 4096, 4096)],
        [table, Far(early_all), Far(early_far)],
        us=0.01,
        name="expand_early",
    )
    (joined,) = call(
        stack_body,
        [out((8 * TOK, TOK), BF)],
        [*[after(v, o_fc1r, late_all[2]) for v in to_cols(ins)], *hidden_got],
        smem=0,
        us=0.01,
        name="stack",
    )
    input_gradient, hidden_out = call(
        unroute_body,
        [out((1024, TOK), F32), out((1024, TOK), BF)],
        [info, joined, lax.ppermute(joined, "col", CORE_SWAP)],
        [order],
        us=2,
        name="unroute",
    )
    o_qr, o_pe, o_qe, o_pr = call(
        expand_late_body,
        [out((COUNT, RANK, w), F32) for w in (1024, 1024, 3072, 1024)],
        [table, *late_all],
        us=0.01,
        name="expand_late",
    )
    return (
        hidden_out,
        input_gradient,
        flip(o_qr),
        o_qe,
        flip(o_pr),
        o_pe,
        flip(o_fc1r),
        o_f1e,
        flip(o_f2r),
        o_f2e,
    )


def solution(mesh):
    placed = (
        P(("dp", "col"), "row"),
        P(("dp", "col"), "row"),
        P("row"),
        P("row"),
        P("row", "col"),
        P(),
        P("col", "row"),
        P("row"),
        P("row"),
        P("row"),
        P("row", "col"),
        P(),
        P("col", "row"),
        P("row"),
        P(None, "row", None),
        P(),
        P(None, "col", None),
        P(None, None, "row"),
        P(None, "row", None),
        P(),
        P(None, "col", None),
        P(None, None, "row"),
        P("dp"),
        P("dp"),
    )
    return jax.shard_map(
        body,
        mesh=mesh,
        in_specs=placed,
        out_specs=(P(("dp", "col"), "row"), P(("dp", "col"), "row")) + (P(),) * 8,
        check_vma=False,
    )
```

```python
import functools

import jax
import jax.numpy as jnp
from jax import lax
from jax.experimental import pallas as pl
from jax.experimental.pallas import tpu as pltpu
from jax.sharding import PartitionSpec as P

D = 1024
HEADS = 16
HEAD = 64
FF = 4096
RANK = 16
COUNT = 8
PROMPT = 1024
CONT = 128
NCONT = 8
GROUPS_DEV = 2

EPSILON = 1e-05
SCALE = 2.0
GELU_A = 0.7978845608028654
GELU_B = 0.044715
ROWS = 4
COLS = 4
TOK = 256
BLOCK = 128
LOW = -1e30
W_SMALL = 5e8
W_BIG = 5e8

BF = jnp.bfloat16
F32 = jnp.float32

VM = pl.BlockSpec(memory_space=pltpu.VMEM)
SM = pl.BlockSpec(memory_space=pltpu.SMEM)
HB = pl.BlockSpec(memory_space=pltpu.HBM)

CORE_SWAP = [(0, 1), (1, 0), (2, 3), (3, 2)]
Y_SWAP = [(0, 2), (2, 0), (1, 3), (3, 1)]
Z_SWAP = [(0, 1), (1, 0), (2, 3), (3, 2)]


def nn(a, b):
    return lax.dot_general(a, b, (((1,), (0,)), ((), ())), preferred_element_type=F32)


def nt(a, b):
    return lax.dot_general(a, b, (((1,), (1,)), ((), ())), preferred_element_type=F32)


def tn(a, b):
    return lax.dot_general(a, b, (((0,), (0,)), ((), ())), preferred_element_type=F32)


def f32(v):
    return v.astype(F32)


def bf(v):
    return v.astype(BF)


class Far:
    def __init__(self, value):
        self.value = value


def far(values):
    return [Far(v) for v in values]


def call(
    body, outs, ins, scratch=(), smem=1, limit=40, us=1, raw=(), weight=W_SMALL, hbm=(), pre=None, name=None
):
    values = [
        pltpu.with_memory_space_constraint(v.value, pltpu.HBM) if isinstance(v, Far) else v
        for v in ins
    ]
    fetched = [i for i, v in enumerate(ins) if isinstance(v, Far) and i not in raw]
    specs = [SM] * smem
    for v in ins[smem:]:
        specs.append(HB if isinstance(v, Far) else VM)
    nbytes = sum(v.size * v.dtype.itemsize for v in values)
    nbytes += sum(o.size * o.dtype.itemsize for o in outs)
    extra = [pltpu.VMEM(values[i].shape, values[i].dtype) for i in fetched]
    extra += [pltpu.VMEM(outs[i].shape, outs[i].dtype) for i in hbm]
    moved = len(extra)
    if moved:
        extra.append(pltpu.SemaphoreType.DMA((moved,)))

    def whole(*refs):
        refs = list(refs)
        stores = []
        if moved:
            sem = refs[-1]
            buffers = refs[-1 - moved : -1]
            refs = refs[: -1 - moved]
            copies = []
            for n, i in enumerate(fetched):
                copies.append(pltpu.make_async_copy(refs[i], buffers[n], sem.at[n]))
                copies[-1].start()
                refs[i] = buffers[n]
            for n, i in enumerate(hbm, len(fetched)):
                at = len(values) + i
                stores.append(pltpu.make_async_copy(buffers[n], refs[at], sem.at[n]))
                refs[at] = buffers[n]
            if pre is not None:
                pre(*refs)
            for copy in copies:
                copy.wait()
        body(*refs)
        for copy in stores:
            copy.start()
        for copy in stores:
            copy.wait()

    return pl.pallas_call(
        whole,
        out_shape=tuple(
            pltpu.HBM(o.shape, o.dtype) if i in hbm else o for i, o in enumerate(outs)
        ),
        in_specs=specs,
        out_specs=tuple(HB if i in hbm else VM for i in range(len(outs))),
        scratch_shapes=list(scratch) + extra,
        compiler_params=pltpu.CompilerParams(vmem_limit_bytes=limit << 20),
        cost_estimate=pl.CostEstimate(
            flops=int(us * weight), bytes_accessed=nbytes // 8, transcendentals=0
        ),
        name=name,
    )(*values)


def after(value, *others):
    res = lax.optimization_barrier((value, others))
    return res[0]


def out(shape, dtype):
    return jax.ShapeDtypeStruct(shape, dtype)


def block_at(zl, c, j):
    return c * 4 + zl + j * (3 - 2 * zl)


def fill_order(info, order):
    base = info[3]
    first = jnp.int32(0)
    second = jnp.int32(NCONT)
    for j in range(GROUPS_DEV * NCONT):
        own = info[16 + j] == base
        slot = jnp.where(own, first, second)
        order[slot] = jnp.int32(j)
        first = first + jnp.where(own, 1, 0)
        second = second + jnp.where(own, 0, 1)


def place_of(info, order, z, core, j):
    prompt = (z // 2) * 8 + block_at(lax.rem(z, 2), core, j)
    cont = order[4 * z + 2 * core + j]
    return jnp.where(info[1] == 0, prompt, cont)


def route_body(info, own, oth, o0, o1, o2, o3, order):
    c = info[2]
    for s, dst in enumerate((o0, o1, o2, o3)):
        z = lax.rem(info[0] + s, ROWS)
        for j in range(2):
            src = place_of(info, order, z, c, j)
            at = pl.ds(pl.multiple_of(lax.rem(src, 8) * BLOCK, BLOCK), BLOCK)
            mine = src // 8 == c

            @pl.when(mine)
            def _():
                dst[pl.ds(j * BLOCK, BLOCK), :] = own[at, :]

            @pl.when(jnp.logical_not(mine))
            def _():
                dst[pl.ds(j * BLOCK, BLOCK), :] = oth[at, :]


def route_copies(
    info, own, oth, g1, c1, pb, g2, c2, fb, qr, fr, pe, fe,
    o0, o1, o2, o3, order, v0, v1, v2, v3, v4, v5, mats, sem,
):
    pairs = list(zip((g1, c1, pb, g2, c2, fb), (v0, v1, v2, v3, v4, v5)))
    for k in range(ROWS):
        which = lax.rem(info[0] + k, ROWS) // 2
        a = jnp.where(which == 0, info[32], info[33])
        pairs += [(v.at[a], mats.at[4 * k + i]) for i, v in enumerate((qr, fr, pe, fe))]
    return [pltpu.make_async_copy(a, b, sem.at[i]) for i, (a, b) in enumerate(pairs)]


def route_pack_pre(*refs):
    for copy in route_copies(*refs):
        copy.start()
    fill_order(refs[0], refs[17])


def route_pack_body(*refs):
    info, own, oth = refs[:3]
    o0, o1, o2, o3, order, v0, v1, v2, v3, v4, v5, mats, _ = refs[13:]
    route_body(info, own, oth, o0, o1, o2, o3, order)
    for copy in route_copies(*refs):
        copy.wait()
    for k, dst in enumerate((o0, o1, o2, o3)):
        head = [f32(v[...]).reshape(1, TOK) for v in (v0, v1, v2, v3, v4, v5)]
        dst[256:272, :] = bf(jnp.concatenate(head + [jnp.zeros((10, TOK), F32)], axis=0))
        for i in range(4):
            dst[272 + 16 * i : 288 + 16 * i, :] = mats[4 * k + i]


def stack_body(a0, a1, a2, a3, h0, h1, h2, h3, dst):
    for k, (a, h) in enumerate(((a0, h0), (a1, h1), (a2, h2), (a3, h3))):
        dst[2 * k * TOK : (2 * k + 1) * TOK, :] = a[...]
        dst[(2 * k + 1) * TOK : (2 * k + 2) * TOK, :] = h[...]


def route_all_body(info, own, oth, w2, dst, order, sem):
    copies = []
    for z in range(ROWS):
        to = dst.at[z, pl.ds(TOK, 512)]
        copies.append(pltpu.make_async_copy(w2.at[rows_at(info[8], 512)], to, sem.at[z]))
    for copy in copies:
        copy.start()
    fill_order(info, order)
    c = info[2]
    for z in range(ROWS):
        for j in range(2):
            src = place_of(info, order, z, c, j)
            at = pl.ds(pl.multiple_of(lax.rem(src, 8) * BLOCK, BLOCK), BLOCK)
            mine = src // 8 == c

            @pl.when(mine)
            def _():
                dst[z, pl.ds(j * BLOCK, BLOCK), :] = own[at, :]

            @pl.when(jnp.logical_not(mine))
            def _():
                dst[z, pl.ds(j * BLOCK, BLOCK), :] = oth[at, :]
    for copy in copies:
        copy.wait()


def unroute_body(info, a, b, grad, hidden, order):
    fill_order(info, order)
    c = info[2]
    for s in range(ROWS):
        z = lax.rem(info[0] + s, ROWS)
        for other, src in ((0, a), (1, b)):
            core = c if other == 0 else 1 - c
            for j in range(2):
                at = place_of(info, order, z, core, j)

                @pl.when(at // 8 == c)
                def _():
                    rows = pl.ds(pl.multiple_of(lax.rem(at, 8) * BLOCK, BLOCK), BLOCK)
                    start = 2 * s * TOK + j * BLOCK
                    grad[rows, :] = f32(src[pl.ds(start, BLOCK), :])
                    hidden[rows, :] = src[pl.ds(start + TOK, BLOCK), :]


def cols(k, width=TOK):
    return pl.ds(k * width, width)


def row_stats(parts):
    total = sum(jnp.sum(v, axis=1, keepdims=True) for v in parts)
    mean = total * (1.0 / D)
    dev = [v - mean for v in parts]
    var = sum(jnp.sum(v * v, axis=1, keepdims=True) for v in dev) * (1.0 / D)
    rstd = lax.rsqrt(var + EPSILON)
    return [v * rstd for v in dev], rstd


def norm1_body(x0, x1, x2, x3, xn):
    for t in range(2):
        rows = pl.ds(t * 128, 128)
        hat, _ = row_stats([f32(v[rows, :]) for v in (x0, x1, x2, x3)])
        for k, pack in enumerate((x0, x1, x2, x3)):
            xn[rows, cols(k)] = bf(hat[k] * f32(pack[256:257, :]) + f32(pack[257:258, :]))


def both(a, b, rows, k):
    return f32(a[rows, cols(k)]) + f32(b[rows, cols(k)])


def norm2_body(a, b, x0, x1, x2, x3, mid, xn):
    for t in range(2):
        rows = pl.ds(t * 128, 128)
        parts = []
        for k, x in enumerate((x0, x1, x2, x3)):
            v = f32(x[rows, :]) + both(a, b, rows, k) + f32(x[258:259, :])
            mid[rows, cols(k)] = v
            parts.append(v)
        hat, _ = row_stats(parts)
        for k, pack in enumerate((x0, x1, x2, x3)):
            xn[rows, cols(k)] = bf(hat[k] * f32(pack[259:260, :]) + f32(pack[260:261, :]))


def norm_back(hat, rstd, grads):
    total = sum(jnp.sum(g, axis=1, keepdims=True) for g in grads) * (1.0 / D)
    along = sum(jnp.sum(g * h, axis=1, keepdims=True) for g, h in zip(grads, hat)) * (1.0 / D)
    return [rstd * (g - total - h * along) for g, h in zip(grads, hat)]


def norm2_back_body(
    a, b, pack, mid, g, x0, x1, x2, x3, d_mid, g_attn
):
    g_attn[256:320, :] = pack[...]
    for t in range(2):
        rows = pl.ds(t * 128, 128)
        hat, rstd = row_stats([mid[rows, cols(k)] for k in range(4)])
        grads = []
        for k, pack in enumerate((x0, x1, x2, x3)):
            grads.append(both(a, b, rows, k) * f32(pack[259:260, :]))
        back = norm_back(hat, rstd, grads)
        for k in range(4):
            v = f32(g[rows, cols(k)]) + back[k]
            d_mid[rows, cols(k)] = v
            g_attn[rows, cols(k)] = bf(v)


def norm1_back_body(a, b, d_mid, x0, x1, x2, x3, i0, i1, i2, i3):
    for t in range(2):
        rows = pl.ds(t * 128, 128)
        hat, rstd = row_stats([f32(v[rows, :]) for v in (x0, x1, x2, x3)])
        grads = []
        for k, pack in enumerate((x0, x1, x2, x3)):
            grads.append(both(a, b, rows, k) * f32(pack[256:257, :]))
        back = norm_back(hat, rstd, grads)
        for k, dst in enumerate((i0, i1, i2, i3)):
            dst[rows, :] = bf(d_mid[rows, cols(k)] + back[k])


def hidden_body(a, b, mid, x0, x1, x2, x3, h0, h1, h2, h3):
    for t in range(2):
        rows = pl.ds(t * 128, 128)
        for k, (pack, dst) in enumerate(zip((x0, x1, x2, x3), (h0, h1, h2, h3))):
            v = mid[rows, cols(k)] + both(a, b, rows, k) + f32(pack[261:262, :])
            dst[rows, :] = bf(v)


def join_body(info, v, dst, w2):
    for k in range(ROWS):
        dst[:, cols(k)] = v[rel(info, k), 0:TOK, :]
    for k in range(1, ROWS):
        w2[k - 1] = v[rel(info, k), TOK:, :]


def rest_body(info, v, dst):
    for k in range(1, ROWS):
        dst[k - 1] = v[rel(info, k)]


def slab_rows(info, b):
    y = jnp.bitwise_xor(info[1], b // 2)
    c = jnp.bitwise_xor(info[2], b % 2)
    return y, c


def low_lanes(rows):
    return lax.broadcasted_iota(jnp.int32, (rows, 128), 1) < HEAD


def rel(info, k):
    return lax.rem(info[0] - k + ROWS, ROWS)


def rel_cols(info, k):
    return pl.ds(pl.multiple_of(rel(info, k) * TOK, TOK), TOK)


def lanes_at(at, size):
    return pl.ds(pl.multiple_of(at, 128), size)


def rows_at(i, size):
    return pl.ds(pl.multiple_of(i * size, size), size)


def prepare_body(
    info, wq, wp, w1, qe, fe, pr, fr, first, c1, o_qe, o_fe, o_pr, o_fr, sem
):
    half = info[8]
    a = jnp.where(info[5] == 0, info[32], info[33])
    rows = rows_at(half, 128)
    pairs = [(wq.at[rows], first.at[:, 0:768]), (wp.at[rows], first.at[:, 768:1024])]
    pairs += [(qe.at[a, :, lanes_at(info[6] * 768, 768)], o_qe)]
    pairs += [(fe.at[a, :, lanes_at(info[6] * 1024, 1024)], o_fe)]
    pairs += [(pr.at[a], o_pr), (fr.at[a], o_fr)]
    for j in range(ROWS):
        pairs += [(w1.at[rows], c1.at[j])]
    copies = [pltpu.make_async_copy(x, y, sem.at[i]) for i, (x, y) in enumerate(pairs)]
    for copy in copies:
        copy.start()
    for copy in copies:
        copy.wait()


def assemble_body(info, own_q, own_p, z1, z2, z3, s1, s2, s3, ws, wp, sem):
    half = info[8]
    copies = [
        pltpu.make_async_copy(own_q, ws.at[0], sem.at[0]),
        pltpu.make_async_copy(own_p, wp.at[0], sem.at[1]),
    ]
    for k, (zv, sv) in enumerate(((z1, s1), (z2, s2), (z3, s3))):
        for n, (v, at) in enumerate(((zv, half), (sv, 1 - half))):
            rows = rows_at(at, 128)
            at = 2 + 4 * k + 2 * n
            copies.append(
                pltpu.make_async_copy(v.at[:, 0:768], ws.at[k + 1, rows], sem.at[at])
            )
            copies.append(
                pltpu.make_async_copy(v.at[:, 768:1024], wp.at[k + 1, rows], sem.at[at + 1])
            )
    for copy in copies:
        copy.start()
    for copy in copies:
        copy.wait()


def qkv_body(
    info, x0, x1, x2, x3, ws, p0, p1, p2, p3, bias, expand, q, kvp, kvc
):
    ps = (p0, p1, p2, p3)
    low = low_lanes(TOK)
    for b, x in enumerate((x0, x1, x2, x3)):
        y, c = slab_rows(info, b)
        acc = sum(nn(x[:, cols(k)], ws[k]) for k in range(4))
        u = bf(sum(nt(x[:, cols(k)], ps[k][272:288, :]) for k in range(4)))
        acc = acc + f32(bias[...]) + SCALE * nn(u, expand[...])
        kv = []
        for pair in range(2):
            at = 384 * pair
            g0, g1, g2 = (acc[:, at + 128 * i : at + 128 * i + 128] for i in range(3))
            q[rows_at(y * 2 + c, TOK), cols(pair, 128)] = bf(
                bf(jnp.where(low, g0, g1)) * BF(0.125)
            )
            kv.append((bf(pltpu.roll(jnp.where(low, g2, g0), 64, 1)), bf(jnp.where(low, g1, g2))))
        rows = rows_at(c, TOK)

        @pl.when(y == 0)
        def _():
            for pair in range(2):
                kvp[rows, cols(pair, 128)] = kv[pair][0]
                kvp[rows, cols(2 + pair, 128)] = kv[pair][1]

        @pl.when(y == 1)
        def _():
            for pair in range(2):
                kvc[rows, cols(pair, 128)] = kv[pair][0]
                kvc[rows, cols(2 + pair, 128)] = kv[pair][1]


WIDE = 256


def stacked(v, low):
    zero = jnp.zeros_like(v)
    return jnp.concatenate([jnp.where(low, v, zero), jnp.where(low, zero, v)], axis=0)


def split_id(shape, axis):
    lane = lax.broadcasted_iota(jnp.int32, shape, axis)
    return lane, jnp.where(lane < BLOCK, lane, lane - BLOCK)


def chunk_place(shape, axis, side, n):
    lane, within = split_id(shape, axis)
    first = block_at(side, n, 0) * BLOCK
    second = block_at(side, n, 1) * BLOCK
    return within + jnp.where(lane < BLOCK, first, second)


def keep_state(state, low):
    top, total, acc = state
    lane = lax.broadcasted_iota(jnp.int32, (2 * BLOCK, 128), 1)
    spot = lax.rem(lane, HEAD)
    row = lax.broadcasted_iota(jnp.int32, (2 * BLOCK, 128), 0)
    own = (lane < HEAD) == (row < BLOCK)
    return jnp.where(own, acc, jnp.where(spot == 0, top, total))


def load_state(v):
    lane = lax.broadcasted_iota(jnp.int32, (2 * BLOCK, 128), 1)
    row = lax.broadcasted_iota(jnp.int32, (2 * BLOCK, 128), 0)
    spot = jnp.where(row < BLOCK, HEAD, 0)
    top = jnp.max(jnp.where(lane == spot, v, LOW), axis=1, keepdims=True)
    total = jnp.sum(jnp.where(lane == spot + 1, v, 0.0), axis=1, keepdims=True)
    return top, total, v


def soft_update(state, s, v):
    if state is None:
        top = jnp.max(s, axis=1, keepdims=True)
        p = jnp.exp(s - top)
        return top, jnp.sum(p, axis=1, keepdims=True), nn(bf(p), v)
    top, total, acc = state
    new = jnp.maximum(top, jnp.max(s, axis=1, keepdims=True))
    p = jnp.exp(s - new)
    shrink = jnp.exp(top - new)
    total = total * shrink + jnp.sum(p, axis=1, keepdims=True)
    return new, total, acc * shrink + nn(bf(p), v)


def head_slopes(slopes, shape, axis):
    lane = lax.broadcasted_iota(jnp.int32, shape, axis)
    return [
        jnp.where(lane < BLOCK, slopes[2 * pair], slopes[2 * pair + 1]) for pair in range(2)
    ]


def attend_chunk(q2, states, kv, rows, place, base, slope, spot, masked):
    res = []
    away = place - base
    for pair in range(2):
        s = nt(q2[pair], kv[rows, cols(pair, 128)]) + slope[pair] * away.astype(F32)
        if masked:
            s = jnp.where(away <= spot, s, LOW)
        res.append(soft_update(states[pair], s, kv[rows, cols(2 + pair, 128)]))
    return res


def attend_first_body(info, slopes, q, kvp, kvc, state):
    zl = info[4]
    low = low_lanes(BLOCK)
    _, spot = split_id((2 * BLOCK, 1), 0)
    slope = head_slopes(slopes, (2 * BLOCK, 1), 0)
    places = [chunk_place((1, WIDE), 1, zl, n) for n in range(2)]

    def load(i):
        return [stacked(q[rows_at(i, BLOCK), cols(pair, 128)], low) for pair in range(2)]

    def save(states, i):
        for pair in range(2):
            state[rows_at(i, WIDE), cols(pair, 128)] = keep_state(states[pair], low)

    def prompt_block(j, _):
        for n in range(2):
            i = 2 * n + j
            base = block_at(zl, n, j) * BLOCK
            q2 = load(i)
            states = [None, None]
            for m in range(n, -1, -1):
                states = attend_chunk(
                    q2, states, kvp, pl.ds(m * WIDE, WIDE), places[m], base, slope, spot, m == n
                )
            save(states, i)
        return 0

    lax.fori_loop(0, 2, prompt_block, 0)

    def cont_block(j, _):
        q2 = load(4 + j)
        own_place = lax.broadcasted_iota(jnp.int32, (1, BLOCK), 1)
        states = attend_chunk(
            q2, [None, None], kvc, rows_at(j, BLOCK), own_place, 0, slope, spot, True
        )
        for m in range(2):
            states = attend_chunk(
                q2, states, kvp, pl.ds(m * WIDE, WIDE), places[m], PROMPT, slope, spot, False
            )
        save(states, 4 + j)
        return 0

    lax.fori_loop(0, 4, cont_block, 0)


def attend_rest_body(
    which, info, slopes, q, kvo, state, ws, reduce, p0, p1, p2, p3, heads, lse, o0, o1
):
    zl = info[4]
    y = info[1] if which == 0 else 1 - info[1]
    low = low_lanes(BLOCK)
    _, spot = split_id((2 * BLOCK, 1), 0)
    slope = head_slopes(slopes, (2 * BLOCK, 1), 0)
    places = [chunk_place((1, WIDE), 1, 1 - zl, n) for n in range(2)]

    def load(i):
        q2 = [stacked(q[rows_at(i, BLOCK), cols(pair, 128)], low) for pair in range(2)]
        states = [load_state(state[rows_at(i, WIDE), cols(pair, 128)]) for pair in range(2)]
        return q2, states

    def finish(states, j):
        for pair in range(2):
            top, total, acc = states[pair]
            res = acc / total
            heads[rows_at(j, BLOCK), cols(pair, 128)] = bf(
                jnp.where(low, res[:BLOCK], res[BLOCK:])
            )
            kept = jnp.transpose(jnp.broadcast_to(top + jnp.log(total), (2 * BLOCK, 128)))
            lse[pl.ds(pair * 4 + j, 1), :] = kept[0:1, :]

    @pl.when(y == 0)
    def _():
        def prompt_block(j, _):
            for n in range(2):
                i = 2 * n + j
                base = block_at(zl, n, j) * BLOCK
                q2, states = load(i)
                for m in range(n + 1):
                    states = attend_chunk(
                        q2, states, kvo, pl.ds(m * WIDE, WIDE), places[m], base, slope, spot, m == n
                    )
                finish(states, i)
            return 0

        lax.fori_loop(0, 2, prompt_block, 0)

    @pl.when(y == 1)
    def _():
        def cont_block(j, _):
            q2, states = load(4 + j)
            for m in range(2):
                states = attend_chunk(
                    q2, states, kvo, pl.ds(m * WIDE, WIDE), places[m], PROMPT, slope, spot, False
                )
            finish(states, j)
            return 0

        lax.fori_loop(0, 4, cont_block, 0)

    ps = (p0, p1, p2, p3)
    for b, dst in enumerate((o0, o1)):
        c = jnp.bitwise_xor(info[2], b)
        h = heads[rows_at(c, TOK), :]
        u = bf(nt(h, reduce[...]))
        for k in range(4):
            dst[:, cols(k)] = bf(nn(h, ws[k]) + SCALE * nn(u, ps[k][304:320, :]))


def mlp_pre_body(info, x0, x1, w1, p0, p1, p2, p3, bias, expand, act, slope):
    ps = (p0, p1, p2, p3)
    for b, x in enumerate((x0, x1)):
        u = bf(sum(nt(x[:, cols(k)], ps[k][288:304, :]) for k in range(4)))
        pre = sum(nn(x[:, cols(k)], w1[rel(info, k)]) for k in range(4))
        pre = pre + f32(bias[...]) + SCALE * nn(u, expand[...])
        sq = pre * pre
        t = jnp.tanh(pre * (GELU_A + (GELU_A * GELU_B) * sq))
        half = 0.5 + 0.5 * t
        act[b] = bf(pre * half)
        slope[b] = bf(
            half + (0.5 * pre) * (1.0 - t * t) * (GELU_A + (3.0 * GELU_A * GELU_B) * sq)
        )


def mlp_back_body(
    info, x0, x1, g0, g1, slope, w1, w2, p0, p1, p2, p3, expand, reduce, r_in, e_in,
    d0, d1, r_out, e_out,
):
    ps = (p0, p1, p2, p3)
    rv, ev = r_in[...], e_in[...]
    for b, (x, g, dx) in enumerate(((x0, g0, d0), (x1, g1, d1))):
        u = bf(sum(nt(x[:, cols(k)], ps[k][288:304, :]) for k in range(4)))
        du2 = bf(SCALE * sum(nt(g[:, cols(k)], ps[k][320:336, :]) for k in range(4)))
        d_act = sum(nt(g[:, cols(k)], w2[rel(info, k)]) for k in range(4)) + nn(du2, reduce[...])
        d_pre = bf(d_act * f32(slope[b]))
        du = bf(SCALE * nt(d_pre, expand[...]))
        for k in range(4):
            dx[:, cols(k)] = bf(nt(d_pre, w1[rel(info, k)]) + nn(du, ps[k][288:304, :]))
        rv = rv + tn(du, x[...])
        ev = ev + tn(u, d_pre)
    r_out[...] = rv
    e_out[...] = ev


def fc2_body(
    info, a0, a1, g0, g1, g2, g3, w2, reduce, p0, p1, p2, p3, r1, e1,
    m0, m1, m2, m3, grads,
):
    ps = (p0, p1, p2, p3)
    rv = ev = 0.0
    for b, (g, m) in enumerate(zip((g0, g1, g2, g3), (m0, m1, m2, m3))):
        act = a0[b] if b < 2 else a1[b - 2]
        du = bf(SCALE * sum(nt(g[:, cols(k)], ps[k][320:336, :]) for k in range(4)))
        u = bf(nt(act, reduce[...]))
        for k in range(4):
            m[:, cols(k)] = bf(nn(act, w2[rel(info, k)]) + SCALE * nn(u, ps[k][320:336, :]))
        rv = rv + tn(du, act)
        ev = ev + SCALE * tn(u, g[...])
    for k in range(4):
        grads[0:16, rel_cols(info, k)] = bf(r1[:, cols(k)])
        grads[16:32, rel_cols(info, k)] = bf(ev[:, k * TOK : k * TOK + TOK])
    grads[32:48, :] = bf(SCALE * e1[...])
    grads[48:64, :] = bf(rv)


def d_heads_body(
    info, g0, g1, ws, p0, p1, p2, p3, reduce, heads, r_in, e_in, dh, r_out, e_out
):
    ps = (p0, p1, p2, p3)
    rv, ev = r_in[...], e_in[...]
    for b, g in enumerate((g0, g1)):
        rows = rows_at(jnp.bitwise_xor(info[2], b), TOK)
        h = heads[rows, :]
        u = bf(nt(h, reduce[...]))
        du = bf(SCALE * sum(nt(g[0:256, cols(k)], ps[k][304:320, :]) for k in range(4)))
        v = sum(nt(g[0:256, cols(k)], ws[k]) for k in range(4)) + nn(du, reduce[...])
        dh[rows, :] = bf(v)
        rv = rv + tn(du, h)
        ev = ev + SCALE * tn(u, g[0:256, :])
    r_out[...] = rv
    e_out[...] = ev


def back_load(heads, d_heads, lse, q, qi, j, low):
    res = []
    for pair in range(2):
        lane = cols(pair, 128)
        q2 = stacked(q[rows_at(qi, BLOCK), lane], low)
        do = d_heads[rows_at(j, BLOCK), lane]
        both = jnp.transpose(f32(do) * f32(heads[rows_at(j, BLOCK), lane]))
        delta = jnp.concatenate(
            [
                jnp.sum(both[:HEAD], axis=0, keepdims=True),
                jnp.sum(both[HEAD:], axis=0, keepdims=True),
            ],
            axis=1,
        )
        res.append((q2, stacked(do, low), delta, lse[pl.ds(pair * 4 + j, 1), :]))
    return res


def back_chunk(args, kv, d_kv, d_at, rows, place, base, slope, spot, masked, store, d_qs):
    away = place - base
    res = []
    for pair in range(2):
        q2, do2, delta, kept = args[pair]
        lane = cols(pair, 128)
        vlane = cols(2 + pair, 128)
        k = kv[rows, lane]
        s = nt(k, q2) + (away.astype(F32) * slope[pair] - kept)
        p = jnp.exp(s)
        if masked:
            p = jnp.where(away <= spot, p, 0.0)
        ds = bf(p * (nt(kv[rows, vlane], do2) - delta))
        dk = nn(ds, q2)
        dv = nn(bf(p), do2)
        if store:
            d_kv[d_at, lane] = bf(dk)
            d_kv[d_at, vlane] = bf(dv)
        else:
            d_kv[d_at, lane] += dk
            d_kv[d_at, vlane] += dv
        d_q = tn(ds, k)
        res.append(d_q if d_qs is None else d_qs[pair] + d_q)
    return res


def back_common(info, slopes):
    low = low_lanes(BLOCK)
    _, spot = split_id((1, 2 * BLOCK), 1)
    slope = head_slopes(slopes, (1, 2 * BLOCK), 1)
    zl = info[4]
    own = [chunk_place((WIDE, 1), 0, zl, n) for n in range(2)]
    oth = [chunk_place((WIDE, 1), 0, 1 - zl, n) for n in range(2)]
    return zl, low, spot, slope, own, oth


def fold(d_q, low):
    return jnp.where(low, d_q[:BLOCK], d_q[BLOCK:]) * 0.125


def back_sweep(info, slopes, y, q, heads, d_heads, lse, sides, kvc, dkc, finish):
    zl, low, spot, slope, own, oth = back_common(info, slopes)
    place_sets = {"own": own, "oth": oth}

    @pl.when(y == 0)
    def _():
        def prompt_block(j, _):
            for n in range(2):
                i = 2 * n + j
                args = back_load(heads, d_heads, lse, q, i, i, low)
                base = block_at(zl, n, j) * BLOCK
                d_qs = None
                for side, kv, d_kv in sides:
                    for m in range(n + 1):
                        rows = pl.ds(m * WIDE, WIDE)
                        d_qs = back_chunk(
                            args, kv, d_kv, rows, rows, place_sets[side][m], base, slope, spot,
                            m == n, False, d_qs,
                        )
                finish(d_qs, i, low)
            return 0

        lax.fori_loop(0, 2, prompt_block, 0)

    @pl.when(y == 1)
    def _():
        def cont_block(j, _):
            args = back_load(heads, d_heads, lse, q, 4 + j, j, low)
            d_qs = None
            if kvc is not None:
                mine = rows_at(j, BLOCK)
                own_place = lax.broadcasted_iota(jnp.int32, (BLOCK, 1), 0)
                d_qs = back_chunk(
                    args, kvc, dkc, mine, mine, own_place, 0, slope, spot, True, True, d_qs
                )
            for side, kv, d_kv in sides:
                for m in range(2):
                    rows = pl.ds(m * WIDE, WIDE)
                    d_qs = back_chunk(
                        args, kv, d_kv, rows, rows, place_sets[side][m], PROMPT, slope, spot,
                        False, False, d_qs,
                    )
            finish(d_qs, j, low)
            return 0

        lax.fori_loop(0, 4, cont_block, 0)


def clear_back(*refs):
    for ref in refs[10:13]:
        ref[...] = jnp.zeros_like(ref)


def attend_back_a_body(
    info, slopes, q, kvp, kvo, kvc, heads, d_heads, lse, dq, dkp, dko, dkc
):

    def finish(d_qs, j, low):
        for pair in range(2):
            dq[rows_at(j, BLOCK), cols(pair, 128)] = bf(fold(d_qs[pair], low))

    back_sweep(
        info, slopes, info[1], q, heads, d_heads, lse,
        (("own", kvp, dkp), ("oth", kvo, dko)), kvc, dkc, finish,
    )


def attend_back_b_body(
    info, slopes, q, kvo, heads, d_heads, lse, dko_in, early, dq, dko, acc
):
    acc[...] = dko_in[...]

    def finish(d_qs, j, low):
        for pair in range(2):
            dq[rows_at(j, BLOCK), cols(pair, 128)] = fold(d_qs[pair], low)

    back_sweep(
        info, slopes, 1 - info[1], q, heads, d_heads, lse,
        (("oth", kvo, acc),), None, None, finish,
    )
    dko[0:512, :] = bf(acc[...])
    dko[512:592, :] = early[:, 0:512]
    dko[592:672, :] = early[:, 512:1024]


def early_sum_body(own, other, dst):
    dst[:, 0:512] = bf(f32(own[:, 0:512]) + f32(other[512:592, :]))
    dst[:, 512:1024] = bf(f32(own[:, 512:1024]) + f32(other[592:672, :]))


def attend_back_c_body(
    info, slopes, q, kvp, kvc, heads, d_heads, lse, dkp_in, dkc_in, dq_in, dq, dkp, dkc
):
    dkp[...] = dkp_in[...]
    dkc[...] = dkc_in[...]

    def finish(d_qs, j, low):
        for pair in range(2):
            lane = cols(pair, 128)
            rows = rows_at(j, BLOCK)
            dq[rows, lane] = bf(dq_in[rows, lane] + fold(d_qs[pair], low))

    back_sweep(
        info, slopes, 1 - info[1], q, heads, d_heads, lse,
        (("own", kvp, dkp),), kvc, dkc, finish,
    )


def qkv_back_body(
    info, dq0, dq1, dkp, dkr, dkc, x0, x1, x2, x3, ws, p0, p1, p2, p3, expand, pr, pe,
    o0, o1, o2, o3, grads,
):
    ps = (p0, p1, p2, p3)
    low = low_lanes(TOK)
    sr = se = 0.0
    for b, (x, dst) in enumerate(zip((x0, x1, x2, x3), (o0, o1, o2, o3))):
        y, c = slab_rows(info, b)
        half = rows_at(c, TOK)
        groups = []
        dq = dq0 if b < 2 else dq1
        for pair in range(2):
            vq = f32(dq[half, cols(pair, 128)])
            got = []
            for lane in (cols(pair, 128), cols(2 + pair, 128)):
                prompt = dkp[half, lane] + f32(dkr[half, lane])
                got.append(jnp.where(y == 0, prompt, f32(dkc[half, lane])))
            vk = pltpu.roll(got[0], 64, 1)
            vv = got[1]
            groups += [jnp.where(low, vq, vk), jnp.where(low, vv, vq), jnp.where(low, vk, vv)]
        d = bf(jnp.concatenate(groups, axis=1))
        u = bf(sum(nt(x[:, cols(k)], ps[k][272:288, :]) for k in range(4)))
        du = bf(SCALE * nt(d, expand[...]))
        for k in range(4):
            dst[:, cols(k)] = bf(nt(d, ws[k]) + nn(du, ps[k][272:288, :]))
        sr = sr + tn(du, x[...])
        se = se + SCALE * tn(u, d)
    for k in range(4):
        grads[0:16, rel_cols(info, k)] = bf(sr[:, k * TOK : k * TOK + TOK])
        grads[16:32, rel_cols(info, k)] = bf(pe[:, cols(k)])
    grads[32:48, 0:768] = bf(se)
    grads[32:48, 768:1024] = bf(pr[...])


def add_body(a, b, dst):
    dst[...] = bf(f32(a[...]) + f32(b[...]))


def add(a, b):
    return call(add_body, [out(a.shape, BF)], [a, b], smem=0, us=0.01, name="add")[0]


def add32_body(a, b, dst):
    dst[...] = f32(a[...]) + f32(b[...])


def add32(a, b, us=8):
    return call(add32_body, [out(a.shape, F32)], [a, b], smem=0, us=us, name="add32")[0]


def stage_body(*refs):
    n = len(refs) // 2
    for src, dst in zip(refs[:n], refs[n:]):
        dst[...] = src[...]


def stage(values):
    return call(
        stage_body, [out(v.shape, v.dtype) for v in values], far(values), smem=0, us=0.01, name="stage"
    )


def stage_weight_body(size, info, own, wr, ws, w, sem):
    copies = [pltpu.make_async_copy(own, w.at[info[0]], sem.at[6])]
    for n, (src, at) in enumerate(((wr, info[8]), (ws, 1 - info[8]))):
        for k in range(1, ROWS):
            to = w.at[rel(info, k), rows_at(at, size)]
            copies.append(pltpu.make_async_copy(src.at[k - 1], to, sem.at[3 * n + k - 1]))
    for copy in copies:
        copy.start()
    for copy in copies:
        copy.wait()


def merge_body(info, v0, v1, v2, v3, dst):
    four = (v0, v1, v2, v3)

    def fill(c):
        total = sum(f32(v[256 + 16 * c : 272 + 16 * c, :]) for v in four)
        dst[0:16, :] = bf(total)
        for b, v in enumerate(four):
            rows = pl.ds(pl.multiple_of(16 + 16 * jnp.bitwise_xor(info[6], b), 16), 16)
            dst[rows, :] = v[288 + 16 * c : 304 + 16 * c, :]

    @pl.when(info[2] == 0)
    def _():
        fill(0)

    @pl.when(info[2] == 1)
    def _():
        fill(1)


def pile_body(*refs):
    dst = refs[-1]
    for n, src in enumerate(refs[:-1]):
        dst[n] = src[...]


def clear_early(*refs):
    for ref in refs[3:7]:
        ref[...] = jnp.zeros_like(ref)


def expand_early_body(info, own, oth, r1, e2, e1, r2):

    def fill(src, shared, split):
        for n in range(own.shape[0]):
            group = info[5] if n % 2 == 0 else 1 - info[5]
            a = info[40 + n // 2 * GROUPS_DEV + group]
            shared[a] += f32(src[n, 0:16, :])
            for j in range(COLS):
                at = 16 + 16 * j
                split[a, :, cols(j, 1024)] += f32(src[n, at : at + 16, :])

    @pl.when(info[2] == 0)
    def _():
        fill(own, r1, e1)
        fill(oth, e2, r2)

    @pl.when(info[2] == 1)
    def _():
        fill(oth, r1, e1)
        fill(own, e2, r2)


def expand_late_body(info, v0, v1, v2, v3, qr, pe, qe, pr):
    four = (v0, v1, v2, v3)
    for v in (qr, pe, qe, pr):
        v[...] = jnp.zeros_like(v)
    for k in range(v0.shape[0]):
        group = info[5] if k % 2 == 0 else 1 - info[5]
        a = info[40 + k // 2 * GROUPS_DEV + group]
        qr[a] += sum(f32(v[k, 0:16, :]) for v in four)
        pe[a] += sum(f32(v[k, 16:32, :]) for v in four)
        for b, v in enumerate(four):
            j = jnp.bitwise_xor(info[6], b)
            qe[a, :, lanes_at(j * 768, 768)] += f32(v[k, 32:48, :768])
            pr[a, :, lanes_at(j * 256, 256)] += f32(v[k, 32:48, 768:])


def shift(v, k, axis="row"):
    if k == 0:
        return v
    size = lax.axis_size(axis)
    return lax.ppermute(v, axis, [(s, (s + k) % size) for s in range(size)])


def gather_row(v):
    return [v] + [shift(v, k) for k in range(1, ROWS)]


def gather_col(v):
    core = lax.ppermute(v, "col", CORE_SWAP)
    side = lax.ppermute(v, "col", Y_SWAP)
    return [v, core, side, lax.ppermute(side, "col", CORE_SWAP)]


def to_cols(pieces):
    return [pieces[0]] + [shift(pieces[k], ROWS - k) for k in range(1, ROWS)]


def spread(mine, other):
    return [mine, other] + [
        shift(v, k, "dp") for k in range(1, lax.axis_size("dp")) for v in (mine, other)
    ]


def pile(parts):
    shape = (len(parts), *parts[0].shape)
    return call(pile_body, [out(shape, BF)], parts, smem=0, us=0.01, name="pile")[0]

def body(
    hidden_in,
    out_grad,
    first_norm_gain,
    first_norm_bias,
    qkv_weight,
    qkv_bias,
    proj_weight,
    proj_bias,
    second_norm_gain,
    second_norm_bias,
    fc1_weight,
    fc1_bias,
    fc2_weight,
    second_feed_bias,
    qkv_reduce,
    qkv_expand,
    proj_reduce,
    proj_expand,
    fc1_reduce,
    fc1_expand,
    fc2_reduce,
    fc2_expand,
    adapter_choice,
    cont_prompt,
):
    r = lax.axis_index("row")
    col = lax.axis_index("col")
    dp = lax.axis_index("dp")
    y = col // 2
    c = lax.rem(col, 2)
    zl = lax.rem(r, 2)
    group = r // 2
    half = lax.rem(dp, 2)
    dp_swap = [(k, k ^ 1) for k in range(lax.axis_size("dp"))]
    slopes = jnp.exp2(
        -8.0 * (col * 4 + 1 + jnp.arange(4, dtype=jnp.int32)).astype(F32) / HEADS
    )
    adapter = jnp.where(group == 0, adapter_choice[0], adapter_choice[1])
    dp_size = jnp.int32(lax.axis_size("dp"))
    info = jnp.stack([r, y, c, dp * GROUPS_DEV, zl, group, col, dp, half] + [half, dp_size] + [half] * 5)
    info = jnp.concatenate([info.astype(jnp.int32), cont_prompt, adapter_choice])
    order = pltpu.SMEM((GROUPS_DEV * NCONT,), jnp.int32)
    flip = functools.partial(jnp.transpose, axes=(0, 2, 1))
    big = out((TOK, D), BF)
    small = out((RANK, D), F32)

    other = lax.ppermute(hidden_in, "col", CORE_SWAP)
    vectors = [
        first_norm_gain, first_norm_bias, proj_bias,
        second_norm_gain, second_norm_bias, second_feed_bias,
    ]
    factors = [flip(qkv_reduce), flip(fc1_reduce), proj_expand, fc2_expand]
    pieces = call(
        route_pack_body,
        [out((336, TOK), BF)] * 4,
        [info, Far(hidden_in), Far(other), *far(vectors), *far(factors)],
        [
            order,
            *[pltpu.VMEM((TOK,), BF)] * 6,
            pltpu.VMEM((16, RANK, TOK), BF),
            pltpu.SemaphoreType.DMA((22,)),
        ],
        raw=range(3, 13),
        pre=route_pack_pre,
        us=1.5,
        name="route_x",
    )
    xs = [pieces[0]] + [shift(pieces[k], k) for k in range(1, ROWS)]
    packs = far(xs)
    first_half, w1_copies, qkv_e, fc1_e, proj_r, fc2_r = call(
        prepare_body,
        [
            out((128, D), BF), out((ROWS, 128, D), BF),
            out((RANK, 768), BF), out((RANK, D), BF), out((RANK, TOK), BF), out((RANK, D), BF),
        ],
        [
            after(info, pieces[0]),
            *far([qkv_weight, proj_weight, fc1_weight, qkv_expand, fc1_expand]),
            *far([flip(proj_reduce), flip(fc2_reduce)]),
        ],
        [pltpu.SemaphoreType.DMA((10,))],
        raw=range(1, 8),
        us=3,
        name="prepare",
    )
    first_half = after(first_half, xs[1])
    z_parts = [shift(first_half, k) for k in range(1, ROWS)]
    s_parts = [lax.ppermute(v, "dp", dp_swap) for v in z_parts]
    wq, wp = call(
        assemble_body,
        [out((ROWS, TOK, 768), BF), out((ROWS, TOK, TOK), BF)],
        [info, *far([qkv_weight, proj_weight, *z_parts, *s_parts])],
        [pltpu.SemaphoreType.DMA((14,))],
        raw=range(1, 9),
        us=15,
        name="assemble",
    )

    qkv_b = lax.dynamic_slice_in_dim(qkv_bias, col * 768, 768, 0)[None, :]
    fc1_b = lax.dynamic_slice_in_dim(fc1_bias, col * 1024, 1024, 0)[None, :]

    choices = [adapter_choice] + [
        shift(adapter_choice, k, "dp") for k in range(1, lax.axis_size("dp"))
    ]
    first = after(xs[0], qkv_b, fc1_b, w1_copies, *choices)
    (xn1,) = call(norm1_body, [big], [first, *xs[1:]], smem=0, us=8, name="norm1")
    xn1s = gather_col(xn1)
    q, kvp, kvc = call(
        qkv_body,
        [out((1024, 256), BF), out((512, 512), BF), out((512, 512), BF)],
        [info, *xn1s, wq, *packs, Far(qkv_b), Far(qkv_e)],
        us=6.5,
        name="qkv",
    )
    kvo = lax.ppermute(kvp, "row", Z_SWAP)

    g_other = lax.ppermute(after(out_grad, kvp), "col", CORE_SWAP)
    (pieces,) = call(
        route_all_body,
        [out((ROWS, 3 * TOK, TOK), BF)],
        [info, Far(out_grad), Far(g_other), Far(fc2_weight)],
        [order, pltpu.SemaphoreType.DMA((4,))],
        raw=(3,),
        us=1,
        name="route_g",
    )
    (state,) = call(
        attend_first_body,
        [out((2048, 256), F32)],
        [info, slopes, q, kvp, kvc],
        smem=2,
        us=9,
        name="attend_first",
    )
    (w1r,) = call(
        rest_body,
        [out((3, 128, D), BF)],
        [info, after(lax.all_to_all(after(w1_copies, *z_parts), "row", 0, 0), state)],
        us=0.01,
        name="rest",
    )
    w1s = lax.ppermute(w1r, "dp", dp_swap)
    pieces = after(pieces, state, kvo)
    g_own, w2r = call(
        join_body,
        [big, out((3, 512, TOK), BF)],
        [info, lax.all_to_all(pieces, "row", 0, 0)],
        us=0.01,
        name="join",
    )
    g_side = lax.ppermute(g_own, "col", Y_SWAP)
    w2s = lax.ppermute(w2r, "dp", dp_swap)

    def attend_rest(which, q, state):
        return call(
            functools.partial(attend_rest_body, which),
            [out((512, 256), BF), out((8, 256), F32), big, big],
            [info, slopes, Far(q), kvo, state, Far(wp), Far(proj_r), *packs],
            smem=2,
            us=20 if which else 0.01,
            name="attend_rest",
        )

    heads1, lse1, p2, p3 = attend_rest(1, q, after(state, w1r))
    g_core = lax.ppermute(g_own, "col", CORE_SWAP)
    g_all = [g_own, g_core, g_side, lax.ppermute(g_side, "col", CORE_SWAP)]
    p_far = lax.ppermute(p3, "col", CORE_SWAP)
    p_side = add(p2, p_far)
    heads0, lse0, p0, p1 = attend_rest(0, q, Far(after(state, p_side)))
    p_side = lax.ppermute(p_side, "col", Y_SWAP)
    p_core = lax.ppermute(p1, "col", CORE_SWAP)
    staged = stage([after(xs[0], p0), *xs[1:]])
    mid, xn2 = call(
        norm2_body,
        [out((TOK, D), F32), big],
        [add32(after(p0, w1s), p_side), p_core, *staged],
        smem=0,
        us=1.5,
        hbm=(0,),
        name="norm2",
    )
    (w1,) = call(
        functools.partial(stage_weight_body, 128),
        [out((ROWS, TOK, D), BF)],
        [info, Far(fc1_weight), Far(after(w1r, p0)), Far(w1s)],
        [pltpu.SemaphoreType.DMA((7,))],
        raw=(1, 2, 3),
        us=2,
        name="stage_w1",
    )
    zero = jnp.zeros((RANK, D), F32)
    xn2_core = lax.ppermute(xn2, "col", CORE_SWAP)
    xn2_side = lax.ppermute(xn2, "col", Y_SWAP)

    def mlp_pre(first, blocks):
        return call(
            mlp_pre_body,
            [out((2, TOK, D), BF)] * 2,
            [info, *blocks, w1, *staged, Far(fc1_b), Far(fc1_e)],
            us=0.01,
            name="mlp_pre",
        )

    act0, slope0 = mlp_pre(0, [xn2, xn2_core])
    xn2_far = lax.ppermute(after(xn2_side, act0), "col", CORE_SWAP)
    xn2s = [xn2, xn2_core, xn2_side, xn2_far]
    act1, slope1 = mlp_pre(1, xn2s[2:])
    (w2,) = call(
        functools.partial(stage_weight_body, 512),
        [out((ROWS, D, TOK), BF)],
        [info, Far(fc2_weight), Far(after(w2r, act0)), Far(w2s)],
        [pltpu.SemaphoreType.DMA((7,))],
        raw=(1, 2, 3),
        us=20,
        name="stage_w2",
    )

    def mlp_back(blocks, slope, r_in, e_in):
        xa, xb = (xn2s[b] for b in blocks)
        ga, gb = (g_all[b] for b in blocks)
        return call(
            mlp_back_body,
            [big, big, small, small],
            [info, xa, xb, ga, gb, slope, w1, w2, *staged, Far(fc1_e), Far(fc2_r), r_in, e_in],
            us=0.01,
            name="mlp_back",
        )

    d2, d3, r1, e1 = mlp_back((2, 3), slope1, zero, zero)
    d_far = lax.ppermute(d3, "col", CORE_SWAP)
    d_side = add(d2, d_far)
    d0, d1, r1, e1 = mlp_back((0, 1), slope0, after(r1, d_side), e1)
    d_side = lax.ppermute(d_side, "col", Y_SWAP)
    d_core = lax.ppermute(d1, "col", CORE_SWAP)
    res = call(
        fc2_body,
        [big] * 4 + [out((64, D), BF)],
        [info, act0, act1, *g_all, w2, Far(fc2_r), *staged, r1, e1],
        us=0.01,
        name="fc2",
    )
    m_parts, mlp_pack = res[:4], res[4]
    staged_back = stage([after(mid, mlp_pack), g_own, *xs])
    d_mid, g_attn = call(
        norm2_back_body,
        [out((TOK, D), F32), out((320, D), BF)],
        [add32(d0, d_side), d_core, mlp_pack, *staged_back],
        smem=0,
        us=1.5,
        hbm=(0,),
        name="norm2_back",
    )
    ga_core = lax.ppermute(g_attn, "col", CORE_SWAP)
    ga_side = lax.ppermute(g_attn, "col", Y_SWAP)
    shared = far([q, kvp, kvo, kvc])

    def d_heads(blocks, heads, r_in, e_in):
        return call(
            d_heads_body,
            [out((512, 256), BF), out((RANK, TOK), F32), small],
            [info, *blocks, Far(wp), *packs, Far(proj_r), Far(heads), r_in, e_in],
            us=1.5,
            name="d_heads",
        )

    dh0, pr, pe = d_heads([g_attn, ga_core], heads0, jnp.zeros((RANK, TOK), F32), zero)
    dq0, dkp, dko, dkc = call(
        attend_back_a_body,
        [out((512, 256), BF), out((512, 512), F32), out((512, 512), F32), out((512, 512), BF)],
        [info, slopes, *shared, Far(heads0), dh0, Far(lse0)],
        smem=2,
        us=16,
        weight=W_BIG,
        hbm=(1, 2, 3),
        pre=clear_back,
        name="attend_back_a",
    )
    ga_side = after(ga_side, dq0)
    ga_far = lax.ppermute(ga_side, "col", CORE_SWAP)
    (early_half,) = call(
        merge_body,
        [out((80, D), BF)],
        [info, g_attn, ga_core, ga_side, ga_far],
        us=0.7,
        name="merge",
    )
    dh1, pr, pe = d_heads([ga_side, ga_far], heads1, pr, pe)
    dq1_part, dko = call(
        attend_back_b_body,
        [out((512, 256), F32), out((672, 512), BF)],
        [info, slopes, Far(q), Far(kvo), Far(heads1), dh1, Far(lse1), Far(dko), early_half],
        [pltpu.VMEM((512, 512), F32)],
        smem=2,
        us=8,
        hbm=(0,),
        name="attend_back_b",
    )
    dkr = lax.ppermute(dko, "row", Z_SWAP)
    dq1, dkp, dkc = call(
        attend_back_c_body,
        [out((512, 256), BF), out((512, 512), F32), out((512, 512), BF)],
        [info, slopes, Far(q), Far(kvp), Far(kvc), Far(heads1), dh1, Far(lse1), *far([dkp, dkc, dq1_part])],
        smem=2,
        us=8,
        hbm=(2,),
        name="attend_back_c",
    )
    (early_sum,) = call(
        early_sum_body, [out((80, D), BF)], [early_half, dkr], smem=0, us=0.01, name="early_sum"
    )
    m_far = lax.ppermute(after(m_parts[3], dq0), "col", CORE_SWAP)
    m_core = lax.ppermute(after(m_parts[1], dq0), "col", CORE_SWAP)
    m_sum = add(after(m_parts[2], dko), m_far)
    m_side = lax.ppermute(m_sum, "col", Y_SWAP)
    hidden = call(
        hidden_body,
        [out((TOK, TOK), BF)] * 4,
        [add32(m_parts[0], m_side, 0.01), m_core, Far(mid), *packs],
        smem=0,
        us=0.01,
        name="hidden",
    )
    res = call(
        qkv_back_body,
        [big] * 4 + [out((48, D), BF)],
        [
            info, dq0, dq1, dkp, after(dkr, early_sum, hidden[0]), Far(dkc),
            *far(xn1s), Far(wq), *packs, Far(qkv_e), pr, pe,
        ],
        us=20,
        name="qkv_back",
    )
    q_parts, late_pack = res[:4], res[4]
    early_next = shift(early_sum, 2)
    n_dp = lax.axis_size("dp")
    early_mine = [early_sum] + [shift(early_sum, k, "dp") for k in range(1, n_dp)]
    ready = after(q_parts[3], m_side, early_next, *early_mine)
    q_sum = add(q_parts[2], lax.ppermute(ready, "col", CORE_SWAP))
    hidden_got = to_cols(hidden)
    k0, rc = q_parts[0], lax.ppermute(q_parts[1], "col", CORE_SWAP)
    ry = lax.ppermute(q_sum, "col", Y_SWAP)
    late_sum = add(late_pack, lax.ppermute(after(late_pack, q_sum), "row", Z_SWAP))
    late_next = shift(late_sum, 2)
    early_rest = after(early_next, late_sum)
    early_rest = [early_next] + [shift(early_rest, k, "dp") for k in range(1, n_dp)]
    early_parts = [v for pair in zip(early_mine, early_rest) for v in pair]
    late_four = pile(spread(late_sum, late_next))
    late_all = gather_col(late_four)
    staged_last = stage([after(d_mid, k0, rc), *xs])
    ins = call(
        norm1_back_body,
        [out((TOK, TOK), BF)] * 4,
        [add32(after(k0, late_next, *hidden_got), ry), rc, *staged_last],
        smem=0,
        us=1,
        name="norm1_back",
    )
    early_all = pile(early_parts)
    early_far = lax.ppermute(after(early_all, ins[0]), "col", CORE_SWAP)
    table = jnp.concatenate([info, jnp.zeros((40 - 34,), jnp.int32), *choices])
    o_fc1r, o_f2e, o_f1e, o_f2r = call(
        expand_early_body,
        [out((COUNT, RANK, w), F32) for w in (1024, 1024, 4096, 4096)],
        [table, Far(early_all), Far(early_far)],
        us=0.01,
        pre=clear_early,
        name="expand_early",
    )
    (joined,) = call(
        stack_body,
        [out((8 * TOK, TOK), BF)],
        [*[after(v, o_fc1r, late_all[2]) for v in to_cols(ins)], *hidden_got],
        smem=0,
        us=0.01,
        name="stack",
    )
    input_gradient, hidden_out = call(
        unroute_body,
        [out((1024, TOK), F32), out((1024, TOK), BF)],
        [info, joined, lax.ppermute(joined, "col", CORE_SWAP)],
        [order],
        us=2,
        name="unroute",
    )
    o_qr, o_pe, o_qe, o_pr = call(
        expand_late_body,
        [out((COUNT, RANK, w), F32) for w in (1024, 1024, 3072, 1024)],
        [table, *late_all],
        us=0.01,
        name="expand_late",
    )
    return (
        hidden_out,
        input_gradient,
        flip(o_qr),
        o_qe,
        flip(o_pr),
        o_pe,
        flip(o_fc1r),
        o_f1e,
        flip(o_f2r),
        o_f2e,
    )


def solution(mesh):
    placed = (
        P(("dp", "col"), "row"),
        P(("dp", "col"), "row"),
        P("row"),
        P("row"),
        P("row", "col"),
        P(),
        P("col", "row"),
        P("row"),
        P("row"),
        P("row"),
        P("row", "col"),
        P(),
        P("col", "row"),
        P("row"),
        P(None, "row", None),
        P(),
        P(None, "col", None),
        P(None, None, "row"),
        P(None, "row", None),
        P(),
        P(None, "col", None),
        P(None, None, "row"),
        P("dp"),
        P("dp"),
    )
    return jax.shard_map(
        body,
        mesh=mesh,
        in_specs=placed,
        out_specs=(P(("dp", "col"), "row"), P(("dp", "col"), "row")) + (P(),) * 8,
        check_vma=False,
    )
```
